32 devices in a mesh: dp: 16 (over z, y, x), head: 2 (over core).
Axes of the slice: x: 2, y: 2, z: 4, core: 2. Of those that a mesh axis runs over, the one named last changes fastest.
Arguments:
- tokens: bfloat16 [16, 1024, 1024], P('dp', 'head'), may hold values from -6 to 6
- lengths: int32 [16], P('dp'), may hold values from 193 to 1024, as said below
- initial_memory: float32 [16, 4, 128, 256], P('dp', 'head'), may hold values from -12 to 12
- norm_attn_gain: float32 [1024], replicated, may hold values from 0.1 to 1.9
- w_query: bfloat16 [1024, 512], P(None, 'head'), may hold values from -0.1875 to 0.1875
- w_key: bfloat16 [1024, 512], P(None, 'head'), may hold values from -0.1875 to 0.1875
- w_value: bfloat16 [1024, 1024], P(None, 'head'), may hold values from -0.1875 to 0.1875
- w_gate_out: bfloat16 [1024, 1024], P(None, 'head'), may hold values from -0.1875 to 0.1875
- w_low_in: bfloat16 [1024, 16], replicated, may hold values from -0.1875 to 0.1875
- w_low_out: bfloat16 [16, 512], P(None, 'head'), may hold values from -1.5 to 1.5
- decay_bias: float32 [512], P('head'), may hold values from -1 to 6
- out_gain: float32 [256], replicated, may hold values from 0.1 to 1.9
- w_out: bfloat16 [1024, 1024], P('head'), may hold values from -0.1875 to 0.1875
- norm_mlp_gain: float32 [1024], replicated, may hold values from 0.1 to 1.9
- w_mlp: bfloat16 [1024, 8448], P(('dp', 'head')), may hold values from -0.1875 to 0.1875
- cotangent: bfloat16 [16, 1024, 1024], P('dp', 'head'), may hold values from -6 to 6
Outputs:
- output: bfloat16 [16, 1024, 1024], P('dp', 'head')
- grad_tokens: float32 [16, 1024, 1024], P('dp', 'head')
- grad_norm_attn_gain: float32 [1024], replicated
- grad_w_query: float32 [1024, 512], P('dp', 'head')
- grad_w_key: float32 [1024, 512], P('dp', 'head')
- grad_w_value: float32 [1024, 1024], P('dp', 'head')
- grad_w_gate_out: float32 [1024, 1024], P('dp', 'head')
- grad_w_low_in: float32 [1024, 16], replicated
- grad_w_low_out: float32 [16, 512], P(None, 'head')
- grad_decay_bias: float32 [512], P('head')
- grad_out_gain: float32 [256], replicated
- grad_w_out: float32 [1024, 1024], P('head', 'dp')
- grad_norm_mlp_gain: float32 [1024], replicated
- grad_w_mlp: float32 [1024, 8448], P(('dp', 'head'))
The draws below stay inside these ranges and needn't reach their ends.
Inputs may be any that keep to these rules, and one draw needn't show every extreme that they name: lengths holds each sequence's number of valid leading positions; later positions are padding. In every draw one sequence fills all 1024 positions.
All inputs are finite; a program needn't handle non-finite values.
Results may differ from the reference program's by a relative error of at most 0.017.
Values may be sent and summed in bfloat16 or wider, within the bound.
A program may use at most 256 MiB of HBM per device.

```python
import jax
import jax.numpy as jnp
from jax import lax

D = 1024
HEADS = 4
KEY = 512
VALUE = 1024
FF = 2816
LOWRANK = 16
BLOCK = 64
SEQ = 1024
SEQS = 16


def draw_lengths(key, part):
    key_scale, key_offset, key_place = jax.random.split(key, 3)
    levels = jnp.minimum(jax.random.randint(key_scale, (SEQS,), 0, 4), 2)
    offsets = jax.random.randint(key_offset, (SEQS,), 0, SEQ // 4)
    drawn = jnp.right_shift(jnp.full((SEQS,), SEQ, jnp.int32), levels) - jnp.right_shift(offsets, levels)
    where_full = jax.random.randint(key_place, (), 0, SEQS)
    drawn = drawn.at[where_full].set(SEQ)
    drawn = drawn.at[(where_full + 1) % SEQS].set(3 * SEQ // 16 + 1)
    return drawn.astype(jnp.int32)


def spiked(values, key, source, target, parts, factor):
    def block_of(dim):
        return (jnp.arange(values.shape[dim]) // (values.shape[dim] // parts)).reshape((-1,) + (1,) * (values.ndim - 1 - dim))

    first = jax.random.permutation(key, parts)[block_of(target)]
    second = (block_of(target) + parts // 2) % parts
    return jnp.where((block_of(source) == first) | (block_of(source) == second), factor * values, values)


def block_scale(own_key, shape, pieces, smallest, top_value):
    gain = 1.0
    for position, shards_of in pieces:
        heights = jax.random.uniform(jax.random.fold_in(jax.random.fold_in(own_key, 6), position), (shards_of,), jnp.float32, smallest / len(pieces), top_value / len(pieces))
        gain = gain * jnp.repeat(jnp.exp(heights), shape[position] // shards_of).reshape((-1,) + (1,) * (len(shape) - 1 - position))
    return gain


def normal_values(key, dims, deviation, bound, cuts=(), kind=jnp.bfloat16):
    factor_of = block_scale(key, dims, cuts, -0.22, 0.18) if cuts else 1.0
    array = jax.random.normal(key, dims, jnp.float32) * deviation * factor_of
    return jnp.minimum(jnp.maximum(array, -bound), bound).astype(kind)


def gaussian_with(stream_key, shape, spread, most, pieces, heavy, held_as=jnp.bfloat16):
    entries = spread * jax.random.normal(stream_key, shape, jnp.float32)
    if pieces:
        entries = entries * block_scale(stream_key, shape, pieces, -0.22, 0.18)
    return jnp.clip(spiked(entries, jax.random.fold_in(stream_key, 3), *heavy), -most, most).astype(held_as)


def setup_inputs(seed: int = 0) -> dict:
    seeds = jax.random.split(jax.random.key(seed), 17)
    tokens = normal_values(seeds[0], (SEQS, SEQ, D), 1.0, 6.0, ((0, 16), (1, 2)))
    lengths = draw_lengths(jax.random.fold_in(seeds[16], 71), 0)
    initial_memory = normal_values(seeds[2], (SEQS, HEADS, KEY // HEADS, VALUE // HEADS), 2.0, 12.0, ((0, 16), (1, 2)), jnp.float32)
    norm_attn_gain = jnp.clip(1.0 + 0.18 * jax.random.normal(seeds[3], (D,), jnp.float32), 0.1, 1.9)
    w_query = normal_values(seeds[4], (D, KEY), D ** -0.5, 0.1875, ((1, 2),))
    w_key = normal_values(seeds[5], (D, KEY), D ** -0.5, 0.1875, ((1, 2),))
    w_value = normal_values(seeds[6], (D, VALUE), D ** -0.5, 0.1875, ((1, 2),))
    w_gate_out = normal_values(seeds[7], (D, VALUE), D ** -0.5, 0.1875, ((1, 2),))
    w_low_in = normal_values(seeds[8], (D, LOWRANK), D ** -0.5, 0.1875)
    w_low_out = normal_values(seeds[9], (LOWRANK, KEY), LOWRANK ** -0.5, 1.5, ((1, 2),))
    decay_bias = jnp.clip(-1.0 + 7.0 * jax.random.uniform(seeds[10], (KEY,), jnp.float32) ** block_scale(seeds[10], (KEY,), ((0, 2),), -0.2, 0.2), -1.0, 6.0)
    out_gain = jnp.clip(1.0 + 0.18 * jax.random.normal(seeds[11], (VALUE // HEADS,), jnp.float32), 0.1, 1.9)
    w_out = normal_values(seeds[12], (VALUE, D), VALUE ** -0.5, 0.1875, ((0, 2),))
    norm_mlp_gain = jnp.clip(1.0 + 0.18 * jax.random.normal(seeds[13], (D,), jnp.float32), 0.1, 1.9)
    w_mlp = normal_values(seeds[14], (D, 3 * FF), D ** -0.5, 0.1875, ((0, 32),))
    cotangent = gaussian_with(seeds[15], (SEQS, SEQ, D), 1.0, 6.0, ((0, 16), (1, 2)), (0, 2, 16, 2.0))
    return {"tokens": tokens, "lengths": lengths, "initial_memory": initial_memory, "norm_attn_gain": norm_attn_gain, "w_query": w_query, "w_key": w_key, "w_value": w_value, "w_gate_out": w_gate_out, "w_low_in": w_low_in, "w_low_out": w_low_out, "decay_bias": decay_bias, "out_gain": out_gain, "w_out": w_out, "norm_mlp_gain": norm_mlp_gain, "w_mlp": w_mlp, "cotangent": cotangent}


EPSILON = 1e-05
HIGHEST = lax.Precision.HIGHEST

@jax.custom_vjp
def low(v):
    return lax.optimization_barrier(v.astype(jnp.bfloat16)).astype(jnp.float32)

@jax.custom_vjp
def low_back(v):
    return v

def low_keep(v):
    return (low(v), None)

def low_pass(kept, grad):
    return (grad,)

def back_keep(v):
    return (v, None)

def back_low(kept, grad):
    return (low(grad),)
low.defvjp(low_keep, low_pass)
low_back.defvjp(back_keep, back_low)

def normalize(values_in):
    return values_in * lax.rsqrt(lax.optimization_barrier(jnp.mean(values_in * values_in, axis=-1, keepdims=True)) + EPSILON)

def product(left, right):
    return jnp.dot(left, right, precision=HIGHEST)

def gated_linear_attention(query_in, key_in, value_in, log_decay, initial):
    heads_here, length, key_width = query_in.shape
    value_width = value_in.shape[2]
    blocks_count = length // BLOCK

    def to_blocks(tensor):
        return tensor.reshape(heads_here, blocks_count, BLOCK, tensor.shape[2])
    query_blocks = to_blocks(query_in)
    key_blocks = to_blocks(key_in)
    value_blocks = to_blocks(value_in)
    cumulative = jnp.cumsum(to_blocks(log_decay), axis=2)
    block_end = cumulative[:, :, BLOCK - 1:, :]
    query_scaled = query_blocks * jnp.exp(cumulative) * key_width ** (-0.5)
    key_early = key_blocks * jnp.exp(-cumulative)
    key_late = key_blocks * jnp.exp(block_end - cumulative)
    causal = (lax.iota(jnp.int32, BLOCK)[:, None] >= lax.iota(jnp.int32, BLOCK)[None, :]).astype(jnp.float32)
    scores = jnp.einsum('hncd,hned->hnce', query_scaled, key_early, precision=HIGHEST) * causal
    within = jnp.einsum('hnce,hnev->hncv', scores, value_blocks, precision=HIGHEST)
    decay_end = jnp.exp(block_end[:, :, 0, :])

    def advance(memory, block_parts):
        query_part, key_part, value_part, decay_part = block_parts
        carried = jnp.einsum('hcd,hdv->hcv', query_part, memory, precision=HIGHEST)
        memory = decay_part[:, :, None] * memory + jnp.einsum('hcd,hcv->hdv', key_part, value_part, precision=HIGHEST)
        return (memory, carried)
    moved = (jnp.moveaxis(query_scaled, 1, 0), jnp.moveaxis(key_late, 1, 0), jnp.moveaxis(value_blocks, 1, 0), jnp.moveaxis(decay_end, 1, 0))
    final_memory, carried = lax.scan(jax.checkpoint(advance), initial, moved)
    return (within + jnp.moveaxis(carried, 0, 1)).reshape(heads_here, length, value_width)

def sublayer(tokens_in, mask_in, memory_in, params):
    gain_one, w_query, w_key, w_value, w_gate_out, w_low_in, w_low_out, decay_bias, out_gain, w_out, gain_two, w_mlp = params
    groups, length, width = tokens_in.shape
    h_low = low(normalize(tokens_in) * gain_one)
    query_all = low(low_back(product(h_low, w_query)))
    key_all = low(low_back(product(h_low, w_key)))
    value_all = low(low_back(product(h_low, w_value)))
    gate_all = low_back(product(h_low, w_gate_out))
    low_rank = low_back(product(h_low, w_low_in))
    logits = product(low_rank, w_low_out) + decay_bias
    log_decay = jax.nn.log_sigmoid(logits) / 16.0

    def split_heads(tensor):
        return tensor.reshape(groups, length, HEADS, -1).transpose(0, 2, 1, 3)
    attended = jax.vmap(gated_linear_attention)(split_heads(query_all), split_heads(key_all), split_heads(value_all), split_heads(log_decay), memory_in)
    normed = normalize(attended) * out_gain
    gate_heads = split_heads(gate_all)
    mixed = low((normed * jax.nn.silu(gate_heads)).transpose(0, 2, 1, 3).reshape(groups, length, VALUE))
    attn = low_back(product(mixed, w_out))
    resid = tokens_in + attn
    h_two = low(normalize(resid) * gain_two)
    pre_gate = low_back(product(h_two, w_mlp[:, :FF]))
    up_part = low_back(product(h_two, w_mlp[:, FF:2 * FF]))
    inner = low(jax.nn.silu(pre_gate) * up_part)
    mlp_out = low_back(jnp.einsum('gsf,df->gsd', inner, w_mlp[:, 2 * FF:], precision=HIGHEST))
    return mask_in[:, :, None] * (resid + mlp_out)

def reference(tokens, lengths, initial_memory, norm_attn_gain, w_query, w_key, w_value, w_gate_out, w_low_in, w_low_out, decay_bias, out_gain, w_out, norm_mlp_gain, w_mlp, cotangent):
    wide = jnp.float32
    params = (norm_attn_gain.astype(wide), w_query.astype(wide), w_key.astype(wide), w_value.astype(wide), w_gate_out.astype(wide), w_low_in.astype(wide), w_low_out.astype(wide), decay_bias.astype(wide), out_gain.astype(wide), w_out.astype(wide), norm_mlp_gain.astype(wide), w_mlp.astype(wide))
    positions = jnp.arange(SEQ, dtype=jnp.int32)
    mask_all = (positions[None, :] < lengths[:, None]).astype(wide)
    memory_all = initial_memory.astype(wide)

    def forward(tokens_in, weights_in):

        def one_group(carry_value, group_parts):
            return (carry_value, jax.checkpoint(sublayer)(group_parts[0], group_parts[1], group_parts[2], weights_in))
        init_value = jnp.zeros((), wide)
        grouped = (tokens_in.reshape(SEQS // 4, 4, SEQ, D), mask_all.reshape(SEQS // 4, 4, SEQ), memory_all.reshape(SEQS // 4, 4, HEADS, KEY // HEADS, VALUE // HEADS))
        final_value, results = lax.scan(one_group, init_value, grouped)
        return results.reshape(SEQS, SEQ, D)
    output_full, backward = jax.vjp(forward, tokens.astype(wide), params)
    tokens_grad, weight_grads = backward(cotangent.astype(wide))
    return (output_full.astype(jnp.bfloat16), tokens_grad, weight_grads[0], weight_grads[1], weight_grads[2], weight_grads[3], weight_grads[4], weight_grads[5], weight_grads[6], weight_grads[7], weight_grads[8], weight_grads[9], weight_grads[10], weight_grads[11])
```

```python
import functools

import jax
import jax.numpy as jnp
from jax import lax
from jax.experimental import pallas as pl
from jax.experimental.pallas import tpu as pltpu
from jax.sharding import PartitionSpec as P

HEADS = 4
KEY = 512
VALUE = 1024
BLOCK = 128
KEY_HEAD = KEY // HEADS
VALUE_HEAD = VALUE // HEADS

EPSILON = 1e-05
F32 = jnp.float32
BF16 = jnp.bfloat16
SCALE = KEY_HEAD ** (-0.5)


def dot(left, right, left_dim=1, right_dim=0):
    return lax.dot_general(
        left, right, (((left_dim,), (right_dim,)), ((), ())), preferred_element_type=F32
    )


def split_low(value):
    high = value.astype(BF16)
    return high, (value - high.astype(F32)).astype(BF16)


def sigmoid(value):
    return 1.0 / (1.0 + jnp.exp(-value))


def log_sigmoid(value):
    return jnp.minimum(value, 0.0) - jnp.log1p(jnp.exp(-jnp.abs(value)))


def triangle(lower):
    rows = lax.broadcasted_iota(jnp.int32, (BLOCK, BLOCK), 0)
    columns = lax.broadcasted_iota(jnp.int32, (BLOCK, BLOCK), 1)
    return rows >= columns if lower else rows <= columns


def decay_terms(logits):
    log_decay = log_sigmoid(logits) * (1.0 / 16.0)
    ones = jnp.where(triangle(True), 1.0, 0.0).astype(BF16)
    high, low = split_low(log_decay)
    total = dot(ones, high) + dot(ones, low)
    middle = total[BLOCK // 2 - 1 : BLOCK // 2, :]
    end = total[BLOCK - 1 :, :]
    rise = jnp.exp(total - middle)
    fall = jnp.exp(middle - total)
    early = rise * (jnp.exp(middle) * SCALE)
    late = fall * jnp.exp(end - middle)
    return rise * SCALE, fall, early, late, jnp.exp(end)


def as_column(row, width):
    column = jnp.transpose(jnp.broadcast_to(row, (KEY_HEAD, KEY_HEAD)))
    return jnp.concatenate([column] * (width // KEY_HEAD), axis=1)


def forward_kernel(
    query_ref, key_ref, value_ref, logits_ref, gate_ref, gain_ref, start_ref,
    attended_ref, mixed_ref, states_ref, memory
):
    heads = start_ref.shape[0]

    @pl.when(pl.program_id(0) == 0)
    def _():
        memory[...] = start_ref[...]

    rise, fall, early, late, decay = decay_terms(logits_ref[...])
    lower = triangle(True)
    for head in range(heads):
        keys_at = slice(head * KEY_HEAD, (head + 1) * KEY_HEAD)
        values_at = slice(head * VALUE_HEAD, (head + 1) * VALUE_HEAD)
        query = query_ref[:, keys_at].astype(F32)
        key = key_ref[:, keys_at].astype(F32)
        value = value_ref[:, values_at]
        state = memory[head]
        state_low = state.astype(BF16)
        states_ref[0, head] = state_low
        scores = dot((query * rise[:, keys_at]).astype(BF16), (key * fall[:, keys_at]).astype(BF16), 1, 1)
        scores = jnp.where(lower, scores, 0.0).astype(BF16)
        left = jnp.concatenate([scores, (query * early[:, keys_at]).astype(BF16)], axis=1)
        attended = dot(left, jnp.concatenate([value, state_low], axis=0))
        memory[head] = as_column(decay[:, keys_at], VALUE_HEAD) * state + dot(
            (key * late[:, keys_at]).astype(BF16), value, 0, 0
        )
        attended_ref[:, values_at] = attended
        scale = lax.rsqrt(jnp.mean(attended * attended, axis=1, keepdims=True) + EPSILON)
        gate = gate_ref[:, values_at]
        mixed_ref[:, values_at] = (attended * scale * gain_ref[...] * gate * sigmoid(gate)).astype(BF16)


def attention_forward(query, key, value, logits, gate, gain, start):
    length, keys = query.shape
    values = value.shape[1]
    heads = start.shape[0]
    steps = length // BLOCK

    def rows(width):
        return pl.BlockSpec((BLOCK, width), lambda i: (i, 0))

    return pl.pallas_call(
        forward_kernel,
        grid=(steps,),
        in_specs=[
            rows(keys), rows(keys), rows(values), rows(keys), rows(values),
            pl.BlockSpec((1, VALUE_HEAD), lambda i: (0, 0)),
            pl.BlockSpec((heads, KEY_HEAD, VALUE_HEAD), lambda i: (0, 0, 0)),
        ],
        out_specs=[
            rows(values), rows(values),
            pl.BlockSpec((1, heads, KEY_HEAD, VALUE_HEAD), lambda i: (i, 0, 0, 0)),
        ],
        out_shape=[
            jax.ShapeDtypeStruct((length, values), F32),
            jax.ShapeDtypeStruct((length, values), BF16),
            jax.ShapeDtypeStruct((steps, heads, KEY_HEAD, VALUE_HEAD), BF16),
        ],
        scratch_shapes=[pltpu.VMEM((heads, KEY_HEAD, VALUE_HEAD), F32)],
        compiler_params=pltpu.CompilerParams(vmem_limit_bytes=48 << 20),
        name="attention_forward",
    )(query, key, value, logits, gate, gain.reshape(1, -1), start)


def backward_kernel(
    mixed_grad_ref, query_ref, key_ref, value_ref, logits_ref, gate_ref, attended_ref, states_ref, gain_ref,
    query_grad_ref, key_grad_ref, value_grad_ref, gate_grad_ref, logits_grad_ref, gain_grad_ref, memory_grad
):
    heads = memory_grad.shape[0]

    @pl.when(pl.program_id(0) == 0)
    def _():
        memory_grad[...] = jnp.zeros_like(memory_grad)
        gain_grad_ref[...] = jnp.zeros_like(gain_grad_ref)

    logits = logits_ref[...]
    rise, fall, early, late, decay = decay_terms(logits)
    lower = triangle(True)
    upper = triangle(False)
    last = lax.broadcasted_iota(jnp.int32, (BLOCK, KEY_HEAD), 0) == BLOCK - 1
    total_grads = []
    gain_grad = jnp.zeros((1, VALUE_HEAD), F32)
    for head in range(heads):
        keys_at = slice(head * KEY_HEAD, (head + 1) * KEY_HEAD)
        values_at = slice(head * VALUE_HEAD, (head + 1) * VALUE_HEAD)
        attended = attended_ref[:, values_at]
        scale = lax.rsqrt(jnp.mean(attended * attended, axis=1, keepdims=True) + EPSILON)
        normal = attended * scale
        gain = gain_ref[...]
        gate = gate_ref[:, values_at]
        gate_sigmoid = sigmoid(gate)
        mixed_grad = mixed_grad_ref[:, values_at]
        gate_grad_ref[:, values_at] = (
            mixed_grad * normal * gain * gate_sigmoid * (1.0 + gate * (1.0 - gate_sigmoid))
        ).astype(BF16)
        normed_grad = mixed_grad * gate * gate_sigmoid
        gain_grad += jnp.sum(normed_grad * normal, axis=0, keepdims=True)
        scaled = normed_grad * gain
        attended_grad = (
            scale * (scaled - normal * jnp.mean(scaled * normal, axis=1, keepdims=True))
        ).astype(BF16)

        query = query_ref[:, keys_at].astype(F32)
        key = key_ref[:, keys_at].astype(F32)
        value = value_ref[:, values_at]
        query_middle = query * rise[:, keys_at]
        key_middle = key * fall[:, keys_at]
        query_early = query * early[:, keys_at]
        key_late = key * late[:, keys_at]
        query_middle_low = query_middle.astype(BF16)
        key_middle_low = key_middle.astype(BF16)
        state = states_ref[0, head]
        after = memory_grad[head]
        after_low = after.astype(BF16)

        scores_turned = jnp.where(upper, dot(key_middle_low, query_middle_low, 1, 1), 0.0).astype(BF16)
        from_values = dot(attended_grad, jnp.concatenate([value, state], axis=0), 1, 1)
        to_values = jnp.concatenate([attended_grad, after_low], axis=0)
        from_grads = dot(value, to_values, 1, 1)
        scores_grad = jnp.where(lower, from_values[:, :BLOCK], 0.0).astype(BF16)
        scores_grad_turned = jnp.where(upper, from_grads[:, :BLOCK], 0.0).astype(BF16)
        query_early_grad = from_values[:, BLOCK:]
        key_late_grad = from_grads[:, BLOCK:]
        query_middle_grad = dot(scores_grad, key_middle_low)
        key_middle_grad = dot(scores_grad_turned, query_middle_low)
        value_grad_ref[:, values_at] = dot(
            jnp.concatenate([scores_turned, key_late.astype(BF16)], axis=1), to_values
        ).astype(BF16)
        decay_column = as_column(decay[:, keys_at], VALUE_HEAD)
        carried = decay_column * after
        memory_grad[head] = carried + dot(query_early.astype(BF16), attended_grad, 0, 0)

        query_grad_ref[:, keys_at] = (
            query_early_grad * early[:, keys_at] + query_middle_grad * rise[:, keys_at]
        ).astype(BF16)
        key_grad_ref[:, keys_at] = (
            key_middle_grad * fall[:, keys_at] + key_late_grad * late[:, keys_at]
        ).astype(BF16)
        late_part = key_late_grad * key_late
        end_high, end_low = split_low(carried * state.astype(F32))
        ones = jnp.ones((8, VALUE_HEAD), BF16)
        end_grad = (dot(ones, end_high, 1, 1) + dot(ones, end_low, 1, 1))[:1] + jnp.sum(
            late_part, axis=0, keepdims=True
        )
        total_grads.append(
            query_early_grad * query_early
            + query_middle_grad * query_middle
            - key_middle_grad * key_middle
            - late_part
            + jnp.where(last, end_grad, 0.0)
        )
    gain_grad_ref[...] += gain_grad
    ones = jnp.where(upper, 1.0, 0.0).astype(BF16)
    high, low = split_low(jnp.concatenate(total_grads, axis=1))
    decay_grad = dot(ones, high) + dot(ones, low)
    logits_grad_ref[...] = decay_grad * sigmoid(-logits) * (1.0 / 16.0)


def attention_backward(mixed_grad, query, key, value, logits, gate, attended, states, gain):
    length, keys = query.shape
    values = value.shape[1]
    heads = states.shape[1]
    steps = length // BLOCK

    def rows(width):
        return pl.BlockSpec((BLOCK, width), lambda i: (steps - 1 - i, 0))

    return pl.pallas_call(
        backward_kernel,
        grid=(steps,),
        in_specs=[
            rows(values), rows(keys), rows(keys), rows(values), rows(keys), rows(values), rows(values),
            pl.BlockSpec((1, heads, KEY_HEAD, VALUE_HEAD), lambda i: (steps - 1 - i, 0, 0, 0)),
            pl.BlockSpec((1, VALUE_HEAD), lambda i: (0, 0)),
        ],
        out_specs=[
            rows(keys), rows(keys), rows(values), rows(values), rows(keys),
            pl.BlockSpec((1, VALUE_HEAD), lambda i: (0, 0)),
        ],
        out_shape=[
            jax.ShapeDtypeStruct((length, keys), BF16),
            jax.ShapeDtypeStruct((length, keys), BF16),
            jax.ShapeDtypeStruct((length, values), BF16),
            jax.ShapeDtypeStruct((length, values), BF16),
            jax.ShapeDtypeStruct((length, keys), F32),
            jax.ShapeDtypeStruct((1, VALUE_HEAD), F32),
        ],
        scratch_shapes=[pltpu.VMEM((heads, KEY_HEAD, VALUE_HEAD), F32)],
        compiler_params=pltpu.CompilerParams(vmem_limit_bytes=48 << 20),
        name="attention_backward",
    )(mixed_grad, query, key, value, logits, gate, attended, states, gain.reshape(1, -1))


def swap(value):
    return lax.ppermute(value, "head", [(0, 1), (1, 0)])


def ordered(own, other, axis):
    size = own.shape[axis]
    joined = jnp.concatenate([own, other, own], axis=axis)
    return lax.dynamic_slice_in_dim(joined, lax.axis_index("head") * size, 2 * size, axis)


def half_of(value, which, axis):
    size = value.shape[axis] // 2
    return lax.dynamic_slice_in_dim(value, which * size, size, axis)


def sum_rows(partial, here):
    other = swap(half_of(partial, 1 - here, 0).astype(BF16))
    return half_of(partial, here, 0) + other.astype(F32)


def norm_backward(grad_in, gain, normed_in, scale_in):
    scaled = grad_in * gain
    return scale_in * (scaled - normed_in * jnp.mean(scaled * normed_in, axis=-1, keepdims=True))


def per_device(
    tokens, lengths, initial_memory, norm_attn_gain, w_query, w_key, w_value, w_gate_out, w_low_in, w_low_out,
    decay_bias, out_gain, w_out, norm_mlp_gain, w_mlp, cotangent,
):
    here = lax.axis_index("head")
    own_rows = tokens.shape[1]
    keys = w_query.shape[1]
    values = w_value.shape[1]
    hidden = w_mlp.shape[1] // 3
    half = hidden // 2
    shard_rows = w_mlp.shape[0]

    pieces = w_mlp.reshape(shard_rows, 3, 2, half)
    own_piece = half_of(pieces, here, 2).reshape(shard_rows, 3 * half)
    other_piece = swap(half_of(pieces, 1 - here, 2).reshape(shard_rows, 3 * half))
    weights = lax.all_gather(ordered(own_piece, other_piece, 0), "dp", axis=0, tiled=True)

    tokens_own = tokens[0]
    tokens_wide = ordered(tokens_own, swap(tokens_own), 0).astype(F32)
    length = tokens_wide.shape[0]
    scale_one = lax.rsqrt(jnp.mean(tokens_wide * tokens_wide, axis=1, keepdims=True) + EPSILON)
    h_low = (tokens_wide * scale_one * norm_attn_gain).astype(BF16)
    query = dot(h_low, w_query).astype(BF16)
    key = dot(h_low, w_key).astype(BF16)
    value = dot(h_low, w_value).astype(BF16)
    gate = dot(h_low, w_gate_out)
    low_rank = dot(h_low, w_low_in)
    low_high, low_rest = split_low(low_rank)
    logits = dot(low_high, w_low_out) + dot(low_rest, w_low_out) + decay_bias
    attended, mixed, states = attention_forward(query, key, value, logits, gate, out_gain, initial_memory[0])
    resid = tokens_own.astype(F32) + sum_rows(dot(mixed, w_out), here)

    positions = here * own_rows + lax.iota(jnp.int32, own_rows)
    row_mask = (positions < lengths[0]).astype(F32)[:, None]
    scale_two = lax.rsqrt(jnp.mean(resid * resid, axis=1, keepdims=True) + EPSILON)
    normal_two = resid * scale_two
    h_two_own = (normal_two * norm_mlp_gain).astype(BF16)
    h_two = ordered(h_two_own, swap(h_two_own), 0)
    resid_grad = row_mask * cotangent[0].astype(F32)
    low_own = resid_grad.astype(BF16)
    resid_low = ordered(low_own, swap(low_own), 0)
    pre_gate = dot(h_two, weights[:, :half])
    up_part = dot(h_two, weights[:, half : 2 * half])
    pre_sigmoid = sigmoid(pre_gate)
    inner = (pre_gate * pre_sigmoid * up_part).astype(BF16)
    inner_grad = dot(resid_low, weights[:, 2 * half :])
    pre_grad = (
        inner_grad * up_part * pre_sigmoid * (1.0 + pre_gate * (1.0 - pre_sigmoid))
    ).astype(BF16)
    up_grad = (inner_grad * pre_gate * pre_sigmoid).astype(BF16)
    mlp_out = sum_rows(dot(inner, weights[:, 2 * half :], 1, 1), here)
    output = (row_mask * (resid + mlp_out)).astype(BF16)[None]
    h_two_grad = sum_rows(
        dot(pre_grad, weights[:, :half], 1, 1) + dot(up_grad, weights[:, half : 2 * half], 1, 1), here
    )
    grad_mlp = jnp.concatenate(
        [
            dot(h_two, pre_grad, 0, 0).astype(BF16),
            dot(h_two, up_grad, 0, 0).astype(BF16),
            dot(resid_low, inner, 0, 0).astype(BF16),
        ],
        axis=1,
    )
    grad_mlp = lax.psum_scatter(grad_mlp, "dp", scatter_dimension=0, tiled=True)
    resid_total = resid_grad + norm_backward(h_two_grad, norm_mlp_gain, normal_two, scale_two)
    gain_two_grad = jnp.sum(h_two_grad * normal_two, axis=0)

    attn_own = resid_total.astype(BF16)
    attn_low = ordered(attn_own, swap(attn_own), 0)
    mixed_grad = dot(attn_low, w_out, 1, 1)
    out_grad = dot(attn_low, mixed, 0, 0)
    query_grad, key_grad, value_grad, gate_grad, logits_grad, out_gain_grad = attention_backward(
        mixed_grad, query, key, value, logits, gate, attended, states, out_gain
    )
    bias_grad = jnp.sum(logits_grad, axis=0)
    grad_high, grad_rest = split_low(logits_grad)
    low_out_grad = (
        dot(low_high, grad_high, 0, 0) + dot(low_rest, grad_high, 0, 0) + dot(low_high, grad_rest, 0, 0)
    )
    low_rank_low = (dot(grad_high, w_low_out, 1, 1) + dot(grad_rest, w_low_out, 1, 1)).astype(BF16)
    low_in_grad = dot(h_low, low_rank_low, 0, 0)
    attn_grads = jnp.concatenate(
        [
            dot(h_low, query_grad, 0, 0).astype(BF16),
            dot(h_low, key_grad, 0, 0).astype(BF16),
            dot(h_low, value_grad, 0, 0).astype(BF16),
            dot(h_low, gate_grad, 0, 0).astype(BF16),
            out_grad.astype(BF16),
        ],
        axis=1,
    )
    attn_grads = lax.psum_scatter(attn_grads, "dp", scatter_dimension=0, tiled=True).astype(F32)
    h_grad = sum_rows(
        dot(query_grad, w_query, 1, 1)
        + dot(key_grad, w_key, 1, 1)
        + dot(value_grad, w_value, 1, 1)
        + dot(gate_grad, w_gate_out, 1, 1)
        + dot(low_rank_low, w_low_in, 1, 1),
        here,
    )
    own_wide = tokens_own.astype(F32)
    own_scale = lax.rsqrt(jnp.mean(own_wide * own_wide, axis=1, keepdims=True) + EPSILON)
    normal_own = own_wide * own_scale
    tokens_grad = resid_total + norm_backward(h_grad, norm_attn_gain, normal_own, own_scale)
    gain_one_grad = jnp.sum(h_grad * normal_own, axis=0)

    low_rank_width = w_low_out.shape[0]
    decay_part = jnp.concatenate([low_out_grad, bias_grad[None]], axis=0)
    slots = jnp.zeros((2,) + decay_part.shape, F32)
    slots = lax.dynamic_update_slice(slots, decay_part[None], (here, 0, 0))
    packed = jnp.concatenate(
        [
            gain_one_grad, gain_two_grad, out_gain_grad.reshape(-1), low_in_grad.reshape(-1), slots.reshape(-1),
        ]
    )
    packed = lax.psum(packed, ("dp", "head"))
    width = gain_one_grad.shape[0]
    edges = [width, 2 * width, 2 * width + VALUE_HEAD]
    edges.append(edges[-1] + width * low_rank_width)
    low_in_grad = packed[edges[2] : edges[3]].reshape(width, low_rank_width)
    decay_part = lax.dynamic_index_in_dim(packed[edges[3] :].reshape(slots.shape), here, 0, keepdims=False)

    own_half = half_of(grad_mlp, here, 0)
    other_half = swap(half_of(grad_mlp, 1 - here, 0))
    grad_mlp = ordered(
        own_half.reshape(shard_rows, 3, 1, half), other_half.reshape(shard_rows, 3, 1, half), 2
    ).reshape(shard_rows, 3 * hidden).astype(F32)
    return (
        output,
        tokens_grad[None],
        packed[: edges[0]],
        attn_grads[:, :keys],
        attn_grads[:, keys : 2 * keys],
        attn_grads[:, 2 * keys : 2 * keys + values],
        attn_grads[:, 2 * keys + values : 2 * keys + 2 * values],
        low_in_grad,
        decay_part[:low_rank_width],
        decay_part[low_rank_width],
        packed[edges[1] : edges[2]],
        attn_grads[:, 2 * keys + 2 * values :].T,
        packed[edges[0] : edges[1]],
        grad_mlp,
    )


def solution(mesh):
    return jax.shard_map(
        per_device,
        mesh=mesh,
        in_specs=(
            P("dp", "head", None),
            P("dp"),
            P("dp", "head", None, None),
            P(),
            P(None, "head"),
            P(None, "head"),
            P(None, "head"),
            P(None, "head"),
            P(),
            P(None, "head"),
            P("head"),
            P(),
            P("head", None),
            P(),
            P(("dp", "head"), None),
            P("dp", "head", None),
        ),
        out_specs=(
            P("dp", "head", None),
            P("dp", "head", None),
            P(),
            P("dp", "head"),
            P("dp", "head"),
            P("dp", "head"),
            P("dp", "head"),
            P(),
            P(None, "head"),
            P("head"),
            P(),
            P("head", "dp"),
            P(),
            P(("dp", "head"), None),
        ),
        check_vma=False,
    )
```

```python
import functools

import jax
import jax.numpy as jnp
from jax import lax
from jax.experimental import pallas as pl
from jax.experimental.pallas import tpu as pltpu
from jax.sharding import PartitionSpec as P

HEADS = 4
KEY = 512
VALUE = 1024
BLOCK = 128
KEY_HEAD = KEY // HEADS
VALUE_HEAD = VALUE // HEADS

EPSILON = 1e-05
F32 = jnp.float32
BF16 = jnp.bfloat16
SCALE = KEY_HEAD ** (-0.5)


def dot(left, right, left_dim=1, right_dim=0):
    return lax.dot_general(
        left, right, (((left_dim,), (right_dim,)), ((), ())), preferred_element_type=F32
    )


def split_low(value):
    high = value.astype(BF16)
    return high, (value - high.astype(F32)).astype(BF16)


def sigmoid(value):
    return 1.0 / (1.0 + jnp.exp(-value))


def log_sigmoid(value):
    return jnp.minimum(value, 0.0) - jnp.log1p(jnp.exp(-jnp.abs(value)))


def triangle(lower):
    rows = lax.broadcasted_iota(jnp.int32, (BLOCK, BLOCK), 0)
    columns = lax.broadcasted_iota(jnp.int32, (BLOCK, BLOCK), 1)
    return rows >= columns if lower else rows <= columns


def decay_terms(logits):
    log_decay = log_sigmoid(logits) * (1.0 / 16.0)
    ones = jnp.where(triangle(True), 1.0, 0.0).astype(BF16)
    high, low = split_low(log_decay)
    total = dot(ones, high) + dot(ones, low)
    middle = total[BLOCK // 2 - 1 : BLOCK // 2, :]
    end = total[BLOCK - 1 :, :]
    rise = jnp.exp(total - middle)
    fall = jnp.exp(middle - total)
    early = rise * (jnp.exp(middle) * SCALE)
    late = fall * jnp.exp(end - middle)
    return rise * SCALE, fall, early, late, jnp.exp(end)


def as_column(row, width):
    column = jnp.transpose(jnp.broadcast_to(row, (KEY_HEAD, KEY_HEAD)))
    return jnp.concatenate([column] * (width // KEY_HEAD), axis=1)


def forward_kernel(
    query_ref, key_ref, value_ref, logits_ref, gate_ref, gain_ref, start_ref,
    attended_ref, mixed_ref, states_ref, memory
):
    heads = start_ref.shape[0]

    @pl.when(pl.program_id(0) == 0)
    def _():
        memory[...] = start_ref[...]

    rise, fall, early, late, decay = decay_terms(logits_ref[...])
    lower = triangle(True)
    for head in range(heads):
        keys_at = slice(head * KEY_HEAD, (head + 1) * KEY_HEAD)
        values_at = slice(head * VALUE_HEAD, (head + 1) * VALUE_HEAD)
        query = query_ref[:, keys_at].astype(F32)
        key = key_ref[:, keys_at].astype(F32)
        value = value_ref[:, values_at]
        state = memory[head]
        state_low = state.astype(BF16)
        states_ref[0, head] = state_low
        scores = dot((query * rise[:, keys_at]).astype(BF16), (key * fall[:, keys_at]).astype(BF16), 1, 1)
        scores = jnp.where(lower, scores, 0.0).astype(BF16)
        left = jnp.concatenate([scores, (query * early[:, keys_at]).astype(BF16)], axis=1)
        attended = dot(left, jnp.concatenate([value, state_low], axis=0))
        memory[head] = as_column(decay[:, keys_at], VALUE_HEAD) * state + dot(
            (key * late[:, keys_at]).astype(BF16), value, 0, 0
        )
        attended_ref[:, values_at] = attended
        scale = lax.rsqrt(jnp.mean(attended * attended, axis=1, keepdims=True) + EPSILON)
        gate = gate_ref[:, values_at]
        mixed_ref[:, values_at] = (attended * scale * gain_ref[...] * gate * sigmoid(gate)).astype(BF16)


def attention_forward(query, key, value, logits, gate, gain, start):
    length, keys = query.shape
    values = value.shape[1]
    heads = start.shape[0]
    steps = length // BLOCK

    def rows(width):
        return pl.BlockSpec((BLOCK, width), lambda i: (i, 0))

    return pl.pallas_call(
        forward_kernel,
        grid=(steps,),
        in_specs=[
            rows(keys), rows(keys), rows(values), rows(keys), rows(values),
            pl.BlockSpec((1, VALUE_HEAD), lambda i: (0, 0)),
            pl.BlockSpec((heads, KEY_HEAD, VALUE_HEAD), lambda i: (0, 0, 0)),
        ],
        out_specs=[
            rows(values), rows(values),
            pl.BlockSpec((1, heads, KEY_HEAD, VALUE_HEAD), lambda i: (i, 0, 0, 0)),
        ],
        out_shape=[
            jax.ShapeDtypeStruct((length, values), F32),
            jax.ShapeDtypeStruct((length, values), BF16),
            jax.ShapeDtypeStruct((steps, heads, KEY_HEAD, VALUE_HEAD), BF16),
        ],
        scratch_shapes=[pltpu.VMEM((heads, KEY_HEAD, VALUE_HEAD), F32)],
        compiler_params=pltpu.CompilerParams(vmem_limit_bytes=48 << 20),
        name="attention_forward",
    )(query, key, value, logits, gate, gain.reshape(1, -1), start)


def backward_kernel(
    mixed_grad_ref, query_ref, key_ref, value_ref, logits_ref, gate_ref, attended_ref, states_ref, gain_ref,
    query_grad_ref, key_grad_ref, value_grad_ref, gate_grad_ref, logits_grad_ref, gain_grad_ref, memory_grad
):
    heads = memory_grad.shape[0]

    @pl.when(pl.program_id(0) == 0)
    def _():
        memory_grad[...] = jnp.zeros_like(memory_grad)
        gain_grad_ref[...] = jnp.zeros_like(gain_grad_ref)

    logits = logits_ref[...]
    rise, fall, early, late, decay = decay_terms(logits)
    lower = triangle(True)
    upper = triangle(False)
    last = lax.broadcasted_iota(jnp.int32, (BLOCK, KEY_HEAD), 0) == BLOCK - 1
    total_grads = []
    gain_grad = jnp.zeros((1, VALUE_HEAD), F32)
    for head in range(heads):
        keys_at = slice(head * KEY_HEAD, (head + 1) * KEY_HEAD)
        values_at = slice(head * VALUE_HEAD, (head + 1) * VALUE_HEAD)
        attended = attended_ref[:, values_at]
        scale = lax.rsqrt(jnp.mean(attended * attended, axis=1, keepdims=True) + EPSILON)
        normal = attended * scale
        gain = gain_ref[...]
        gate = gate_ref[:, values_at]
        gate_sigmoid = sigmoid(gate)
        mixed_grad = mixed_grad_ref[:, values_at]
        gate_grad_ref[:, values_at] = (
            mixed_grad * normal * gain * gate_sigmoid * (1.0 + gate * (1.0 - gate_sigmoid))
        ).astype(BF16)
        normed_grad = mixed_grad * gate * gate_sigmoid
        gain_grad += jnp.sum(normed_grad * normal, axis=0, keepdims=True)
        scaled = normed_grad * gain
        attended_grad = (
            scale * (scaled - normal * jnp.mean(scaled * normal, axis=1, keepdims=True))
        ).astype(BF16)

        query = query_ref[:, keys_at].astype(F32)
        key = key_ref[:, keys_at].astype(F32)
        value = value_ref[:, values_at]
        query_middle = query * rise[:, keys_at]
        key_middle = key * fall[:, keys_at]
        query_early = query * early[:, keys_at]
        key_late = key * late[:, keys_at]
        query_middle_low = query_middle.astype(BF16)
        key_middle_low = key_middle.astype(BF16)
        state = states_ref[0, head]
        after = memory_grad[head]
        after_low = after.astype(BF16)

        scores_turned = jnp.where(upper, dot(key_middle_low, query_middle_low, 1, 1), 0.0).astype(BF16)
        from_values = dot(attended_grad, jnp.concatenate([value, state], axis=0), 1, 1)
        to_values = jnp.concatenate([attended_grad, after_low], axis=0)
        from_grads = dot(value, to_values, 1, 1)
        scores_grad = jnp.where(lower, from_values[:, :BLOCK], 0.0).astype(BF16)
        scores_grad_turned = jnp.where(upper, from_grads[:, :BLOCK], 0.0).astype(BF16)
        query_early_grad = from_values[:, BLOCK:]
        key_late_grad = from_grads[:, BLOCK:]
        query_middle_grad = dot(scores_grad, key_middle_low)
        key_middle_grad = dot(scores_grad_turned, query_middle_low)
        value_grad_ref[:, values_at] = dot(
            jnp.concatenate([scores_turned, key_late.astype(BF16)], axis=1), to_values
        ).astype(BF16)
        decay_column = as_column(decay[:, keys_at], VALUE_HEAD)
        carried = decay_column * after
        memory_grad[head] = carried + dot(query_early.astype(BF16), attended_grad, 0, 0)

        query_grad_ref[:, keys_at] = (
            query_early_grad * early[:, keys_at] + query_middle_grad * rise[:, keys_at]
        ).astype(BF16)
        key_grad_ref[:, keys_at] = (
            key_middle_grad * fall[:, keys_at] + key_late_grad * late[:, keys_at]
        ).astype(BF16)
        late_part = key_late_grad * key_late
        end_high, end_low = split_low(carried * state.astype(F32))
        ones = jnp.ones((8, VALUE_HEAD), BF16)
        end_grad = (dot(ones, end_high, 1, 1) + dot(ones, end_low, 1, 1))[:1] + jnp.sum(
            late_part, axis=0, keepdims=True
        )
        total_grads.append(
            query_early_grad * query_early
            + query_middle_grad * query_middle
            - key_middle_grad * key_middle
            - late_part
            + jnp.where(last, end_grad, 0.0)
        )
    gain_grad_ref[...] += gain_grad
    ones = jnp.where(upper, 1.0, 0.0).astype(BF16)
    high, low = split_low(jnp.concatenate(total_grads, axis=1))
    decay_grad = dot(ones, high) + dot(ones, low)
    logits_grad_ref[...] = decay_grad * sigmoid(-logits) * (1.0 / 16.0)


def attention_backward(mixed_grad, query, key, value, logits, gate, attended, states, gain):
    length, keys = query.shape
    values = value.shape[1]
    heads = states.shape[1]
    steps = length // BLOCK

    def rows(width):
        return pl.BlockSpec((BLOCK, width), lambda i: (steps - 1 - i, 0))

    return pl.pallas_call(
        backward_kernel,
        grid=(steps,),
        in_specs=[
            rows(values), rows(keys), rows(keys), rows(values), rows(keys), rows(values), rows(values),
            pl.BlockSpec((1, heads, KEY_HEAD, VALUE_HEAD), lambda i: (steps - 1 - i, 0, 0, 0)),
            pl.BlockSpec((1, VALUE_HEAD), lambda i: (0, 0)),
        ],
        out_specs=[
            rows(keys), rows(keys), rows(values), rows(values), rows(keys),
            pl.BlockSpec((1, VALUE_HEAD), lambda i: (0, 0)),
        ],
        out_shape=[
            jax.ShapeDtypeStruct((length, keys), BF16),
            jax.ShapeDtypeStruct((length, keys), BF16),
            jax.ShapeDtypeStruct((length, values), BF16),
            jax.ShapeDtypeStruct((length, values), BF16),
            jax.ShapeDtypeStruct((length, keys), F32),
            jax.ShapeDtypeStruct((1, VALUE_HEAD), F32),
        ],
        scratch_shapes=[pltpu.VMEM((heads, KEY_HEAD, VALUE_HEAD), F32)],
        compiler_params=pltpu.CompilerParams(vmem_limit_bytes=48 << 20),
        name="attention_backward",
    )(mixed_grad, query, key, value, logits, gate, attended, states, gain.reshape(1, -1))


MESH = pl.DeviceIdType.MESH
ANY = pl.BlockSpec(memory_space=pl.ANY)


class Place:
    def __init__(self):
        self.dp = lax.axis_index("dp")
        self.head = lax.axis_index("head")
        self.z = self.dp // 4
        self.flat = self.dp % 4
        self.flat_x = self.flat + 1 - 2 * (self.flat % 2)
        self.flat_y = self.flat + 2 - 4 * (self.flat // 2)
        self.flat_xy = 3 - self.flat
        self.sibling = (self.dp, 1 - self.head)
        self.beside_x = (self.z * 4 + self.flat_x, self.head)
        self.beside_y = (self.z * 4 + self.flat_y, self.head)
        self.along_z = [(((self.z + i) % 4) * 4 + self.flat, self.head) for i in range(1, 4)]

    def meet(self):
        barrier = pltpu.get_barrier_semaphore()
        others = [self.sibling, self.beside_x, self.beside_y] + self.along_z
        for other in others:
            pl.semaphore_signal(barrier, 1, device_id=other, device_id_type=MESH)
        pl.semaphore_wait(barrier, len(others))


def send(source, target, out_sem, in_sem, device):
    copy = pltpu.make_async_remote_copy(
        src_ref=source, dst_ref=target, send_sem=out_sem, recv_sem=in_sem, device_id=device, device_id_type=MESH
    )
    copy.start()
    return copy


def arrived(target, out_sem, in_sem, device):
    pltpu.make_async_remote_copy(
        src_ref=target, dst_ref=target, send_sem=out_sem, recv_sem=in_sem, device_id=device, device_id_type=MESH
    ).wait_recv()


def chunk_columns(width, sizes):
    starts = [sum(sizes[:i]) * 128 for i in range(len(sizes))]
    assert sum(sizes) * 128 == width
    return [slice(start, start + size * 128) for start, size in zip(starts, sizes)]


class Gather:
    def __init__(self, place, own, other, out, chunks, local_sem, out_sems, in_sems):
        self.place, self.own, self.other, self.out, self.chunks = place, own, other, out, chunks
        self.local_sem, self.out_sems, self.in_sems = local_sem, out_sems, in_sems
        self.sent = []

    def put(self, source, target, index, device):
        chunk, slot = index
        self.sent.append(send(source, target, self.out_sems.at[chunk, slot], self.in_sems.at[chunk, slot], device))

    def wait(self, target, index):
        chunk, slot = index
        arrived(target, self.out_sems.at[chunk, slot], self.in_sems.at[chunk, slot], self.place.sibling)

    def start(self):
        at, rows = self.place, self.own.shape[0]
        count = len(self.chunks)
        mine = pl.ds(at.head * rows, rows)
        theirs = pl.ds((1 - at.head) * rows, rows)
        copy = pltpu.make_async_copy(self.own, self.out.at[at.z, at.flat, mine], self.local_sem)
        copy.start()
        self.put(self.other, self.out.at[at.z, at.flat, mine], (count, 0), at.sibling)
        copy.wait()
        self.wait(self.out.at[at.z, at.flat, theirs], (count, 0))

    def stage(self, number, chunk):
        at, out, columns = self.place, self.out, self.chunks[chunk]
        everything = slice(None)
        if number == 0:
            block = out.at[at.z, at.flat, everything, columns]
            for i in range(3):
                self.put(block, block, (chunk, i), at.along_z[i])
        if number == 1:
            for i in range(3):
                self.wait(out.at[(at.z + 3 - i) % 4, at.flat, everything, columns], (chunk, i))
            block = out.at[everything, at.flat, everything, columns]
            self.put(block, block, (chunk, 3), at.beside_x)
            self.put(block, block, (chunk, 4), at.beside_y)
        if number == 2:
            self.wait(out.at[everything, at.flat_x, everything, columns], (chunk, 3))
            block = out.at[pl.ds(0, 2), at.flat_x, everything, columns]
            self.put(block, block, (chunk, 5), at.beside_y)
            self.wait(out.at[everything, at.flat_y, everything, columns], (chunk, 4))
            block = out.at[pl.ds(2, 2), at.flat_y, everything, columns]
            self.put(block, block, (chunk, 6), at.beside_x)
        if number == 3:
            self.wait(out.at[pl.ds(0, 2), at.flat_xy, everything, columns], (chunk, 5))
            self.wait(out.at[pl.ds(2, 2), at.flat_xy, everything, columns], (chunk, 6))

    def finish(self):
        for copy in self.sent:
            copy.wait_send()


def gather_kernel(chunks, own_ref, other_ref, out_ref, local_sem, out_sems, in_sems):
    place = Place()
    place.meet()
    gather = Gather(place, own_ref, other_ref, out_ref, chunks, local_sem, out_sems, in_sems)
    gather.start()
    count = len(chunks)
    for tick in range(count + 3):
        for number in range(3, -1, -1):
            if 0 <= tick - number < count:
                gather.stage(number, tick - number)
    gather.finish()


def gather_weights(own, other):
    rows, width = own.shape
    tiles = width // 128
    count = 6
    first = max(tiles // 12, 1)
    rest = tiles - first
    sizes = [first] + [rest // (count - 1) + (1 if i < rest % (count - 1) else 0) for i in range(count - 1)]
    chunks = chunk_columns(width, sizes)
    return pl.pallas_call(
        functools.partial(gather_kernel, chunks),
        in_specs=[ANY, ANY],
        out_specs=ANY,
        out_shape=jax.ShapeDtypeStruct((4, 4, 2 * rows, width), own.dtype),
        scratch_shapes=[
            pltpu.SemaphoreType.DMA,
            pltpu.SemaphoreType.DMA((count + 1, 7)),
            pltpu.SemaphoreType.DMA((count + 1, 7)),
        ],
        compiler_params=pltpu.CompilerParams(collective_id=0, has_side_effects=True),
        name="gather_weights",
    )(own, other).reshape(32 * rows, width)


class Reduce:
    def __init__(self, place, partial, via_x, via_y, from_x, from_y, from_z, chunks, out_sems, in_sems):
        self.place, self.partial, self.chunks = place, partial, chunks
        self.via_x, self.via_y, self.from_x, self.from_y, self.from_z = via_x, via_y, from_x, from_y, from_z
        self.out_sems, self.in_sems = out_sems, in_sems
        self.sent = []

    def put(self, source, target, index, device):
        self.sent.append(send(source, target, self.out_sems.at[index], self.in_sems.at[index], device))

    def wait(self, target, index):
        arrived(target, self.out_sems.at[index], self.in_sems.at[index], self.place.sibling)

    def stage(self, number, chunk):
        at, partial, columns = self.place, self.partial, self.chunks[chunk]
        everything = slice(None)
        low, high = pl.ds(0, 2), pl.ds(2, 2)
        view = (everything, everything, columns)
        if number == 0:
            self.put(partial.at[low, at.flat_xy, everything, columns], self.via_x.at[view], (chunk, 0), at.beside_x)
            self.put(partial.at[high, at.flat_xy, everything, columns], self.via_y.at[view], (chunk, 1), at.beside_y)
        if number == 1:
            self.wait(self.via_x.at[view], (chunk, 0))
            block = (low, at.flat_y, everything, columns)
            partial[block] = (partial[block].astype(F32) + self.via_x[view].astype(F32)).astype(BF16)
            self.put(partial.at[everything, at.flat_y, everything, columns], self.from_y.at[view], (chunk, 2), at.beside_y)
            self.wait(self.via_y.at[view], (chunk, 1))
            block = (high, at.flat_x, everything, columns)
            partial[block] = (partial[block].astype(F32) + self.via_y[view].astype(F32)).astype(BF16)
            self.put(partial.at[everything, at.flat_x, everything, columns], self.from_x.at[view], (chunk, 3), at.beside_x)
        if number == 2:
            self.wait(self.from_y.at[view], (chunk, 2))
            self.wait(self.from_x.at[view], (chunk, 3))
            block = (everything, at.flat, everything, columns)
            partial[block] = (
                partial[block].astype(F32) + self.from_x[view].astype(F32) + self.from_y[view].astype(F32)
            ).astype(BF16)
            for i in range(3):
                self.put(
                    partial.at[(at.z + 1 + i) % 4, at.flat, everything, columns],
                    self.from_z.at[i, everything, columns],
                    (chunk, 4 + i),
                    at.along_z[i],
                )

    def result(self, chunk):
        at, columns = self.place, self.chunks[chunk]
        total = self.partial[at.z, at.flat, :, columns].astype(F32)
        for i in range(3):
            self.wait(self.from_z.at[i, :, columns], (chunk, 4 + i))
            total += self.from_z[i, :, columns].astype(F32)
        return total

    def finish(self):
        for copy in self.sent:
            copy.wait_send()


def reduce_kernel(
    half, mlp_chunks, attn_chunks, mlp_ref, attn_ref, small_ref, mlp_out, attn_out, small_out,
    mlp, attn, mlp_via_x, mlp_via_y, mlp_from_x, mlp_from_y, mlp_from_z,
    attn_via_x, attn_via_y, attn_from_x, attn_from_y, attn_from_z, summed, swapped, small_in, small_z,
    load_sems, mlp_sems_out, mlp_sems_in, attn_sems_out, attn_sems_in, other_sems_out, other_sems_in,
):
    at = Place()
    loads = []
    for i, columns in enumerate(mlp_chunks):
        loads.append(pltpu.make_async_copy(mlp_ref.at[:, :, :, columns], mlp.at[:, :, :, columns], load_sems.at[i]))
    for i, columns in enumerate(attn_chunks):
        loads.append(
            pltpu.make_async_copy(
                attn_ref.at[:, :, :, columns], attn.at[:, :, :, columns], load_sems.at[len(mlp_chunks) + i]
            )
        )
    for load in loads:
        load.start()
    at.meet()
    sides = [
        Reduce(at, mlp, mlp_via_x, mlp_via_y, mlp_from_x, mlp_from_y, mlp_from_z, mlp_chunks, mlp_sems_out, mlp_sems_in),
        Reduce(
            at, attn, attn_via_x, attn_via_y, attn_from_x, attn_from_y, attn_from_z, attn_chunks,
            attn_sems_out, attn_sems_in,
        ),
    ]
    order = [(0, i) for i in range(len(mlp_chunks))] + [(1, i) for i in range(len(attn_chunks))]
    count = len(order)
    rows = mlp.shape[2] // 2
    sent = []

    def put(source, target, slot, device):
        sent.append(send(source, target, other_sems_out.at[slot], other_sems_in.at[slot], device))

    def wait(target, slot):
        arrived(target, other_sems_out.at[slot], other_sems_in.at[slot], at.sibling)

    def small(step):
        if step == 0:
            put(small_ref, small_in.at[0], 0, at.sibling)
        elif step in (1, 2):
            source = small_ref if step == 1 else small_z.at[step - 2]
            wait(small_in.at[step - 1], step - 1)
            small_z[step - 1] = source[...] + small_in[step - 1]
            put(small_z.at[step - 1], small_in.at[step], step, at.beside_x if step == 1 else at.beside_y)
        elif step == 3:
            wait(small_in.at[2], 2)
            small_z[2 + at.z] = small_z[1] + small_in[2]
            for i in range(3):
                put(small_z.at[2 + at.z], small_z.at[2 + at.z], 3 + i, at.along_z[i])
        elif step == 4:
            for i in range(3):
                wait(small_z.at[2 + (at.z + 3 - i) % 4], 3 + i)
            small_out[...] = small_z[2] + small_z[3] + small_z[4] + small_z[5]

    def result(side, chunk):
        total = sides[side].result(chunk)
        if side == 0:
            columns = mlp_chunks[chunk]
            summed[:, columns] = total
            put(
                summed.at[pl.ds((1 - at.head) * rows, rows), columns], swapped.at[:, columns], 6 + chunk, at.sibling
            )
        else:
            attn_out[:, attn_chunks[chunk]] = total

    for tick in range(count + 3):
        if 0 <= tick - 3 < count:
            result(*order[tick - 3])
        for number in range(2, -1, -1):
            if 0 <= tick - number < count:
                if number == 0:
                    loads[tick].wait()
                side, chunk = order[tick - number]
                sides[side].stage(number, chunk)
        if tick < 5:
            small(tick)
    for part in range(3):
        columns = slice(part * half, (part + 1) * half)
        mine = pl.ds(pl.multiple_of(part * 2 * half + at.head * half, 128), half)
        mlp_out[:, mine] = summed[pl.ds(pl.multiple_of(at.head * rows, 8), rows), columns]
    for chunk, columns in enumerate(mlp_chunks):
        wait(swapped.at[:, columns], 6 + chunk)
    for part in range(3):
        columns = slice(part * half, (part + 1) * half)
        other = pl.ds(pl.multiple_of(part * 2 * half + (1 - at.head) * half, 128), half)
        mlp_out[:, other] = swapped[:, columns]
    for copy in sent:
        copy.wait_send()
    for side in sides:
        side.finish()


def reduce_gradients(mlp, attn, small):
    rows = mlp.shape[0] // 16
    half = mlp.shape[1] // 3
    tiles = mlp.shape[1] // 128
    mlp_count = 6
    mlp_chunks = chunk_columns(
        mlp.shape[1], [tiles // mlp_count + (1 if i < tiles % mlp_count else 0) for i in range(mlp_count)]
    )
    attn_tiles = attn.shape[1] // 128
    attn_count = 4
    attn_chunks = chunk_columns(
        attn.shape[1], [attn_tiles // attn_count + (1 if i < attn_tiles % attn_count else 0) for i in range(attn_count)]
    )
    vmem = pl.BlockSpec(memory_space=pltpu.VMEM)
    buffers = []
    for width in (mlp.shape[1], attn.shape[1]):
        buffers += [
            pltpu.VMEM((2, rows, width), BF16),
            pltpu.VMEM((2, rows, width), BF16),
            pltpu.VMEM((4, rows, width), BF16),
            pltpu.VMEM((4, rows, width), BF16),
            pltpu.VMEM((3, rows, width), BF16),
        ]
    return pl.pallas_call(
        functools.partial(reduce_kernel, half, mlp_chunks, attn_chunks),
        in_specs=[ANY, ANY, vmem],
        out_specs=[vmem, vmem, vmem],
        out_shape=[
            jax.ShapeDtypeStruct((rows // 2, 6 * half), F32),
            jax.ShapeDtypeStruct((rows, attn.shape[1]), F32),
            jax.ShapeDtypeStruct(small.shape, F32),
        ],
        scratch_shapes=[
            pltpu.VMEM((4, 4, rows, mlp.shape[1]), BF16),
            pltpu.VMEM((4, 4, rows, attn.shape[1]), BF16),
            *buffers,
            pltpu.VMEM((rows, mlp.shape[1]), F32),
            pltpu.VMEM((rows // 2, mlp.shape[1]), F32),
            pltpu.VMEM((3,) + small.shape, F32),
            pltpu.VMEM((6,) + small.shape, F32),
            pltpu.SemaphoreType.DMA((mlp_count + attn_count,)),
            pltpu.SemaphoreType.DMA((mlp_count, 7)),
            pltpu.SemaphoreType.DMA((mlp_count, 7)),
            pltpu.SemaphoreType.DMA((attn_count, 7)),
            pltpu.SemaphoreType.DMA((attn_count, 7)),
            pltpu.SemaphoreType.DMA((6 + mlp_count,)),
            pltpu.SemaphoreType.DMA((6 + mlp_count,)),
        ],
        compiler_params=pltpu.CompilerParams(
            collective_id=1, has_side_effects=True, vmem_limit_bytes=58 << 20
        ),
        name="reduce_gradients",
    )(mlp.reshape(4, 4, rows, -1), attn.reshape(4, 4, rows, -1), small)


def swap(value):
    return lax.ppermute(value, "head", [(0, 1), (1, 0)])


def ordered(own, other, axis):
    size = own.shape[axis]
    joined = jnp.concatenate([own, other, own], axis=axis)
    return lax.dynamic_slice_in_dim(joined, lax.axis_index("head") * size, 2 * size, axis)


def half_of(value, which, axis):
    size = value.shape[axis] // 2
    return lax.dynamic_slice_in_dim(value, which * size, size, axis)


def sum_rows(partial, here):
    other = swap(half_of(partial, 1 - here, 0).astype(BF16))
    return half_of(partial, here, 0) + other.astype(F32)


def norm_backward(grad_in, gain, normed_in, scale_in):
    scaled = grad_in * gain
    return scale_in * (scaled - normed_in * jnp.mean(scaled * normed_in, axis=-1, keepdims=True))


def per_device(
    tokens, lengths, initial_memory, norm_attn_gain, w_query, w_key, w_value, w_gate_out, w_low_in, w_low_out,
    decay_bias, out_gain, w_out, norm_mlp_gain, w_mlp, cotangent,
):
    here = lax.axis_index("head")
    own_rows = tokens.shape[1]
    keys = w_query.shape[1]
    values = w_value.shape[1]
    hidden = w_mlp.shape[1] // 3
    half = hidden // 2
    shard_rows = w_mlp.shape[0]
    square = lax.axis_size("dp") == 16

    pieces = w_mlp.reshape(shard_rows, 3, 2, half)
    own_piece = half_of(pieces, here, 2).reshape(shard_rows, 3 * half)
    other_piece = half_of(pieces, 1 - here, 2).reshape(shard_rows, 3 * half)
    if square:
        weights = gather_weights(own_piece, other_piece)
    else:
        weights = lax.all_gather(ordered(own_piece, swap(other_piece), 0), "dp", axis=0, tiled=True)

    tokens_own = tokens[0]
    tokens_wide = ordered(tokens_own, swap(tokens_own), 0).astype(F32)
    length = tokens_wide.shape[0]
    scale_one = lax.rsqrt(jnp.mean(tokens_wide * tokens_wide, axis=1, keepdims=True) + EPSILON)
    h_low = (tokens_wide * scale_one * norm_attn_gain).astype(BF16)
    query = dot(h_low, w_query).astype(BF16)
    key = dot(h_low, w_key).astype(BF16)
    value = dot(h_low, w_value).astype(BF16)
    gate = dot(h_low, w_gate_out)
    low_rank = dot(h_low, w_low_in)
    low_high, low_rest = split_low(low_rank)
    logits = dot(low_high, w_low_out) + dot(low_rest, w_low_out) + decay_bias
    attended, mixed, states = attention_forward(query, key, value, logits, gate, out_gain, initial_memory[0])
    resid = tokens_own.astype(F32) + sum_rows(dot(mixed, w_out), here)

    positions = here * own_rows + lax.iota(jnp.int32, own_rows)
    row_mask = (positions < lengths[0]).astype(F32)[:, None]
    scale_two = lax.rsqrt(jnp.mean(resid * resid, axis=1, keepdims=True) + EPSILON)
    normal_two = resid * scale_two
    h_two_own = (normal_two * norm_mlp_gain).astype(BF16)
    h_two = ordered(h_two_own, swap(h_two_own), 0)
    resid_grad = row_mask * cotangent[0].astype(F32)
    low_own = resid_grad.astype(BF16)
    resid_low = ordered(low_own, swap(low_own), 0)
    pre_gate = dot(h_two, weights[:, :half])
    up_part = dot(h_two, weights[:, half : 2 * half])
    pre_sigmoid = sigmoid(pre_gate)
    inner = (pre_gate * pre_sigmoid * up_part).astype(BF16)
    inner_grad = dot(resid_low, weights[:, 2 * half :])
    pre_grad = (
        inner_grad * up_part * pre_sigmoid * (1.0 + pre_gate * (1.0 - pre_sigmoid))
    ).astype(BF16)
    up_grad = (inner_grad * pre_gate * pre_sigmoid).astype(BF16)
    mlp_out = sum_rows(dot(inner, weights[:, 2 * half :], 1, 1), here)
    output = (row_mask * (resid + mlp_out)).astype(BF16)[None]
    h_two_grad = sum_rows(
        dot(pre_grad, weights[:, :half], 1, 1) + dot(up_grad, weights[:, half : 2 * half], 1, 1), here
    )
    grad_mlp = jnp.concatenate(
        [
            dot(h_two, pre_grad, 0, 0).astype(BF16),
            dot(h_two, up_grad, 0, 0).astype(BF16),
            dot(resid_low, inner, 0, 0).astype(BF16),
        ],
        axis=1,
    )
    resid_total = resid_grad + norm_backward(h_two_grad, norm_mlp_gain, normal_two, scale_two)
    gain_two_grad = jnp.sum(h_two_grad * normal_two, axis=0)

    attn_own = resid_total.astype(BF16)
    attn_low = ordered(attn_own, swap(attn_own), 0)
    mixed_grad = dot(attn_low, w_out, 1, 1)
    out_grad = dot(attn_low, mixed, 0, 0)
    query_grad, key_grad, value_grad, gate_grad, logits_grad, out_gain_grad = attention_backward(
        mixed_grad, query, key, value, logits, gate, attended, states, out_gain
    )
    bias_grad = jnp.sum(logits_grad, axis=0)
    grad_high, grad_rest = split_low(logits_grad)
    low_out_grad = (
        dot(low_high, grad_high, 0, 0) + dot(low_rest, grad_high, 0, 0) + dot(low_high, grad_rest, 0, 0)
    )
    low_rank_low = (dot(grad_high, w_low_out, 1, 1) + dot(grad_rest, w_low_out, 1, 1)).astype(BF16)
    low_in_grad = dot(h_low, low_rank_low, 0, 0)
    attn_grads = jnp.concatenate(
        [
            dot(h_low, query_grad, 0, 0).astype(BF16),
            dot(h_low, key_grad, 0, 0).astype(BF16),
            dot(h_low, value_grad, 0, 0).astype(BF16),
            dot(h_low, gate_grad, 0, 0).astype(BF16),
            out_grad.astype(BF16),
        ],
        axis=1,
    )
    h_grad = sum_rows(
        dot(query_grad, w_query, 1, 1)
        + dot(key_grad, w_key, 1, 1)
        + dot(value_grad, w_value, 1, 1)
        + dot(gate_grad, w_gate_out, 1, 1)
        + dot(low_rank_low, w_low_in, 1, 1),
        here,
    )
    own_wide = tokens_own.astype(F32)
    own_scale = lax.rsqrt(jnp.mean(own_wide * own_wide, axis=1, keepdims=True) + EPSILON)
    normal_own = own_wide * own_scale
    tokens_grad = resid_total + norm_backward(h_grad, norm_attn_gain, normal_own, own_scale)
    gain_one_grad = jnp.sum(h_grad * normal_own, axis=0)

    low_rank_width = w_low_out.shape[0]
    decay_part = jnp.concatenate([low_out_grad, bias_grad[None]], axis=0)
    slots = jnp.zeros((2,) + decay_part.shape, F32)
    slots = lax.dynamic_update_slice(slots, decay_part[None], (here, 0, 0))
    packed = jnp.concatenate(
        [
            gain_one_grad, gain_two_grad, out_gain_grad.reshape(-1), low_in_grad.reshape(-1), slots.reshape(-1),
        ]
    )
    if square:
        packed = packed.reshape(-1, 128)
        grad_mlp, attn_grads, packed = reduce_gradients(grad_mlp, attn_grads, packed)
        packed = packed.reshape(-1)
    else:
        packed = lax.psum(packed, ("dp", "head"))
        attn_grads = lax.psum_scatter(attn_grads, "dp", scatter_dimension=0, tiled=True).astype(F32)
        grad_mlp = lax.psum_scatter(grad_mlp, "dp", scatter_dimension=0, tiled=True)
        own_half = half_of(grad_mlp, here, 0)
        other_half = swap(half_of(grad_mlp, 1 - here, 0))
        grad_mlp = ordered(
            own_half.reshape(shard_rows, 3, 1, half), other_half.reshape(shard_rows, 3, 1, half), 2
        ).reshape(shard_rows, 3 * hidden).astype(F32)
    width = gain_one_grad.shape[0]
    edges = [width, 2 * width, 2 * width + VALUE_HEAD]
    edges.append(edges[-1] + width * low_rank_width)
    low_in_grad = packed[edges[2] : edges[3]].reshape(width, low_rank_width)
    decay_part = lax.dynamic_index_in_dim(packed[edges[3] :].reshape(slots.shape), here, 0, keepdims=False)

    return (
        output,
        tokens_grad[None],
        packed[: edges[0]],
        attn_grads[:, :keys],
        attn_grads[:, keys : 2 * keys],
        attn_grads[:, 2 * keys : 2 * keys + values],
        attn_grads[:, 2 * keys + values : 2 * keys + 2 * values],
        low_in_grad,
        decay_part[:low_rank_width],
        decay_part[low_rank_width],
        packed[edges[1] : edges[2]],
        attn_grads[:, 2 * keys + 2 * values :].T,
        packed[edges[0] : edges[1]],
        grad_mlp,
    )


def solution(mesh):
    return jax.shard_map(
        per_device,
        mesh=mesh,
        in_specs=(
            P("dp", "head", None),
            P("dp"),
            P("dp", "head", None, None),
            P(),
            P(None, "head"),
            P(None, "head"),
            P(None, "head"),
            P(None, "head"),
            P(),
            P(None, "head"),
            P("head"),
            P(),
            P("head", None),
            P(),
            P(("dp", "head"), None),
            P("dp", "head", None),
        ),
        out_specs=(
            P("dp", "head", None),
            P("dp", "head", None),
            P(),
            P("dp", "head"),
            P("dp", "head"),
            P("dp", "head"),
            P("dp", "head"),
            P(),
            P(None, "head"),
            P("head"),
            P(),
            P("head", "dp"),
            P(),
            P(("dp", "head"), None),
        ),
        check_vma=False,
    )
```

```python
import functools

import jax
import jax.numpy as jnp
from jax import lax
from jax.experimental import pallas as pl
from jax.experimental.pallas import tpu as pltpu
from jax.sharding import PartitionSpec as P

HEADS = 4
KEY = 512
VALUE = 1024
BLOCK = 128
KEY_HEAD = KEY // HEADS
VALUE_HEAD = VALUE // HEADS

EPSILON = 1e-05
F32 = jnp.float32
BF16 = jnp.bfloat16
SCALE = KEY_HEAD ** (-0.5)


def dot(left, right, left_dim=1, right_dim=0):
    return lax.dot_general(
        left, right, (((left_dim,), (right_dim,)), ((), ())), preferred_element_type=F32
    )


def split_low(value):
    high = value.astype(BF16)
    return high, (value - high.astype(F32)).astype(BF16)


def sigmoid(value):
    return 1.0 / (1.0 + jnp.exp(-value))


def log_sigmoid(value):
    return jnp.minimum(value, 0.0) - jnp.log1p(jnp.exp(-jnp.abs(value)))


def triangle(lower):
    rows = lax.broadcasted_iota(jnp.int32, (BLOCK, BLOCK), 0)
    columns = lax.broadcasted_iota(jnp.int32, (BLOCK, BLOCK), 1)
    return rows >= columns if lower else rows <= columns


def decay_terms(logits):
    log_decay = log_sigmoid(logits) * (1.0 / 16.0)
    ones = jnp.where(triangle(True), 1.0, 0.0).astype(BF16)
    high, low = split_low(log_decay)
    total = dot(ones, high) + dot(ones, low)
    middle = total[BLOCK // 2 - 1 : BLOCK // 2, :]
    end = total[BLOCK - 1 :, :]
    rise = jnp.exp(total - middle)
    fall = jnp.exp(middle - total)
    early = rise * (jnp.exp(middle) * SCALE)
    late = fall * jnp.exp(end - middle)
    return rise * SCALE, fall, early, late, jnp.exp(end)


def as_column(row, width):
    column = jnp.transpose(jnp.broadcast_to(row, (KEY_HEAD, KEY_HEAD)))
    return jnp.concatenate([column] * (width // KEY_HEAD), axis=1)


def forward_kernel(
    query_ref, key_ref, value_ref, logits_ref, gate_ref, gain_ref, start_ref,
    attended_ref, mixed_ref, states_ref, memory
):
    heads = start_ref.shape[0]

    @pl.when(pl.program_id(0) == 0)
    def _():
        memory[...] = start_ref[...]

    rise, fall, early, late, decay = decay_terms(logits_ref[...])
    lower = triangle(True)
    for head in range(heads):
        keys_at = slice(head * KEY_HEAD, (head + 1) * KEY_HEAD)
        values_at = slice(head * VALUE_HEAD, (head + 1) * VALUE_HEAD)
        query = query_ref[:, keys_at].astype(F32)
        key = key_ref[:, keys_at].astype(F32)
        value = value_ref[:, values_at]
        state = memory[head]
        state_low = state.astype(BF16)
        states_ref[0, head] = state_low
        scores = dot((query * rise[:, keys_at]).astype(BF16), (key * fall[:, keys_at]).astype(BF16), 1, 1)
        scores = jnp.where(lower, scores, 0.0).astype(BF16)
        left = jnp.concatenate([scores, (query * early[:, keys_at]).astype(BF16)], axis=1)
        attended = dot(left, jnp.concatenate([value, state_low], axis=0))
        memory[head] = as_column(decay[:, keys_at], VALUE_HEAD) * state + dot(
            (key * late[:, keys_at]).astype(BF16), value, 0, 0
        )
        attended_ref[:, values_at] = attended
        scale = lax.rsqrt(jnp.mean(attended * attended, axis=1, keepdims=True) + EPSILON)
        gate = gate_ref[:, values_at]
        mixed_ref[:, values_at] = (attended * scale * gain_ref[...] * gate * sigmoid(gate)).astype(BF16)


def attention_forward(query, key, value, logits, gate, gain, start):
    length, keys = query.shape
    values = value.shape[1]
    heads = start.shape[0]
    steps = length // BLOCK

    def rows(width):
        return pl.BlockSpec((BLOCK, width), lambda i: (i, 0))

    return pl.pallas_call(
        forward_kernel,
        grid=(steps,),
        in_specs=[
            rows(keys), rows(keys), rows(values), rows(keys), rows(values),
            pl.BlockSpec((1, VALUE_HEAD), lambda i: (0, 0)),
            pl.BlockSpec((heads, KEY_HEAD, VALUE_HEAD), lambda i: (0, 0, 0)),
        ],
        out_specs=[
            rows(values), rows(values),
            pl.BlockSpec((1, heads, KEY_HEAD, VALUE_HEAD), lambda i: (i, 0, 0, 0)),
        ],
        out_shape=[
            jax.ShapeDtypeStruct((length, values), F32),
            jax.ShapeDtypeStruct((length, values), BF16),
            jax.ShapeDtypeStruct((steps, heads, KEY_HEAD, VALUE_HEAD), BF16),
        ],
        scratch_shapes=[pltpu.VMEM((heads, KEY_HEAD, VALUE_HEAD), F32)],
        compiler_params=pltpu.CompilerParams(vmem_limit_bytes=48 << 20),
        name="attention_forward",
    )(query, key, value, logits, gate, gain.reshape(1, -1), start)


def backward_kernel(
    mixed_grad_ref, query_ref, key_ref, value_ref, logits_ref, gate_ref, attended_ref, states_ref, gain_ref,
    query_grad_ref, key_grad_ref, value_grad_ref, gate_grad_ref, logits_grad_ref, gain_grad_ref, memory_grad
):
    heads = memory_grad.shape[0]

    @pl.when(pl.program_id(0) == 0)
    def _():
        memory_grad[...] = jnp.zeros_like(memory_grad)
        gain_grad_ref[...] = jnp.zeros_like(gain_grad_ref)

    logits = logits_ref[...]
    rise, fall, early, late, decay = decay_terms(logits)
    lower = triangle(True)
    upper = triangle(False)
    last = lax.broadcasted_iota(jnp.int32, (BLOCK, KEY_HEAD), 0) == BLOCK - 1
    total_grads = []
    gain_grad = jnp.zeros((1, VALUE_HEAD), F32)
    for head in range(heads):
        keys_at = slice(head * KEY_HEAD, (head + 1) * KEY_HEAD)
        values_at = slice(head * VALUE_HEAD, (head + 1) * VALUE_HEAD)
        attended = attended_ref[:, values_at]
        scale = lax.rsqrt(jnp.mean(attended * attended, axis=1, keepdims=True) + EPSILON)
        normal = attended * scale
        gain = gain_ref[...]
        gate = gate_ref[:, values_at]
        gate_sigmoid = sigmoid(gate)
        mixed_grad = mixed_grad_ref[:, values_at]
        gate_grad_ref[:, values_at] = (
            mixed_grad * normal * gain * gate_sigmoid * (1.0 + gate * (1.0 - gate_sigmoid))
        ).astype(BF16)
        normed_grad = mixed_grad * gate * gate_sigmoid
        gain_grad += jnp.sum(normed_grad * normal, axis=0, keepdims=True)
        scaled = normed_grad * gain
        attended_grad = (
            scale * (scaled - normal * jnp.mean(scaled * normal, axis=1, keepdims=True))
        ).astype(BF16)

        query = query_ref[:, keys_at].astype(F32)
        key = key_ref[:, keys_at].astype(F32)
        value = value_ref[:, values_at]
        query_middle = query * rise[:, keys_at]
        key_middle = key * fall[:, keys_at]
        query_early = query * early[:, keys_at]
        key_late = key * late[:, keys_at]
        query_middle_low = query_middle.astype(BF16)
        key_middle_low = key_middle.astype(BF16)
        state = states_ref[0, head]
        after = memory_grad[head]
        after_low = after.astype(BF16)

        scores_turned = jnp.where(upper, dot(key_middle_low, query_middle_low, 1, 1), 0.0).astype(BF16)
        from_values = dot(attended_grad, jnp.concatenate([value, state], axis=0), 1, 1)
        to_values = jnp.concatenate([attended_grad, after_low], axis=0)
        from_grads = dot(value, to_values, 1, 1)
        scores_grad = jnp.where(lower, from_values[:, :BLOCK], 0.0).astype(BF16)
        scores_grad_turned = jnp.where(upper, from_grads[:, :BLOCK], 0.0).astype(BF16)
        query_early_grad = from_values[:, BLOCK:]
        key_late_grad = from_grads[:, BLOCK:]
        query_middle_grad = dot(scores_grad, key_middle_low)
        key_middle_grad = dot(scores_grad_turned, query_middle_low)
        value_grad_ref[:, values_at] = dot(
            jnp.concatenate([scores_turned, key_late.astype(BF16)], axis=1), to_values
        ).astype(BF16)
        decay_column = as_column(decay[:, keys_at], VALUE_HEAD)
        carried = decay_column * after
        memory_grad[head] = carried + dot(query_early.astype(BF16), attended_grad, 0, 0)

        query_grad_ref[:, keys_at] = (
            query_early_grad * early[:, keys_at] + query_middle_grad * rise[:, keys_at]
        ).astype(BF16)
        key_grad_ref[:, keys_at] = (
            key_middle_grad * fall[:, keys_at] + key_late_grad * late[:, keys_at]
        ).astype(BF16)
        late_part = key_late_grad * key_late
        end_high, end_low = split_low(carried * state.astype(F32))
        ones = jnp.ones((8, VALUE_HEAD), BF16)
        end_grad = (dot(ones, end_high, 1, 1) + dot(ones, end_low, 1, 1))[:1] + jnp.sum(
            late_part, axis=0, keepdims=True
        )
        total_grads.append(
            query_early_grad * query_early
            + query_middle_grad * query_middle
            - key_middle_grad * key_middle
            - late_part
            + jnp.where(last, end_grad, 0.0)
        )
    gain_grad_ref[...] += gain_grad
    ones = jnp.where(upper, 1.0, 0.0).astype(BF16)
    high, low = split_low(jnp.concatenate(total_grads, axis=1))
    decay_grad = dot(ones, high) + dot(ones, low)
    logits_grad_ref[...] = decay_grad * sigmoid(-logits) * (1.0 / 16.0)


def attention_backward(mixed_grad, query, key, value, logits, gate, attended, states, gain):
    length, keys = query.shape
    values = value.shape[1]
    heads = states.shape[1]
    steps = length // BLOCK

    def rows(width):
        return pl.BlockSpec((BLOCK, width), lambda i: (steps - 1 - i, 0))

    return pl.pallas_call(
        backward_kernel,
        grid=(steps,),
        in_specs=[
            rows(values), rows(keys), rows(keys), rows(values), rows(keys), rows(values), rows(values),
            pl.BlockSpec((1, heads, KEY_HEAD, VALUE_HEAD), lambda i: (steps - 1 - i, 0, 0, 0)),
            pl.BlockSpec((1, VALUE_HEAD), lambda i: (0, 0)),
        ],
        out_specs=[
            rows(keys), rows(keys), rows(values), rows(values), rows(keys),
            pl.BlockSpec((1, VALUE_HEAD), lambda i: (0, 0)),
        ],
        out_shape=[
            jax.ShapeDtypeStruct((length, keys), BF16),
            jax.ShapeDtypeStruct((length, keys), BF16),
            jax.ShapeDtypeStruct((length, values), BF16),
            jax.ShapeDtypeStruct((length, values), BF16),
            jax.ShapeDtypeStruct((length, keys), F32),
            jax.ShapeDtypeStruct((1, VALUE_HEAD), F32),
        ],
        scratch_shapes=[pltpu.VMEM((heads, KEY_HEAD, VALUE_HEAD), F32)],
        compiler_params=pltpu.CompilerParams(vmem_limit_bytes=48 << 20),
        name="attention_backward",
    )(mixed_grad, query, key, value, logits, gate, attended, states, gain.reshape(1, -1))


MESH = pl.DeviceIdType.MESH
ANY = pl.BlockSpec(memory_space=pl.ANY)


class Place:
    def __init__(self):
        self.dp = lax.axis_index("dp")
        self.head = lax.axis_index("head")
        self.z = self.dp // 4
        self.flat = self.dp % 4
        self.flat_x = self.flat + 1 - 2 * (self.flat % 2)
        self.flat_y = self.flat + 2 - 4 * (self.flat // 2)
        self.flat_xy = 3 - self.flat
        self.sibling = (self.dp, 1 - self.head)
        self.beside_x = (self.z * 4 + self.flat_x, self.head)
        self.beside_y = (self.z * 4 + self.flat_y, self.head)
        self.along_z = [(((self.z + i) % 4) * 4 + self.flat, self.head) for i in range(1, 4)]

    def meet(self):
        barrier = pltpu.get_barrier_semaphore()
        others = [self.sibling, self.beside_x, self.beside_y] + self.along_z
        for other in others:
            pl.semaphore_signal(barrier, 1, device_id=other, device_id_type=MESH)
        pl.semaphore_wait(barrier, len(others))


def send(source, target, out_sem, in_sem, device):
    copy = pltpu.make_async_remote_copy(
        src_ref=source, dst_ref=target, send_sem=out_sem, recv_sem=in_sem, device_id=device, device_id_type=MESH
    )
    copy.start()
    return copy


def arrived(target, out_sem, in_sem, device):
    pltpu.make_async_remote_copy(
        src_ref=target, dst_ref=target, send_sem=out_sem, recv_sem=in_sem, device_id=device, device_id_type=MESH
    ).wait_recv()


def chunk_columns(width, sizes):
    starts = [sum(sizes[:i]) * 128 for i in range(len(sizes))]
    assert sum(sizes) * 128 == width
    return [slice(start, start + size * 128) for start, size in zip(starts, sizes)]


ROWS = 256


class Gather:
    def __init__(self, place, pieces, others, blocks, local_sems, out_sems, in_sems):
        self.place, self.pieces, self.others, self.blocks = place, pieces, others, blocks
        self.local_sems, self.out_sems, self.in_sems = local_sems, out_sems, in_sems

    def put(self, source, target, chunk, slot, device):
        send(source, target, self.out_sems.at[chunk, slot], self.in_sems.at[chunk, slot], device)

    def wait(self, target, chunk, slot):
        arrived(target, self.out_sems.at[chunk, slot], self.in_sems.at[chunk, slot], self.place.sibling)

    def start(self):
        at, count = self.place, len(self.blocks)
        rows = self.pieces[0].shape[0]
        mine = pl.ds(at.head * rows, rows)
        theirs = pl.ds((1 - at.head) * rows, rows)
        for chunk in range(count):
            target = self.blocks[chunk].at[at.z, at.flat, mine]
            pltpu.make_async_copy(self.pieces[chunk], target, self.local_sems.at[chunk]).start()
            self.put(self.others[chunk], target, chunk, 7, at.sibling)
        for chunk in range(count):
            target = self.blocks[chunk].at[at.z, at.flat, mine]
            pltpu.make_async_copy(self.pieces[chunk], target, self.local_sems.at[chunk]).wait()
            self.wait(self.blocks[chunk].at[at.z, at.flat, theirs], chunk, 7)

    def stage(self, number, chunk):
        at, out = self.place, self.blocks[chunk]
        everything = slice(None)
        if number == 0:
            block = out.at[at.z, at.flat]
            for i in range(3):
                self.put(block, block, chunk, i, at.along_z[i])
        if number == 1:
            for i in range(3):
                self.wait(out.at[(at.z + 3 - i) % 4, at.flat], chunk, i)
            block = out.at[everything, at.flat]
            self.put(block, block, chunk, 3, at.beside_x)
            self.put(block, block, chunk, 4, at.beside_y)
        if number == 2:
            self.wait(out.at[everything, at.flat_x], chunk, 3)
            block = out.at[pl.ds(0, 2), at.flat_x]
            self.put(block, block, chunk, 5, at.beside_y)
            self.wait(out.at[everything, at.flat_y], chunk, 4)
            block = out.at[pl.ds(2, 2), at.flat_y]
            self.put(block, block, chunk, 6, at.beside_x)
        if number == 3:
            self.wait(out.at[pl.ds(0, 2), at.flat_xy], chunk, 5)
            self.wait(out.at[pl.ds(2, 2), at.flat_xy], chunk, 6)

    def tick(self, number):
        for stage in range(3, -1, -1):
            if 0 <= number - stage < len(self.blocks):
                self.stage(stage, number - stage)

    def finish(self):
        for chunk, block in enumerate(self.blocks):
            everything = slice(None)
            shapes = [block.at[0, 0]] * 3 + [block.at[everything, 0]] * 2 + [block.at[pl.ds(0, 2), 0]] * 2
            shapes.append(self.others[chunk])
            for slot, ref in enumerate(shapes):
                sent(ref, self.out_sems.at[chunk, slot], self.in_sems.at[chunk, slot], self.place.sibling)


def sent(source, out_sem, in_sem, device):
    pltpu.make_async_remote_copy(
        src_ref=source, dst_ref=source, send_sem=out_sem, recv_sem=in_sem, device_id=device, device_id_type=MESH
    ).wait_send()


def forward_block(query, key, value, logits, gate, gain, memory, states):
    rise, fall, early, late, decay = decay_terms(logits)
    lower = triangle(True)
    attended_parts = []
    mixed_parts = []
    for head in range(memory.shape[0]):
        keys_at = slice(head * KEY_HEAD, (head + 1) * KEY_HEAD)
        values_at = slice(head * VALUE_HEAD, (head + 1) * VALUE_HEAD)
        query_wide = query[:, keys_at].astype(F32)
        key_wide = key[:, keys_at].astype(F32)
        value_head = value[:, values_at]
        state = memory[head]
        state_low = state.astype(BF16)
        states[head] = state_low
        scores = dot(
            (query_wide * rise[:, keys_at]).astype(BF16), (key_wide * fall[:, keys_at]).astype(BF16), 1, 1
        )
        scores = jnp.where(lower, scores, 0.0).astype(BF16)
        left = jnp.concatenate([scores, (query_wide * early[:, keys_at]).astype(BF16)], axis=1)
        attended = dot(left, jnp.concatenate([value_head, state_low], axis=0))
        memory[head] = as_column(decay[:, keys_at], VALUE_HEAD) * state + dot(
            (key_wide * late[:, keys_at]).astype(BF16), value_head, 0, 0
        )
        scale = lax.rsqrt(jnp.mean(attended * attended, axis=1, keepdims=True) + EPSILON)
        gate_head = gate[:, values_at]
        attended_parts.append(attended)
        mixed_parts.append((attended * scale * gain * gate_head * sigmoid(gate_head)).astype(BF16))
    return jnp.concatenate(attended_parts, axis=1), jnp.concatenate(mixed_parts, axis=1)


def layer_kernel(
    count,
    tokens_ref, low_ref, mask_ref, gain_one_ref, gain_two_ref, gain_out_ref, bias_ref, start_ref,
    w_query, w_key, w_value, w_gate, w_low_in, w_low_out, w_out, piece_zero, pieces, other_zero, others,
    h_ref, query_ref, key_ref, value_ref, gate_ref, logits_ref, low_rank_ref, attended_ref, mixed_ref, states_ref,
    grad_zero_ref, grad_ref, output_ref, total_ref, attn_ref, gain_grad_ref,
    tokens, low, low_turned, h_two, h_two_turned, weights_zero, weights, resid, part_out, part_in,
    mlp_sum, grad_sum, inner_all, pair_all, sums_out, sums_in, memory,
    local_sems, gather_local, gather_out, gather_in, pair_out, pair_in,
):
    step = pl.program_id(0)
    at = Place()
    own = tokens_ref.shape[0]
    length = 2 * own
    tiles = length // ROWS
    own_tiles = own // ROWS
    own_at = at.head * own
    gather = Gather(
        at,
        [piece_zero] + [pieces.at[i] for i in range(count - 1)],
        [other_zero] + [others.at[i] for i in range(count - 1)],
        [weights_zero] + [weights.at[i] for i in range(count - 1)],
        gather_local, gather_out, gather_in,
    )
    attention_steps = tiles
    first_step = attention_steps + 1
    last_step = first_step + count - 1

    def own_rows(i, size=ROWS):
        return pl.ds(pl.multiple_of(own_at + i * ROWS, ROWS), size)

    def other_rows(i, size=ROWS):
        return pl.ds(pl.multiple_of(own - own_at + i * ROWS, ROWS), size)

    def put(source, target, slot):
        send(source, target, pair_out.at[slot], pair_in.at[slot], at.sibling)

    def wait(target, slot):
        arrived(target, pair_out.at[slot], pair_in.at[slot], at.sibling)

    @pl.when(step == 0)
    def _():
        at.meet()
        put(tokens_ref, tokens.at[own_rows(0, own)], 0)
        put(low_ref, low.at[own_rows(0, own)], 1)
        here = [
            pltpu.make_async_copy(tokens_ref, tokens.at[own_rows(0, own)], local_sems.at[0]),
            pltpu.make_async_copy(low_ref, low.at[own_rows(0, own)], local_sems.at[1]),
        ]
        for copy in here:
            copy.start()
        memory[...] = start_ref[...]
        gain_grad_ref[...] = jnp.zeros_like(gain_grad_ref)
        gather.start()
        gather.tick(0)
        for copy in here:
            copy.wait()
        wait(tokens.at[other_rows(0, own)], 0)
        wait(low.at[other_rows(0, own)], 1)

    for number in range(1, count + 3):

        @pl.when(step == number)
        def _():
            gather.tick(number)

    @pl.when(step < attention_steps)
    def _():
        rows = pl.ds(pl.multiple_of(step * ROWS, ROWS), ROWS)
        wide = tokens[rows, :].astype(F32)
        scale = lax.rsqrt(jnp.mean(wide * wide, axis=1, keepdims=True) + EPSILON)
        h_low = (wide * scale * gain_one_ref[...]).astype(BF16)
        h_ref[...] = h_low
        query = dot(h_low, w_query[...]).astype(BF16)
        key = dot(h_low, w_key[...]).astype(BF16)
        value = dot(h_low, w_value[...]).astype(BF16)
        gate = dot(h_low, w_gate[...])
        low_rank = dot(h_low, w_low_in[...])
        high, rest = split_low(low_rank)
        logits = dot(high, w_low_out[...]) + dot(rest, w_low_out[...]) + bias_ref[...]
        query_ref[...] = query
        key_ref[...] = key
        value_ref[...] = value
        gate_ref[...] = gate
        low_rank_ref[...] = low_rank
        logits_ref[...] = logits
        for i in range(ROWS // BLOCK):
            block = slice(i * BLOCK, (i + 1) * BLOCK)
            attended, mixed = forward_block(
                query[block], key[block], value[block], logits[block], gate[block], gain_out_ref[...],
                memory, states_ref.at[i],
            )
            attended_ref[block, :] = attended
            mixed_ref[block, :] = mixed
        part = dot(mixed_ref[...], w_out[...])
        tile = step % own_tiles
        tile_rows = pl.ds(pl.multiple_of(tile * ROWS, ROWS), ROWS)
        mine = step // own_tiles == at.head

        @pl.when(mine)
        def _():
            resid[tile_rows, :] = part

        @pl.when(jnp.logical_not(mine))
        def _():
            part_out[tile_rows, :] = part.astype(BF16)
            put(part_out.at[tile_rows], part_in.at[tile_rows], 2 + tile)

    @pl.when(step == attention_steps)
    def _():
        for i in range(own_tiles):
            rows = pl.ds(i * ROWS, ROWS)
            wait(part_in.at[rows], 2 + i)
            full = tokens[own_rows(i), :].astype(F32) + resid[rows, :] + part_in[rows, :].astype(F32)
            resid[rows, :] = full
            scale = lax.rsqrt(jnp.mean(full * full, axis=1, keepdims=True) + EPSILON)
            h_two[own_rows(i), :] = (full * scale * gain_two_ref[...]).astype(BF16)
            put(h_two.at[own_rows(i)], h_two.at[own_rows(i)], 4 + i)

        def turn(i, carry):
            rows = pl.ds(pl.multiple_of(i * ROWS, ROWS), ROWS)
            low_turned[:, rows] = jnp.transpose(low[rows, :])
            return carry

        lax.fori_loop(0, tiles, turn, 0)
        for i in range(own_tiles):
            wait(h_two.at[other_rows(i)], 4 + i)

        def turn_two(i, carry):
            rows = pl.ds(pl.multiple_of(i * ROWS, ROWS), ROWS)
            h_two_turned[:, rows] = jnp.transpose(h_two[rows, :])
            return carry

        lax.fori_loop(0, tiles, turn_two, 0)

    def hidden_rows(block, first):
        width = block.shape[3] // 3

        def body(i, carry):
            rows = pl.ds(pl.multiple_of(i * ROWS, ROWS), ROWS)
            w_pair = block[:, :, :, : 2 * width].reshape(-1, 2 * width)
            w_down = block[:, :, :, 2 * width :].reshape(-1, width)
            pair = dot(h_two[rows, :], w_pair)
            inner_grad = dot(low[rows, :], w_down)
            pre_gate = pair[:, :width]
            up_part = pair[:, width:]
            pre_sigmoid = sigmoid(pre_gate)
            swish = pre_gate * pre_sigmoid
            inner = (swish * up_part).astype(BF16)
            pre_grad = inner_grad * up_part * pre_sigmoid * (1.0 + pre_gate * (1.0 - pre_sigmoid))
            both = jnp.concatenate([pre_grad.astype(BF16), (inner_grad * swish).astype(BF16)], axis=1)
            inner_all[rows, :width] = inner
            pair_all[rows, : 2 * width] = both
            out_part = dot(inner, w_down, 1, 1)
            grad_part = dot(both, w_pair, 1, 1)
            if first:
                mlp_sum[rows, :] = out_part
                grad_sum[rows, :] = grad_part
            else:
                mlp_sum[rows, :] += out_part
                grad_sum[rows, :] += grad_part
            return carry

        lax.fori_loop(0, tiles, body, 0)

    def weight_rows(block, target):
        width = block.shape[3] // 3

        def body(i, carry):
            rows = pl.ds(pl.multiple_of(i * ROWS, ROWS), ROWS)
            shape = (target.shape[1], target.shape[2], -1)
            target[i, :, :, : 2 * width] = (
                dot(h_two_turned[rows, :], pair_all[:, : 2 * width]).astype(BF16).reshape(shape)
            )
            target[i, :, :, 2 * width :] = (
                dot(low_turned[rows, :], inner_all[:, :width]).astype(BF16).reshape(shape)
            )
            return carry

        lax.fori_loop(0, tiles, body, 0)

    @pl.when(step == first_step)
    def _():
        hidden_rows(weights_zero, True)
        weight_rows(weights_zero, grad_zero_ref)

    @pl.when(step > first_step)
    def _():
        block = weights.at[step - first_step - 1]
        hidden_rows(block, False)

        @pl.when(step == last_step)
        def _():
            for i in range(own_tiles):
                rows = pl.ds(i * ROWS, ROWS)
                for k, source in enumerate((mlp_sum, grad_sum)):
                    sums_out[k, rows, :] = source[other_rows(i), :].astype(BF16)
                    put(sums_out.at[k, rows], sums_in.at[k, rows], 6 + 2 * i + k)

        weight_rows(block, grad_ref.at[0])

    @pl.when(step == last_step)
    def _():
        for i in range(own_tiles):
            sent(h_two.at[pl.ds(0, ROWS)], pair_out.at[4 + i], pair_in.at[4 + i], at.sibling)
        for i in range(own_tiles):
            rows = pl.ds(i * ROWS, ROWS)
            for k in range(2):
                wait(sums_in.at[k, rows], 6 + 2 * i + k)
            full = resid[rows, :]
            scale = lax.rsqrt(jnp.mean(full * full, axis=1, keepdims=True) + EPSILON)
            normal = full * scale
            mlp_out = mlp_sum[own_rows(i), :] + sums_in[0, rows, :].astype(F32)
            output_ref[rows, :] = (mask_ref[rows, :] * (full + mlp_out)).astype(BF16)
            grad = grad_sum[own_rows(i), :] + sums_in[1, rows, :].astype(F32)
            total = low[own_rows(i), :].astype(F32) + norm_backward(grad, gain_two_ref[...], normal, scale)
            total_ref[rows, :] = total
            gain_grad_ref[...] += jnp.sum(grad * normal, axis=0, keepdims=True)
            h_two[own_rows(i), :] = total.astype(BF16)
            put(h_two.at[own_rows(i)], h_two.at[own_rows(i)], 10 + i)
            pltpu.make_async_copy(h_two.at[own_rows(i)], attn_ref.at[own_rows(i)], local_sems.at[i]).start()
        gather.finish()
        for i in range(own_tiles):
            wait(h_two.at[other_rows(i)], 10 + i)
            pltpu.make_async_copy(
                h_two.at[other_rows(i)], attn_ref.at[other_rows(i)], local_sems.at[own_tiles + i]
            ).start()
        for slot, ref in enumerate(
            [tokens_ref, low_ref] + [part_out.at[pl.ds(0, ROWS)]] * 8 + [h_two.at[pl.ds(0, ROWS)]] * 2
        ):
            if slot not in (4, 5):
                sent(ref, pair_out.at[slot], pair_in.at[slot], at.sibling)
        for i in range(tiles):
            rows = own_rows(i) if i < own_tiles else other_rows(i - own_tiles)
            pltpu.make_async_copy(h_two.at[rows], attn_ref.at[rows], local_sems.at[i]).wait()


def whole(shape):
    return pl.BlockSpec(shape, lambda i: (0,) * len(shape), pipeline_mode=pl.Buffered(1))


def chunked(pieces, first):
    rows, _, half = pieces.shape
    rest = pieces[:, :, first:].reshape(rows, 3, -1, 2 * first)
    return pieces[:, :, :first].reshape(rows, -1), rest.transpose(2, 0, 1, 3).reshape(-1, rows, 6 * first)


def layer(
    tokens, low, mask, gain_one, gain_two, gain_out, bias, start,
    w_query, w_key, w_value, w_gate, w_low_in, w_low_out, w_out, own_piece, other_piece,
):
    own, width = tokens.shape
    length = 2 * own
    keys, values, heads = w_query.shape[1], w_value.shape[1], start.shape[0]
    rank = w_low_in.shape[1]
    piece_zero, pieces = chunked(own_piece, 128)
    other_zero, others = chunked(other_piece, 128)
    count = pieces.shape[0] + 1
    group = 2 * piece_zero.shape[0]
    tiles = length // ROWS
    first_step = tiles + 1
    steps = first_step + count

    def rows_spec(columns):
        return pl.BlockSpec((ROWS, columns), lambda i: (jnp.minimum(i, tiles - 1), 0))

    vmem = pl.BlockSpec(memory_space=pltpu.VMEM)
    row_shapes = [
        (width, BF16), (keys, BF16), (keys, BF16), (values, BF16), (values, F32), (keys, F32), (rank, F32),
        (values, F32), (values, BF16),
    ]
    blocks = ROWS // BLOCK
    return pl.pallas_call(
        functools.partial(layer_kernel, count),
        grid=(steps,),
        in_specs=[
            ANY, ANY, whole(mask.shape), whole((1, width)), whole((1, width)), whole((1, VALUE_HEAD)),
            whole((1, keys)), whole(start.shape), whole(w_query.shape), whole(w_key.shape), whole(w_value.shape),
            whole(w_gate.shape), whole(w_low_in.shape), whole(w_low_out.shape), whole(w_out.shape),
            ANY, ANY, ANY, ANY,
        ],
        out_specs=[rows_spec(columns) for columns, _ in row_shapes]
        + [
            pl.BlockSpec((blocks, heads, KEY_HEAD, VALUE_HEAD), lambda i: (jnp.minimum(i, tiles - 1), 0, 0, 0)),
            whole((4, 4, group, 384)),
            pl.BlockSpec(
                (1, 4, 4, group, 768), lambda i: (jnp.clip(i - first_step - 1, 0, count - 2), 0, 0, 0, 0)
            ),
            vmem, vmem, ANY, vmem,
        ],
        out_shape=[jax.ShapeDtypeStruct((length, columns), kind) for columns, kind in row_shapes]
        + [
            jax.ShapeDtypeStruct((length // BLOCK, heads, KEY_HEAD, VALUE_HEAD), BF16),
            jax.ShapeDtypeStruct((4, 4, group, 384), BF16),
            jax.ShapeDtypeStruct((count - 1, 4, 4, group, 768), BF16),
            jax.ShapeDtypeStruct((own, width), BF16),
            jax.ShapeDtypeStruct((own, width), F32),
            jax.ShapeDtypeStruct((length, width), BF16),
            jax.ShapeDtypeStruct((1, width), F32),
        ],
        scratch_shapes=[
            pltpu.VMEM((length, width), BF16),
            pltpu.VMEM((length, width), BF16),
            pltpu.VMEM((width, length), BF16),
            pltpu.VMEM((length, width), BF16),
            pltpu.VMEM((width, length), BF16),
            pltpu.VMEM((4, 4, group, 384), BF16),
            pltpu.VMEM((count - 1, 4, 4, group, 768), BF16),
            pltpu.VMEM((own, width), F32),
            pltpu.VMEM((own, width), BF16),
            pltpu.VMEM((own, width), BF16),
            pltpu.VMEM((length, width), F32),
            pltpu.VMEM((length, width), F32),
            pltpu.VMEM((length, 256), BF16),
            pltpu.VMEM((length, 512), BF16),
            pltpu.VMEM((2, own, width), BF16),
            pltpu.VMEM((2, own, width), BF16),
            pltpu.VMEM((heads, KEY_HEAD, VALUE_HEAD), F32),
            pltpu.SemaphoreType.DMA((tiles,)),
            pltpu.SemaphoreType.DMA((count,)),
            pltpu.SemaphoreType.DMA((count, 8)),
            pltpu.SemaphoreType.DMA((count, 8)),
            pltpu.SemaphoreType.DMA((12,)),
            pltpu.SemaphoreType.DMA((12,)),
        ],
        compiler_params=pltpu.CompilerParams(
            collective_id=0, has_side_effects=True, vmem_limit_bytes=63 << 20
        ),
        name="layer",
    )(
        tokens, low, mask, gain_one.reshape(1, -1), gain_two.reshape(1, -1), gain_out.reshape(1, -1),
        bias.reshape(1, -1), start, w_query, w_key, w_value, w_gate, w_low_in, w_low_out, w_out,
        piece_zero, pieces, other_zero, others,
    )


class Reduce:
    def __init__(self, place, partial, via_x, via_y, from_x, from_y, from_z, chunks, out_sems, in_sems):
        self.place, self.partial, self.chunks = place, partial, chunks
        self.via_x, self.via_y, self.from_x, self.from_y, self.from_z = via_x, via_y, from_x, from_y, from_z
        self.out_sems, self.in_sems = out_sems, in_sems
        self.sent = []

    def put(self, source, target, index, device):
        self.sent.append(send(source, target, self.out_sems.at[index], self.in_sems.at[index], device))

    def wait(self, target, index):
        arrived(target, self.out_sems.at[index], self.in_sems.at[index], self.place.sibling)

    def stage(self, number, chunk):
        at, partial, columns = self.place, self.partial, self.chunks[chunk]
        everything = slice(None)
        low, high = pl.ds(0, 2), pl.ds(2, 2)
        view = (everything, everything, columns)
        if number == 0:
            self.put(partial.at[low, at.flat_xy, everything, columns], self.via_x.at[view], (chunk, 0), at.beside_x)
            self.put(partial.at[high, at.flat_xy, everything, columns], self.via_y.at[view], (chunk, 1), at.beside_y)
        if number == 1:
            self.wait(self.via_x.at[view], (chunk, 0))
            block = (low, at.flat_y, everything, columns)
            partial[block] = (partial[block].astype(F32) + self.via_x[view].astype(F32)).astype(BF16)
            self.put(partial.at[everything, at.flat_y, everything, columns], self.from_y.at[view], (chunk, 2), at.beside_y)
            self.wait(self.via_y.at[view], (chunk, 1))
            block = (high, at.flat_x, everything, columns)
            partial[block] = (partial[block].astype(F32) + self.via_y[view].astype(F32)).astype(BF16)
            self.put(partial.at[everything, at.flat_x, everything, columns], self.from_x.at[view], (chunk, 3), at.beside_x)
        if number == 2:
            self.wait(self.from_y.at[view], (chunk, 2))
            self.wait(self.from_x.at[view], (chunk, 3))
            block = (everything, at.flat, everything, columns)
            partial[block] = (
                partial[block].astype(F32) + self.from_x[view].astype(F32) + self.from_y[view].astype(F32)
            ).astype(BF16)
            for i in range(3):
                self.put(
                    partial.at[(at.z + 1 + i) % 4, at.flat, everything, columns],
                    self.from_z.at[i, everything, columns],
                    (chunk, 4 + i),
                    at.along_z[i],
                )

    def result(self, chunk):
        at, columns = self.place, self.chunks[chunk]
        total = self.partial[at.z, at.flat, :, columns].astype(F32)
        for i in range(3):
            self.wait(self.from_z.at[i, :, columns], (chunk, 4 + i))
            total += self.from_z[i, :, columns].astype(F32)
        return total

    def finish(self):
        for copy in self.sent:
            copy.wait_send()


def reduce_kernel(
    half, mlp_chunks, attn_chunks, zero_ref, mlp_ref, attn_ref, small_ref, mlp_out, attn_out, small_out,
    mlp, attn, mlp_via_x, mlp_via_y, mlp_from_x, mlp_from_y, mlp_from_z,
    attn_via_x, attn_via_y, attn_from_x, attn_from_y, attn_from_z, summed, swapped, small_in, small_z,
    load_sems, mlp_sems_out, mlp_sems_in, attn_sems_out, attn_sems_in, other_sems_out, other_sems_in,
):
    at = Place()
    loads = []
    for i, columns in enumerate(mlp_chunks):
        source = mlp_ref.at[i - 1] if i else zero_ref
        loads.append(pltpu.make_async_copy(source, mlp.at[:, :, :, columns], load_sems.at[i]))
    for i, columns in enumerate(attn_chunks):
        loads.append(
            pltpu.make_async_copy(
                attn_ref.at[:, :, :, columns], attn.at[:, :, :, columns], load_sems.at[len(mlp_chunks) + i]
            )
        )
    for load in loads:
        load.start()
    at.meet()
    sides = [
        Reduce(at, mlp, mlp_via_x, mlp_via_y, mlp_from_x, mlp_from_y, mlp_from_z, mlp_chunks, mlp_sems_out, mlp_sems_in),
        Reduce(
            at, attn, attn_via_x, attn_via_y, attn_from_x, attn_from_y, attn_from_z, attn_chunks,
            attn_sems_out, attn_sems_in,
        ),
    ]
    order = [(0, i) for i in range(len(mlp_chunks))] + [(1, i) for i in range(len(attn_chunks))]
    count = len(order)
    rows = mlp.shape[2] // 2
    sent = []

    def put(source, target, slot, device):
        sent.append(send(source, target, other_sems_out.at[slot], other_sems_in.at[slot], device))

    def wait(target, slot):
        arrived(target, other_sems_out.at[slot], other_sems_in.at[slot], at.sibling)

    def small(step):
        if step == 0:
            put(small_ref, small_in.at[0], 0, at.sibling)
        elif step in (1, 2):
            source = small_ref if step == 1 else small_z.at[step - 2]
            wait(small_in.at[step - 1], step - 1)
            small_z[step - 1] = source[...] + small_in[step - 1]
            put(small_z.at[step - 1], small_in.at[step], step, at.beside_x if step == 1 else at.beside_y)
        elif step == 3:
            wait(small_in.at[2], 2)
            small_z[2 + at.z] = small_z[1] + small_in[2]
            for i in range(3):
                put(small_z.at[2 + at.z], small_z.at[2 + at.z], 3 + i, at.along_z[i])
        elif step == 4:
            for i in range(3):
                wait(small_z.at[2 + (at.z + 3 - i) % 4], 3 + i)
            small_out[...] = small_z[2] + small_z[3] + small_z[4] + small_z[5]

    def result(side, chunk):
        total = sides[side].result(chunk)
        if side == 0:
            columns = mlp_chunks[chunk]
            summed[:, columns] = total
            put(
                summed.at[pl.ds((1 - at.head) * rows, rows), columns], swapped.at[:, columns], 6 + chunk, at.sibling
            )
        else:
            attn_out[:, attn_chunks[chunk]] = total

    for tick in range(count + 3):
        if 0 <= tick - 3 < count:
            result(*order[tick - 3])
        for number in range(2, -1, -1):
            if 0 <= tick - number < count:
                if number == 0:
                    loads[tick].wait()
                side, chunk = order[tick - number]
                sides[side].stage(number, chunk)
        if tick < 5:
            small(tick)
    def spread(source, head):
        offset = 0
        for columns in mlp_chunks:
            size = (columns.stop - columns.start) // 3
            for part in range(3):
                start = columns.start + part * size
                target = pl.ds(pl.multiple_of(part * 2 * half + head * half + offset, 128), size)
                mlp_out[:, target] = source[:, start : start + size]
            offset += size

    spread(summed.at[pl.ds(pl.multiple_of(at.head * rows, 8), rows)], at.head)
    for chunk, columns in enumerate(mlp_chunks):
        wait(swapped.at[:, columns], 6 + chunk)
    spread(swapped, 1 - at.head)
    for copy in sent:
        copy.wait_send()
    for side in sides:
        side.finish()


def reduce_gradients(zero, mlp, attn, small):
    rows = attn.shape[0] // 16
    mlp_count = mlp.shape[0] + 1
    edges = [0] + [zero.shape[-1] + i * mlp.shape[-1] for i in range(mlp_count)]
    mlp_chunks = [slice(edges[i], edges[i + 1]) for i in range(mlp_count)]
    width = edges[-1]
    half = width // 3
    attn_tiles = attn.shape[1] // 128
    attn_count = 4
    attn_chunks = chunk_columns(
        attn.shape[1], [attn_tiles // attn_count + (1 if i < attn_tiles % attn_count else 0) for i in range(attn_count)]
    )
    vmem = pl.BlockSpec(memory_space=pltpu.VMEM)
    buffers = []
    for columns in (width, attn.shape[1]):
        buffers += [
            pltpu.VMEM((2, rows, columns), BF16),
            pltpu.VMEM((2, rows, columns), BF16),
            pltpu.VMEM((4, rows, columns), BF16),
            pltpu.VMEM((4, rows, columns), BF16),
            pltpu.VMEM((3, rows, columns), BF16),
        ]
    return pl.pallas_call(
        functools.partial(reduce_kernel, half, mlp_chunks, attn_chunks),
        in_specs=[ANY, ANY, ANY, vmem],
        out_specs=[vmem, vmem, vmem],
        out_shape=[
            jax.ShapeDtypeStruct((rows // 2, 6 * half), F32),
            jax.ShapeDtypeStruct((rows, attn.shape[1]), F32),
            jax.ShapeDtypeStruct(small.shape, F32),
        ],
        scratch_shapes=[
            pltpu.VMEM((4, 4, rows, width), BF16),
            pltpu.VMEM((4, 4, rows, attn.shape[1]), BF16),
            *buffers,
            pltpu.VMEM((rows, width), F32),
            pltpu.VMEM((rows // 2, width), F32),
            pltpu.VMEM((3,) + small.shape, F32),
            pltpu.VMEM((6,) + small.shape, F32),
            pltpu.SemaphoreType.DMA((mlp_count + attn_count,)),
            pltpu.SemaphoreType.DMA((mlp_count, 7)),
            pltpu.SemaphoreType.DMA((mlp_count, 7)),
            pltpu.SemaphoreType.DMA((attn_count, 7)),
            pltpu.SemaphoreType.DMA((attn_count, 7)),
            pltpu.SemaphoreType.DMA((6 + mlp_count,)),
            pltpu.SemaphoreType.DMA((6 + mlp_count,)),
        ],
        compiler_params=pltpu.CompilerParams(
            collective_id=1, has_side_effects=True, vmem_limit_bytes=58 << 20
        ),
        name="reduce_gradients",
    )(zero, mlp, attn.reshape(4, 4, rows, -1), small)


def swap(value):
    return lax.ppermute(value, "head", [(0, 1), (1, 0)])


def ordered(own, other, axis):
    size = own.shape[axis]
    joined = jnp.concatenate([own, other, own], axis=axis)
    return lax.dynamic_slice_in_dim(joined, lax.axis_index("head") * size, 2 * size, axis)


def half_of(value, which, axis):
    size = value.shape[axis] // 2
    return lax.dynamic_slice_in_dim(value, which * size, size, axis)


def sum_rows(partial, here):
    other = swap(half_of(partial, 1 - here, 0).astype(BF16))
    return half_of(partial, here, 0) + other.astype(F32)


def norm_backward(grad_in, gain, normed_in, scale_in):
    scaled = grad_in * gain
    return scale_in * (scaled - normed_in * jnp.mean(scaled * normed_in, axis=-1, keepdims=True))


def per_device(
    tokens, lengths, initial_memory, norm_attn_gain, w_query, w_key, w_value, w_gate_out, w_low_in, w_low_out,
    decay_bias, out_gain, w_out, norm_mlp_gain, w_mlp, cotangent,
):
    here = lax.axis_index("head")
    own_rows = tokens.shape[1]
    keys = w_query.shape[1]
    values = w_value.shape[1]
    hidden = w_mlp.shape[1] // 3
    half = hidden // 2
    shard_rows = w_mlp.shape[0]
    square = lax.axis_size("dp") == 16

    pieces = w_mlp.reshape(shard_rows, 3, 2, half)
    own_piece = lax.dynamic_index_in_dim(pieces, here, 2, keepdims=False)
    other_piece = lax.dynamic_index_in_dim(pieces, 1 - here, 2, keepdims=False)
    tokens_own = tokens[0]
    positions = here * own_rows + lax.iota(jnp.int32, own_rows)
    row_mask = (positions < lengths[0]).astype(F32)[:, None]
    resid_grad = row_mask * cotangent[0].astype(F32)
    low_own = resid_grad.astype(BF16)
    if square:
        (
            h_low, query, key, value, gate, logits, low_rank, attended, mixed, states,
            grad_zero, grad_mlp, output, resid_total, attn_low, gain_two_grad,
        ) = layer(
            tokens_own, low_own, row_mask, norm_attn_gain, norm_mlp_gain, out_gain, decay_bias, initial_memory[0],
            w_query, w_key, w_value, w_gate_out, w_low_in, w_low_out, w_out, own_piece, other_piece,
        )
        low_high, low_rest = split_low(low_rank)
        output, gain_two_grad = output[None], gain_two_grad[0]
    else:
        pair = swap(other_piece.reshape(shard_rows, 3 * half))
        weights = lax.all_gather(
            ordered(own_piece.reshape(shard_rows, 3 * half), pair, 0), "dp", axis=0, tiled=True
        )
        tokens_wide = ordered(tokens_own, swap(tokens_own), 0).astype(F32)
        length = tokens_wide.shape[0]
        scale_one = lax.rsqrt(jnp.mean(tokens_wide * tokens_wide, axis=1, keepdims=True) + EPSILON)
        h_low = (tokens_wide * scale_one * norm_attn_gain).astype(BF16)
        query = dot(h_low, w_query).astype(BF16)
        key = dot(h_low, w_key).astype(BF16)
        value = dot(h_low, w_value).astype(BF16)
        gate = dot(h_low, w_gate_out)
        low_rank = dot(h_low, w_low_in)
        low_high, low_rest = split_low(low_rank)
        logits = dot(low_high, w_low_out) + dot(low_rest, w_low_out) + decay_bias
        attended, mixed, states = attention_forward(query, key, value, logits, gate, out_gain, initial_memory[0])
        resid = tokens_own.astype(F32) + sum_rows(dot(mixed, w_out), here)
        scale_two = lax.rsqrt(jnp.mean(resid * resid, axis=1, keepdims=True) + EPSILON)
        normal_two = resid * scale_two
        h_two_own = (normal_two * norm_mlp_gain).astype(BF16)
        h_two = ordered(h_two_own, swap(h_two_own), 0)
        resid_low = ordered(low_own, swap(low_own), 0)
        pre_gate = dot(h_two, weights[:, :half])
        up_part = dot(h_two, weights[:, half : 2 * half])
        pre_sigmoid = sigmoid(pre_gate)
        inner = (pre_gate * pre_sigmoid * up_part).astype(BF16)
        inner_grad = dot(resid_low, weights[:, 2 * half :])
        pre_grad = (
            inner_grad * up_part * pre_sigmoid * (1.0 + pre_gate * (1.0 - pre_sigmoid))
        ).astype(BF16)
        up_grad = (inner_grad * pre_gate * pre_sigmoid).astype(BF16)
        mlp_out = sum_rows(dot(inner, weights[:, 2 * half :], 1, 1), here)
        output = (row_mask * (resid + mlp_out)).astype(BF16)[None]
        h_two_grad = sum_rows(
            dot(pre_grad, weights[:, :half], 1, 1) + dot(up_grad, weights[:, half : 2 * half], 1, 1), here
        )
        grad_mlp = jnp.concatenate(
            [
                dot(h_two, pre_grad, 0, 0).astype(BF16),
                dot(h_two, up_grad, 0, 0).astype(BF16),
                dot(resid_low, inner, 0, 0).astype(BF16),
            ],
            axis=1,
        )
        resid_total = resid_grad + norm_backward(h_two_grad, norm_mlp_gain, normal_two, scale_two)
        gain_two_grad = jnp.sum(h_two_grad * normal_two, axis=0)
        attn_own = resid_total.astype(BF16)
        attn_low = ordered(attn_own, swap(attn_own), 0)

    mixed_grad = dot(attn_low, w_out, 1, 1)
    out_grad = dot(attn_low, mixed, 0, 0)
    query_grad, key_grad, value_grad, gate_grad, logits_grad, out_gain_grad = attention_backward(
        mixed_grad, query, key, value, logits, gate, attended, states, out_gain
    )
    bias_grad = jnp.sum(logits_grad, axis=0)
    grad_high, grad_rest = split_low(logits_grad)
    low_out_grad = (
        dot(low_high, grad_high, 0, 0) + dot(low_rest, grad_high, 0, 0) + dot(low_high, grad_rest, 0, 0)
    )
    low_rank_low = (dot(grad_high, w_low_out, 1, 1) + dot(grad_rest, w_low_out, 1, 1)).astype(BF16)
    low_in_grad = dot(h_low, low_rank_low, 0, 0)
    attn_grads = jnp.concatenate(
        [
            dot(h_low, query_grad, 0, 0).astype(BF16),
            dot(h_low, key_grad, 0, 0).astype(BF16),
            dot(h_low, value_grad, 0, 0).astype(BF16),
            dot(h_low, gate_grad, 0, 0).astype(BF16),
            out_grad.astype(BF16),
        ],
        axis=1,
    )
    h_grad = sum_rows(
        dot(query_grad, w_query, 1, 1)
        + dot(key_grad, w_key, 1, 1)
        + dot(value_grad, w_value, 1, 1)
        + dot(gate_grad, w_gate_out, 1, 1)
        + dot(low_rank_low, w_low_in, 1, 1),
        here,
    )
    own_wide = tokens_own.astype(F32)
    own_scale = lax.rsqrt(jnp.mean(own_wide * own_wide, axis=1, keepdims=True) + EPSILON)
    normal_own = own_wide * own_scale
    tokens_grad = resid_total + norm_backward(h_grad, norm_attn_gain, normal_own, own_scale)
    gain_one_grad = jnp.sum(h_grad * normal_own, axis=0)

    low_rank_width = w_low_out.shape[0]
    decay_part = jnp.concatenate([low_out_grad, bias_grad[None]], axis=0)
    slots = jnp.zeros((2,) + decay_part.shape, F32)
    slots = lax.dynamic_update_slice(slots, decay_part[None], (here, 0, 0))
    packed = jnp.concatenate(
        [
            gain_one_grad, gain_two_grad, out_gain_grad.reshape(-1), low_in_grad.reshape(-1), slots.reshape(-1),
        ]
    )
    if square:
        packed = packed.reshape(-1, 128)
        grad_mlp, attn_grads, packed = reduce_gradients(grad_zero, grad_mlp, attn_grads, packed)
        packed = packed.reshape(-1)
    else:
        packed = lax.psum(packed, ("dp", "head"))
        attn_grads = lax.psum_scatter(attn_grads, "dp", scatter_dimension=0, tiled=True).astype(F32)
        grad_mlp = lax.psum_scatter(grad_mlp, "dp", scatter_dimension=0, tiled=True)
        own_half = half_of(grad_mlp, here, 0)
        other_half = swap(half_of(grad_mlp, 1 - here, 0))
        grad_mlp = ordered(
            own_half.reshape(shard_rows, 3, 1, half), other_half.reshape(shard_rows, 3, 1, half), 2
        ).reshape(shard_rows, 3 * hidden).astype(F32)
    width = gain_one_grad.shape[0]
    edges = [width, 2 * width, 2 * width + VALUE_HEAD]
    edges.append(edges[-1] + width * low_rank_width)
    low_in_grad = packed[edges[2] : edges[3]].reshape(width, low_rank_width)
    decay_part = lax.dynamic_index_in_dim(packed[edges[3] :].reshape(slots.shape), here, 0, keepdims=False)

    return (
        output,
        tokens_grad[None],
        packed[: edges[0]],
        attn_grads[:, :keys],
        attn_grads[:, keys : 2 * keys],
        attn_grads[:, 2 * keys : 2 * keys + values],
        attn_grads[:, 2 * keys + values : 2 * keys + 2 * values],
        low_in_grad,
        decay_part[:low_rank_width],
        decay_part[low_rank_width],
        packed[edges[1] : edges[2]],
        attn_grads[:, 2 * keys + 2 * values :].T,
        packed[edges[0] : edges[1]],
        grad_mlp,
    )


def solution(mesh):
    return jax.shard_map(
        per_device,
        mesh=mesh,
        in_specs=(
            P("dp", "head", None),
            P("dp"),
            P("dp", "head", None, None),
            P(),
            P(None, "head"),
            P(None, "head"),
            P(None, "head"),
            P(None, "head"),
            P(),
            P(None, "head"),
            P("head"),
            P(),
            P("head", None),
            P(),
            P(("dp", "head"), None),
            P("dp", "head", None),
        ),
        out_specs=(
            P("dp", "head", None),
            P("dp", "head", None),
            P(),
            P("dp", "head"),
            P("dp", "head"),
            P("dp", "head"),
            P("dp", "head"),
            P(),
            P(None, "head"),
            P("head"),
            P(),
            P("head", "dp"),
            P(),
            P(("dp", "head"), None),
        ),
        check_vma=False,
    )
```

```python
import functools

import jax
import jax.numpy as jnp
from jax import lax
from jax.experimental import pallas as pl
from jax.experimental.pallas import tpu as pltpu
from jax.sharding import PartitionSpec as P

HEADS = 4
KEY = 512
VALUE = 1024
BLOCK = 128
KEY_HEAD = KEY // HEADS
VALUE_HEAD = VALUE // HEADS

EPSILON = 1e-05
F32 = jnp.float32
BF16 = jnp.bfloat16
SCALE = KEY_HEAD ** (-0.5)


def dot(left, right, left_dim=1, right_dim=0):
    return lax.dot_general(
        left, right, (((left_dim,), (right_dim,)), ((), ())), preferred_element_type=F32
    )


def split_low(value):
    high = value.astype(BF16)
    return high, (value - high.astype(F32)).astype(BF16)


def sigmoid(value):
    return 1.0 / (1.0 + jnp.exp(-value))


def log_sigmoid(value):
    return jnp.minimum(value, 0.0) - jnp.log1p(jnp.exp(-jnp.abs(value)))


def triangle(lower):
    rows = lax.broadcasted_iota(jnp.int32, (BLOCK, BLOCK), 0)
    columns = lax.broadcasted_iota(jnp.int32, (BLOCK, BLOCK), 1)
    return rows >= columns if lower else rows <= columns


def decay_terms(logits):
    log_decay = log_sigmoid(logits) * (1.0 / 16.0)
    ones = jnp.where(triangle(True), 1.0, 0.0).astype(BF16)
    high, low = split_low(log_decay)
    total = dot(ones, high) + dot(ones, low)
    middle = total[BLOCK // 2 - 1 : BLOCK // 2, :]
    end = total[BLOCK - 1 :, :]
    rise = jnp.exp(total - middle)
    fall = jnp.exp(middle - total)
    early = rise * (jnp.exp(middle) * SCALE)
    late = fall * jnp.exp(end - middle)
    return rise * SCALE, fall, early, late, jnp.exp(end)


def as_column(row, width):
    column = jnp.transpose(jnp.broadcast_to(row, (KEY_HEAD, KEY_HEAD)))
    return jnp.concatenate([column] * (width // KEY_HEAD), axis=1)


def forward_block(query, key, value, logits, gate, gain, memory, states):
    rise, fall, early, late, decay = decay_terms(logits)
    lower = triangle(True)
    attended_parts = []
    mixed_parts = []
    for head in range(memory.shape[0]):
        keys_at = slice(head * KEY_HEAD, (head + 1) * KEY_HEAD)
        values_at = slice(head * VALUE_HEAD, (head + 1) * VALUE_HEAD)
        query_wide = query[:, keys_at].astype(F32)
        key_wide = key[:, keys_at].astype(F32)
        value_head = value[:, values_at]
        state = memory[head]
        state_low = state.astype(BF16)
        states[head] = state_low
        scores = dot(
            (query_wide * rise[:, keys_at]).astype(BF16), (key_wide * fall[:, keys_at]).astype(BF16), 1, 1
        )
        scores = jnp.where(lower, scores, 0.0).astype(BF16)
        left = jnp.concatenate([scores, (query_wide * early[:, keys_at]).astype(BF16)], axis=1)
        attended = dot(left, jnp.concatenate([value_head, state_low], axis=0))
        memory[head] = as_column(decay[:, keys_at], VALUE_HEAD) * state + dot(
            (key_wide * late[:, keys_at]).astype(BF16), value_head, 0, 0
        )
        scale = lax.rsqrt(jnp.mean(attended * attended, axis=1, keepdims=True) + EPSILON)
        gate_head = gate[:, values_at]
        attended_parts.append(attended)
        mixed_parts.append((attended * scale * gain * gate_head * sigmoid(gate_head)).astype(BF16))
    return jnp.concatenate(attended_parts, axis=1), jnp.concatenate(mixed_parts, axis=1)


def forward_kernel(
    query_ref, key_ref, value_ref, logits_ref, gate_ref, gain_ref, start_ref,
    attended_ref, mixed_ref, states_ref, memory
):
    @pl.when(pl.program_id(0) == 0)
    def _():
        memory[...] = start_ref[...]

    attended_ref[...], mixed_ref[...] = forward_block(
        query_ref[...], key_ref[...], value_ref[...], logits_ref[...], gate_ref[...], gain_ref[...],
        memory, states_ref.at[0],
    )


def attention_forward(query, key, value, logits, gate, gain, start):
    length, keys = query.shape
    values = value.shape[1]
    heads = start.shape[0]
    steps = length // BLOCK

    def rows(width):
        return pl.BlockSpec((BLOCK, width), lambda i: (i, 0))

    return pl.pallas_call(
        forward_kernel,
        grid=(steps,),
        in_specs=[
            rows(keys), rows(keys), rows(values), rows(keys), rows(values),
            pl.BlockSpec((1, VALUE_HEAD), lambda i: (0, 0)),
            pl.BlockSpec((heads, KEY_HEAD, VALUE_HEAD), lambda i: (0, 0, 0)),
        ],
        out_specs=[
            rows(values), rows(values),
            pl.BlockSpec((1, heads, KEY_HEAD, VALUE_HEAD), lambda i: (i, 0, 0, 0)),
        ],
        out_shape=[
            jax.ShapeDtypeStruct((length, values), F32),
            jax.ShapeDtypeStruct((length, values), BF16),
            jax.ShapeDtypeStruct((steps, heads, KEY_HEAD, VALUE_HEAD), BF16),
        ],
        scratch_shapes=[pltpu.VMEM((heads, KEY_HEAD, VALUE_HEAD), F32)],
        compiler_params=pltpu.CompilerParams(vmem_limit_bytes=48 << 20),
        name="attention_forward",
    )(query, key, value, logits, gate, gain.reshape(1, -1), start)


def backward_block(mixed_grad, query, key, value, logits, gate, attended, states, gain, memory_grad):
    rise, fall, early, late, decay = decay_terms(logits)
    lower = triangle(True)
    upper = triangle(False)
    last = lax.broadcasted_iota(jnp.int32, (BLOCK, KEY_HEAD), 0) == BLOCK - 1
    query_grads, key_grads, value_grads, gate_grads, total_grads = [], [], [], [], []
    gain_grad = jnp.zeros((1, VALUE_HEAD), F32)
    for head in range(memory_grad.shape[0]):
        keys_at = slice(head * KEY_HEAD, (head + 1) * KEY_HEAD)
        values_at = slice(head * VALUE_HEAD, (head + 1) * VALUE_HEAD)
        attended_head = attended[:, values_at]
        scale = lax.rsqrt(jnp.mean(attended_head * attended_head, axis=1, keepdims=True) + EPSILON)
        normal = attended_head * scale
        gate_head = gate[:, values_at]
        gate_sigmoid = sigmoid(gate_head)
        mixed_head = mixed_grad[:, values_at]
        gate_grads.append(
            (mixed_head * normal * gain * gate_sigmoid * (1.0 + gate_head * (1.0 - gate_sigmoid))).astype(BF16)
        )
        normed_grad = mixed_head * gate_head * gate_sigmoid
        gain_grad += jnp.sum(normed_grad * normal, axis=0, keepdims=True)
        scaled = normed_grad * gain
        attended_grad = (
            scale * (scaled - normal * jnp.mean(scaled * normal, axis=1, keepdims=True))
        ).astype(BF16)

        query_wide = query[:, keys_at].astype(F32)
        key_wide = key[:, keys_at].astype(F32)
        value_head = value[:, values_at]
        query_middle = query_wide * rise[:, keys_at]
        key_middle = key_wide * fall[:, keys_at]
        query_early = query_wide * early[:, keys_at]
        key_late = key_wide * late[:, keys_at]
        query_middle_low = query_middle.astype(BF16)
        key_middle_low = key_middle.astype(BF16)
        state = states[head]
        after = memory_grad[head]

        scores_turned = jnp.where(upper, dot(key_middle_low, query_middle_low, 1, 1), 0.0).astype(BF16)
        from_values = dot(attended_grad, jnp.concatenate([value_head, state], axis=0), 1, 1)
        to_values = jnp.concatenate([attended_grad, after.astype(BF16)], axis=0)
        from_grads = dot(value_head, to_values, 1, 1)
        scores_grad = jnp.where(lower, from_values[:, :BLOCK], 0.0).astype(BF16)
        scores_grad_turned = jnp.where(upper, from_grads[:, :BLOCK], 0.0).astype(BF16)
        query_early_grad = from_values[:, BLOCK:]
        key_late_grad = from_grads[:, BLOCK:]
        query_middle_grad = dot(scores_grad, key_middle_low)
        key_middle_grad = dot(scores_grad_turned, query_middle_low)
        value_grads.append(
            dot(jnp.concatenate([scores_turned, key_late.astype(BF16)], axis=1), to_values).astype(BF16)
        )
        carried = as_column(decay[:, keys_at], VALUE_HEAD) * after
        memory_grad[head] = carried + dot(query_early.astype(BF16), attended_grad, 0, 0)
        query_grads.append(
            (query_early_grad * early[:, keys_at] + query_middle_grad * rise[:, keys_at]).astype(BF16)
        )
        key_grads.append((key_middle_grad * fall[:, keys_at] + key_late_grad * late[:, keys_at]).astype(BF16))
        late_part = key_late_grad * key_late
        end_high, end_low = split_low(carried * state.astype(F32))
        ones = jnp.ones((8, VALUE_HEAD), BF16)
        end_grad = (dot(ones, end_high, 1, 1) + dot(ones, end_low, 1, 1))[:1] + jnp.sum(
            late_part, axis=0, keepdims=True
        )
        total_grads.append(
            query_early_grad * query_early
            + query_middle_grad * query_middle
            - key_middle_grad * key_middle
            - late_part
            + jnp.where(last, end_grad, 0.0)
        )
    ones = jnp.where(upper, 1.0, 0.0).astype(BF16)
    high, rest = split_low(jnp.concatenate(total_grads, axis=1))
    logits_grad = (dot(ones, high) + dot(ones, rest)) * sigmoid(-logits) * (1.0 / 16.0)
    grads = query_grads + key_grads + value_grads + gate_grads
    return jnp.concatenate(grads, axis=1), logits_grad, gain_grad


def backward_kernel_plain(
    mixed_grad_ref, query_ref, key_ref, value_ref, logits_ref, gate_ref, attended_ref, states_ref, gain_ref,
    query_grad_ref, key_grad_ref, value_grad_ref, gate_grad_ref, logits_grad_ref, gain_grad_ref, memory_grad
):
    @pl.when(pl.program_id(0) == 0)
    def _():
        memory_grad[...] = jnp.zeros_like(memory_grad)
        gain_grad_ref[...] = jnp.zeros_like(gain_grad_ref)

    grads, logits_grad, gain_grad = backward_block(
        mixed_grad_ref[...], query_ref[...], key_ref[...], value_ref[...], logits_ref[...], gate_ref[...],
        attended_ref[...], states_ref[0], gain_ref[...], memory_grad,
    )
    start = 0
    for ref in (query_grad_ref, key_grad_ref, value_grad_ref, gate_grad_ref):
        ref[...] = grads[:, start : start + ref.shape[1]]
        start += ref.shape[1]
    logits_grad_ref[...] = logits_grad
    gain_grad_ref[...] += gain_grad


def attention_backward(mixed_grad, query, key, value, logits, gate, attended, states, gain):
    length, keys = query.shape
    values = value.shape[1]
    heads = states.shape[1]
    steps = length // BLOCK

    def rows(width):
        return pl.BlockSpec((BLOCK, width), lambda i: (steps - 1 - i, 0))

    return pl.pallas_call(
        backward_kernel_plain,
        grid=(steps,),
        in_specs=[
            rows(values), rows(keys), rows(keys), rows(values), rows(keys), rows(values), rows(values),
            pl.BlockSpec((1, heads, KEY_HEAD, VALUE_HEAD), lambda i: (steps - 1 - i, 0, 0, 0)),
            pl.BlockSpec((1, VALUE_HEAD), lambda i: (0, 0)),
        ],
        out_specs=[
            rows(keys), rows(keys), rows(values), rows(values), rows(keys),
            pl.BlockSpec((1, VALUE_HEAD), lambda i: (0, 0)),
        ],
        out_shape=[
            jax.ShapeDtypeStruct((length, keys), BF16),
            jax.ShapeDtypeStruct((length, keys), BF16),
            jax.ShapeDtypeStruct((length, values), BF16),
            jax.ShapeDtypeStruct((length, values), BF16),
            jax.ShapeDtypeStruct((length, keys), F32),
            jax.ShapeDtypeStruct((1, VALUE_HEAD), F32),
        ],
        scratch_shapes=[pltpu.VMEM((heads, KEY_HEAD, VALUE_HEAD), F32)],
        compiler_params=pltpu.CompilerParams(vmem_limit_bytes=48 << 20),
        name="attention_backward",
    )(mixed_grad, query, key, value, logits, gate, attended, states, gain.reshape(1, -1))


MESH = pl.DeviceIdType.MESH
ANY = pl.BlockSpec(memory_space=pl.ANY)


class Place:
    def __init__(self):
        self.dp = lax.axis_index("dp")
        self.head = lax.axis_index("head")
        self.z = self.dp // 4
        self.flat = self.dp % 4
        self.flat_x = self.flat + 1 - 2 * (self.flat % 2)
        self.flat_y = self.flat + 2 - 4 * (self.flat // 2)
        self.flat_xy = 3 - self.flat
        self.sibling = (self.dp, 1 - self.head)
        self.beside_x = (self.z * 4 + self.flat_x, self.head)
        self.beside_y = (self.z * 4 + self.flat_y, self.head)
        self.along_z = [(((self.z + i) % 4) * 4 + self.flat, self.head) for i in range(1, 4)]

    def meet(self):
        barrier = pltpu.get_barrier_semaphore()
        others = [self.sibling, self.beside_x, self.beside_y] + self.along_z
        for other in others:
            pl.semaphore_signal(barrier, 1, device_id=other, device_id_type=MESH)
        pl.semaphore_wait(barrier, len(others))


def send(source, target, out_sem, in_sem, device):
    copy = pltpu.make_async_remote_copy(
        src_ref=source, dst_ref=target, send_sem=out_sem, recv_sem=in_sem, device_id=device, device_id_type=MESH
    )
    copy.start()
    return copy


def arrived(target, out_sem, in_sem, device):
    pltpu.make_async_remote_copy(
        src_ref=target, dst_ref=target, send_sem=out_sem, recv_sem=in_sem, device_id=device, device_id_type=MESH
    ).wait_recv()


def chunk_columns(width, sizes):
    starts = [sum(sizes[:i]) * 128 for i in range(len(sizes))]
    assert sum(sizes) * 128 == width
    return [slice(start, start + size * 128) for start, size in zip(starts, sizes)]


ROWS = 256


class Gather:
    def __init__(self, place, pieces, others, blocks, local_sems, out_sems, in_sems):
        self.place, self.pieces, self.others, self.blocks = place, pieces, others, blocks
        self.local_sems, self.out_sems, self.in_sems = local_sems, out_sems, in_sems

    def put(self, source, target, chunk, slot, device):
        send(source, target, self.out_sems.at[chunk, slot], self.in_sems.at[chunk, slot], device)

    def wait(self, target, chunk, slot):
        arrived(target, self.out_sems.at[chunk, slot], self.in_sems.at[chunk, slot], self.place.sibling)

    def start(self):
        at, count = self.place, len(self.blocks)
        rows = self.pieces[0].shape[0]
        mine = pl.ds(at.head * rows, rows)
        theirs = pl.ds((1 - at.head) * rows, rows)
        for chunk in range(count):
            target = self.blocks[chunk].at[at.z, at.flat, mine]
            pltpu.make_async_copy(self.pieces[chunk], target, self.local_sems.at[chunk]).start()
            self.put(self.others[chunk], target, chunk, 7, at.sibling)
        for chunk in range(count):
            target = self.blocks[chunk].at[at.z, at.flat, mine]
            pltpu.make_async_copy(self.pieces[chunk], target, self.local_sems.at[chunk]).wait()
            self.wait(self.blocks[chunk].at[at.z, at.flat, theirs], chunk, 7)

    def stage(self, number, chunk):
        at, out = self.place, self.blocks[chunk]
        everything = slice(None)
        if number == 0:
            block = out.at[at.z, at.flat]
            for i in range(3):
                self.put(block, block, chunk, i, at.along_z[i])
        if number == 1:
            for i in range(3):
                self.wait(out.at[(at.z + 3 - i) % 4, at.flat], chunk, i)
            block = out.at[everything, at.flat]
            self.put(block, block, chunk, 3, at.beside_x)
            self.put(block, block, chunk, 4, at.beside_y)
        if number == 2:
            self.wait(out.at[everything, at.flat_x], chunk, 3)
            block = out.at[pl.ds(0, 2), at.flat_x]
            self.put(block, block, chunk, 5, at.beside_y)
            self.wait(out.at[everything, at.flat_y], chunk, 4)
            block = out.at[pl.ds(2, 2), at.flat_y]
            self.put(block, block, chunk, 6, at.beside_x)
        if number == 3:
            self.wait(out.at[pl.ds(0, 2), at.flat_xy], chunk, 5)
            self.wait(out.at[pl.ds(2, 2), at.flat_xy], chunk, 6)

    def tick(self, number):
        for stage in range(3, -1, -1):
            if 0 <= number - stage < len(self.blocks):
                self.stage(stage, number - stage)

    def finish(self):
        for chunk, block in enumerate(self.blocks):
            everything = slice(None)
            shapes = [block.at[0, 0]] * 3 + [block.at[everything, 0]] * 2 + [block.at[pl.ds(0, 2), 0]] * 2
            shapes.append(self.others[chunk])
            for slot, ref in enumerate(shapes):
                sent(ref, self.out_sems.at[chunk, slot], self.in_sems.at[chunk, slot], self.place.sibling)


def sent(source, out_sem, in_sem, device):
    pltpu.make_async_remote_copy(
        src_ref=source, dst_ref=source, send_sem=out_sem, recv_sem=in_sem, device_id=device, device_id_type=MESH
    ).wait_send()


def layer_kernel(
    count,
    tokens_ref, low_ref, mask_ref, gain_one_ref, gain_two_ref, gain_out_ref, bias_ref, start_ref,
    w_query, w_key, w_value, w_gate, w_low_in, w_low_out, w_out, piece_zero, pieces, other_zero, others,
    h_ref, query_ref, key_ref, value_ref, gate_ref, logits_ref, low_rank_ref, attended_ref, mixed_ref, states_ref,
    grad_zero_ref, grad_ref, output_ref, total_ref, attn_ref, gain_grad_ref,
    tokens, low, low_turned, h_two, h_two_turned, weights_zero, weights, resid, part_out, part_in,
    mlp_sum, grad_sum, inner_all, pair_all, sums_out, sums_in, memory,
    local_sems, gather_local, gather_out, gather_in, pair_out, pair_in,
):
    step = pl.program_id(0)
    at = Place()
    own = tokens_ref.shape[0]
    length = 2 * own
    tiles = length // ROWS
    own_tiles = own // ROWS
    own_at = at.head * own
    gather = Gather(
        at,
        [piece_zero] + [pieces.at[i] for i in range(count - 1)],
        [other_zero] + [others.at[i] for i in range(count - 1)],
        [weights_zero] + [weights.at[i] for i in range(count - 1)],
        gather_local, gather_out, gather_in,
    )
    attention_steps = tiles
    first_step = attention_steps + 1
    last_step = first_step + count - 1

    def own_rows(i, size=ROWS):
        return pl.ds(pl.multiple_of(own_at + i * ROWS, ROWS), size)

    def other_rows(i, size=ROWS):
        return pl.ds(pl.multiple_of(own - own_at + i * ROWS, ROWS), size)

    def put(source, target, slot):
        send(source, target, pair_out.at[slot], pair_in.at[slot], at.sibling)

    def wait(target, slot):
        arrived(target, pair_out.at[slot], pair_in.at[slot], at.sibling)

    @pl.when(step == 0)
    def _():
        at.meet()
        put(tokens_ref, tokens.at[own_rows(0, own)], 0)
        put(low_ref, low.at[own_rows(0, own)], 1)
        here = [
            pltpu.make_async_copy(tokens_ref, tokens.at[own_rows(0, own)], local_sems.at[0]),
            pltpu.make_async_copy(low_ref, low.at[own_rows(0, own)], local_sems.at[1]),
        ]
        for copy in here:
            copy.start()
        memory[...] = start_ref[...]
        gain_grad_ref[...] = jnp.zeros_like(gain_grad_ref)
        gather.start()
        gather.tick(0)
        for copy in here:
            copy.wait()
        wait(tokens.at[other_rows(0, own)], 0)
        wait(low.at[other_rows(0, own)], 1)

    for number in range(1, count + 3):

        @pl.when(step == number)
        def _():
            gather.tick(number)

    @pl.when(step < attention_steps)
    def _():
        rows = pl.ds(pl.multiple_of(step * ROWS, ROWS), ROWS)
        wide = tokens[rows, :].astype(F32)
        scale = lax.rsqrt(jnp.mean(wide * wide, axis=1, keepdims=True) + EPSILON)
        h_low = (wide * scale * gain_one_ref[...]).astype(BF16)
        h_ref[...] = h_low
        query = dot(h_low, w_query[...]).astype(BF16)
        key = dot(h_low, w_key[...]).astype(BF16)
        value = dot(h_low, w_value[...]).astype(BF16)
        gate = dot(h_low, w_gate[...])
        low_rank = dot(h_low, w_low_in[...])
        high, rest = split_low(low_rank)
        logits = dot(high, w_low_out[...]) + dot(rest, w_low_out[...]) + bias_ref[...]
        query_ref[...] = query
        key_ref[...] = key
        value_ref[...] = value
        gate_ref[...] = gate
        low_rank_ref[...] = low_rank
        logits_ref[...] = logits
        for i in range(ROWS // BLOCK):
            block = slice(i * BLOCK, (i + 1) * BLOCK)
            attended, mixed = forward_block(
                query[block], key[block], value[block], logits[block], gate[block], gain_out_ref[...],
                memory, states_ref.at[i],
            )
            attended_ref[block, :] = attended
            mixed_ref[block, :] = mixed
        part = dot(mixed_ref[...], w_out[...])
        tile = step % own_tiles
        tile_rows = pl.ds(pl.multiple_of(tile * ROWS, ROWS), ROWS)
        mine = step // own_tiles == at.head

        @pl.when(mine)
        def _():
            resid[tile_rows, :] = part

        @pl.when(jnp.logical_not(mine))
        def _():
            part_out[tile_rows, :] = part.astype(BF16)
            put(part_out.at[tile_rows], part_in.at[tile_rows], 2 + tile)

    @pl.when(step == attention_steps)
    def _():
        for i in range(own_tiles):
            rows = pl.ds(i * ROWS, ROWS)
            wait(part_in.at[rows], 2 + i)
            full = tokens[own_rows(i), :].astype(F32) + resid[rows, :] + part_in[rows, :].astype(F32)
            resid[rows, :] = full
            scale = lax.rsqrt(jnp.mean(full * full, axis=1, keepdims=True) + EPSILON)
            h_two[own_rows(i), :] = (full * scale * gain_two_ref[...]).astype(BF16)
            put(h_two.at[own_rows(i)], h_two.at[own_rows(i)], 4 + i)

        def turn(i, carry):
            rows = pl.ds(pl.multiple_of(i * ROWS, ROWS), ROWS)
            low_turned[:, rows] = jnp.transpose(low[rows, :])
            return carry

        lax.fori_loop(0, tiles, turn, 0)
        for i in range(own_tiles):
            wait(h_two.at[other_rows(i)], 4 + i)

        def turn_two(i, carry):
            rows = pl.ds(pl.multiple_of(i * ROWS, ROWS), ROWS)
            h_two_turned[:, rows] = jnp.transpose(h_two[rows, :])
            return carry

        lax.fori_loop(0, tiles, turn_two, 0)

    def hidden_rows(block, first):
        width = block.shape[3] // 3

        def body(i, carry):
            rows = pl.ds(pl.multiple_of(i * ROWS, ROWS), ROWS)
            w_pair = block[:, :, :, : 2 * width].reshape(-1, 2 * width)
            w_down = block[:, :, :, 2 * width :].reshape(-1, width)
            pair = dot(h_two[rows, :], w_pair)
            inner_grad = dot(low[rows, :], w_down)
            pre_gate = pair[:, :width]
            up_part = pair[:, width:]
            pre_sigmoid = sigmoid(pre_gate)
            swish = pre_gate * pre_sigmoid
            inner = (swish * up_part).astype(BF16)
            pre_grad = inner_grad * up_part * pre_sigmoid * (1.0 + pre_gate * (1.0 - pre_sigmoid))
            both = jnp.concatenate([pre_grad.astype(BF16), (inner_grad * swish).astype(BF16)], axis=1)
            inner_all[rows, :width] = inner
            pair_all[rows, : 2 * width] = both
            out_part = dot(inner, w_down, 1, 1)
            grad_part = dot(both, w_pair, 1, 1)
            if first:
                mlp_sum[rows, :] = out_part
                grad_sum[rows, :] = grad_part
            else:
                mlp_sum[rows, :] += out_part
                grad_sum[rows, :] += grad_part
            return carry

        lax.fori_loop(0, tiles, body, 0)

    def weight_rows(block, target):
        width = block.shape[3] // 3

        def body(i, carry):
            rows = pl.ds(pl.multiple_of(i * ROWS, ROWS), ROWS)
            shape = (target.shape[1], target.shape[2], -1)
            target[i, :, :, : 2 * width] = (
                dot(h_two_turned[rows, :], pair_all[:, : 2 * width]).astype(BF16).reshape(shape)
            )
            target[i, :, :, 2 * width :] = (
                dot(low_turned[rows, :], inner_all[:, :width]).astype(BF16).reshape(shape)
            )
            return carry

        lax.fori_loop(0, tiles, body, 0)

    @pl.when(step == first_step)
    def _():
        hidden_rows(weights_zero, True)
        weight_rows(weights_zero, grad_zero_ref)

    @pl.when(step > first_step)
    def _():
        block = weights.at[step - first_step - 1]
        hidden_rows(block, False)

        @pl.when(step == last_step)
        def _():
            for i in range(own_tiles):
                rows = pl.ds(i * ROWS, ROWS)
                for k, source in enumerate((mlp_sum, grad_sum)):
                    sums_out[k, rows, :] = source[other_rows(i), :].astype(BF16)
                    put(sums_out.at[k, rows], sums_in.at[k, rows], 6 + 2 * i + k)

        weight_rows(block, grad_ref.at[0])

    @pl.when(step == last_step)
    def _():
        for i in range(own_tiles):
            sent(h_two.at[pl.ds(0, ROWS)], pair_out.at[4 + i], pair_in.at[4 + i], at.sibling)
        for i in range(own_tiles):
            rows = pl.ds(i * ROWS, ROWS)
            for k in range(2):
                wait(sums_in.at[k, rows], 6 + 2 * i + k)
            full = resid[rows, :]
            scale = lax.rsqrt(jnp.mean(full * full, axis=1, keepdims=True) + EPSILON)
            normal = full * scale
            mlp_out = mlp_sum[own_rows(i), :] + sums_in[0, rows, :].astype(F32)
            output_ref[rows, :] = (mask_ref[rows, :] * (full + mlp_out)).astype(BF16)
            grad = grad_sum[own_rows(i), :] + sums_in[1, rows, :].astype(F32)
            total = low[own_rows(i), :].astype(F32) + norm_backward(grad, gain_two_ref[...], normal, scale)
            total_ref[rows, :] = total
            gain_grad_ref[...] += jnp.sum(grad * normal, axis=0, keepdims=True)
            h_two[own_rows(i), :] = total.astype(BF16)
            put(h_two.at[own_rows(i)], h_two.at[own_rows(i)], 10 + i)
            pltpu.make_async_copy(h_two.at[own_rows(i)], attn_ref.at[own_rows(i)], local_sems.at[i]).start()
        gather.finish()
        for i in range(own_tiles):
            wait(h_two.at[other_rows(i)], 10 + i)
            pltpu.make_async_copy(
                h_two.at[other_rows(i)], attn_ref.at[other_rows(i)], local_sems.at[own_tiles + i]
            ).start()
        for slot, ref in enumerate(
            [tokens_ref, low_ref] + [part_out.at[pl.ds(0, ROWS)]] * 8 + [h_two.at[pl.ds(0, ROWS)]] * 2
        ):
            if slot not in (4, 5):
                sent(ref, pair_out.at[slot], pair_in.at[slot], at.sibling)
        for i in range(tiles):
            rows = own_rows(i) if i < own_tiles else other_rows(i - own_tiles)
            pltpu.make_async_copy(h_two.at[rows], attn_ref.at[rows], local_sems.at[i]).wait()


def whole(shape):
    return pl.BlockSpec(shape, lambda i: (0,) * len(shape), pipeline_mode=pl.Buffered(1))


def chunked(pieces, first):
    rows, _, half = pieces.shape
    rest = pieces[:, :, first:].reshape(rows, 3, -1, 2 * first)
    return pieces[:, :, :first].reshape(rows, -1), rest.transpose(2, 0, 1, 3).reshape(-1, rows, 6 * first)


def layer(
    tokens, low, mask, gain_one, gain_two, gain_out, bias, start,
    w_query, w_key, w_value, w_gate, w_low_in, w_low_out, w_out, own_piece, other_piece,
):
    own, width = tokens.shape
    length = 2 * own
    keys, values, heads = w_query.shape[1], w_value.shape[1], start.shape[0]
    rank = w_low_in.shape[1]
    piece_zero, pieces = chunked(own_piece, 128)
    other_zero, others = chunked(other_piece, 128)
    count = pieces.shape[0] + 1
    group = 2 * piece_zero.shape[0]
    tiles = length // ROWS
    first_step = tiles + 1
    steps = first_step + count

    def rows_spec(columns):
        return pl.BlockSpec((ROWS, columns), lambda i: (jnp.minimum(i, tiles - 1), 0))

    vmem = pl.BlockSpec(memory_space=pltpu.VMEM)
    row_shapes = [
        (width, BF16), (keys, BF16), (keys, BF16), (values, BF16), (values, F32), (keys, F32), (rank, F32),
        (values, F32), (values, BF16),
    ]
    blocks = ROWS // BLOCK
    return pl.pallas_call(
        functools.partial(layer_kernel, count),
        grid=(steps,),
        in_specs=[
            ANY, ANY, whole(mask.shape), whole((1, width)), whole((1, width)), whole((1, VALUE_HEAD)),
            whole((1, keys)), whole(start.shape), whole(w_query.shape), whole(w_key.shape), whole(w_value.shape),
            whole(w_gate.shape), whole(w_low_in.shape), whole(w_low_out.shape), whole(w_out.shape),
            ANY, ANY, ANY, ANY,
        ],
        out_specs=[rows_spec(columns) for columns, _ in row_shapes]
        + [
            pl.BlockSpec((blocks, heads, KEY_HEAD, VALUE_HEAD), lambda i: (jnp.minimum(i, tiles - 1), 0, 0, 0)),
            whole((4, 4, group, 384)),
            pl.BlockSpec(
                (1, 4, 4, group, 768), lambda i: (jnp.clip(i - first_step - 1, 0, count - 2), 0, 0, 0, 0)
            ),
            vmem, vmem, ANY, vmem,
        ],
        out_shape=[jax.ShapeDtypeStruct((length, columns), kind) for columns, kind in row_shapes]
        + [
            jax.ShapeDtypeStruct((length // BLOCK, heads, KEY_HEAD, VALUE_HEAD), BF16),
            jax.ShapeDtypeStruct((4, 4, group, 384), BF16),
            jax.ShapeDtypeStruct((count - 1, 4, 4, group, 768), BF16),
            jax.ShapeDtypeStruct((own, width), BF16),
            jax.ShapeDtypeStruct((own, width), F32),
            jax.ShapeDtypeStruct((length, width), BF16),
            jax.ShapeDtypeStruct((1, width), F32),
        ],
        scratch_shapes=[
            pltpu.VMEM((length, width), BF16),
            pltpu.VMEM((length, width), BF16),
            pltpu.VMEM((width, length), BF16),
            pltpu.VMEM((length, width), BF16),
            pltpu.VMEM((width, length), BF16),
            pltpu.VMEM((4, 4, group, 384), BF16),
            pltpu.VMEM((count - 1, 4, 4, group, 768), BF16),
            pltpu.VMEM((own, width), F32),
            pltpu.VMEM((own, width), BF16),
            pltpu.VMEM((own, width), BF16),
            pltpu.VMEM((length, width), F32),
            pltpu.VMEM((length, width), F32),
            pltpu.VMEM((length, 256), BF16),
            pltpu.VMEM((length, 512), BF16),
            pltpu.VMEM((2, own, width), BF16),
            pltpu.VMEM((2, own, width), BF16),
            pltpu.VMEM((heads, KEY_HEAD, VALUE_HEAD), F32),
            pltpu.SemaphoreType.DMA((tiles,)),
            pltpu.SemaphoreType.DMA((count,)),
            pltpu.SemaphoreType.DMA((count, 8)),
            pltpu.SemaphoreType.DMA((count, 8)),
            pltpu.SemaphoreType.DMA((12,)),
            pltpu.SemaphoreType.DMA((12,)),
        ],
        compiler_params=pltpu.CompilerParams(
            collective_id=0, has_side_effects=True, vmem_limit_bytes=63 << 20
        ),
        name="layer",
    )(
        tokens, low, mask, gain_one.reshape(1, -1), gain_two.reshape(1, -1), gain_out.reshape(1, -1),
        bias.reshape(1, -1), start, w_query, w_key, w_value, w_gate, w_low_in, w_low_out, w_out,
        piece_zero, pieces, other_zero, others,
    )


class Reduce:
    def __init__(self, place, partial, via_x, via_y, from_x, from_y, from_z, chunks, out_sems, in_sems):
        self.place, self.partial, self.chunks = place, partial, chunks
        self.via_x, self.via_y, self.from_x, self.from_y, self.from_z = via_x, via_y, from_x, from_y, from_z
        self.out_sems, self.in_sems = out_sems, in_sems

    def put(self, source, target, chunk, slot, device):
        send(source, target, self.out_sems.at[chunk, slot], self.in_sems.at[chunk, slot], device)

    def wait(self, target, chunk, slot):
        arrived(target, self.out_sems.at[chunk, slot], self.in_sems.at[chunk, slot], self.place.sibling)

    def stage(self, number, chunk):
        at, partial, columns = self.place, self.partial, self.chunks[chunk]
        everything = slice(None)
        low, high = pl.ds(0, 2), pl.ds(2, 2)
        view = (everything, everything, columns)
        if number == 0:
            self.put(partial.at[low, at.flat_xy, everything, columns], self.via_x.at[view], chunk, 0, at.beside_x)
            self.put(partial.at[high, at.flat_xy, everything, columns], self.via_y.at[view], chunk, 1, at.beside_y)
        if number == 1:
            self.wait(self.via_x.at[view], chunk, 0)
            block = (low, at.flat_y, everything, columns)
            partial[block] = (partial[block].astype(F32) + self.via_x[view].astype(F32)).astype(BF16)
            self.put(
                partial.at[everything, at.flat_y, everything, columns], self.from_y.at[view], chunk, 2, at.beside_y
            )
            self.wait(self.via_y.at[view], chunk, 1)
            block = (high, at.flat_x, everything, columns)
            partial[block] = (partial[block].astype(F32) + self.via_y[view].astype(F32)).astype(BF16)
            self.put(
                partial.at[everything, at.flat_x, everything, columns], self.from_x.at[view], chunk, 3, at.beside_x
            )
        if number == 2:
            self.wait(self.from_y.at[view], chunk, 2)
            self.wait(self.from_x.at[view], chunk, 3)
            block = (everything, at.flat, everything, columns)
            partial[block] = (
                partial[block].astype(F32) + self.from_x[view].astype(F32) + self.from_y[view].astype(F32)
            ).astype(BF16)
            for i in range(3):
                self.put(
                    partial.at[(at.z + 1 + i) % 4, at.flat, everything, columns],
                    self.from_z.at[i, everything, columns],
                    chunk,
                    4 + i,
                    at.along_z[i],
                )

    def result(self, chunk):
        at, columns = self.place, self.chunks[chunk]
        total = self.partial[at.z, at.flat, :, columns].astype(F32)
        for i in range(3):
            self.wait(self.from_z.at[i, :, columns], chunk, 4 + i)
            total += self.from_z[i, :, columns].astype(F32)
        return total

    def finish(self):
        for chunk, columns in enumerate(self.chunks):
            pair, four, one = [self.partial.at[pl.ds(0, n), 0, :, columns] for n in (2, 4, 1)]
            for slot, ref in enumerate([pair] * 2 + [four] * 2 + [one] * 3):
                sent(ref, self.out_sems.at[chunk, slot], self.in_sems.at[chunk, slot], self.place.sibling)


GAIN_ONE, GAIN_TWO, GAIN_OUT, LOW_IN = 0, 8, 16, 24


def small_rows(width, rank, keys):
    decay = LOW_IN + rank * width // 128
    slot = -(-(rank + 1) * keys // 128 // 8) * 8
    return decay, slot, decay + 2 * slot


def backward_kernel(
    half, mlp_chunks, attn_chunks,
    zero_ref, groups_ref, attn_ref, h_ref, query_ref, key_ref, value_ref, gate_ref, logits_ref, low_rank_ref,
    attended_ref, mixed_ref, states_ref, w_query, w_key, w_value, w_gate, w_low_in, w_low_out, w_out,
    tokens_ref, total_ref, gain_one_ref, gain_out_ref, gain_two_grad_ref,
    mlp_out, attn_out, small_out, tokens_out,
    mlp, attn, mlp_via_x, mlp_via_y, mlp_from_x, mlp_from_y, mlp_from_z,
    attn_via_x, attn_via_y, attn_from_x, attn_from_y, attn_from_z, summed, swapped,
    small_own, small_in, small_z, h_turned, attn_turned, right, mixed_all, h_grad, h_grad_out, h_grad_in,
    memory_grad, gain_out_sum, low_in_sum, low_out_sum, bias_sum,
    load_sems, mlp_sems_out, mlp_sems_in, attn_sems_out, attn_sems_in, pair_out, pair_in, small_sems_out, small_sems_in,
):
    step = pl.program_id(0)
    at = Place()
    own = tokens_ref.shape[0]
    own_tiles = own // ROWS
    tiles = 2 * own_tiles
    keys, values = w_query.shape[1], w_value.shape[1]
    rank, width = w_low_out.shape[0], tokens_ref.shape[1]
    decay_at, decay_slot, _ = small_rows(width, rank, keys)
    last_step = 2 * tiles
    sides = [
        Reduce(at, mlp, mlp_via_x, mlp_via_y, mlp_from_x, mlp_from_y, mlp_from_z, mlp_chunks, mlp_sems_out, mlp_sems_in),
        Reduce(
            at, attn, attn_via_x, attn_via_y, attn_from_x, attn_from_y, attn_from_z, attn_chunks,
            attn_sems_out, attn_sems_in,
        ),
    ]
    order = [(0, i) for i in range(len(mlp_chunks))] + [(1, i) for i in range(len(attn_chunks))]
    count = len(order)
    rows = mlp.shape[2] // 2

    def load(chunk):
        source = groups_ref.at[chunk - 1] if chunk else zero_ref
        return pltpu.make_async_copy(source, mlp.at[:, :, :, mlp_chunks[chunk]], load_sems.at[chunk])

    def put(source, target, slot):
        send(source, target, pair_out.at[slot], pair_in.at[slot], at.sibling)

    def wait(target, slot):
        arrived(target, pair_out.at[slot], pair_in.at[slot], at.sibling)

    def small(number):
        def put_small(source, target, slot, device):
            send(source, target, small_sems_out.at[slot], small_sems_in.at[slot], device)

        def wait_small(target, slot):
            arrived(target, small_sems_out.at[slot], small_sems_in.at[slot], at.sibling)

        if number == 0:
            put_small(small_own, small_in.at[0], 0, at.sibling)
        elif number in (1, 2):
            source = small_own if number == 1 else small_z.at[number - 2]
            wait_small(small_in.at[number - 1], number - 1)
            small_z[number - 1] = source[...] + small_in[number - 1]
            put_small(small_z.at[number - 1], small_in.at[number], number, at.beside_x if number == 1 else at.beside_y)
        elif number == 3:
            wait_small(small_in.at[2], 2)
            small_z[2 + at.z] = small_z[1] + small_in[2]
            for i in range(3):
                put_small(small_z.at[2 + at.z], small_z.at[2 + at.z], 3 + i, at.along_z[i])
        elif number == 4:
            for i in range(3):
                wait_small(small_z.at[2 + (at.z + 3 - i) % 4], 3 + i)
            small_out[...] = small_z[2] + small_z[3] + small_z[4] + small_z[5]
            for slot in range(6):
                sent(small_own, small_sems_out.at[slot], small_sems_in.at[slot], at.sibling)

    def result(side, chunk):
        total = sides[side].result(chunk)
        if side == 0:
            columns = mlp_chunks[chunk]
            summed[:, columns] = total
            put(
                summed.at[pl.ds(pl.multiple_of((1 - at.head) * rows, 8), rows), columns], swapped.at[:, columns],
                2 + chunk,
            )
        else:
            attn_out[:, attn_chunks[chunk]] = total

    def tick(number):
        if 0 <= number - 3 < count:
            result(*order[number - 3])
        for stage in range(2, -1, -1):
            if 0 <= number - stage < count:
                side, chunk = order[number - stage]
                if stage == 0 and side == 0:
                    load(chunk).wait()
                sides[side].stage(stage, chunk)

    def own_rows(i):
        return pl.ds(pl.multiple_of(i * ROWS, ROWS), ROWS)

    @pl.when(step == 0)
    def _():
        for chunk in range(len(mlp_chunks)):
            load(chunk).start()
        memory_grad[...] = jnp.zeros_like(memory_grad)
        gain_out_sum[...] = jnp.zeros_like(gain_out_sum)
        low_in_sum[...] = jnp.zeros_like(low_in_sum)
        low_out_sum[...] = jnp.zeros_like(low_out_sum)
        bias_sum[...] = jnp.zeros_like(bias_sum)
        at.meet()

    early_ticks = min(len(mlp_chunks), last_step)
    for number in range(early_ticks):

        @pl.when(step == number)
        def _():
            tick(number)

    @pl.when(step < tiles)
    def _():
        tile = tiles - 1 - step
        here = pl.ds(pl.multiple_of(tile * ROWS, ROWS), ROWS)
        attn_tile = attn_ref[...]
        h_tile = h_ref[...]
        attn_turned[:, here] = jnp.transpose(attn_tile)
        h_turned[:, here] = jnp.transpose(h_tile)
        mixed_all[here, :] = mixed_ref[...]
        mixed_grad = dot(attn_tile, w_out[...], 1, 1)
        logits_parts = []
        for i in range(ROWS // BLOCK - 1, -1, -1):
            block = slice(i * BLOCK, (i + 1) * BLOCK)
            grads, logits_grad, gain_grad = backward_block(
                mixed_grad[block], query_ref[block, :], key_ref[block, :], value_ref[block, :], logits_ref[block, :],
                gate_ref[block, :], attended_ref[block, :], states_ref[i], gain_out_ref[...], memory_grad,
            )
            right[pl.ds(pl.multiple_of(tile * ROWS + i * BLOCK, BLOCK), BLOCK), :] = grads
            gain_out_sum[...] += gain_grad
            logits_parts.append(logits_grad)
        logits_grad = jnp.concatenate(logits_parts[::-1], axis=0)
        high, rest = split_low(logits_grad)
        rank_high, rank_rest = split_low(low_rank_ref[...])
        bias_sum[...] += jnp.sum(logits_grad, axis=0, keepdims=True)
        low_out_sum[...] += dot(rank_high, high, 0, 0) + dot(rank_rest, high, 0, 0) + dot(rank_high, rest, 0, 0)
        low_rank_low = (dot(high, w_low_out[...], 1, 1) + dot(rest, w_low_out[...], 1, 1)).astype(BF16)
        low_in_sum[...] += dot(low_rank_low, h_tile, 0, 0)
        grads = right[here, :]
        part = (
            dot(grads[:, :keys], w_query[...], 1, 1)
            + dot(grads[:, keys : 2 * keys], w_key[...], 1, 1)
            + dot(grads[:, 2 * keys : 2 * keys + values], w_value[...], 1, 1)
            + dot(grads[:, 2 * keys + values :], w_gate[...], 1, 1)
            + dot(low_rank_low, w_low_in[...], 1, 1)
        )
        place = tile % own_tiles
        mine = tile // own_tiles == at.head

        @pl.when(mine)
        def _():
            h_grad[own_rows(place), :] = part

        @pl.when(jnp.logical_not(mine))
        def _():
            h_grad_out[own_rows(place), :] = part.astype(BF16)
            put(h_grad_out.at[own_rows(place)], h_grad_in.at[own_rows(place)], place)

    @pl.when(step == tiles)
    def _():
        gain_one = jnp.zeros((1, width), F32)
        for i in range(own_tiles):
            here = own_rows(i)
            wait(h_grad_in.at[here], i)
            wide = tokens_ref[here, :].astype(F32)
            scale = lax.rsqrt(jnp.mean(wide * wide, axis=1, keepdims=True) + EPSILON)
            normal = wide * scale
            grad = h_grad[here, :] + h_grad_in[here, :].astype(F32)
            tokens_out[here, :] = total_ref[here, :] + norm_backward(grad, gain_one_ref[...], normal, scale)
            gain_one += jnp.sum(grad * normal, axis=0, keepdims=True)
        small_own[...] = jnp.zeros_like(small_own)
        for i in range(width // 128):
            columns = slice(i * 128, (i + 1) * 128)
            small_own[GAIN_ONE + i : GAIN_ONE + i + 1, :] = gain_one[:, columns]
            small_own[GAIN_TWO + i : GAIN_TWO + i + 1, :] = gain_two_grad_ref[:, columns]
            small_own[LOW_IN + i * rank : LOW_IN + (i + 1) * rank, :] = low_in_sum[:, columns]
        for i in range(VALUE_HEAD // 128):
            small_own[GAIN_OUT + i : GAIN_OUT + i + 1, :] = gain_out_sum[:, i * 128 : (i + 1) * 128]
        for head in range(2):

            @pl.when(at.head == head)
            def _():
                base = decay_at + head * decay_slot
                for i in range(keys // 128):
                    columns = slice(i * 128, (i + 1) * 128)
                    small_own[base + i * rank : base + (i + 1) * rank, :] = low_out_sum[:, columns]
                    bias_at = base + keys // 128 * rank + i
                    small_own[bias_at : bias_at + 1, :] = bias_sum[:, columns]

        small(0)

    for number in range(1, 5):

        @pl.when(step == tiles + number)
        def _():
            small(number)

    @pl.when(jnp.logical_and(step >= tiles, step < 2 * tiles))
    def _():
        part = step - tiles
        here = pl.ds(pl.multiple_of(part * ROWS, ROWS), ROWS)
        shape = (attn.shape[1], attn.shape[2], -1)
        edge = right.shape[1]
        attn[part, :, :, :edge] = dot(h_turned[here, :], right[...]).astype(BF16).reshape(shape)
        attn[part, :, :, edge:] = dot(attn_turned[here, :], mixed_all[...]).astype(BF16).reshape(shape)

    def spread(source, head):
        offset = 0
        for columns in mlp_chunks:
            size = (columns.stop - columns.start) // 3
            for part in range(3):
                start = columns.start + part * size
                target = pl.ds(pl.multiple_of(part * 2 * half + head * half + offset, 128), size)
                mlp_out[:, target] = source[:, start : start + size]
            offset += size

    @pl.when(step == last_step)
    def _():
        for number in range(early_ticks, count + 3):
            tick(number)
            if number == len(mlp_chunks) + 3:
                spread(summed.at[pl.ds(pl.multiple_of(at.head * rows, 8), rows)], at.head)
                for chunk, columns in enumerate(mlp_chunks):
                    wait(swapped.at[:, columns], 2 + chunk)
                spread(swapped, 1 - at.head)
        for i in range(own_tiles):
            sent(h_grad_out.at[own_rows(i)], pair_out.at[i], pair_in.at[i], at.sibling)
        for chunk, columns in enumerate(mlp_chunks):
            sent(swapped.at[:, columns], pair_out.at[2 + chunk], pair_in.at[2 + chunk], at.sibling)
        for side in sides:
            side.finish()


def backward(
    zero, groups, attn_low, h_low, query, key, value, gate, logits, low_rank, attended, mixed, states,
    w_query, w_key, w_value, w_gate, w_low_in, w_low_out, w_out, tokens, total, gain_one, gain_out, gain_two_grad,
):
    length, width = h_low.shape
    keys, values, heads = query.shape[1], value.shape[1], states.shape[1]
    rank = w_low_out.shape[0]
    own = tokens.shape[0]
    tiles = length // ROWS
    rows = width // 16
    mlp_count = groups.shape[0] + 1
    edges = [0] + [zero.shape[-1] + i * groups.shape[-1] for i in range(mlp_count)]
    mlp_chunks = [slice(edges[i], edges[i + 1]) for i in range(mlp_count)]
    mlp_width = edges[-1]
    attn_width = 2 * keys + 3 * values
    attn_count = 4
    attn_chunks = chunk_columns(attn_width, [attn_width // 128 // attn_count] * attn_count)
    small_shape = (small_rows(width, rank, keys)[2], 128)
    vmem = pl.BlockSpec(memory_space=pltpu.VMEM)

    def rows_spec(columns):
        return pl.BlockSpec((ROWS, columns), lambda i: (jnp.maximum(tiles - 1 - i, 0), 0))

    buffers = []
    for columns in (mlp_width, attn_width):
        buffers += [pltpu.VMEM((n, rows, columns), BF16) for n in (2, 2, 4, 4, 3)]
    streamed = [attn_low, h_low, query, key, value, gate, logits, low_rank, attended, mixed]
    constant = [
        w_query, w_key, w_value, w_gate, w_low_in, w_low_out, w_out, tokens, total,
        gain_one.reshape(1, -1), gain_out.reshape(1, -1), gain_two_grad.reshape(1, -1),
    ]
    return pl.pallas_call(
        functools.partial(backward_kernel, mlp_width // 3, mlp_chunks, attn_chunks),
        grid=(2 * tiles + 1,),
        in_specs=[ANY, ANY]
        + [rows_spec(a.shape[1]) for a in streamed]
        + [
            pl.BlockSpec(
                (ROWS // BLOCK, heads, KEY_HEAD, VALUE_HEAD), lambda i: (jnp.maximum(tiles - 1 - i, 0), 0, 0, 0)
            )
        ]
        + [whole(a.shape) for a in constant],
        out_specs=[vmem, vmem, vmem, vmem],
        out_shape=[
            jax.ShapeDtypeStruct((rows // 2, 2 * mlp_width), F32),
            jax.ShapeDtypeStruct((rows, attn_width), F32),
            jax.ShapeDtypeStruct(small_shape, F32),
            jax.ShapeDtypeStruct((own, width), F32),
        ],
        scratch_shapes=[
            pltpu.VMEM((4, 4, rows, mlp_width), BF16),
            pltpu.VMEM((4, 4, rows, attn_width), BF16),
            *buffers,
            pltpu.VMEM((rows, mlp_width), F32),
            pltpu.VMEM((rows // 2, mlp_width), F32),
            pltpu.VMEM(small_shape, F32),
            pltpu.VMEM((3,) + small_shape, F32),
            pltpu.VMEM((6,) + small_shape, F32),
            pltpu.VMEM((width, length), BF16),
            pltpu.VMEM((width, length), BF16),
            pltpu.VMEM((length, 2 * keys + 2 * values), BF16),
            pltpu.VMEM((length, values), BF16),
            pltpu.VMEM((own, width), F32),
            pltpu.VMEM((own, width), BF16),
            pltpu.VMEM((own, width), BF16),
            pltpu.VMEM((heads, KEY_HEAD, VALUE_HEAD), F32),
            pltpu.VMEM((1, VALUE_HEAD), F32),
            pltpu.VMEM((rank, width), F32),
            pltpu.VMEM((rank, keys), F32),
            pltpu.VMEM((1, keys), F32),
            pltpu.SemaphoreType.DMA((mlp_count,)),
            pltpu.SemaphoreType.DMA((mlp_count, 7)),
            pltpu.SemaphoreType.DMA((mlp_count, 7)),
            pltpu.SemaphoreType.DMA((attn_count, 7)),
            pltpu.SemaphoreType.DMA((attn_count, 7)),
            pltpu.SemaphoreType.DMA((2 + mlp_count,)),
            pltpu.SemaphoreType.DMA((2 + mlp_count,)),
            pltpu.SemaphoreType.DMA((6,)),
            pltpu.SemaphoreType.DMA((6,)),
        ],
        compiler_params=pltpu.CompilerParams(
            collective_id=1, has_side_effects=True, vmem_limit_bytes=63 << 20
        ),
        name="backward",
    )(zero, groups, *streamed, states, *constant)


def swap(value):
    return lax.ppermute(value, "head", [(0, 1), (1, 0)])


def ordered(own, other, axis):
    size = own.shape[axis]
    joined = jnp.concatenate([own, other, own], axis=axis)
    return lax.dynamic_slice_in_dim(joined, lax.axis_index("head") * size, 2 * size, axis)


def half_of(value, which, axis):
    size = value.shape[axis] // 2
    return lax.dynamic_slice_in_dim(value, which * size, size, axis)


def sum_rows(partial, here):
    other = swap(half_of(partial, 1 - here, 0).astype(BF16))
    return half_of(partial, here, 0) + other.astype(F32)


def norm_backward(grad_in, gain, normed_in, scale_in):
    scaled = grad_in * gain
    return scale_in * (scaled - normed_in * jnp.mean(scaled * normed_in, axis=-1, keepdims=True))


def per_device(
    tokens, lengths, initial_memory, norm_attn_gain, w_query, w_key, w_value, w_gate_out, w_low_in, w_low_out,
    decay_bias, out_gain, w_out, norm_mlp_gain, w_mlp, cotangent,
):
    here = lax.axis_index("head")
    own_rows = tokens.shape[1]
    keys = w_query.shape[1]
    values = w_value.shape[1]
    hidden = w_mlp.shape[1] // 3
    half = hidden // 2
    shard_rows = w_mlp.shape[0]
    square = lax.axis_size("dp") == 16

    pieces = w_mlp.reshape(shard_rows, 3, 2, half)
    own_piece = lax.dynamic_index_in_dim(pieces, here, 2, keepdims=False)
    other_piece = lax.dynamic_index_in_dim(pieces, 1 - here, 2, keepdims=False)
    tokens_own = tokens[0]
    positions = here * own_rows + lax.iota(jnp.int32, own_rows)
    row_mask = (positions < lengths[0]).astype(F32)[:, None]
    resid_grad = row_mask * cotangent[0].astype(F32)
    low_own = resid_grad.astype(BF16)
    if square:
        (
            h_low, query, key, value, gate, logits, low_rank, attended, mixed, states,
            grad_zero, grad_mlp, output, resid_total, attn_low, gain_two_grad,
        ) = layer(
            tokens_own, low_own, row_mask, norm_attn_gain, norm_mlp_gain, out_gain, decay_bias, initial_memory[0],
            w_query, w_key, w_value, w_gate_out, w_low_in, w_low_out, w_out, own_piece, other_piece,
        )
        grad_mlp, attn_grads, packed, tokens_grad = backward(
            grad_zero, grad_mlp, attn_low, h_low, query, key, value, gate, logits, low_rank, attended, mixed, states,
            w_query, w_key, w_value, w_gate_out, w_low_in, w_low_out, w_out, tokens_own, resid_total,
            norm_attn_gain, out_gain, gain_two_grad,
        )
        output = output[None]
        rank = w_low_out.shape[0]
        model = tokens_own.shape[1]
        decay_at, decay_slot, _ = small_rows(model, rank, keys)
        gain_one_grad = packed[GAIN_ONE : GAIN_ONE + model // 128].reshape(-1)
        gain_two_grad = packed[GAIN_TWO : GAIN_TWO + model // 128].reshape(-1)
        out_gain_grad = packed[GAIN_OUT : GAIN_OUT + VALUE_HEAD // 128].reshape(-1)
        low_in_grad = packed[LOW_IN:decay_at].reshape(-1, rank, 128).transpose(0, 2, 1).reshape(model, rank)
        decay_part = lax.dynamic_slice_in_dim(packed, decay_at + here * decay_slot, decay_slot, 0)
        edge = keys // 128 * rank
        low_out_grad = decay_part[:edge].reshape(-1, rank, 128).transpose(1, 0, 2).reshape(rank, keys)
        bias_grad = decay_part[edge : edge + keys // 128].reshape(-1)
    else:
        pair = swap(other_piece.reshape(shard_rows, 3 * half))
        weights = lax.all_gather(
            ordered(own_piece.reshape(shard_rows, 3 * half), pair, 0), "dp", axis=0, tiled=True
        )
        tokens_wide = ordered(tokens_own, swap(tokens_own), 0).astype(F32)
        length = tokens_wide.shape[0]
        scale_one = lax.rsqrt(jnp.mean(tokens_wide * tokens_wide, axis=1, keepdims=True) + EPSILON)
        h_low = (tokens_wide * scale_one * norm_attn_gain).astype(BF16)
        query = dot(h_low, w_query).astype(BF16)
        key = dot(h_low, w_key).astype(BF16)
        value = dot(h_low, w_value).astype(BF16)
        gate = dot(h_low, w_gate_out)
        low_rank = dot(h_low, w_low_in)
        low_high, low_rest = split_low(low_rank)
        logits = dot(low_high, w_low_out) + dot(low_rest, w_low_out) + decay_bias
        attended, mixed, states = attention_forward(query, key, value, logits, gate, out_gain, initial_memory[0])
        resid = tokens_own.astype(F32) + sum_rows(dot(mixed, w_out), here)
        scale_two = lax.rsqrt(jnp.mean(resid * resid, axis=1, keepdims=True) + EPSILON)
        normal_two = resid * scale_two
        h_two_own = (normal_two * norm_mlp_gain).astype(BF16)
        h_two = ordered(h_two_own, swap(h_two_own), 0)
        resid_low = ordered(low_own, swap(low_own), 0)
        pre_gate = dot(h_two, weights[:, :half])
        up_part = dot(h_two, weights[:, half : 2 * half])
        pre_sigmoid = sigmoid(pre_gate)
        inner = (pre_gate * pre_sigmoid * up_part).astype(BF16)
        inner_grad = dot(resid_low, weights[:, 2 * half :])
        pre_grad = (
            inner_grad * up_part * pre_sigmoid * (1.0 + pre_gate * (1.0 - pre_sigmoid))
        ).astype(BF16)
        up_grad = (inner_grad * pre_gate * pre_sigmoid).astype(BF16)
        mlp_out = sum_rows(dot(inner, weights[:, 2 * half :], 1, 1), here)
        output = (row_mask * (resid + mlp_out)).astype(BF16)[None]
        h_two_grad = sum_rows(
            dot(pre_grad, weights[:, :half], 1, 1) + dot(up_grad, weights[:, half : 2 * half], 1, 1), here
        )
        grad_mlp = jnp.concatenate(
            [
                dot(h_two, pre_grad, 0, 0).astype(BF16),
                dot(h_two, up_grad, 0, 0).astype(BF16),
                dot(resid_low, inner, 0, 0).astype(BF16),
            ],
            axis=1,
        )
        resid_total = resid_grad + norm_backward(h_two_grad, norm_mlp_gain, normal_two, scale_two)
        gain_two_grad = jnp.sum(h_two_grad * normal_two, axis=0)
        attn_own = resid_total.astype(BF16)
        attn_low = ordered(attn_own, swap(attn_own), 0)

        mixed_grad = dot(attn_low, w_out, 1, 1)
        out_grad = dot(attn_low, mixed, 0, 0)
        query_grad, key_grad, value_grad, gate_grad, logits_grad, out_gain_grad = attention_backward(
            mixed_grad, query, key, value, logits, gate, attended, states, out_gain
        )
        bias_grad = jnp.sum(logits_grad, axis=0)
        grad_high, grad_rest = split_low(logits_grad)
        low_out_grad = (
            dot(low_high, grad_high, 0, 0) + dot(low_rest, grad_high, 0, 0) + dot(low_high, grad_rest, 0, 0)
        )
        low_rank_low = (dot(grad_high, w_low_out, 1, 1) + dot(grad_rest, w_low_out, 1, 1)).astype(BF16)
        low_in_grad = dot(h_low, low_rank_low, 0, 0)
        attn_grads = jnp.concatenate(
            [
                dot(h_low, query_grad, 0, 0).astype(BF16),
                dot(h_low, key_grad, 0, 0).astype(BF16),
                dot(h_low, value_grad, 0, 0).astype(BF16),
                dot(h_low, gate_grad, 0, 0).astype(BF16),
                out_grad.astype(BF16),
            ],
            axis=1,
        )
        h_grad = sum_rows(
            dot(query_grad, w_query, 1, 1)
            + dot(key_grad, w_key, 1, 1)
            + dot(value_grad, w_value, 1, 1)
            + dot(gate_grad, w_gate_out, 1, 1)
            + dot(low_rank_low, w_low_in, 1, 1),
            here,
        )
        own_wide = tokens_own.astype(F32)
        own_scale = lax.rsqrt(jnp.mean(own_wide * own_wide, axis=1, keepdims=True) + EPSILON)
        normal_own = own_wide * own_scale
        tokens_grad = resid_total + norm_backward(h_grad, norm_attn_gain, normal_own, own_scale)
        gain_one_grad = jnp.sum(h_grad * normal_own, axis=0)
        low_rank_width = w_low_out.shape[0]
        decay_part = jnp.concatenate([low_out_grad, bias_grad[None]], axis=0)
        slots = jnp.zeros((2,) + decay_part.shape, F32)
        slots = lax.dynamic_update_slice(slots, decay_part[None], (here, 0, 0))
        packed = jnp.concatenate(
            [
                gain_one_grad, gain_two_grad, out_gain_grad.reshape(-1), low_in_grad.reshape(-1), slots.reshape(-1),
            ]
        )
        packed = lax.psum(packed, ("dp", "head"))
        attn_grads = lax.psum_scatter(attn_grads, "dp", scatter_dimension=0, tiled=True).astype(F32)
        grad_mlp = lax.psum_scatter(grad_mlp, "dp", scatter_dimension=0, tiled=True)
        own_half = half_of(grad_mlp, here, 0)
        other_half = swap(half_of(grad_mlp, 1 - here, 0))
        grad_mlp = ordered(
            own_half.reshape(shard_rows, 3, 1, half), other_half.reshape(shard_rows, 3, 1, half), 2
        ).reshape(shard_rows, 3 * hidden).astype(F32)
        width = gain_one_grad.shape[0]
        edges = [width, 2 * width, 2 * width + VALUE_HEAD]
        edges.append(edges[-1] + width * low_rank_width)
        low_in_grad = packed[edges[2] : edges[3]].reshape(width, low_rank_width)
        decay_part = lax.dynamic_index_in_dim(packed[edges[3] :].reshape(slots.shape), here, 0, keepdims=False)
        low_out_grad, bias_grad = decay_part[:low_rank_width], decay_part[low_rank_width]
        gain_one_grad, gain_two_grad = packed[: edges[0]], packed[edges[0] : edges[1]]
        out_gain_grad = packed[edges[1] : edges[2]]
    return (
        output,
        tokens_grad[None],
        gain_one_grad,
        attn_grads[:, :keys],
        attn_grads[:, keys : 2 * keys],
        attn_grads[:, 2 * keys : 2 * keys + values],
        attn_grads[:, 2 * keys + values : 2 * keys + 2 * values],
        low_in_grad,
        low_out_grad,
        bias_grad,
        out_gain_grad,
        attn_grads[:, 2 * keys + 2 * values :].T,
        gain_two_grad,
        grad_mlp,
    )


def solution(mesh):
    return jax.shard_map(
        per_device,
        mesh=mesh,
        in_specs=(
            P("dp", "head", None),
            P("dp"),
            P("dp", "head", None, None),
            P(),
            P(None, "head"),
            P(None, "head"),
            P(None, "head"),
            P(None, "head"),
            P(),
            P(None, "head"),
            P("head"),
            P(),
            P("head", None),
            P(),
            P(("dp", "head"), None),
            P("dp", "head", None),
        ),
        out_specs=(
            P("dp", "head", None),
            P("dp", "head", None),
            P(),
            P("dp", "head"),
            P("dp", "head"),
            P("dp", "head"),
            P("dp", "head"),
            P(),
            P(None, "head"),
            P("head"),
            P(),
            P("head", "dp"),
            P(),
            P(("dp", "head"), None),
        ),
        check_vma=False,
    )
```

```python
import functools

import jax
import jax.numpy as jnp
from jax import lax
from jax.experimental import pallas as pl
from jax.experimental.pallas import tpu as pltpu
from jax.sharding import PartitionSpec as P

HEADS = 4
KEY = 512
VALUE = 1024
BLOCK = 128
KEY_HEAD = KEY // HEADS
VALUE_HEAD = VALUE // HEADS

EPSILON = 1e-05
F32 = jnp.float32
BF16 = jnp.bfloat16
SCALE = KEY_HEAD ** (-0.5)


def dot(left, right, left_dim=1, right_dim=0):
    return lax.dot_general(
        left, right, (((left_dim,), (right_dim,)), ((), ())), preferred_element_type=F32
    )


def split_low(value):
    high = value.astype(BF16)
    return high, (value - high.astype(F32)).astype(BF16)


def sigmoid(value):
    return 1.0 / (1.0 + jnp.exp(-value))


def log_sigmoid(value):
    return jnp.minimum(value, 0.0) - jnp.log1p(jnp.exp(-jnp.abs(value)))


def triangle(lower):
    rows = lax.broadcasted_iota(jnp.int32, (BLOCK, BLOCK), 0)
    columns = lax.broadcasted_iota(jnp.int32, (BLOCK, BLOCK), 1)
    return rows >= columns if lower else rows <= columns


def decay_terms(logits):
    log_decay = log_sigmoid(logits) * (1.0 / 16.0)
    ones = jnp.where(triangle(True), 1.0, 0.0).astype(BF16)
    high, low = split_low(log_decay)
    total = dot(ones, high) + dot(ones, low)
    middle = total[BLOCK // 2 - 1 : BLOCK // 2, :]
    end = total[BLOCK - 1 :, :]
    rise = jnp.exp(total - middle)
    fall = jnp.exp(middle - total)
    early = rise * (jnp.exp(middle) * SCALE)
    late = fall * jnp.exp(end - middle)
    return rise * SCALE, fall, early, late, jnp.exp(end)


def as_column(row, width):
    column = jnp.transpose(jnp.broadcast_to(row, (KEY_HEAD, KEY_HEAD)))
    return jnp.concatenate([column] * (width // KEY_HEAD), axis=1)


def forward_block(query, key, value, logits, gate, gain, memory, states):
    rise, fall, early, late, decay = decay_terms(logits)
    lower = triangle(True)
    attended_parts = []
    mixed_parts = []
    for head in range(memory.shape[0]):
        keys_at = slice(head * KEY_HEAD, (head + 1) * KEY_HEAD)
        values_at = slice(head * VALUE_HEAD, (head + 1) * VALUE_HEAD)
        query_wide = query[:, keys_at].astype(F32)
        key_wide = key[:, keys_at].astype(F32)
        value_head = value[:, values_at]
        state = memory[head]
        state_low = state.astype(BF16)
        states[head] = state_low
        scores = dot(
            (query_wide * rise[:, keys_at]).astype(BF16), (key_wide * fall[:, keys_at]).astype(BF16), 1, 1
        )
        scores = jnp.where(lower, scores, 0.0).astype(BF16)
        left = jnp.concatenate([scores, (query_wide * early[:, keys_at]).astype(BF16)], axis=1)
        attended = dot(left, jnp.concatenate([value_head, state_low], axis=0))
        memory[head] = as_column(decay[:, keys_at], VALUE_HEAD) * state + dot(
            (key_wide * late[:, keys_at]).astype(BF16), value_head, 0, 0
        )
        scale = lax.rsqrt(jnp.mean(attended * attended, axis=1, keepdims=True) + EPSILON)
        gate_head = gate[:, values_at]
        attended_parts.append(attended)
        mixed_parts.append((attended * scale * gain * gate_head * sigmoid(gate_head)).astype(BF16))
    return jnp.concatenate(attended_parts, axis=1), jnp.concatenate(mixed_parts, axis=1)


def forward_kernel(
    query_ref, key_ref, value_ref, logits_ref, gate_ref, gain_ref, start_ref,
    attended_ref, mixed_ref, states_ref, memory
):
    @pl.when(pl.program_id(0) == 0)
    def _():
        memory[...] = start_ref[...]

    attended_ref[...], mixed_ref[...] = forward_block(
        query_ref[...], key_ref[...], value_ref[...], logits_ref[...], gate_ref[...], gain_ref[...],
        memory, states_ref.at[0],
    )


def attention_forward(query, key, value, logits, gate, gain, start):
    length, keys = query.shape
    values = value.shape[1]
    heads = start.shape[0]
    steps = length // BLOCK

    def rows(width):
        return pl.BlockSpec((BLOCK, width), lambda i: (i, 0))

    return pl.pallas_call(
        forward_kernel,
        grid=(steps,),
        in_specs=[
            rows(keys), rows(keys), rows(values), rows(keys), rows(values),
            pl.BlockSpec((1, VALUE_HEAD), lambda i: (0, 0)),
            pl.BlockSpec((heads, KEY_HEAD, VALUE_HEAD), lambda i: (0, 0, 0)),
        ],
        out_specs=[
            rows(values), rows(values),
            pl.BlockSpec((1, heads, KEY_HEAD, VALUE_HEAD), lambda i: (i, 0, 0, 0)),
        ],
        out_shape=[
            jax.ShapeDtypeStruct((length, values), F32),
            jax.ShapeDtypeStruct((length, values), BF16),
            jax.ShapeDtypeStruct((steps, heads, KEY_HEAD, VALUE_HEAD), BF16),
        ],
        scratch_shapes=[pltpu.VMEM((heads, KEY_HEAD, VALUE_HEAD), F32)],
        compiler_params=pltpu.CompilerParams(vmem_limit_bytes=48 << 20),
        name="attention_forward",
    )(query, key, value, logits, gate, gain.reshape(1, -1), start)


def backward_block(mixed_grad, query, key, value, logits, gate, attended, states, gain, memory_grad):
    rise, fall, early, late, decay = decay_terms(logits)
    lower = triangle(True)
    upper = triangle(False)
    last = lax.broadcasted_iota(jnp.int32, (BLOCK, KEY_HEAD), 0) == BLOCK - 1
    query_grads, key_grads, value_grads, gate_grads, total_grads = [], [], [], [], []
    gain_grad = jnp.zeros((1, VALUE_HEAD), F32)
    for head in range(memory_grad.shape[0]):
        keys_at = slice(head * KEY_HEAD, (head + 1) * KEY_HEAD)
        values_at = slice(head * VALUE_HEAD, (head + 1) * VALUE_HEAD)
        attended_head = attended[:, values_at]
        scale = lax.rsqrt(jnp.mean(attended_head * attended_head, axis=1, keepdims=True) + EPSILON)
        normal = attended_head * scale
        gate_head = gate[:, values_at]
        gate_sigmoid = sigmoid(gate_head)
        mixed_head = mixed_grad[:, values_at]
        gate_grads.append(
            (mixed_head * normal * gain * gate_sigmoid * (1.0 + gate_head * (1.0 - gate_sigmoid))).astype(BF16)
        )
        normed_grad = mixed_head * gate_head * gate_sigmoid
        gain_grad += jnp.sum(normed_grad * normal, axis=0, keepdims=True)
        scaled = normed_grad * gain
        attended_grad = (
            scale * (scaled - normal * jnp.mean(scaled * normal, axis=1, keepdims=True))
        ).astype(BF16)

        query_wide = query[:, keys_at].astype(F32)
        key_wide = key[:, keys_at].astype(F32)
        value_head = value[:, values_at]
        query_middle = query_wide * rise[:, keys_at]
        key_middle = key_wide * fall[:, keys_at]
        query_early = query_wide * early[:, keys_at]
        key_late = key_wide * late[:, keys_at]
        query_middle_low = query_middle.astype(BF16)
        key_middle_low = key_middle.astype(BF16)
        state = states[head]
        after = memory_grad[head]

        scores_turned = jnp.where(upper, dot(key_middle_low, query_middle_low, 1, 1), 0.0).astype(BF16)
        from_values = dot(attended_grad, jnp.concatenate([value_head, state], axis=0), 1, 1)
        to_values = jnp.concatenate([attended_grad, after.astype(BF16)], axis=0)
        from_grads = dot(value_head, to_values, 1, 1)
        scores_grad = jnp.where(lower, from_values[:, :BLOCK], 0.0).astype(BF16)
        scores_grad_turned = jnp.where(upper, from_grads[:, :BLOCK], 0.0).astype(BF16)
        query_early_grad = from_values[:, BLOCK:]
        key_late_grad = from_grads[:, BLOCK:]
        query_middle_grad = dot(scores_grad, key_middle_low)
        key_middle_grad = dot(scores_grad_turned, query_middle_low)
        value_grads.append(
            dot(jnp.concatenate([scores_turned, key_late.astype(BF16)], axis=1), to_values).astype(BF16)
        )
        carried = as_column(decay[:, keys_at], VALUE_HEAD) * after
        memory_grad[head] = carried + dot(query_early.astype(BF16), attended_grad, 0, 0)
        query_grads.append(
            (query_early_grad * early[:, keys_at] + query_middle_grad * rise[:, keys_at]).astype(BF16)
        )
        key_grads.append((key_middle_grad * fall[:, keys_at] + key_late_grad * late[:, keys_at]).astype(BF16))
        late_part = key_late_grad * key_late
        end_high, end_low = split_low(carried * state.astype(F32))
        ones = jnp.ones((8, VALUE_HEAD), BF16)
        end_grad = (dot(ones, end_high, 1, 1) + dot(ones, end_low, 1, 1))[:1] + jnp.sum(
            late_part, axis=0, keepdims=True
        )
        total_grads.append(
            query_early_grad * query_early
            + query_middle_grad * query_middle
            - key_middle_grad * key_middle
            - late_part
            + jnp.where(last, end_grad, 0.0)
        )
    ones = jnp.where(upper, 1.0, 0.0).astype(BF16)
    high, rest = split_low(jnp.concatenate(total_grads, axis=1))
    logits_grad = (dot(ones, high) + dot(ones, rest)) * sigmoid(-logits) * (1.0 / 16.0)
    grads = query_grads + key_grads + value_grads + gate_grads
    return jnp.concatenate(grads, axis=1), logits_grad, gain_grad


def backward_kernel_plain(
    mixed_grad_ref, query_ref, key_ref, value_ref, logits_ref, gate_ref, attended_ref, states_ref, gain_ref,
    query_grad_ref, key_grad_ref, value_grad_ref, gate_grad_ref, logits_grad_ref, gain_grad_ref, memory_grad
):
    @pl.when(pl.program_id(0) == 0)
    def _():
        memory_grad[...] = jnp.zeros_like(memory_grad)
        gain_grad_ref[...] = jnp.zeros_like(gain_grad_ref)

    grads, logits_grad, gain_grad = backward_block(
        mixed_grad_ref[...], query_ref[...], key_ref[...], value_ref[...], logits_ref[...], gate_ref[...],
        attended_ref[...], states_ref[0], gain_ref[...], memory_grad,
    )
    start = 0
    for ref in (query_grad_ref, key_grad_ref, value_grad_ref, gate_grad_ref):
        ref[...] = grads[:, start : start + ref.shape[1]]
        start += ref.shape[1]
    logits_grad_ref[...] = logits_grad
    gain_grad_ref[...] += gain_grad


def attention_backward(mixed_grad, query, key, value, logits, gate, attended, states, gain):
    length, keys = query.shape
    values = value.shape[1]
    heads = states.shape[1]
    steps = length // BLOCK

    def rows(width):
        return pl.BlockSpec((BLOCK, width), lambda i: (steps - 1 - i, 0))

    return pl.pallas_call(
        backward_kernel_plain,
        grid=(steps,),
        in_specs=[
            rows(values), rows(keys), rows(keys), rows(values), rows(keys), rows(values), rows(values),
            pl.BlockSpec((1, heads, KEY_HEAD, VALUE_HEAD), lambda i: (steps - 1 - i, 0, 0, 0)),
            pl.BlockSpec((1, VALUE_HEAD), lambda i: (0, 0)),
        ],
        out_specs=[
            rows(keys), rows(keys), rows(values), rows(values), rows(keys),
            pl.BlockSpec((1, VALUE_HEAD), lambda i: (0, 0)),
        ],
        out_shape=[
            jax.ShapeDtypeStruct((length, keys), BF16),
            jax.ShapeDtypeStruct((length, keys), BF16),
            jax.ShapeDtypeStruct((length, values), BF16),
            jax.ShapeDtypeStruct((length, values), BF16),
            jax.ShapeDtypeStruct((length, keys), F32),
            jax.ShapeDtypeStruct((1, VALUE_HEAD), F32),
        ],
        scratch_shapes=[pltpu.VMEM((heads, KEY_HEAD, VALUE_HEAD), F32)],
        compiler_params=pltpu.CompilerParams(vmem_limit_bytes=48 << 20),
        name="attention_backward",
    )(mixed_grad, query, key, value, logits, gate, attended, states, gain.reshape(1, -1))


MESH = pl.DeviceIdType.MESH
ANY = pl.BlockSpec(memory_space=pl.ANY)


class Place:
    def __init__(self):
        self.dp = lax.axis_index("dp")
        self.head = lax.axis_index("head")
        self.z = self.dp // 4
        self.flat = self.dp % 4
        self.flat_x = self.flat + 1 - 2 * (self.flat % 2)
        self.flat_y = self.flat + 2 - 4 * (self.flat // 2)
        self.flat_xy = 3 - self.flat
        self.sibling = (self.dp, 1 - self.head)
        self.beside_x = (self.z * 4 + self.flat_x, self.head)
        self.beside_y = (self.z * 4 + self.flat_y, self.head)
        self.along_z = [(((self.z + i) % 4) * 4 + self.flat, self.head) for i in range(1, 4)]

    def meet(self):
        barrier = pltpu.get_barrier_semaphore()
        others = [self.sibling, self.beside_x, self.beside_y] + self.along_z
        for other in others:
            pl.semaphore_signal(barrier, 1, device_id=other, device_id_type=MESH)
        pl.semaphore_wait(barrier, len(others))


def send(source, target, out_sem, in_sem, device):
    copy = pltpu.make_async_remote_copy(
        src_ref=source, dst_ref=target, send_sem=out_sem, recv_sem=in_sem, device_id=device, device_id_type=MESH
    )
    copy.start()
    return copy


def arrived(target, out_sem, in_sem, device):
    pltpu.make_async_remote_copy(
        src_ref=target, dst_ref=target, send_sem=out_sem, recv_sem=in_sem, device_id=device, device_id_type=MESH
    ).wait_recv()


def chunk_columns(width, sizes):
    starts = [sum(sizes[:i]) * 128 for i in range(len(sizes))]
    assert sum(sizes) * 128 == width
    return [slice(start, start + size * 128) for start, size in zip(starts, sizes)]


ROWS = 256


class Gather:
    LAGS = (0, 1, 3)

    def __init__(self, place, source, targets, blocks, local_sems, swap_out, swap_in, out_sems, in_sems):
        self.place, self.source, self.targets, self.blocks = place, source, targets, blocks
        self.local_sems, self.swap_out, self.swap_in = local_sems, swap_out, swap_in
        self.out_sems, self.in_sems = out_sems, in_sems
        self.ticks = len(blocks) + self.LAGS[-1]

    def put(self, source, target, chunk, slot, device):
        send(source, target, self.out_sems.at[chunk, slot], self.in_sems.at[chunk, slot], device)

    def wait(self, target, chunk, slot):
        arrived(target, self.out_sems.at[chunk, slot], self.in_sems.at[chunk, slot], self.place.sibling)

    def start(self):
        at, source = self.place, self.source
        rows, half = source.shape[0], source.shape[1] // 6
        mine = pl.ds(at.head * rows, rows)
        theirs = pl.ds((1 - at.head) * rows, rows)
        offset = 0
        for i, block in enumerate(self.targets):
            size = block.shape[3] // 3
            for part in range(3):
                target = block.at[at.z, at.flat, mine, part * size : (part + 1) * size]
                base = 2 * part * half + offset
                here = pl.ds(pl.multiple_of(base + at.head * half, 128), size)
                there = pl.ds(pl.multiple_of(base + (1 - at.head) * half, 128), size)
                pltpu.make_async_copy(source.at[:, here], target, self.local_sems.at[i]).start()
                send(source.at[:, there], target, self.swap_out.at[i], self.swap_in.at[i], at.sibling)
            offset += size
        for i, block in enumerate(self.targets):
            target = block.at[at.z, at.flat, mine]
            pltpu.make_async_copy(target, target, self.local_sems.at[i]).wait()
            arrived(block.at[at.z, at.flat, theirs], self.swap_out.at[i], self.swap_in.at[i], at.sibling)

    def stage(self, number, chunk):
        at, out = self.place, self.blocks[chunk]
        everything = slice(None)
        if number == 0:
            block = out.at[at.z, at.flat]
            for i in range(3):
                self.put(block, block, chunk, i, at.along_z[i])
        if number == 1:
            for i in range(3):
                self.wait(out.at[(at.z + 3 - i) % 4, at.flat], chunk, i)
            block = out.at[everything, at.flat]
            self.put(block, block, chunk, 3, at.beside_x)
            self.put(block, block, chunk, 4, at.beside_y)
        if number == 2:
            self.wait(out.at[everything, at.flat_x], chunk, 3)
            block = out.at[pl.ds(0, 2), at.flat_x]
            self.put(block, block, chunk, 5, at.beside_y)
            self.wait(out.at[everything, at.flat_y], chunk, 4)
            block = out.at[pl.ds(2, 2), at.flat_y]
            self.put(block, block, chunk, 6, at.beside_x)

    def complete(self, chunk):
        at, out = self.place, self.blocks[chunk]
        self.wait(out.at[pl.ds(0, 2), at.flat_xy], chunk, 5)
        self.wait(out.at[pl.ds(2, 2), at.flat_xy], chunk, 6)

    def tick(self, number):
        for stage in (2, 1, 0):
            chunk = number - self.LAGS[stage]
            if 0 <= chunk < len(self.blocks):
                self.stage(stage, chunk)

    def finish(self):
        everything = slice(None)
        for chunk, block in enumerate(self.blocks):
            shapes = [block.at[0, 0]] * 3 + [block.at[everything, 0]] * 2 + [block.at[pl.ds(0, 2), 0]] * 2
            for slot, ref in enumerate(shapes):
                sent(ref, self.out_sems.at[chunk, slot], self.in_sems.at[chunk, slot], self.place.sibling)
        rows = self.source.shape[0]
        for i, block in enumerate(self.targets):
            sent(block.at[0, 0, pl.ds(0, rows)], self.swap_out.at[i], self.swap_in.at[i], self.place.sibling)


def sent(source, out_sem, in_sem, device):
    pltpu.make_async_remote_copy(
        src_ref=source, dst_ref=source, send_sem=out_sem, recv_sem=in_sem, device_id=device, device_id_type=MESH
    ).wait_send()


def layer_kernel(
    count,
    tokens_ref, cotangent_ref, length_ref, gain_one_ref, gain_two_ref, gain_out_ref, bias_ref, start_ref,
    w_query, w_key, w_value, w_gate, w_low_in, w_low_out, w_out, w_mlp,
    h_ref, query_ref, key_ref, value_ref, gate_ref, logits_ref, low_rank_ref, attended_ref, mixed_ref, states_ref,
    grad_zero_ref, grad_ref, output_ref, total_ref, attn_ref, gain_grad_ref,
    tokens, low, low_turned, h_two, h_two_turned, weights_zero, weights, resid, part_out, part_in,
    mlp_sum, grad_sum, inner_all, pair_all, sums_out, sums_in, memory,
    local_sems, gather_local, swap_out, swap_in, gather_out, gather_in, pair_out, pair_in,
):
    step = pl.program_id(0)
    at = Place()
    own = tokens_ref.shape[0]
    length = 2 * own
    tiles = length // ROWS
    own_tiles = own // ROWS
    own_at = at.head * own
    gather = Gather(
        at,
        w_mlp,
        [weights_zero] + [weights.at[i] for i in range(count - 1)],
        [weights_zero]
        + [weights.at[i, :, :, :, j * 384 : (j + 1) * 384] for i in range(count - 1) for j in range(2)],
        gather_local, swap_out, swap_in, gather_out, gather_in,
    )
    plan = {(0, 0): (0, 1), (1, 0): (2,), (2, 0): (3,), (3, 0): (4,), (4, 0): (5,), (4, 1): (6,)}
    places = [(5, 1), (6, 0), (6, 1), (7, 1), (8, 0), (8, 1), (9, 1)]
    for i, key in enumerate(places):
        plan[key] = (7 + i,) if i < len(places) - 1 else tuple(range(7 + i, gather.ticks))
    attention_steps = tiles
    first_step = attention_steps + 1
    last_step = first_step + count - 1

    def own_rows(i, size=ROWS):
        return pl.ds(pl.multiple_of(own_at + i * ROWS, ROWS), size)

    def other_rows(i, size=ROWS):
        return pl.ds(pl.multiple_of(own - own_at + i * ROWS, ROWS), size)

    def row_mask(i):
        positions = own_at + i * ROWS + lax.broadcasted_iota(jnp.int32, (ROWS, 1), 0)
        return jnp.where(positions < length_ref[0], 1.0, 0.0)

    def put(source, target, slot):
        send(source, target, pair_out.at[slot], pair_in.at[slot], at.sibling)

    def wait(target, slot):
        arrived(target, pair_out.at[slot], pair_in.at[slot], at.sibling)

    @pl.when(step == 0)
    def _():
        here = [
            pltpu.make_async_copy(cotangent_ref, low.at[own_rows(0, own)], local_sems.at[1]),
            pltpu.make_async_copy(tokens_ref, tokens.at[own_rows(0, own)], local_sems.at[0]),
        ]
        for copy in here:
            copy.start()
        at.meet()
        put(tokens_ref, tokens.at[own_rows(0, own)], 0)
        memory[...] = start_ref[...]
        gain_grad_ref[...] = jnp.zeros_like(gain_grad_ref)
        gather.start()
        for number in plan[0, 0]:
            gather.tick(number)
        for copy in here:
            copy.wait()
        for i in range(own_tiles):
            low[own_rows(i), :] = (low[own_rows(i), :].astype(F32) * row_mask(i)).astype(BF16)
        put(low.at[own_rows(0, own)], low.at[own_rows(0, own)], 1)
        wait(tokens.at[other_rows(0, own)], 0)

    def gather_at(inside, among):
        for (when, which), numbers in plan.items():
            if which == inside and when in among:

                @pl.when(step == when)
                def _():
                    for number in numbers:
                        gather.tick(number)

    gather_at(0, range(1, attention_steps + 1))
    @pl.when(step < attention_steps)
    def _():
        rows = pl.ds(pl.multiple_of(step * ROWS, ROWS), ROWS)
        wide = tokens[rows, :].astype(F32)
        scale = lax.rsqrt(jnp.mean(wide * wide, axis=1, keepdims=True) + EPSILON)
        h_low = (wide * scale * gain_one_ref[...]).astype(BF16)
        h_ref[...] = h_low
        query = dot(h_low, w_query[...]).astype(BF16)
        key = dot(h_low, w_key[...]).astype(BF16)
        value = dot(h_low, w_value[...]).astype(BF16)
        gate = dot(h_low, w_gate[...])
        low_rank = dot(h_low, w_low_in[...], 1, 1)
        high, rest = split_low(low_rank)
        logits = dot(high, w_low_out[...]) + dot(rest, w_low_out[...]) + bias_ref[...]
        query_ref[...] = query
        key_ref[...] = key
        value_ref[...] = value
        gate_ref[...] = gate
        low_rank_ref[...] = low_rank
        logits_ref[...] = logits
        for i in range(ROWS // BLOCK):
            block = slice(i * BLOCK, (i + 1) * BLOCK)
            attended, mixed = forward_block(
                query[block], key[block], value[block], logits[block], gate[block], gain_out_ref[...],
                memory, states_ref.at[i],
            )
            attended_ref[block, :] = attended
            mixed_ref[block, :] = mixed
        part = dot(mixed_ref[...], w_out[...])
        tile = step % own_tiles
        tile_rows = pl.ds(pl.multiple_of(tile * ROWS, ROWS), ROWS)
        mine = step // own_tiles == at.head

        @pl.when(mine)
        def _():
            resid[tile_rows, :] = part

        @pl.when(jnp.logical_not(mine))
        def _():
            part_out[tile_rows, :] = part.astype(BF16)
            put(part_out.at[tile_rows], part_in.at[tile_rows], 2 + tile)

    @pl.when(step == attention_steps)
    def _():
        wait(low.at[other_rows(0, own)], 1)
        for i in range(own_tiles):
            rows = pl.ds(i * ROWS, ROWS)
            wait(part_in.at[rows], 2 + i)
            full = tokens[own_rows(i), :].astype(F32) + resid[rows, :] + part_in[rows, :].astype(F32)
            resid[rows, :] = full
            scale = lax.rsqrt(jnp.mean(full * full, axis=1, keepdims=True) + EPSILON)
            h_two[own_rows(i), :] = (full * scale * gain_two_ref[...]).astype(BF16)
            put(h_two.at[own_rows(i)], h_two.at[own_rows(i)], 4 + i)
        gather_at(1, [attention_steps])

        def turn(i, carry):
            rows = pl.ds(pl.multiple_of(i * ROWS, ROWS), ROWS)
            low_turned[:, rows] = jnp.transpose(low[rows, :])
            return carry

        lax.fori_loop(0, tiles, turn, 0)
        for i in range(own_tiles):
            wait(h_two.at[other_rows(i)], 4 + i)

        def turn_two(i, carry):
            rows = pl.ds(pl.multiple_of(i * ROWS, ROWS), ROWS)
            h_two_turned[:, rows] = jnp.transpose(h_two[rows, :])
            return carry

        lax.fori_loop(0, tiles, turn_two, 0)

    def hidden_rows(block, first):
        width = block.shape[3] // 3

        def body(i, carry):
            rows = pl.ds(pl.multiple_of(i * ROWS, ROWS), ROWS)
            w_pair = block[:, :, :, : 2 * width].reshape(-1, 2 * width)
            w_down = block[:, :, :, 2 * width :].reshape(-1, width)
            pair = dot(h_two[rows, :], w_pair)
            inner_grad = dot(low[rows, :], w_down)
            pre_gate = pair[:, :width]
            up_part = pair[:, width:]
            pre_sigmoid = sigmoid(pre_gate)
            swish = pre_gate * pre_sigmoid
            inner = (swish * up_part).astype(BF16)
            pre_grad = inner_grad * up_part * pre_sigmoid * (1.0 + pre_gate * (1.0 - pre_sigmoid))
            both = jnp.concatenate([pre_grad.astype(BF16), (inner_grad * swish).astype(BF16)], axis=1)
            inner_all[rows, :width] = inner
            pair_all[rows, : 2 * width] = both
            out_part = dot(inner, w_down, 1, 1)
            grad_part = dot(both, w_pair, 1, 1)
            if first:
                mlp_sum[rows, :] = out_part
                grad_sum[rows, :] = grad_part
            else:
                mlp_sum[rows, :] += out_part
                grad_sum[rows, :] += grad_part
            return carry

        lax.fori_loop(0, tiles, body, 0)

    def weight_rows(block, target):
        width = block.shape[3] // 3

        def body(i, carry):
            rows = pl.ds(pl.multiple_of(i * ROWS, ROWS), ROWS)
            shape = (target.shape[1], target.shape[2], -1)
            target[i, :, :, : 2 * width] = (
                dot(h_two_turned[rows, :], pair_all[:, : 2 * width]).astype(BF16).reshape(shape)
            )
            target[i, :, :, 2 * width :] = (
                dot(low_turned[rows, :], inner_all[:, :width]).astype(BF16).reshape(shape)
            )
            return carry

        lax.fori_loop(0, tiles, body, 0)

    @pl.when(step == first_step)
    def _():
        gather.complete(0)
        hidden_rows(weights_zero, True)
        gather_at(1, [first_step])
        weight_rows(weights_zero, grad_zero_ref)

    for group in range(1, count):

        @pl.when(step == first_step + group)
        def _():
            gather_at(0, [first_step + group])
            gather.complete(2 * group - 1)
            gather.complete(2 * group)

    @pl.when(step > first_step)
    def _():
        block = weights.at[step - first_step - 1]
        hidden_rows(block, False)
        gather_at(1, range(first_step + 1, last_step))

        @pl.when(step == last_step)
        def _():
            for i in range(own_tiles):
                rows = pl.ds(i * ROWS, ROWS)
                for k, source in enumerate((mlp_sum, grad_sum)):
                    sums_out[k, rows, :] = source[other_rows(i), :].astype(BF16)
                    put(sums_out.at[k, rows], sums_in.at[k, rows], 6 + 2 * i + k)

        weight_rows(block, grad_ref.at[0])

    @pl.when(step == last_step)
    def _():
        for i in range(own_tiles):
            sent(h_two.at[pl.ds(0, ROWS)], pair_out.at[4 + i], pair_in.at[4 + i], at.sibling)
        for i in range(own_tiles):
            rows = pl.ds(i * ROWS, ROWS)
            for k in range(2):
                wait(sums_in.at[k, rows], 6 + 2 * i + k)
            full = resid[rows, :]
            scale = lax.rsqrt(jnp.mean(full * full, axis=1, keepdims=True) + EPSILON)
            normal = full * scale
            mlp_out = mlp_sum[own_rows(i), :] + sums_in[0, rows, :].astype(F32)
            output_ref[rows, :] = (row_mask(i) * (full + mlp_out)).astype(BF16)
            grad = grad_sum[own_rows(i), :] + sums_in[1, rows, :].astype(F32)
            total = low[own_rows(i), :].astype(F32) + norm_backward(grad, gain_two_ref[...], normal, scale)
            total_ref[rows, :] = total
            gain_grad_ref[...] += jnp.sum(grad * normal, axis=0, keepdims=True)
            h_two[own_rows(i), :] = total.astype(BF16)
            put(h_two.at[own_rows(i)], h_two.at[own_rows(i)], 10 + i)
            pltpu.make_async_copy(h_two.at[own_rows(i)], attn_ref.at[own_rows(i)], local_sems.at[i]).start()
        gather.finish()
        for i in range(own_tiles):
            wait(h_two.at[other_rows(i)], 10 + i)
            pltpu.make_async_copy(
                h_two.at[other_rows(i)], attn_ref.at[other_rows(i)], local_sems.at[own_tiles + i]
            ).start()
        for slot, ref in enumerate(
            [tokens_ref, low.at[pl.ds(0, own)]] + [part_out.at[pl.ds(0, ROWS)]] * 8 + [h_two.at[pl.ds(0, ROWS)]] * 2
        ):
            if slot not in (4, 5):
                sent(ref, pair_out.at[slot], pair_in.at[slot], at.sibling)
        for i in range(tiles):
            rows = own_rows(i) if i < own_tiles else other_rows(i - own_tiles)
            pltpu.make_async_copy(h_two.at[rows], attn_ref.at[rows], local_sems.at[i]).wait()


def whole(shape):
    return pl.BlockSpec(shape, lambda i: (0,) * len(shape), pipeline_mode=pl.Buffered(1))


def layer(
    tokens, cotangent, lengths, gain_one, gain_two, gain_out, bias, start,
    w_query, w_key, w_value, w_gate, w_low_in, w_low_out, w_out, w_mlp,
):
    own, width = tokens.shape
    length = 2 * own
    keys, values, heads = w_query.shape[1], w_value.shape[1], start.shape[0]
    rank = w_low_in.shape[0]
    count = (w_mlp.shape[1] // 6 - 128) // 256 + 1
    group = 2 * w_mlp.shape[0]
    tiles = length // ROWS
    first_step = tiles + 1
    steps = first_step + count

    def rows_spec(columns):
        return pl.BlockSpec((ROWS, columns), lambda i: (jnp.minimum(i, tiles - 1), 0))

    vmem = pl.BlockSpec(memory_space=pltpu.VMEM)
    row_shapes = [
        (width, BF16), (keys, BF16), (keys, BF16), (values, BF16), (values, F32), (keys, F32), (rank, F32),
        (values, F32), (values, BF16),
    ]
    blocks = ROWS // BLOCK
    return pl.pallas_call(
        functools.partial(layer_kernel, count),
        grid=(steps,),
        in_specs=[
            ANY, ANY, pl.BlockSpec(memory_space=pltpu.SMEM), whole((1, width)), whole((1, width)), whole((1, VALUE_HEAD)),
            whole((1, keys)), whole(start.shape), whole(w_query.shape), whole(w_key.shape), whole(w_value.shape),
            whole(w_gate.shape), whole(w_low_in.shape), whole(w_low_out.shape), whole(w_out.shape),
            ANY,
        ],
        out_specs=[rows_spec(columns) for columns, _ in row_shapes]
        + [
            pl.BlockSpec((blocks, heads, KEY_HEAD, VALUE_HEAD), lambda i: (jnp.minimum(i, tiles - 1), 0, 0, 0)),
            whole((4, 4, group, 384)),
            pl.BlockSpec(
                (1, 4, 4, group, 768), lambda i: (jnp.clip(i - first_step - 1, 0, count - 2), 0, 0, 0, 0)
            ),
            vmem, vmem, ANY, vmem,
        ],
        out_shape=[jax.ShapeDtypeStruct((length, columns), kind) for columns, kind in row_shapes]
        + [
            jax.ShapeDtypeStruct((length // BLOCK, heads, KEY_HEAD, VALUE_HEAD), BF16),
            jax.ShapeDtypeStruct((4, 4, group, 384), BF16),
            jax.ShapeDtypeStruct((count - 1, 4, 4, group, 768), BF16),
            jax.ShapeDtypeStruct((own, width), BF16),
            jax.ShapeDtypeStruct((own, width), F32),
            jax.ShapeDtypeStruct((length, width), BF16),
            jax.ShapeDtypeStruct((1, width), F32),
        ],
        scratch_shapes=[
            pltpu.VMEM((length, width), BF16),
            pltpu.VMEM((length, width), BF16),
            pltpu.VMEM((width, length), BF16),
            pltpu.VMEM((length, width), BF16),
            pltpu.VMEM((width, length), BF16),
            pltpu.VMEM((4, 4, group, 384), BF16),
            pltpu.VMEM((count - 1, 4, 4, group, 768), BF16),
            pltpu.VMEM((own, width), F32),
            pltpu.VMEM((own, width), BF16),
            pltpu.VMEM((own, width), BF16),
            pltpu.VMEM((length, width), F32),
            pltpu.VMEM((length, width), F32),
            pltpu.VMEM((length, 256), BF16),
            pltpu.VMEM((length, 512), BF16),
            pltpu.VMEM((2, own, width), BF16),
            pltpu.VMEM((2, own, width), BF16),
            pltpu.VMEM((heads, KEY_HEAD, VALUE_HEAD), F32),
            pltpu.SemaphoreType.DMA((tiles,)),
            pltpu.SemaphoreType.DMA((count,)),
            pltpu.SemaphoreType.DMA((count,)),
            pltpu.SemaphoreType.DMA((count,)),
            pltpu.SemaphoreType.DMA((2 * count - 1, 7)),
            pltpu.SemaphoreType.DMA((2 * count - 1, 7)),
            pltpu.SemaphoreType.DMA((12,)),
            pltpu.SemaphoreType.DMA((12,)),
        ],
        compiler_params=pltpu.CompilerParams(
            collective_id=0, has_side_effects=True, vmem_limit_bytes=63 << 20
        ),
        name="layer",
    )(
        tokens, cotangent, lengths, gain_one.reshape(1, -1), gain_two.reshape(1, -1), gain_out.reshape(1, -1),
        bias.reshape(1, -1), start, w_query, w_key, w_value, w_gate, w_low_in, w_low_out, w_out,
        w_mlp,
    )


class Reduce:
    def __init__(self, place, partial, via_x, via_y, from_x, from_y, from_z, chunks, out_sems, in_sems):
        self.place, self.partial, self.chunks = place, partial, chunks
        self.via_x, self.via_y, self.from_x, self.from_y, self.from_z = via_x, via_y, from_x, from_y, from_z
        self.out_sems, self.in_sems = out_sems, in_sems

    def put(self, source, target, chunk, slot, device):
        send(source, target, self.out_sems.at[chunk, slot], self.in_sems.at[chunk, slot], device)

    def wait(self, target, chunk, slot):
        arrived(target, self.out_sems.at[chunk, slot], self.in_sems.at[chunk, slot], self.place.sibling)

    def stage(self, number, chunk):
        at, partial, columns = self.place, self.partial, self.chunks[chunk]
        everything = slice(None)
        low, high = pl.ds(0, 2), pl.ds(2, 2)
        view = (everything, everything, columns)
        if number == 0:
            self.put(partial.at[low, at.flat_xy, everything, columns], self.via_x.at[view], chunk, 0, at.beside_x)
            self.put(partial.at[high, at.flat_xy, everything, columns], self.via_y.at[view], chunk, 1, at.beside_y)
        if number == 1:
            self.wait(self.via_x.at[view], chunk, 0)
            block = (low, at.flat_y, everything, columns)
            partial[block] = (partial[block].astype(F32) + self.via_x[view].astype(F32)).astype(BF16)
            self.put(
                partial.at[everything, at.flat_y, everything, columns], self.from_y.at[view], chunk, 2, at.beside_y
            )
            self.wait(self.via_y.at[view], chunk, 1)
            block = (high, at.flat_x, everything, columns)
            partial[block] = (partial[block].astype(F32) + self.via_y[view].astype(F32)).astype(BF16)
            self.put(
                partial.at[everything, at.flat_x, everything, columns], self.from_x.at[view], chunk, 3, at.beside_x
            )
        if number == 2:
            self.wait(self.from_y.at[view], chunk, 2)
            self.wait(self.from_x.at[view], chunk, 3)
            block = (everything, at.flat, everything, columns)
            partial[block] = (
                partial[block].astype(F32) + self.from_x[view].astype(F32) + self.from_y[view].astype(F32)
            ).astype(BF16)
            for i in range(3):
                self.put(
                    partial.at[(at.z + 1 + i) % 4, at.flat, everything, columns],
                    self.from_z.at[i, everything, columns],
                    chunk,
                    4 + i,
                    at.along_z[i],
                )

    def result(self, chunk):
        at, columns = self.place, self.chunks[chunk]
        total = self.partial[at.z, at.flat, :, columns].astype(F32)
        for i in range(3):
            self.wait(self.from_z.at[i, :, columns], chunk, 4 + i)
            total += self.from_z[i, :, columns].astype(F32)
        return total

    def finish(self):
        for chunk, columns in enumerate(self.chunks):
            pair, four, one = [self.partial.at[pl.ds(0, n), 0, :, columns] for n in (2, 4, 1)]
            for slot, ref in enumerate([pair] * 2 + [four] * 2 + [one] * 3):
                sent(ref, self.out_sems.at[chunk, slot], self.in_sems.at[chunk, slot], self.place.sibling)


GAIN_ONE, GAIN_TWO, GAIN_OUT, LOW_IN = 0, 8, 16, 24


def small_rows(width, rank, keys):
    decay = LOW_IN + rank * width // 128
    slot = -(-(rank + 1) * keys // 128 // 8) * 8
    return decay, slot, decay + 2 * slot


def backward_kernel(
    half, mlp_chunks, attn_chunks,
    zero_ref, groups_ref, attn_ref, h_ref, query_ref, key_ref, value_ref, gate_ref, logits_ref, low_rank_ref,
    attended_ref, mixed_ref, states_ref, w_query, w_key, w_value, w_gate, w_low_in, w_low_out, w_out,
    tokens_ref, total_ref, gain_one_ref, gain_out_ref, gain_two_grad_ref,
    mlp_out, attn_out, small_out, tokens_out,
    mlp, attn, mlp_via_x, mlp_via_y, mlp_from_x, mlp_from_y, mlp_from_z,
    attn_via_x, attn_via_y, attn_from_x, attn_from_y, attn_from_z, summed, swapped,
    small_own, small_in, small_z, h_turned, attn_turned, right, mixed_all, h_grad, h_grad_out, h_grad_in,
    memory_grad, gain_out_sum, low_in_sum, low_out_sum, bias_sum,
    load_sems, mlp_sems_out, mlp_sems_in, attn_sems_out, attn_sems_in, pair_out, pair_in, small_sems_out, small_sems_in,
):
    step = pl.program_id(0)
    at = Place()
    own = tokens_ref.shape[0]
    own_tiles = own // ROWS
    tiles = 2 * own_tiles
    keys, values = w_query.shape[1], w_value.shape[1]
    rank, width = w_low_out.shape[0], tokens_ref.shape[1]
    decay_at, decay_slot, _ = small_rows(width, rank, keys)
    last_step = 2 * tiles
    sides = [
        Reduce(at, mlp, mlp_via_x, mlp_via_y, mlp_from_x, mlp_from_y, mlp_from_z, mlp_chunks, mlp_sems_out, mlp_sems_in),
        Reduce(
            at, attn, attn_via_x, attn_via_y, attn_from_x, attn_from_y, attn_from_z, attn_chunks,
            attn_sems_out, attn_sems_in,
        ),
    ]
    order = [(0, i) for i in range(len(mlp_chunks))] + [(1, i) for i in range(len(attn_chunks))]
    count = len(order)
    rows = mlp.shape[2] // 2

    loads = [0] + list(range(1, len(mlp_chunks), 2))
    ticks = count + 6
    slots = [(i, j) for i in range(tiles) for j in range(2)] + [(tiles + i, 0) for i in range(tiles)]
    early = min(len(slots), len(mlp_chunks))
    plan = {slot: (i,) for i, slot in enumerate(slots[:early])}

    def load(chunk):
        if chunk == 0:
            return pltpu.make_async_copy(zero_ref, mlp.at[:, :, :, mlp_chunks[0]], load_sems.at[0])
        columns = slice(mlp_chunks[chunk].start, mlp_chunks[chunk + 1].stop)
        return pltpu.make_async_copy(groups_ref.at[chunk // 2], mlp.at[:, :, :, columns], load_sems.at[chunk])

    def put(source, target, slot):
        send(source, target, pair_out.at[slot], pair_in.at[slot], at.sibling)

    def wait(target, slot):
        arrived(target, pair_out.at[slot], pair_in.at[slot], at.sibling)

    def small(number):
        def put_small(source, target, slot, device):
            send(source, target, small_sems_out.at[slot], small_sems_in.at[slot], device)

        def wait_small(target, slot):
            arrived(target, small_sems_out.at[slot], small_sems_in.at[slot], at.sibling)

        if number == 0:
            put_small(small_own, small_in.at[0], 0, at.sibling)
        elif number in (1, 2):
            source = small_own if number == 1 else small_z.at[number - 2]
            wait_small(small_in.at[number - 1], number - 1)
            small_z[number - 1] = source[...] + small_in[number - 1]
            put_small(small_z.at[number - 1], small_in.at[number], number, at.beside_x if number == 1 else at.beside_y)
        elif number == 3:
            wait_small(small_in.at[2], 2)
            small_z[2 + at.z] = small_z[1] + small_in[2]
            for i in range(3):
                put_small(small_z.at[2 + at.z], small_z.at[2 + at.z], 3 + i, at.along_z[i])
        elif number == 4:
            for i in range(3):
                wait_small(small_z.at[2 + (at.z + 3 - i) % 4], 3 + i)
            small_out[...] = small_z[2] + small_z[3] + small_z[4] + small_z[5]
            for slot in range(6):
                sent(small_own, small_sems_out.at[slot], small_sems_in.at[slot], at.sibling)

    def result(side, chunk):
        total = sides[side].result(chunk)
        if side == 0:
            columns = mlp_chunks[chunk]
            summed[:, columns] = total
            put(
                summed.at[pl.ds(pl.multiple_of((1 - at.head) * rows, 8), rows), columns], swapped.at[:, columns],
                2 + chunk,
            )
        else:
            attn_out[:, attn_chunks[chunk]] = total

    def tick(number):
        for stage, lag in ((3, 6), (2, 4), (1, 2), (0, 0)):
            if 0 <= number - lag < count:
                side, chunk = order[number - lag]
                if stage == 3:
                    result(side, chunk)
                    continue
                if stage == 0 and side == 0 and chunk in loads:
                    load(chunk).wait()
                sides[side].stage(stage, chunk)

    def ticks_at(where, inside):
        for number in plan.get((where, inside), ()):
            tick(number)

    def own_rows(i):
        return pl.ds(pl.multiple_of(i * ROWS, ROWS), ROWS)

    @pl.when(step == 0)
    def _():
        for chunk in loads:
            load(chunk).start()
        memory_grad[...] = jnp.zeros_like(memory_grad)
        gain_out_sum[...] = jnp.zeros_like(gain_out_sum)
        low_in_sum[...] = jnp.zeros_like(low_in_sum)
        low_out_sum[...] = jnp.zeros_like(low_out_sum)
        bias_sum[...] = jnp.zeros_like(bias_sum)
        at.meet()

    for where in range(2 * tiles):

        @pl.when(step == where)
        def _():
            ticks_at(where, 0)

    @pl.when(step < tiles)
    def _():
        tile = tiles - 1 - step
        here = pl.ds(pl.multiple_of(tile * ROWS, ROWS), ROWS)
        attn_tile = attn_ref[...]
        h_tile = h_ref[...]
        attn_turned[:, here] = jnp.transpose(attn_tile)
        h_turned[:, here] = jnp.transpose(h_tile)
        mixed_all[here, :] = mixed_ref[...]
        mixed_grad = dot(attn_tile, w_out[...], 1, 1)
        logits_parts = []
        for i in range(ROWS // BLOCK - 1, -1, -1):
            block = slice(i * BLOCK, (i + 1) * BLOCK)
            grads, logits_grad, gain_grad = backward_block(
                mixed_grad[block], query_ref[block, :], key_ref[block, :], value_ref[block, :], logits_ref[block, :],
                gate_ref[block, :], attended_ref[block, :], states_ref[i], gain_out_ref[...], memory_grad,
            )
            right[pl.ds(pl.multiple_of(tile * ROWS + i * BLOCK, BLOCK), BLOCK), :] = grads
            gain_out_sum[...] += gain_grad
            logits_parts.append(logits_grad)
            if i == ROWS // BLOCK - 1:
                for where in range(tiles):

                    @pl.when(step == where)
                    def _():
                        ticks_at(where, 1)

        logits_grad = jnp.concatenate(logits_parts[::-1], axis=0)
        high, rest = split_low(logits_grad)
        rank_high, rank_rest = split_low(low_rank_ref[...])
        bias_sum[...] += jnp.sum(logits_grad, axis=0, keepdims=True)
        low_out_sum[...] += dot(rank_high, high, 0, 0) + dot(rank_rest, high, 0, 0) + dot(rank_high, rest, 0, 0)
        low_rank_low = (dot(high, w_low_out[...], 1, 1) + dot(rest, w_low_out[...], 1, 1)).astype(BF16)
        low_in_sum[...] += dot(low_rank_low, h_tile, 0, 0)
        grads = right[here, :]
        part = (
            dot(grads[:, :keys], w_query[...], 1, 1)
            + dot(grads[:, keys : 2 * keys], w_key[...], 1, 1)
            + dot(grads[:, 2 * keys : 2 * keys + values], w_value[...], 1, 1)
            + dot(grads[:, 2 * keys + values :], w_gate[...], 1, 1)
            + dot(low_rank_low, w_low_in[...])
        )
        place = tile % own_tiles
        mine = tile // own_tiles == at.head

        @pl.when(mine)
        def _():
            h_grad[own_rows(place), :] = part

        @pl.when(jnp.logical_not(mine))
        def _():
            h_grad_out[own_rows(place), :] = part.astype(BF16)
            put(h_grad_out.at[own_rows(place)], h_grad_in.at[own_rows(place)], place)

    @pl.when(step == tiles)
    def _():
        gain_one = jnp.zeros((1, width), F32)
        for i in range(own_tiles):
            here = own_rows(i)
            wait(h_grad_in.at[here], i)
            wide = tokens_ref[here, :].astype(F32)
            scale = lax.rsqrt(jnp.mean(wide * wide, axis=1, keepdims=True) + EPSILON)
            normal = wide * scale
            grad = h_grad[here, :] + h_grad_in[here, :].astype(F32)
            tokens_out[here, :] = total_ref[here, :] + norm_backward(grad, gain_one_ref[...], normal, scale)
            gain_one += jnp.sum(grad * normal, axis=0, keepdims=True)
        small_own[...] = jnp.zeros_like(small_own)
        for i in range(width // 128):
            columns = slice(i * 128, (i + 1) * 128)
            small_own[GAIN_ONE + i : GAIN_ONE + i + 1, :] = gain_one[:, columns]
            small_own[GAIN_TWO + i : GAIN_TWO + i + 1, :] = gain_two_grad_ref[:, columns]
            small_own[LOW_IN + i * rank : LOW_IN + (i + 1) * rank, :] = low_in_sum[:, columns]
        for i in range(VALUE_HEAD // 128):
            small_own[GAIN_OUT + i : GAIN_OUT + i + 1, :] = gain_out_sum[:, i * 128 : (i + 1) * 128]
        for head in range(2):

            @pl.when(at.head == head)
            def _():
                base = decay_at + head * decay_slot
                for i in range(keys // 128):
                    columns = slice(i * 128, (i + 1) * 128)
                    small_own[base + i * rank : base + (i + 1) * rank, :] = low_out_sum[:, columns]
                    bias_at = base + keys // 128 * rank + i
                    small_own[bias_at : bias_at + 1, :] = bias_sum[:, columns]

        small(0)

    for number in range(1, 5):

        @pl.when(step == tiles + number)
        def _():
            small(number)

    @pl.when(jnp.logical_and(step >= tiles, step < 2 * tiles))
    def _():
        part = step - tiles
        here = pl.ds(pl.multiple_of(part * ROWS, ROWS), ROWS)
        shape = (attn.shape[1], attn.shape[2], -1)
        edge = right.shape[1]
        attn[part, :, :, :edge] = dot(h_turned[here, :], right[...]).astype(BF16).reshape(shape)
        attn[part, :, :, edge:] = dot(attn_turned[here, :], mixed_all[...]).astype(BF16).reshape(shape)

    def spread(source, head):
        offset, start = 0, 0
        for size in [mlp_chunks[0].stop // 3] + [2 * mlp_chunks[0].stop // 3] * (len(mlp_chunks) // 2):
            for part in range(3):
                target = pl.ds(pl.multiple_of(part * 2 * half + head * half + offset, 128), size)
                mlp_out[:, target] = source[:, start : start + size]
                start += size
            offset += size

    @pl.when(step == last_step)
    def _():
        for number in range(early, ticks):
            tick(number)
            if number == len(mlp_chunks) + 7:
                spread(summed.at[pl.ds(pl.multiple_of(at.head * rows, 8), rows)], at.head)
                for chunk, columns in enumerate(mlp_chunks):
                    wait(swapped.at[:, columns], 2 + chunk)
                spread(swapped, 1 - at.head)
        for i in range(own_tiles):
            sent(h_grad_out.at[own_rows(i)], pair_out.at[i], pair_in.at[i], at.sibling)
        for chunk, columns in enumerate(mlp_chunks):
            sent(swapped.at[:, columns], pair_out.at[2 + chunk], pair_in.at[2 + chunk], at.sibling)
        for side in sides:
            side.finish()


def backward(
    zero, groups, attn_low, h_low, query, key, value, gate, logits, low_rank, attended, mixed, states,
    w_query, w_key, w_value, w_gate, w_low_in, w_low_out, w_out, tokens, total, gain_one, gain_out, gain_two_grad,
):
    length, width = h_low.shape
    keys, values, heads = query.shape[1], value.shape[1], states.shape[1]
    rank = w_low_out.shape[0]
    own = tokens.shape[0]
    tiles = length // ROWS
    rows = width // 16
    mlp_count = 2 * groups.shape[0] + 1
    mlp_width = zero.shape[-1] * mlp_count
    mlp_chunks = chunk_columns(mlp_width, [zero.shape[-1] // 128] * mlp_count)
    attn_width = 2 * keys + 3 * values
    attn_tiles = attn_width // 128
    sizes = [3] * ((attn_tiles - 4) // 3) + [(attn_tiles - 4) % 3 + 1, 2, 1]
    attn_chunks = chunk_columns(attn_width, sizes)
    attn_count = len(attn_chunks)
    small_shape = (small_rows(width, rank, keys)[2], 128)
    vmem = pl.BlockSpec(memory_space=pltpu.VMEM)

    def rows_spec(columns):
        return pl.BlockSpec((ROWS, columns), lambda i: (jnp.maximum(tiles - 1 - i, 0), 0))

    buffers = []
    for columns in (mlp_width, attn_width):
        buffers += [pltpu.VMEM((n, rows, columns), BF16) for n in (2, 2, 4, 4, 3)]
    streamed = [attn_low, h_low, query, key, value, gate, logits, low_rank, attended, mixed]
    constant = [
        w_query, w_key, w_value, w_gate, w_low_in, w_low_out, w_out, tokens, total,
        gain_one.reshape(1, -1), gain_out.reshape(1, -1), gain_two_grad.reshape(1, -1),
    ]
    return pl.pallas_call(
        functools.partial(backward_kernel, mlp_width // 3, mlp_chunks, attn_chunks),
        grid=(2 * tiles + 1,),
        in_specs=[ANY, ANY]
        + [rows_spec(a.shape[1]) for a in streamed]
        + [
            pl.BlockSpec(
                (ROWS // BLOCK, heads, KEY_HEAD, VALUE_HEAD), lambda i: (jnp.maximum(tiles - 1 - i, 0), 0, 0, 0)
            )
        ]
        + [whole(a.shape) for a in constant],
        out_specs=[vmem, vmem, vmem, vmem],
        out_shape=[
            jax.ShapeDtypeStruct((rows // 2, 2 * mlp_width), F32),
            jax.ShapeDtypeStruct((rows, attn_width), F32),
            jax.ShapeDtypeStruct(small_shape, F32),
            jax.ShapeDtypeStruct((own, width), F32),
        ],
        scratch_shapes=[
            pltpu.VMEM((4, 4, rows, mlp_width), BF16),
            pltpu.VMEM((4, 4, rows, attn_width), BF16),
            *buffers,
            pltpu.VMEM((rows, mlp_width), F32),
            pltpu.VMEM((rows // 2, mlp_width), F32),
            pltpu.VMEM(small_shape, F32),
            pltpu.VMEM((3,) + small_shape, F32),
            pltpu.VMEM((6,) + small_shape, F32),
            pltpu.VMEM((width, length), BF16),
            pltpu.VMEM((width, length), BF16),
            pltpu.VMEM((length, 2 * keys + 2 * values), BF16),
            pltpu.VMEM((length, values), BF16),
            pltpu.VMEM((own, width), F32),
            pltpu.VMEM((own, width), BF16),
            pltpu.VMEM((own, width), BF16),
            pltpu.VMEM((heads, KEY_HEAD, VALUE_HEAD), F32),
            pltpu.VMEM((1, VALUE_HEAD), F32),
            pltpu.VMEM((rank, width), F32),
            pltpu.VMEM((rank, keys), F32),
            pltpu.VMEM((1, keys), F32),
            pltpu.SemaphoreType.DMA((mlp_count,)),
            pltpu.SemaphoreType.DMA((mlp_count, 7)),
            pltpu.SemaphoreType.DMA((mlp_count, 7)),
            pltpu.SemaphoreType.DMA((attn_count, 7)),
            pltpu.SemaphoreType.DMA((attn_count, 7)),
            pltpu.SemaphoreType.DMA((2 + mlp_count,)),
            pltpu.SemaphoreType.DMA((2 + mlp_count,)),
            pltpu.SemaphoreType.DMA((6,)),
            pltpu.SemaphoreType.DMA((6,)),
        ],
        compiler_params=pltpu.CompilerParams(
            collective_id=1, has_side_effects=True, vmem_limit_bytes=63 << 20
        ),
        name="backward",
    )(zero, groups, *streamed, states, *constant)


def emit_kernel(
    half, edges, mlp_ref, attn_ref, small_ref, tokens_ref, output_ref,
    output_out, tokens_out, gain_one_out, query_out, key_out, value_out, gate_out, low_in_out, low_out_out, bias_out,
    gain_out_out, out_out, gain_two_out, mlp_out, tokens, output, mlp, attn, load_sems, sems,
):
    staged = [(attn_ref, attn), (mlp_ref, mlp), (output_ref, output), (tokens_ref, tokens)]
    loads = [pltpu.make_async_copy(source, target, load_sems.at[i]) for i, (source, target) in enumerate(staged)]
    for load in loads:
        load.start()
    moves = []
    for i, target in enumerate((query_out, key_out, value_out, gate_out, out_out)):
        moves.append((attn.at[:, edges[i] : edges[i + 1]], target))
    moves += [(mlp, mlp_out), (output, output_out), (tokens, tokens_out)]
    copies = [pltpu.make_async_copy(source, target, sems.at[i]) for i, (source, target) in enumerate(moves)]
    for i, load in enumerate(loads):
        load.wait()
        for copy in copies[:5] if i == 0 else copies[4 + i : 5 + i]:
            copy.start()
    rank, width = low_in_out.shape
    keys = low_out_out.shape[1]
    decay_at, decay_slot, _ = small_rows(width, rank, keys)
    for i in range(width // 128):
        columns = slice(i * 128, (i + 1) * 128)
        gain_one_out[:, columns] = small_ref[GAIN_ONE + i : GAIN_ONE + i + 1, :]
        gain_two_out[:, columns] = small_ref[GAIN_TWO + i : GAIN_TWO + i + 1, :]
        low_in_out[:, columns] = small_ref[LOW_IN + i * rank : LOW_IN + (i + 1) * rank, :]
    for i in range(VALUE_HEAD // 128):
        gain_out_out[:, i * 128 : (i + 1) * 128] = small_ref[GAIN_OUT + i : GAIN_OUT + i + 1, :]
    for head in range(2):

        @pl.when(lax.axis_index("head") == head)
        def _():
            base = decay_at + head * decay_slot
            for i in range(keys // 128):
                columns = slice(i * 128, (i + 1) * 128)
                low_out_out[:, columns] = small_ref[base + i * rank : base + (i + 1) * rank, :]
                bias_at = base + keys // 128 * rank + i
                bias_out[:, columns] = small_ref[bias_at : bias_at + 1, :]

    for copy in copies:
        copy.wait()


def emit(mlp, attn, small, tokens, output, keys, values, rank):
    rows, width = attn.shape[0], tokens.shape[1]
    edges = [0, keys, 2 * keys, 2 * keys + values, 2 * keys + 2 * values, 2 * keys + 3 * values]
    vmem = pl.BlockSpec(memory_space=pltpu.VMEM)
    shapes = [
        (output.shape, BF16, ANY), (tokens.shape, F32, ANY), ((1, width), F32, vmem), ((rows, keys), F32, ANY),
        ((rows, keys), F32, ANY), ((rows, values), F32, ANY), ((rows, values), F32, ANY), ((rank, width), F32, vmem),
        ((rank, keys), F32, vmem), ((1, keys), F32, vmem), ((1, VALUE_HEAD), F32, vmem), ((rows, values), F32, ANY),
        ((1, width), F32, vmem), (mlp.shape, F32, ANY),
    ]
    return pl.pallas_call(
        functools.partial(emit_kernel, mlp.shape[1] // 6, edges),
        in_specs=[ANY, ANY, vmem, ANY, ANY],
        out_specs=[space for _, _, space in shapes],
        out_shape=[jax.ShapeDtypeStruct(shape, kind) for shape, kind, _ in shapes],
        scratch_shapes=[
            pltpu.VMEM(tokens.shape, F32),
            pltpu.VMEM(output.shape, BF16),
            pltpu.VMEM(mlp.shape, F32),
            pltpu.VMEM(attn.shape, F32),
            pltpu.SemaphoreType.DMA((4,)),
            pltpu.SemaphoreType.DMA((8,)),
        ],
        compiler_params=pltpu.CompilerParams(vmem_limit_bytes=60 << 20),
        name="emit",
    )(mlp, attn, small, tokens, output)


def swap(value):
    return lax.ppermute(value, "head", [(0, 1), (1, 0)])


def ordered(own, other, axis):
    size = own.shape[axis]
    joined = jnp.concatenate([own, other, own], axis=axis)
    return lax.dynamic_slice_in_dim(joined, lax.axis_index("head") * size, 2 * size, axis)


def half_of(value, which, axis):
    size = value.shape[axis] // 2
    return lax.dynamic_slice_in_dim(value, which * size, size, axis)


def sum_rows(partial, here):
    other = swap(half_of(partial, 1 - here, 0).astype(BF16))
    return half_of(partial, here, 0) + other.astype(F32)


def norm_backward(grad_in, gain, normed_in, scale_in):
    scaled = grad_in * gain
    return scale_in * (scaled - normed_in * jnp.mean(scaled * normed_in, axis=-1, keepdims=True))


def per_device(
    tokens, lengths, initial_memory, norm_attn_gain, w_query, w_key, w_value, w_gate_out, w_low_in, w_low_out,
    decay_bias, out_gain, w_out, norm_mlp_gain, w_mlp, cotangent,
):
    here = lax.axis_index("head")
    own_rows = tokens.shape[1]
    keys = w_query.shape[1]
    values = w_value.shape[1]
    hidden = w_mlp.shape[1] // 3
    half = hidden // 2
    shard_rows = w_mlp.shape[0]
    square = lax.axis_size("dp") == 16

    tokens_own = tokens[0]
    if square:
        (
            h_low, query, key, value, gate, logits, low_rank, attended, mixed, states,
            grad_zero, grad_mlp, output, resid_total, attn_low, gain_two_grad,
        ) = layer(
            tokens_own, cotangent[0], lengths, norm_attn_gain, norm_mlp_gain, out_gain, decay_bias,
            initial_memory[0], w_query, w_key, w_value, w_gate_out, w_low_in.T, w_low_out, w_out, w_mlp,
        )
        grad_mlp, attn_grads, packed, tokens_grad = backward(
            grad_zero, grad_mlp, attn_low, h_low, query, key, value, gate, logits, low_rank, attended, mixed, states,
            w_query, w_key, w_value, w_gate_out, w_low_in.T, w_low_out, w_out, tokens_own, resid_total,
            norm_attn_gain, out_gain, gain_two_grad,
        )
        results = emit(grad_mlp, attn_grads, packed, tokens_grad, output, keys, values, w_low_out.shape[0])
        (
            output, tokens_grad, gain_one_grad, query_grad, key_grad, value_grad, gate_grad, low_in_grad, low_out_grad,
            bias_grad, out_gain_grad, out_grad, gain_two_grad, grad_mlp,
        ) = results
        return (
            output[None], tokens_grad[None], gain_one_grad[0], query_grad, key_grad, value_grad, gate_grad,
            low_in_grad.T, low_out_grad, bias_grad[0], out_gain_grad[0], out_grad.T, gain_two_grad[0], grad_mlp,
        )
    pieces = w_mlp.reshape(shard_rows, 3, 2, half)
    own_piece = lax.dynamic_index_in_dim(pieces, here, 2, keepdims=False)
    other_piece = lax.dynamic_index_in_dim(pieces, 1 - here, 2, keepdims=False)
    positions = here * own_rows + lax.iota(jnp.int32, own_rows)
    row_mask = (positions < lengths[0]).astype(F32)[:, None]
    resid_grad = row_mask * cotangent[0].astype(F32)
    low_own = resid_grad.astype(BF16)
    pair = swap(other_piece.reshape(shard_rows, 3 * half))
    weights = lax.all_gather(
        ordered(own_piece.reshape(shard_rows, 3 * half), pair, 0), "dp", axis=0, tiled=True
    )
    tokens_wide = ordered(tokens_own, swap(tokens_own), 0).astype(F32)
    length = tokens_wide.shape[0]
    scale_one = lax.rsqrt(jnp.mean(tokens_wide * tokens_wide, axis=1, keepdims=True) + EPSILON)
    h_low = (tokens_wide * scale_one * norm_attn_gain).astype(BF16)
    query = dot(h_low, w_query).astype(BF16)
    key = dot(h_low, w_key).astype(BF16)
    value = dot(h_low, w_value).astype(BF16)
    gate = dot(h_low, w_gate_out)
    low_rank = dot(h_low, w_low_in)
    low_high, low_rest = split_low(low_rank)
    logits = dot(low_high, w_low_out) + dot(low_rest, w_low_out) + decay_bias
    attended, mixed, states = attention_forward(query, key, value, logits, gate, out_gain, initial_memory[0])
    resid = tokens_own.astype(F32) + sum_rows(dot(mixed, w_out), here)
    scale_two = lax.rsqrt(jnp.mean(resid * resid, axis=1, keepdims=True) + EPSILON)
    normal_two = resid * scale_two
    h_two_own = (normal_two * norm_mlp_gain).astype(BF16)
    h_two = ordered(h_two_own, swap(h_two_own), 0)
    resid_low = ordered(low_own, swap(low_own), 0)
    pre_gate = dot(h_two, weights[:, :half])
    up_part = dot(h_two, weights[:, half : 2 * half])
    pre_sigmoid = sigmoid(pre_gate)
    inner = (pre_gate * pre_sigmoid * up_part).astype(BF16)
    inner_grad = dot(resid_low, weights[:, 2 * half :])
    pre_grad = (
        inner_grad * up_part * pre_sigmoid * (1.0 + pre_gate * (1.0 - pre_sigmoid))
    ).astype(BF16)
    up_grad = (inner_grad * pre_gate * pre_sigmoid).astype(BF16)
    mlp_out = sum_rows(dot(inner, weights[:, 2 * half :], 1, 1), here)
    output = (row_mask * (resid + mlp_out)).astype(BF16)[None]
    h_two_grad = sum_rows(
        dot(pre_grad, weights[:, :half], 1, 1) + dot(up_grad, weights[:, half : 2 * half], 1, 1), here
    )
    grad_mlp = jnp.concatenate(
        [
            dot(h_two, pre_grad, 0, 0).astype(BF16),
            dot(h_two, up_grad, 0, 0).astype(BF16),
            dot(resid_low, inner, 0, 0).astype(BF16),
        ],
        axis=1,
    )
    resid_total = resid_grad + norm_backward(h_two_grad, norm_mlp_gain, normal_two, scale_two)
    gain_two_grad = jnp.sum(h_two_grad * normal_two, axis=0)
    attn_own = resid_total.astype(BF16)
    attn_low = ordered(attn_own, swap(attn_own), 0)

    mixed_grad = dot(attn_low, w_out, 1, 1)
    out_grad = dot(attn_low, mixed, 0, 0)
    query_grad, key_grad, value_grad, gate_grad, logits_grad, out_gain_grad = attention_backward(
        mixed_grad, query, key, value, logits, gate, attended, states, out_gain
    )
    bias_grad = jnp.sum(logits_grad, axis=0)
    grad_high, grad_rest = split_low(logits_grad)
    low_out_grad = (
        dot(low_high, grad_high, 0, 0) + dot(low_rest, grad_high, 0, 0) + dot(low_high, grad_rest, 0, 0)
    )
    low_rank_low = (dot(grad_high, w_low_out, 1, 1) + dot(grad_rest, w_low_out, 1, 1)).astype(BF16)
    low_in_grad = dot(h_low, low_rank_low, 0, 0)
    attn_grads = jnp.concatenate(
        [
            dot(h_low, query_grad, 0, 0).astype(BF16),
            dot(h_low, key_grad, 0, 0).astype(BF16),
            dot(h_low, value_grad, 0, 0).astype(BF16),
            dot(h_low, gate_grad, 0, 0).astype(BF16),
            out_grad.astype(BF16),
        ],
        axis=1,
    )
    h_grad = sum_rows(
        dot(query_grad, w_query, 1, 1)
        + dot(key_grad, w_key, 1, 1)
        + dot(value_grad, w_value, 1, 1)
        + dot(gate_grad, w_gate_out, 1, 1)
        + dot(low_rank_low, w_low_in, 1, 1),
        here,
    )
    own_wide = tokens_own.astype(F32)
    own_scale = lax.rsqrt(jnp.mean(own_wide * own_wide, axis=1, keepdims=True) + EPSILON)
    normal_own = own_wide * own_scale
    tokens_grad = resid_total + norm_backward(h_grad, norm_attn_gain, normal_own, own_scale)
    gain_one_grad = jnp.sum(h_grad * normal_own, axis=0)
    low_rank_width = w_low_out.shape[0]
    decay_part = jnp.concatenate([low_out_grad, bias_grad[None]], axis=0)
    slots = jnp.zeros((2,) + decay_part.shape, F32)
    slots = lax.dynamic_update_slice(slots, decay_part[None], (here, 0, 0))
    packed = jnp.concatenate(
        [
            gain_one_grad, gain_two_grad, out_gain_grad.reshape(-1), low_in_grad.reshape(-1), slots.reshape(-1),
        ]
    )
    packed = lax.psum(packed, ("dp", "head"))
    attn_grads = lax.psum_scatter(attn_grads, "dp", scatter_dimension=0, tiled=True).astype(F32)
    grad_mlp = lax.psum_scatter(grad_mlp, "dp", scatter_dimension=0, tiled=True)
    own_half = half_of(grad_mlp, here, 0)
    other_half = swap(half_of(grad_mlp, 1 - here, 0))
    grad_mlp = ordered(
        own_half.reshape(shard_rows, 3, 1, half), other_half.reshape(shard_rows, 3, 1, half), 2
    ).reshape(shard_rows, 3 * hidden).astype(F32)
    width = gain_one_grad.shape[0]
    edges = [width, 2 * width, 2 * width + VALUE_HEAD]
    edges.append(edges[-1] + width * low_rank_width)
    low_in_grad = packed[edges[2] : edges[3]].reshape(width, low_rank_width)
    decay_part = lax.dynamic_index_in_dim(packed[edges[3] :].reshape(slots.shape), here, 0, keepdims=False)
    low_out_grad, bias_grad = decay_part[:low_rank_width], decay_part[low_rank_width]
    gain_one_grad, gain_two_grad = packed[: edges[0]], packed[edges[0] : edges[1]]
    out_gain_grad = packed[edges[1] : edges[2]]
    return (
        output,
        tokens_grad[None],
        gain_one_grad,
        attn_grads[:, :keys],
        attn_grads[:, keys : 2 * keys],
        attn_grads[:, 2 * keys : 2 * keys + values],
        attn_grads[:, 2 * keys + values : 2 * keys + 2 * values],
        low_in_grad,
        low_out_grad,
        bias_grad,
        out_gain_grad,
        attn_grads[:, 2 * keys + 2 * values :].T,
        gain_two_grad,
        grad_mlp,
    )


def solution(mesh):
    return jax.shard_map(
        per_device,
        mesh=mesh,
        in_specs=(
            P("dp", "head", None),
            P("dp"),
            P("dp", "head", None, None),
            P(),
            P(None, "head"),
            P(None, "head"),
            P(None, "head"),
            P(None, "head"),
            P(),
            P(None, "head"),
            P("head"),
            P(),
            P("head", None),
            P(),
            P(("dp", "head"), None),
            P("dp", "head", None),
        ),
        out_specs=(
            P("dp", "head", None),
            P("dp", "head", None),
            P(),
            P("dp", "head"),
            P("dp", "head"),
            P("dp", "head"),
            P("dp", "head"),
            P(),
            P(None, "head"),
            P("head"),
            P(),
            P("head", "dp"),
            P(),
            P(("dp", "head"), None),
        ),
        check_vma=False,
    )
```

```python
import functools

import jax
import jax.numpy as jnp
from jax import lax
from jax.experimental import pallas as pl
from jax.experimental.pallas import tpu as pltpu
from jax.sharding import PartitionSpec as P

HEADS = 4
KEY = 512
VALUE = 1024
BLOCK = 128
KEY_HEAD = KEY // HEADS
VALUE_HEAD = VALUE // HEADS

EPSILON = 1e-05
F32 = jnp.float32
BF16 = jnp.bfloat16
SCALE = KEY_HEAD ** (-0.5)


def dot(left, right, left_dim=1, right_dim=0):
    return lax.dot_general(
        left, right, (((left_dim,), (right_dim,)), ((), ())), preferred_element_type=F32
    )


def split_low(value):
    high = value.astype(BF16)
    return high, (value - high.astype(F32)).astype(BF16)


def sigmoid(value):
    return 1.0 / (1.0 + jnp.exp(-value))


def log_sigmoid(value):
    return jnp.minimum(value, 0.0) - jnp.log1p(jnp.exp(-jnp.abs(value)))


def triangle(lower):
    rows = lax.broadcasted_iota(jnp.int32, (BLOCK, BLOCK), 0)
    columns = lax.broadcasted_iota(jnp.int32, (BLOCK, BLOCK), 1)
    return rows >= columns if lower else rows <= columns


def decay_terms(logits):
    log_decay = log_sigmoid(logits) * (1.0 / 16.0)
    ones = jnp.where(triangle(True), 1.0, 0.0).astype(BF16)
    high, low = split_low(log_decay)
    total = dot(ones, high) + dot(ones, low)
    middle = total[BLOCK // 2 - 1 : BLOCK // 2, :]
    end = total[BLOCK - 1 :, :]
    rise = jnp.exp(total - middle)
    fall = jnp.exp(middle - total)
    early = rise * (jnp.exp(middle) * SCALE)
    late = fall * jnp.exp(end - middle)
    return rise * SCALE, fall, early, late, jnp.exp(end)


def as_column(row, width):
    column = jnp.transpose(jnp.broadcast_to(row, (KEY_HEAD, KEY_HEAD)))
    return jnp.concatenate([column] * (width // KEY_HEAD), axis=1)


def forward_block(query, key, value, logits, gate, gain, memory, states):
    rise, fall, early, late, decay = decay_terms(logits)
    lower = triangle(True)
    attended_parts = []
    mixed_parts = []
    for head in range(memory.shape[0]):
        keys_at = slice(head * KEY_HEAD, (head + 1) * KEY_HEAD)
        values_at = slice(head * VALUE_HEAD, (head + 1) * VALUE_HEAD)
        query_wide = query[:, keys_at].astype(F32)
        key_wide = key[:, keys_at].astype(F32)
        value_head = value[:, values_at]
        state = memory[head]
        state_low = state.astype(BF16)
        states[head] = state_low
        scores = dot(
            (query_wide * rise[:, keys_at]).astype(BF16), (key_wide * fall[:, keys_at]).astype(BF16), 1, 1
        )
        scores = jnp.where(lower, scores, 0.0).astype(BF16)
        left = jnp.concatenate([scores, (query_wide * early[:, keys_at]).astype(BF16)], axis=1)
        attended = dot(left, jnp.concatenate([value_head, state_low], axis=0))
        memory[head] = as_column(decay[:, keys_at], VALUE_HEAD) * state + dot(
            (key_wide * late[:, keys_at]).astype(BF16), value_head, 0, 0
        )
        scale = lax.rsqrt(jnp.mean(attended * attended, axis=1, keepdims=True) + EPSILON)
        gate_head = gate[:, values_at]
        attended_parts.append(attended)
        mixed_parts.append((attended * scale * gain * gate_head * sigmoid(gate_head)).astype(BF16))
    return jnp.concatenate(attended_parts, axis=1), jnp.concatenate(mixed_parts, axis=1)


def forward_kernel(
    query_ref, key_ref, value_ref, logits_ref, gate_ref, gain_ref, start_ref,
    attended_ref, mixed_ref, states_ref, memory
):
    @pl.when(pl.program_id(0) == 0)
    def _():
        memory[...] = start_ref[...]

    attended_ref[...], mixed_ref[...] = forward_block(
        query_ref[...], key_ref[...], value_ref[...], logits_ref[...], gate_ref[...], gain_ref[...],
        memory, states_ref.at[0],
    )


def attention_forward(query, key, value, logits, gate, gain, start):
    length, keys = query.shape
    values = value.shape[1]
    heads = start.shape[0]
    steps = length // BLOCK

    def rows(width):
        return pl.BlockSpec((BLOCK, width), lambda i: (i, 0))

    return pl.pallas_call(
        forward_kernel,
        grid=(steps,),
        in_specs=[
            rows(keys), rows(keys), rows(values), rows(keys), rows(values),
            pl.BlockSpec((1, VALUE_HEAD), lambda i: (0, 0)),
            pl.BlockSpec((heads, KEY_HEAD, VALUE_HEAD), lambda i: (0, 0, 0)),
        ],
        out_specs=[
            rows(values), rows(values),
            pl.BlockSpec((1, heads, KEY_HEAD, VALUE_HEAD), lambda i: (i, 0, 0, 0)),
        ],
        out_shape=[
            jax.ShapeDtypeStruct((length, values), F32),
            jax.ShapeDtypeStruct((length, values), BF16),
            jax.ShapeDtypeStruct((steps, heads, KEY_HEAD, VALUE_HEAD), BF16),
        ],
        scratch_shapes=[pltpu.VMEM((heads, KEY_HEAD, VALUE_HEAD), F32)],
        compiler_params=pltpu.CompilerParams(vmem_limit_bytes=48 << 20),
        name="attention_forward",
    )(query, key, value, logits, gate, gain.reshape(1, -1), start)


def backward_block(mixed_grad, query, key, value, logits, gate, attended, states, gain, memory_grad):
    rise, fall, early, late, decay = decay_terms(logits)
    lower = triangle(True)
    upper = triangle(False)
    last = lax.broadcasted_iota(jnp.int32, (BLOCK, KEY_HEAD), 0) == BLOCK - 1
    query_grads, key_grads, value_grads, gate_grads, total_grads = [], [], [], [], []
    gain_grad = jnp.zeros((1, VALUE_HEAD), F32)
    for head in range(memory_grad.shape[0]):
        keys_at = slice(head * KEY_HEAD, (head + 1) * KEY_HEAD)
        values_at = slice(head * VALUE_HEAD, (head + 1) * VALUE_HEAD)
        attended_head = attended[:, values_at]
        scale = lax.rsqrt(jnp.mean(attended_head * attended_head, axis=1, keepdims=True) + EPSILON)
        normal = attended_head * scale
        gate_head = gate[:, values_at]
        gate_sigmoid = sigmoid(gate_head)
        mixed_head = mixed_grad[:, values_at]
        gate_grads.append(
            (mixed_head * normal * gain * gate_sigmoid * (1.0 + gate_head * (1.0 - gate_sigmoid))).astype(BF16)
        )
        normed_grad = mixed_head * gate_head * gate_sigmoid
        gain_grad += jnp.sum(normed_grad * normal, axis=0, keepdims=True)
        scaled = normed_grad * gain
        attended_grad = (
            scale * (scaled - normal * jnp.mean(scaled * normal, axis=1, keepdims=True))
        ).astype(BF16)

        query_wide = query[:, keys_at].astype(F32)
        key_wide = key[:, keys_at].astype(F32)
        value_head = value[:, values_at]
        query_middle = query_wide * rise[:, keys_at]
        key_middle = key_wide * fall[:, keys_at]
        query_early = query_wide * early[:, keys_at]
        key_late = key_wide * late[:, keys_at]
        query_middle_low = query_middle.astype(BF16)
        key_middle_low = key_middle.astype(BF16)
        state = states[head]
        after = memory_grad[head]

        scores_turned = jnp.where(upper, dot(key_middle_low, query_middle_low, 1, 1), 0.0).astype(BF16)
        from_values = dot(attended_grad, jnp.concatenate([value_head, state], axis=0), 1, 1)
        to_values = jnp.concatenate([attended_grad, after.astype(BF16)], axis=0)
        from_grads = dot(value_head, to_values, 1, 1)
        scores_grad = jnp.where(lower, from_values[:, :BLOCK], 0.0).astype(BF16)
        scores_grad_turned = jnp.where(upper, from_grads[:, :BLOCK], 0.0).astype(BF16)
        query_early_grad = from_values[:, BLOCK:]
        key_late_grad = from_grads[:, BLOCK:]
        query_middle_grad = dot(scores_grad, key_middle_low)
        key_middle_grad = dot(scores_grad_turned, query_middle_low)
        value_grads.append(
            dot(jnp.concatenate([scores_turned, key_late.astype(BF16)], axis=1), to_values).astype(BF16)
        )
        carried = as_column(decay[:, keys_at], VALUE_HEAD) * after
        memory_grad[head] = carried + dot(query_early.astype(BF16), attended_grad, 0, 0)
        query_grads.append(
            (query_early_grad * early[:, keys_at] + query_middle_grad * rise[:, keys_at]).astype(BF16)
        )
        key_grads.append((key_middle_grad * fall[:, keys_at] + key_late_grad * late[:, keys_at]).astype(BF16))
        late_part = key_late_grad * key_late
        end_high, end_low = split_low(carried * state.astype(F32))
        ones = jnp.ones((8, VALUE_HEAD), BF16)
        end_grad = (dot(ones, end_high, 1, 1) + dot(ones, end_low, 1, 1))[:1] + jnp.sum(
            late_part, axis=0, keepdims=True
        )
        total_grads.append(
            query_early_grad * query_early
            + query_middle_grad * query_middle
            - key_middle_grad * key_middle
            - late_part
            + jnp.where(last, end_grad, 0.0)
        )
    ones = jnp.where(upper, 1.0, 0.0).astype(BF16)
    high, rest = split_low(jnp.concatenate(total_grads, axis=1))
    logits_grad = (dot(ones, high) + dot(ones, rest)) * sigmoid(-logits) * (1.0 / 16.0)
    grads = query_grads + key_grads + value_grads + gate_grads
    return jnp.concatenate(grads, axis=1), logits_grad, gain_grad


def backward_kernel_plain(
    mixed_grad_ref, query_ref, key_ref, value_ref, logits_ref, gate_ref, attended_ref, states_ref, gain_ref,
    query_grad_ref, key_grad_ref, value_grad_ref, gate_grad_ref, logits_grad_ref, gain_grad_ref, memory_grad
):
    @pl.when(pl.program_id(0) == 0)
    def _():
        memory_grad[...] = jnp.zeros_like(memory_grad)
        gain_grad_ref[...] = jnp.zeros_like(gain_grad_ref)

    grads, logits_grad, gain_grad = backward_block(
        mixed_grad_ref[...], query_ref[...], key_ref[...], value_ref[...], logits_ref[...], gate_ref[...],
        attended_ref[...], states_ref[0], gain_ref[...], memory_grad,
    )
    start = 0
    for ref in (query_grad_ref, key_grad_ref, value_grad_ref, gate_grad_ref):
        ref[...] = grads[:, start : start + ref.shape[1]]
        start += ref.shape[1]
    logits_grad_ref[...] = logits_grad
    gain_grad_ref[...] += gain_grad


def attention_backward(mixed_grad, query, key, value, logits, gate, attended, states, gain):
    length, keys = query.shape
    values = value.shape[1]
    heads = states.shape[1]
    steps = length // BLOCK

    def rows(width):
        return pl.BlockSpec((BLOCK, width), lambda i: (steps - 1 - i, 0))

    return pl.pallas_call(
        backward_kernel_plain,
        grid=(steps,),
        in_specs=[
            rows(values), rows(keys), rows(keys), rows(values), rows(keys), rows(values), rows(values),
            pl.BlockSpec((1, heads, KEY_HEAD, VALUE_HEAD), lambda i: (steps - 1 - i, 0, 0, 0)),
            pl.BlockSpec((1, VALUE_HEAD), lambda i: (0, 0)),
        ],
        out_specs=[
            rows(keys), rows(keys), rows(values), rows(values), rows(keys),
            pl.BlockSpec((1, VALUE_HEAD), lambda i: (0, 0)),
        ],
        out_shape=[
            jax.ShapeDtypeStruct((length, keys), BF16),
            jax.ShapeDtypeStruct((length, keys), BF16),
            jax.ShapeDtypeStruct((length, values), BF16),
            jax.ShapeDtypeStruct((length, values), BF16),
            jax.ShapeDtypeStruct((length, keys), F32),
            jax.ShapeDtypeStruct((1, VALUE_HEAD), F32),
        ],
        scratch_shapes=[pltpu.VMEM((heads, KEY_HEAD, VALUE_HEAD), F32)],
        compiler_params=pltpu.CompilerParams(vmem_limit_bytes=48 << 20),
        name="attention_backward",
    )(mixed_grad, query, key, value, logits, gate, attended, states, gain.reshape(1, -1))


MESH = pl.DeviceIdType.MESH
ANY = pl.BlockSpec(memory_space=pl.ANY)


class Place:
    def __init__(self):
        self.dp = lax.axis_index("dp")
        self.head = lax.axis_index("head")
        self.z = self.dp // 4
        self.flat = self.dp % 4
        self.flat_x = self.flat + 1 - 2 * (self.flat % 2)
        self.flat_y = self.flat + 2 - 4 * (self.flat // 2)
        self.flat_xy = 3 - self.flat
        self.sibling = (self.dp, 1 - self.head)
        self.beside_x = (self.z * 4 + self.flat_x, self.head)
        self.beside_y = (self.z * 4 + self.flat_y, self.head)
        self.along_z = [(((self.z + i) % 4) * 4 + self.flat, self.head) for i in range(1, 4)]

    def meet(self):
        barrier = pltpu.get_barrier_semaphore()
        others = [self.sibling, self.beside_x, self.beside_y] + self.along_z
        for other in others:
            pl.semaphore_signal(barrier, 1, device_id=other, device_id_type=MESH)
        pl.semaphore_wait(barrier, len(others))


def send(source, target, out_sem, in_sem, device):
    copy = pltpu.make_async_remote_copy(
        src_ref=source, dst_ref=target, send_sem=out_sem, recv_sem=in_sem, device_id=device, device_id_type=MESH
    )
    copy.start()
    return copy


def arrived(target, out_sem, in_sem, device):
    pltpu.make_async_remote_copy(
        src_ref=target, dst_ref=target, send_sem=out_sem, recv_sem=in_sem, device_id=device, device_id_type=MESH
    ).wait_recv()


def chunk_columns(width, sizes):
    starts = [sum(sizes[:i]) * 128 for i in range(len(sizes))]
    assert sum(sizes) * 128 == width
    return [slice(start, start + size * 128) for start, size in zip(starts, sizes)]


ROWS = 256
SMALL_TICKS = (0, 2, 5, 8)


class Gather:
    LAGS = (0, 1, 3)

    def __init__(self, place, source, targets, blocks, local_sems, swap_out, swap_in, out_sems, in_sems):
        self.place, self.source, self.targets, self.blocks = place, source, targets, blocks
        self.local_sems, self.swap_out, self.swap_in = local_sems, swap_out, swap_in
        self.out_sems, self.in_sems = out_sems, in_sems
        self.ticks = len(blocks) + self.LAGS[-1]

    def put(self, source, target, chunk, slot, device):
        send(source, target, self.out_sems.at[chunk, slot], self.in_sems.at[chunk, slot], device)

    def wait(self, target, chunk, slot):
        arrived(target, self.out_sems.at[chunk, slot], self.in_sems.at[chunk, slot], self.place.sibling)

    def start(self):
        at, source = self.place, self.source
        rows, half = source.shape[0], source.shape[1] // 6
        mine = pl.ds(at.head * rows, rows)
        offset = 0
        for i, block in enumerate(self.targets):
            size = block.shape[3] // 3
            for part in range(3):
                target = block.at[at.z, at.flat, mine, part * size : (part + 1) * size]
                base = 2 * part * half + offset
                here = pl.ds(pl.multiple_of(base + at.head * half, 128), size)
                there = pl.ds(pl.multiple_of(base + (1 - at.head) * half, 128), size)
                pltpu.make_async_copy(source.at[:, here], target, self.local_sems.at[i]).start()
                send(source.at[:, there], target, self.swap_out.at[i], self.swap_in.at[i], at.sibling)
            offset += size
    def pair_ready(self, i):
        at, block = self.place, self.targets[i]
        rows = self.source.shape[0]
        target = block.at[at.z, at.flat, pl.ds(at.head * rows, rows)]
        pltpu.make_async_copy(target, target, self.local_sems.at[i]).wait()
        theirs = pl.ds((1 - at.head) * rows, rows)
        arrived(block.at[at.z, at.flat, theirs], self.swap_out.at[i], self.swap_in.at[i], at.sibling)

    def stage(self, number, chunk):
        at, out = self.place, self.blocks[chunk]
        everything = slice(None)
        if number == 0:
            if chunk % 2 == 0:
                self.pair_ready(chunk // 2)
            block = out.at[at.z, at.flat]
            for i in range(3):
                self.put(block, block, chunk, i, at.along_z[i])
        if number == 1:
            for i in range(3):
                self.wait(out.at[(at.z + 3 - i) % 4, at.flat], chunk, i)
            block = out.at[everything, at.flat]
            self.put(block, block, chunk, 3, at.beside_x)
            self.put(block, block, chunk, 4, at.beside_y)
        if number == 2:
            self.wait(out.at[everything, at.flat_x], chunk, 3)
            block = out.at[pl.ds(0, 2), at.flat_x]
            self.put(block, block, chunk, 5, at.beside_y)
            self.wait(out.at[everything, at.flat_y], chunk, 4)
            block = out.at[pl.ds(2, 2), at.flat_y]
            self.put(block, block, chunk, 6, at.beside_x)

    def complete(self, chunk):
        at, out = self.place, self.blocks[chunk]
        self.wait(out.at[pl.ds(0, 2), at.flat_xy], chunk, 5)
        self.wait(out.at[pl.ds(2, 2), at.flat_xy], chunk, 6)

    def tick(self, number):
        for stage in (2, 1, 0):
            chunk = number - self.LAGS[stage]
            if 0 <= chunk < len(self.blocks):
                self.stage(stage, chunk)

    def finish(self):
        everything = slice(None)
        for chunk, block in enumerate(self.blocks):
            shapes = [block.at[0, 0]] * 3 + [block.at[everything, 0]] * 2 + [block.at[pl.ds(0, 2), 0]] * 2
            for slot, ref in enumerate(shapes):
                sent(ref, self.out_sems.at[chunk, slot], self.in_sems.at[chunk, slot], self.place.sibling)
        rows = self.source.shape[0]
        for i, block in enumerate(self.targets):
            sent(block.at[0, 0, pl.ds(0, rows)], self.swap_out.at[i], self.swap_in.at[i], self.place.sibling)


def sent(source, out_sem, in_sem, device):
    pltpu.make_async_remote_copy(
        src_ref=source, dst_ref=source, send_sem=out_sem, recv_sem=in_sem, device_id=device, device_id_type=MESH
    ).wait_send()


def layer_kernel(
    count,
    tokens_ref, cotangent_ref, length_ref, gain_one_ref, gain_two_ref, gain_out_ref, bias_ref, start_ref,
    w_query, w_key, w_value, w_gate, w_low_in, w_low_out, w_out, w_mlp,
    h_ref, query_ref, key_ref, value_ref, gate_ref, logits_ref, low_rank_ref, attended_ref, mixed_ref, states_ref,
    grad_zero_ref, grad_ref, output_ref, total_ref, attn_ref, gain_grad_ref,
    tokens, low, low_turned, h_two, h_two_turned, weights_zero, weights, resid, part_out, part_in,
    mlp_sum, grad_sum, inner_all, pair_all, sums_out, sums_in, memory,
    local_sems, gather_local, swap_out, swap_in, gather_out, gather_in, pair_out, pair_in,
):
    step = pl.program_id(0)
    at = Place()
    own = tokens_ref.shape[0]
    length = 2 * own
    tiles = length // ROWS
    own_tiles = own // ROWS
    own_at = at.head * own
    gather = Gather(
        at,
        w_mlp,
        [weights.at[i] for i in range(count - 1)] + [weights_zero],
        [weights.at[i, :, :, :, j * 384 : (j + 1) * 384] for i in range(count - 1) for j in range(2)]
        + [weights_zero],
        gather_local, swap_out, swap_in, gather_out, gather_in,
    )
    plan = {(0, 0): (0, 1), (1, 0): (2,), (2, 0): (3,), (3, 0): (4,), (4, 0): (5,), (4, 1): (6,)}
    places = [(5, 0), (5, 1), (6, 1), (7, 0), (7, 1), (8, 1), (9, 1)]
    for i, key in enumerate(places):
        plan[key] = (7 + i,) if i < len(places) - 1 else tuple(range(7 + i, gather.ticks))
    attention_steps = tiles
    first_step = attention_steps + 1
    last_step = first_step + count - 1

    def own_rows(i, size=ROWS):
        return pl.ds(pl.multiple_of(own_at + i * ROWS, ROWS), size)

    def other_rows(i, size=ROWS):
        return pl.ds(pl.multiple_of(own - own_at + i * ROWS, ROWS), size)

    def row_mask(i):
        positions = own_at + i * ROWS + lax.broadcasted_iota(jnp.int32, (ROWS, 1), 0)
        return jnp.where(positions < length_ref[0], 1.0, 0.0)

    def put(source, target, slot):
        send(source, target, pair_out.at[slot], pair_in.at[slot], at.sibling)

    def wait(target, slot):
        arrived(target, pair_out.at[slot], pair_in.at[slot], at.sibling)

    @pl.when(step == 0)
    def _():
        here = [
            pltpu.make_async_copy(cotangent_ref, low.at[own_rows(0, own)], local_sems.at[1]),
            pltpu.make_async_copy(tokens_ref, tokens.at[own_rows(0, own)], local_sems.at[0]),
        ]
        for copy in here:
            copy.start()
        at.meet()
        put(tokens_ref, tokens.at[own_rows(0, own)], 0)
        memory[...] = start_ref[...]
        gain_grad_ref[...] = jnp.zeros_like(gain_grad_ref)
        gather.start()
        for number in plan[0, 0]:
            gather.tick(number)
        for copy in here:
            copy.wait()
        for i in range(own_tiles):
            low[own_rows(i), :] = (low[own_rows(i), :].astype(F32) * row_mask(i)).astype(BF16)
        put(low.at[own_rows(0, own)], low.at[own_rows(0, own)], 1)
        wait(tokens.at[other_rows(0, own)], 0)

    def gather_at(inside, among):
        for (when, which), numbers in plan.items():
            if which == inside and when in among:

                @pl.when(step == when)
                def _():
                    for number in numbers:
                        gather.tick(number)

    gather_at(0, range(1, attention_steps + 1))
    @pl.when(step < attention_steps)
    def _():
        rows = pl.ds(pl.multiple_of(step * ROWS, ROWS), ROWS)
        wide = tokens[rows, :].astype(F32)
        scale = lax.rsqrt(jnp.mean(wide * wide, axis=1, keepdims=True) + EPSILON)
        h_low = (wide * scale * gain_one_ref[...]).astype(BF16)
        h_ref[...] = h_low
        query = dot(h_low, w_query[...]).astype(BF16)
        key = dot(h_low, w_key[...]).astype(BF16)
        value = dot(h_low, w_value[...]).astype(BF16)
        gate = dot(h_low, w_gate[...])
        low_rank = dot(h_low, w_low_in[...], 1, 1)
        high, rest = split_low(low_rank)
        logits = dot(high, w_low_out[...]) + dot(rest, w_low_out[...]) + bias_ref[...]
        query_ref[...] = query
        key_ref[...] = key
        value_ref[...] = value
        gate_ref[...] = gate
        low_rank_ref[...] = low_rank
        logits_ref[...] = logits
        for i in range(ROWS // BLOCK):
            block = slice(i * BLOCK, (i + 1) * BLOCK)
            attended, mixed = forward_block(
                query[block], key[block], value[block], logits[block], gate[block], gain_out_ref[...],
                memory, states_ref.at[i],
            )
            attended_ref[block, :] = attended
            mixed_ref[block, :] = mixed
        part = dot(mixed_ref[...], w_out[...])
        tile = step % own_tiles
        tile_rows = pl.ds(pl.multiple_of(tile * ROWS, ROWS), ROWS)
        mine = step // own_tiles == at.head

        @pl.when(mine)
        def _():
            resid[tile_rows, :] = part

        @pl.when(jnp.logical_not(mine))
        def _():
            part_out[tile_rows, :] = part.astype(BF16)
            put(part_out.at[tile_rows], part_in.at[tile_rows], 2 + tile)

    @pl.when(step == attention_steps)
    def _():
        wait(low.at[other_rows(0, own)], 1)
        for i in range(own_tiles):
            rows = pl.ds(i * ROWS, ROWS)
            wait(part_in.at[rows], 2 + i)
            full = tokens[own_rows(i), :].astype(F32) + resid[rows, :] + part_in[rows, :].astype(F32)
            resid[rows, :] = full
            scale = lax.rsqrt(jnp.mean(full * full, axis=1, keepdims=True) + EPSILON)
            h_two[own_rows(i), :] = (full * scale * gain_two_ref[...]).astype(BF16)
            put(h_two.at[own_rows(i)], h_two.at[own_rows(i)], 4 + i)
        gather_at(1, [attention_steps])

        def turn(i, carry):
            rows = pl.ds(pl.multiple_of(i * ROWS, ROWS), ROWS)
            low_turned[:, rows] = jnp.transpose(low[rows, :])
            return carry

        lax.fori_loop(0, tiles, turn, 0)
        for i in range(own_tiles):
            wait(h_two.at[other_rows(i)], 4 + i)

        def turn_two(i, carry):
            rows = pl.ds(pl.multiple_of(i * ROWS, ROWS), ROWS)
            h_two_turned[:, rows] = jnp.transpose(h_two[rows, :])
            return carry

        lax.fori_loop(0, tiles, turn_two, 0)

    def hidden_rows(block, first, last=False):
        width = block.shape[3] // 3

        def body(i, carry):
            tile = (i + own_tiles * (1 - at.head)) % tiles if last else i
            rows = pl.ds(pl.multiple_of(tile * ROWS, ROWS), ROWS)
            w_pair = block[:, :, :, : 2 * width].reshape(-1, 2 * width)
            w_down = block[:, :, :, 2 * width :].reshape(-1, width)
            pair = dot(h_two[rows, :], w_pair)
            inner_grad = dot(low[rows, :], w_down)
            pre_gate = pair[:, :width]
            up_part = pair[:, width:]
            pre_sigmoid = sigmoid(pre_gate)
            swish = pre_gate * pre_sigmoid
            inner = (swish * up_part).astype(BF16)
            pre_grad = inner_grad * up_part * pre_sigmoid * (1.0 + pre_gate * (1.0 - pre_sigmoid))
            both = jnp.concatenate([pre_grad.astype(BF16), (inner_grad * swish).astype(BF16)], axis=1)
            inner_all[rows, :width] = inner
            pair_all[rows, : 2 * width] = both
            out_part = dot(inner, w_down, 1, 1)
            grad_part = dot(both, w_pair, 1, 1)
            if first:
                mlp_sum[rows, :] = out_part
                grad_sum[rows, :] = grad_part
            else:
                mlp_sum[rows, :] += out_part
                grad_sum[rows, :] += grad_part
            if last:

                @pl.when(i < own_tiles)
                def _():
                    there = pl.ds(pl.multiple_of(i * ROWS, ROWS), ROWS)
                    for k, source in enumerate((mlp_sum, grad_sum)):
                        sums_out[k, there, :] = source[rows, :].astype(BF16)
                        put(sums_out.at[k, there], sums_in.at[k, there], 6 + 2 * i + k)

            return carry

        lax.fori_loop(0, tiles, body, 0)

    def weight_rows(block, target):
        width = block.shape[3] // 3

        def body(i, carry):
            rows = pl.ds(pl.multiple_of(i * ROWS, ROWS), ROWS)
            shape = (target.shape[1], target.shape[2], -1)
            target[i, :, :, : 2 * width] = (
                dot(h_two_turned[rows, :], pair_all[:, : 2 * width]).astype(BF16).reshape(shape)
            )
            target[i, :, :, 2 * width :] = (
                dot(low_turned[rows, :], inner_all[:, :width]).astype(BF16).reshape(shape)
            )
            return carry

        lax.fori_loop(0, tiles, body, 0)

    for group in range(count):

        @pl.when(step == first_step + group)
        def _():
            gather_at(0, [first_step + group])
            gather.complete(2 * group)
            if group < count - 1:
                gather.complete(2 * group + 1)

    @pl.when(step == first_step)
    def _():
        hidden_rows(weights.at[0], True)
        gather_at(1, [first_step])
        weight_rows(weights.at[0], grad_ref.at[0])

    @pl.when(jnp.logical_and(step > first_step, step < last_step))
    def _():
        block = weights.at[step - first_step]
        hidden_rows(block, False)
        gather_at(1, range(first_step + 1, last_step))
        weight_rows(block, grad_ref.at[0])

    @pl.when(step == last_step)
    def _():
        hidden_rows(weights_zero, False, True)

    @pl.when(step == last_step)
    def _():
        for i in range(own_tiles):
            sent(h_two.at[pl.ds(0, ROWS)], pair_out.at[4 + i], pair_in.at[4 + i], at.sibling)
        for i in range(own_tiles):
            rows = pl.ds(i * ROWS, ROWS)
            for k in range(2):
                wait(sums_in.at[k, rows], 6 + 2 * i + k)
            full = resid[rows, :]
            scale = lax.rsqrt(jnp.mean(full * full, axis=1, keepdims=True) + EPSILON)
            normal = full * scale
            mlp_out = mlp_sum[own_rows(i), :] + sums_in[0, rows, :].astype(F32)
            output_ref[rows, :] = (row_mask(i) * (full + mlp_out)).astype(BF16)
            grad = grad_sum[own_rows(i), :] + sums_in[1, rows, :].astype(F32)
            total = low[own_rows(i), :].astype(F32) + norm_backward(grad, gain_two_ref[...], normal, scale)
            total_ref[rows, :] = total
            gain_grad_ref[...] += jnp.sum(grad * normal, axis=0, keepdims=True)
            h_two[own_rows(i), :] = total.astype(BF16)
            put(h_two.at[own_rows(i)], h_two.at[own_rows(i)], 10 + i)
            pltpu.make_async_copy(h_two.at[own_rows(i)], attn_ref.at[own_rows(i)], local_sems.at[i]).start()
        weight_rows(weights_zero, grad_zero_ref)
        gather.finish()
        for i in range(own_tiles):
            wait(h_two.at[other_rows(i)], 10 + i)
            pltpu.make_async_copy(
                h_two.at[other_rows(i)], attn_ref.at[other_rows(i)], local_sems.at[own_tiles + i]
            ).start()
        for slot, ref in enumerate(
            [tokens_ref, low.at[pl.ds(0, own)]] + [part_out.at[pl.ds(0, ROWS)]] * 8 + [h_two.at[pl.ds(0, ROWS)]] * 2
        ):
            if slot not in (4, 5):
                sent(ref, pair_out.at[slot], pair_in.at[slot], at.sibling)
        for i in range(tiles):
            rows = own_rows(i) if i < own_tiles else other_rows(i - own_tiles)
            pltpu.make_async_copy(h_two.at[rows], attn_ref.at[rows], local_sems.at[i]).wait()


def whole(shape):
    return pl.BlockSpec(shape, lambda i: (0,) * len(shape), pipeline_mode=pl.Buffered(1))


def layer(
    tokens, cotangent, lengths, gain_one, gain_two, gain_out, bias, start,
    w_query, w_key, w_value, w_gate, w_low_in, w_low_out, w_out, w_mlp,
):
    own, width = tokens.shape
    length = 2 * own
    keys, values, heads = w_query.shape[1], w_value.shape[1], start.shape[0]
    rank = w_low_in.shape[0]
    count = (w_mlp.shape[1] // 6 - 128) // 256 + 1
    group = 2 * w_mlp.shape[0]
    tiles = length // ROWS
    first_step = tiles + 1
    steps = first_step + count

    def rows_spec(columns):
        return pl.BlockSpec((ROWS, columns), lambda i: (jnp.minimum(i, tiles - 1), 0))

    vmem = pl.BlockSpec(memory_space=pltpu.VMEM)
    row_shapes = [
        (width, BF16), (keys, BF16), (keys, BF16), (values, BF16), (values, F32), (keys, F32), (rank, F32),
        (values, F32), (values, BF16),
    ]
    blocks = ROWS // BLOCK
    return pl.pallas_call(
        functools.partial(layer_kernel, count),
        grid=(steps,),
        in_specs=[
            ANY, ANY, pl.BlockSpec(memory_space=pltpu.SMEM), whole((1, width)), whole((1, width)), whole((1, VALUE_HEAD)),
            whole((1, keys)), whole(start.shape), whole(w_query.shape), whole(w_key.shape), whole(w_value.shape),
            whole(w_gate.shape), whole(w_low_in.shape), whole(w_low_out.shape), whole(w_out.shape),
            ANY,
        ],
        out_specs=[rows_spec(columns) for columns, _ in row_shapes]
        + [
            pl.BlockSpec((blocks, heads, KEY_HEAD, VALUE_HEAD), lambda i: (jnp.minimum(i, tiles - 1), 0, 0, 0)),
            whole((4, 4, group, 384)),
            pl.BlockSpec(
                (1, 4, 4, group, 768), lambda i: (jnp.clip(i - first_step, 0, count - 2), 0, 0, 0, 0)
            ),
            vmem, vmem, ANY, vmem,
        ],
        out_shape=[jax.ShapeDtypeStruct((length, columns), kind) for columns, kind in row_shapes]
        + [
            jax.ShapeDtypeStruct((length // BLOCK, heads, KEY_HEAD, VALUE_HEAD), BF16),
            jax.ShapeDtypeStruct((4, 4, group, 384), BF16),
            jax.ShapeDtypeStruct((count - 1, 4, 4, group, 768), BF16),
            jax.ShapeDtypeStruct((own, width), BF16),
            jax.ShapeDtypeStruct((own, width), F32),
            jax.ShapeDtypeStruct((length, width), BF16),
            jax.ShapeDtypeStruct((1, width), F32),
        ],
        scratch_shapes=[
            pltpu.VMEM((length, width), BF16),
            pltpu.VMEM((length, width), BF16),
            pltpu.VMEM((width, length), BF16),
            pltpu.VMEM((length, width), BF16),
            pltpu.VMEM((width, length), BF16),
            pltpu.VMEM((4, 4, group, 384), BF16),
            pltpu.VMEM((count - 1, 4, 4, group, 768), BF16),
            pltpu.VMEM((own, width), F32),
            pltpu.VMEM((own, width), BF16),
            pltpu.VMEM((own, width), BF16),
            pltpu.VMEM((length, width), F32),
            pltpu.VMEM((length, width), F32),
            pltpu.VMEM((length, 256), BF16),
            pltpu.VMEM((length, 512), BF16),
            pltpu.VMEM((2, own, width), BF16),
            pltpu.VMEM((2, own, width), BF16),
            pltpu.VMEM((heads, KEY_HEAD, VALUE_HEAD), F32),
            pltpu.SemaphoreType.DMA((tiles,)),
            pltpu.SemaphoreType.DMA((count,)),
            pltpu.SemaphoreType.DMA((count,)),
            pltpu.SemaphoreType.DMA((count,)),
            pltpu.SemaphoreType.DMA((2 * count - 1, 7)),
            pltpu.SemaphoreType.DMA((2 * count - 1, 7)),
            pltpu.SemaphoreType.DMA((12,)),
            pltpu.SemaphoreType.DMA((12,)),
        ],
        compiler_params=pltpu.CompilerParams(
            collective_id=0, has_side_effects=True, vmem_limit_bytes=63 << 20
        ),
        name="layer",
    )(
        tokens, cotangent, lengths, gain_one.reshape(1, -1), gain_two.reshape(1, -1), gain_out.reshape(1, -1),
        bias.reshape(1, -1), start, w_query, w_key, w_value, w_gate, w_low_in, w_low_out, w_out,
        w_mlp,
    )


class Reduce:
    def __init__(self, place, partial, via_x, via_y, from_x, from_y, from_z, chunks, out_sems, in_sems):
        self.place, self.partial, self.chunks = place, partial, chunks
        self.via_x, self.via_y, self.from_x, self.from_y, self.from_z = via_x, via_y, from_x, from_y, from_z
        self.out_sems, self.in_sems = out_sems, in_sems

    def put(self, source, target, chunk, slot, device):
        send(source, target, self.out_sems.at[chunk, slot], self.in_sems.at[chunk, slot], device)

    def wait(self, target, chunk, slot):
        arrived(target, self.out_sems.at[chunk, slot], self.in_sems.at[chunk, slot], self.place.sibling)

    def stage(self, number, chunk):
        at, partial, columns = self.place, self.partial, self.chunks[chunk]
        everything = slice(None)
        low, high = pl.ds(0, 2), pl.ds(2, 2)
        view = (everything, everything, columns)
        if number == 0:
            self.put(partial.at[low, at.flat_xy, everything, columns], self.via_x.at[view], chunk, 0, at.beside_x)
            self.put(partial.at[high, at.flat_xy, everything, columns], self.via_y.at[view], chunk, 1, at.beside_y)
        if number == 1:
            self.wait(self.via_x.at[view], chunk, 0)
            block = (low, at.flat_y, everything, columns)
            partial[block] = (partial[block].astype(F32) + self.via_x[view].astype(F32)).astype(BF16)
            self.put(
                partial.at[everything, at.flat_y, everything, columns], self.from_y.at[view], chunk, 2, at.beside_y
            )
            self.wait(self.via_y.at[view], chunk, 1)
            block = (high, at.flat_x, everything, columns)
            partial[block] = (partial[block].astype(F32) + self.via_y[view].astype(F32)).astype(BF16)
            self.put(
                partial.at[everything, at.flat_x, everything, columns], self.from_x.at[view], chunk, 3, at.beside_x
            )
        if number == 2:
            self.wait(self.from_y.at[view], chunk, 2)
            self.wait(self.from_x.at[view], chunk, 3)
            block = (everything, at.flat, everything, columns)
            partial[block] = (
                partial[block].astype(F32) + self.from_x[view].astype(F32) + self.from_y[view].astype(F32)
            ).astype(BF16)
            for i in range(3):
                self.put(
                    partial.at[(at.z + 1 + i) % 4, at.flat, everything, columns],
                    self.from_z.at[i, everything, columns],
                    chunk,
                    4 + i,
                    at.along_z[i],
                )

    def result(self, chunk):
        at, columns = self.place, self.chunks[chunk]
        total = self.partial[at.z, at.flat, :, columns].astype(F32)
        for i in range(3):
            self.wait(self.from_z.at[i, :, columns], chunk, 4 + i)
            total += self.from_z[i, :, columns].astype(F32)
        return total

    def finish(self):
        for chunk, columns in enumerate(self.chunks):
            pair, four, one = [self.partial.at[pl.ds(0, n), 0, :, columns] for n in (2, 4, 1)]
            for slot, ref in enumerate([pair] * 2 + [four] * 2 + [one] * 3):
                sent(ref, self.out_sems.at[chunk, slot], self.in_sems.at[chunk, slot], self.place.sibling)


GAIN_ONE, GAIN_TWO, GAIN_OUT, LOW_IN = 0, 8, 16, 24


def small_rows(width, rank, keys):
    decay = LOW_IN + rank * width // 128
    slot = -(-(rank + 1) * keys // 128 // 8) * 8
    return decay, slot, -(-(decay + 2 * slot) // 16) * 16


def backward_kernel(
    half, mlp_chunks, attn_chunks,
    zero_ref, groups_ref, attn_ref, h_ref, query_ref, key_ref, value_ref, gate_ref, logits_ref, low_rank_ref,
    attended_ref, mixed_ref, states_ref, w_query, w_key, w_value, w_gate, w_low_in, w_low_out, w_out,
    tokens_ref, total_ref, gain_one_ref, gain_out_ref, gain_two_grad_ref,
    mlp_out, attn_out, small_out, tokens_out,
    mlp, attn, mlp_via_x, mlp_via_y, mlp_from_x, mlp_from_y, mlp_from_z,
    attn_via_x, attn_via_y, attn_from_x, attn_from_y, attn_from_z, summed, swapped,
    small_own, small_in, small_z, h_turned, attn_turned, right, mixed_all, h_grad, h_grad_out, h_grad_in,
    memory_grad, gain_out_sum, low_in_sum, low_out_sum, bias_sum,
    load_sems, mlp_sems_out, mlp_sems_in, attn_sems_out, attn_sems_in, pair_out, pair_in, small_sems_out, small_sems_in,
):
    step = pl.program_id(0)
    at = Place()
    own = tokens_ref.shape[0]
    own_tiles = own // ROWS
    tiles = 2 * own_tiles
    keys, values = w_query.shape[1], w_value.shape[1]
    rank, width = w_low_out.shape[0], tokens_ref.shape[1]
    decay_at, decay_slot, _ = small_rows(width, rank, keys)
    last_step = 2 * tiles
    sides = [
        Reduce(at, mlp, mlp_via_x, mlp_via_y, mlp_from_x, mlp_from_y, mlp_from_z, mlp_chunks, mlp_sems_out, mlp_sems_in),
        Reduce(
            at, attn, attn_via_x, attn_via_y, attn_from_x, attn_from_y, attn_from_z, attn_chunks,
            attn_sems_out, attn_sems_in,
        ),
    ]
    order = [(0, i) for i in range(len(mlp_chunks))] + [(1, i) for i in range(len(attn_chunks))]
    count = len(order)
    rows = mlp.shape[2] // 2

    loads = list(range(0, len(mlp_chunks), 2))
    ticks = count + 6
    slots = [(i, j) for i in range(tiles) for j in range(2)] + [(tiles + i, 0) for i in range(tiles)]
    early = min(len(slots), len(mlp_chunks))
    plan = {slot: (i,) for i, slot in enumerate(slots[:early])}

    def load(chunk):
        if chunk == len(mlp_chunks) - 1:
            return pltpu.make_async_copy(zero_ref, mlp.at[:, :, :, mlp_chunks[chunk]], load_sems.at[chunk])
        columns = slice(mlp_chunks[chunk].start, mlp_chunks[chunk + 1].stop)
        return pltpu.make_async_copy(groups_ref.at[chunk // 2], mlp.at[:, :, :, columns], load_sems.at[chunk])

    def put(source, target, slot):
        send(source, target, pair_out.at[slot], pair_in.at[slot], at.sibling)

    def wait(target, slot):
        arrived(target, pair_out.at[slot], pair_in.at[slot], at.sibling)

    def small(number):
        def put_small(source, target, slot, device):
            send(source, target, small_sems_out.at[slot], small_sems_in.at[slot], device)

        def wait_small(target, slot):
            arrived(target, small_sems_out.at[slot], small_sems_in.at[slot], at.sibling)

        count = small_own.shape[0] // 2
        half = pl.ds(pl.multiple_of(at.head * count, 8), count)
        other = pl.ds(pl.multiple_of((1 - at.head) * count, 8), count)
        if number == 0:
            put_small(small_own, small_in.at[0], 0, at.sibling)
        elif number == 1:
            wait_small(small_in.at[0], 0)
            small_z[0, half] = small_own[half, :] + small_in[0, half]
            put_small(small_z.at[0, half], small_in.at[1, half], 1, at.beside_x)
        elif number == 2:
            wait_small(small_in.at[1, half], 1)
            small_z[1, half] = small_z[0, half] + small_in[1, half]
            put_small(small_z.at[1, half], small_in.at[2, half], 2, at.beside_y)
        elif number == 3:
            wait_small(small_in.at[2, half], 2)
            small_z[2 + at.z, half] = small_z[1, half] + small_in[2, half]
            for i in range(3):
                put_small(small_z.at[2 + at.z, half], small_z.at[2 + at.z, half], 3 + i, at.along_z[i])
        elif number == 4:
            for i in range(3):
                wait_small(small_z.at[2 + (at.z + 3 - i) % 4, half], 3 + i)
            small_z[6, half] = small_z[2, half] + small_z[3, half] + small_z[4, half] + small_z[5, half]
            put_small(small_z.at[6, half], small_z.at[6, half], 6, at.sibling)
        elif number == 5:
            wait_small(small_z.at[6, other], 6)
            small_out[...] = small_z[6]
            for slot in range(7):
                source = small_own if slot == 0 else small_z.at[0, half]
                sent(source, small_sems_out.at[slot], small_sems_in.at[slot], at.sibling)

    def result(side, chunk):
        total = sides[side].result(chunk)
        if side == 0:
            columns = mlp_chunks[chunk]
            summed[:, columns] = total
            put(
                summed.at[pl.ds(pl.multiple_of((1 - at.head) * rows, 8), rows), columns], swapped.at[:, columns],
                2 + chunk,
            )
        else:
            attn_out[:, attn_chunks[chunk]] = total

    def tick(number):
        for stage, lag in ((3, 6), (2, 4), (1, 2), (0, 0)):
            if 0 <= number - lag < count:
                side, chunk = order[number - lag]
                if stage == 3:
                    result(side, chunk)
                    continue
                if stage == 0 and side == 0 and chunk in loads:
                    load(chunk).wait()
                sides[side].stage(stage, chunk)

    def ticks_at(where, inside):
        for number in plan.get((where, inside), ()):
            tick(number)

    def own_rows(i):
        return pl.ds(pl.multiple_of(i * ROWS, ROWS), ROWS)

    @pl.when(step == 0)
    def _():
        for chunk in loads:
            load(chunk).start()
        memory_grad[...] = jnp.zeros_like(memory_grad)
        gain_out_sum[...] = jnp.zeros_like(gain_out_sum)
        low_in_sum[...] = jnp.zeros_like(low_in_sum)
        low_out_sum[...] = jnp.zeros_like(low_out_sum)
        bias_sum[...] = jnp.zeros_like(bias_sum)
        at.meet()

    for where in range(2 * tiles):

        @pl.when(step == where)
        def _():
            ticks_at(where, 0)

    @pl.when(step < tiles)
    def _():
        tile = tiles - 1 - step
        here = pl.ds(pl.multiple_of(tile * ROWS, ROWS), ROWS)
        attn_tile = attn_ref[...]
        h_tile = h_ref[...]
        attn_turned[:, here] = jnp.transpose(attn_tile)
        h_turned[:, here] = jnp.transpose(h_tile)
        mixed_all[here, :] = mixed_ref[...]
        mixed_grad = dot(attn_tile, w_out[...], 1, 1)
        logits_parts = []
        for i in range(ROWS // BLOCK - 1, -1, -1):
            block = slice(i * BLOCK, (i + 1) * BLOCK)
            grads, logits_grad, gain_grad = backward_block(
                mixed_grad[block], query_ref[block, :], key_ref[block, :], value_ref[block, :], logits_ref[block, :],
                gate_ref[block, :], attended_ref[block, :], states_ref[i], gain_out_ref[...], memory_grad,
            )
            right[pl.ds(pl.multiple_of(tile * ROWS + i * BLOCK, BLOCK), BLOCK), :] = grads
            gain_out_sum[...] += gain_grad
            logits_parts.append(logits_grad)
            if i == ROWS // BLOCK - 1:
                for where in range(tiles):

                    @pl.when(step == where)
                    def _():
                        ticks_at(where, 1)

        logits_grad = jnp.concatenate(logits_parts[::-1], axis=0)
        high, rest = split_low(logits_grad)
        rank_high, rank_rest = split_low(low_rank_ref[...])
        bias_sum[...] += jnp.sum(logits_grad, axis=0, keepdims=True)
        low_out_sum[...] += dot(rank_high, high, 0, 0) + dot(rank_rest, high, 0, 0) + dot(rank_high, rest, 0, 0)
        low_rank_low = (dot(high, w_low_out[...], 1, 1) + dot(rest, w_low_out[...], 1, 1)).astype(BF16)
        low_in_sum[...] += dot(low_rank_low, h_tile, 0, 0)
        grads = right[here, :]
        part = (
            dot(grads[:, :keys], w_query[...], 1, 1)
            + dot(grads[:, keys : 2 * keys], w_key[...], 1, 1)
            + dot(grads[:, 2 * keys : 2 * keys + values], w_value[...], 1, 1)
            + dot(grads[:, 2 * keys + values :], w_gate[...], 1, 1)
            + dot(low_rank_low, w_low_in[...])
        )
        place = tile % own_tiles
        mine = tile // own_tiles == at.head

        @pl.when(mine)
        def _():
            h_grad[own_rows(place), :] = part

        @pl.when(jnp.logical_not(mine))
        def _():
            h_grad_out[own_rows(place), :] = part.astype(BF16)
            put(h_grad_out.at[own_rows(place)], h_grad_in.at[own_rows(place)], place)

    @pl.when(step == tiles)
    def _():
        gain_one = jnp.zeros((1, width), F32)
        for i in range(own_tiles):
            here = own_rows(i)
            wait(h_grad_in.at[here], i)
            wide = tokens_ref[here, :].astype(F32)
            scale = lax.rsqrt(jnp.mean(wide * wide, axis=1, keepdims=True) + EPSILON)
            normal = wide * scale
            grad = h_grad[here, :] + h_grad_in[here, :].astype(F32)
            tokens_out[here, :] = total_ref[here, :] + norm_backward(grad, gain_one_ref[...], normal, scale)
            gain_one += jnp.sum(grad * normal, axis=0, keepdims=True)
        small_own[...] = jnp.zeros_like(small_own)
        for i in range(width // 128):
            columns = slice(i * 128, (i + 1) * 128)
            small_own[GAIN_ONE + i : GAIN_ONE + i + 1, :] = gain_one[:, columns]
            small_own[GAIN_TWO + i : GAIN_TWO + i + 1, :] = gain_two_grad_ref[:, columns]
            small_own[LOW_IN + i * rank : LOW_IN + (i + 1) * rank, :] = low_in_sum[:, columns]
        for i in range(VALUE_HEAD // 128):
            small_own[GAIN_OUT + i : GAIN_OUT + i + 1, :] = gain_out_sum[:, i * 128 : (i + 1) * 128]
        for head in range(2):

            @pl.when(at.head == head)
            def _():
                base = decay_at + head * decay_slot
                for i in range(keys // 128):
                    columns = slice(i * 128, (i + 1) * 128)
                    small_own[base + i * rank : base + (i + 1) * rank, :] = low_out_sum[:, columns]
                    bias_at = base + keys // 128 * rank + i
                    small_own[bias_at : bias_at + 1, :] = bias_sum[:, columns]

        small(0)

    @pl.when(jnp.logical_and(step >= tiles, step < 2 * tiles))
    def _():
        part = step - tiles
        here = pl.ds(pl.multiple_of(part * ROWS, ROWS), ROWS)
        shape = (attn.shape[1], attn.shape[2], -1)
        edge = right.shape[1]
        attn[part, :, :, :edge] = dot(h_turned[here, :], right[...]).astype(BF16).reshape(shape)
        attn[part, :, :, edge:] = dot(attn_turned[here, :], mixed_all[...]).astype(BF16).reshape(shape)

    def spread(source, head):
        offset, start = 0, 0
        for size in [2 * mlp_chunks[0].stop // 3] * (len(mlp_chunks) // 2) + [mlp_chunks[0].stop // 3]:
            for part in range(3):
                target = pl.ds(pl.multiple_of(part * 2 * half + head * half + offset, 128), size)
                mlp_out[:, target] = source[:, start : start + size]
                start += size
            offset += size

    @pl.when(step == last_step - 1)
    def _():
        small(1)

    @pl.when(step == last_step)
    def _():
        for number in range(early, ticks):
            tick(number)
            if number - early in SMALL_TICKS:
                small(2 + SMALL_TICKS.index(number - early))
            if number == len(mlp_chunks) + 7:
                spread(summed.at[pl.ds(pl.multiple_of(at.head * rows, 8), rows)], at.head)
                for chunk, columns in enumerate(mlp_chunks):
                    wait(swapped.at[:, columns], 2 + chunk)
                spread(swapped, 1 - at.head)
        for i in range(own_tiles):
            sent(h_grad_out.at[own_rows(i)], pair_out.at[i], pair_in.at[i], at.sibling)
        for chunk, columns in enumerate(mlp_chunks):
            sent(swapped.at[:, columns], pair_out.at[2 + chunk], pair_in.at[2 + chunk], at.sibling)
        for side in sides:
            side.finish()


def backward(
    zero, groups, attn_low, h_low, query, key, value, gate, logits, low_rank, attended, mixed, states,
    w_query, w_key, w_value, w_gate, w_low_in, w_low_out, w_out, tokens, total, gain_one, gain_out, gain_two_grad,
):
    length, width = h_low.shape
    keys, values, heads = query.shape[1], value.shape[1], states.shape[1]
    rank = w_low_out.shape[0]
    own = tokens.shape[0]
    tiles = length // ROWS
    rows = width // 16
    mlp_count = 2 * groups.shape[0] + 1
    mlp_width = zero.shape[-1] * mlp_count
    mlp_chunks = chunk_columns(mlp_width, [zero.shape[-1] // 128] * mlp_count)
    attn_width = 2 * keys + 3 * values
    attn_tiles = attn_width // 128
    sizes = [3] * ((attn_tiles - 4) // 3) + [(attn_tiles - 4) % 3 + 1, 2, 1]
    attn_chunks = chunk_columns(attn_width, sizes)
    attn_count = len(attn_chunks)
    small_shape = (small_rows(width, rank, keys)[2], 128)
    vmem = pl.BlockSpec(memory_space=pltpu.VMEM)

    def rows_spec(columns):
        return pl.BlockSpec((ROWS, columns), lambda i: (jnp.maximum(tiles - 1 - i, 0), 0))

    buffers = []
    for columns in (mlp_width, attn_width):
        buffers += [pltpu.VMEM((n, rows, columns), BF16) for n in (2, 2, 4, 4, 3)]
    streamed = [attn_low, h_low, query, key, value, gate, logits, low_rank, attended, mixed]
    constant = [
        w_query, w_key, w_value, w_gate, w_low_in, w_low_out, w_out, tokens, total,
        gain_one.reshape(1, -1), gain_out.reshape(1, -1), gain_two_grad.reshape(1, -1),
    ]
    return pl.pallas_call(
        functools.partial(backward_kernel, mlp_width // 3, mlp_chunks, attn_chunks),
        grid=(2 * tiles + 1,),
        in_specs=[ANY, ANY]
        + [rows_spec(a.shape[1]) for a in streamed]
        + [
            pl.BlockSpec(
                (ROWS // BLOCK, heads, KEY_HEAD, VALUE_HEAD), lambda i: (jnp.maximum(tiles - 1 - i, 0), 0, 0, 0)
            )
        ]
        + [whole(a.shape) for a in constant],
        out_specs=[vmem, vmem, vmem, vmem],
        out_shape=[
            jax.ShapeDtypeStruct((rows // 2, 2 * mlp_width), F32),
            jax.ShapeDtypeStruct((rows, attn_width), F32),
            jax.ShapeDtypeStruct(small_shape, F32),
            jax.ShapeDtypeStruct((own, width), F32),
        ],
        scratch_shapes=[
            pltpu.VMEM((4, 4, rows, mlp_width), BF16),
            pltpu.VMEM((4, 4, rows, attn_width), BF16),
            *buffers,
            pltpu.VMEM((rows, mlp_width), F32),
            pltpu.VMEM((rows // 2, mlp_width), F32),
            pltpu.VMEM(small_shape, F32),
            pltpu.VMEM((3,) + small_shape, F32),
            pltpu.VMEM((7,) + small_shape, F32),
            pltpu.VMEM((width, length), BF16),
            pltpu.VMEM((width, length), BF16),
            pltpu.VMEM((length, 2 * keys + 2 * values), BF16),
            pltpu.VMEM((length, values), BF16),
            pltpu.VMEM((own, width), F32),
            pltpu.VMEM((own, width), BF16),
            pltpu.VMEM((own, width), BF16),
            pltpu.VMEM((heads, KEY_HEAD, VALUE_HEAD), F32),
            pltpu.VMEM((1, VALUE_HEAD), F32),
            pltpu.VMEM((rank, width), F32),
            pltpu.VMEM((rank, keys), F32),
            pltpu.VMEM((1, keys), F32),
            pltpu.SemaphoreType.DMA((mlp_count,)),
            pltpu.SemaphoreType.DMA((mlp_count, 7)),
            pltpu.SemaphoreType.DMA((mlp_count, 7)),
            pltpu.SemaphoreType.DMA((attn_count, 7)),
            pltpu.SemaphoreType.DMA((attn_count, 7)),
            pltpu.SemaphoreType.DMA((2 + mlp_count,)),
            pltpu.SemaphoreType.DMA((2 + mlp_count,)),
            pltpu.SemaphoreType.DMA((7,)),
            pltpu.SemaphoreType.DMA((7,)),
        ],
        compiler_params=pltpu.CompilerParams(
            collective_id=1, has_side_effects=True, vmem_limit_bytes=63 << 20
        ),
        name="backward",
    )(zero, groups, *streamed, states, *constant)


def emit_kernel(
    half, edges, mlp_ref, attn_ref, small_ref, tokens_ref, output_ref,
    output_out, tokens_out, gain_one_out, query_out, key_out, value_out, gate_out, low_in_out, low_out_out, bias_out,
    gain_out_out, out_out, gain_two_out, mlp_out, tokens, output, mlp, attn, load_sems, sems,
):
    staged = [(attn_ref, attn), (mlp_ref, mlp), (output_ref, output), (tokens_ref, tokens)]
    loads = [pltpu.make_async_copy(source, target, load_sems.at[i]) for i, (source, target) in enumerate(staged)]
    for load in loads:
        load.start()
    moves = []
    for i, target in enumerate((query_out, key_out, value_out, gate_out, out_out)):
        moves.append((attn.at[:, edges[i] : edges[i + 1]], target))
    moves += [(mlp, mlp_out), (output, output_out), (tokens, tokens_out)]
    copies = [pltpu.make_async_copy(source, target, sems.at[i]) for i, (source, target) in enumerate(moves)]
    for i, load in enumerate(loads):
        load.wait()
        for copy in copies[:5] if i == 0 else copies[4 + i : 5 + i]:
            copy.start()
    rank, width = low_in_out.shape
    keys = low_out_out.shape[1]
    decay_at, decay_slot, _ = small_rows(width, rank, keys)
    for i in range(width // 128):
        columns = slice(i * 128, (i + 1) * 128)
        gain_one_out[:, columns] = small_ref[GAIN_ONE + i : GAIN_ONE + i + 1, :]
        gain_two_out[:, columns] = small_ref[GAIN_TWO + i : GAIN_TWO + i + 1, :]
        low_in_out[:, columns] = small_ref[LOW_IN + i * rank : LOW_IN + (i + 1) * rank, :]
    for i in range(VALUE_HEAD // 128):
        gain_out_out[:, i * 128 : (i + 1) * 128] = small_ref[GAIN_OUT + i : GAIN_OUT + i + 1, :]
    for head in range(2):

        @pl.when(lax.axis_index("head") == head)
        def _():
            base = decay_at + head * decay_slot
            for i in range(keys // 128):
                columns = slice(i * 128, (i + 1) * 128)
                low_out_out[:, columns] = small_ref[base + i * rank : base + (i + 1) * rank, :]
                bias_at = base + keys // 128 * rank + i
                bias_out[:, columns] = small_ref[bias_at : bias_at + 1, :]

    for copy in copies:
        copy.wait()


def emit(mlp, attn, small, tokens, output, keys, values, rank):
    rows, width = attn.shape[0], tokens.shape[1]
    edges = [0, keys, 2 * keys, 2 * keys + values, 2 * keys + 2 * values, 2 * keys + 3 * values]
    vmem = pl.BlockSpec(memory_space=pltpu.VMEM)
    shapes = [
        (output.shape, BF16, ANY), (tokens.shape, F32, ANY), ((1, width), F32, vmem), ((rows, keys), F32, ANY),
        ((rows, keys), F32, ANY), ((rows, values), F32, ANY), ((rows, values), F32, ANY), ((rank, width), F32, vmem),
        ((rank, keys), F32, vmem), ((1, keys), F32, vmem), ((1, VALUE_HEAD), F32, vmem), ((rows, values), F32, ANY),
        ((1, width), F32, vmem), (mlp.shape, F32, ANY),
    ]
    return pl.pallas_call(
        functools.partial(emit_kernel, mlp.shape[1] // 6, edges),
        in_specs=[ANY, ANY, vmem, ANY, ANY],
        out_specs=[space for _, _, space in shapes],
        out_shape=[jax.ShapeDtypeStruct(shape, kind) for shape, kind, _ in shapes],
        scratch_shapes=[
            pltpu.VMEM(tokens.shape, F32),
            pltpu.VMEM(output.shape, BF16),
            pltpu.VMEM(mlp.shape, F32),
            pltpu.VMEM(attn.shape, F32),
            pltpu.SemaphoreType.DMA((4,)),
            pltpu.SemaphoreType.DMA((8,)),
        ],
        compiler_params=pltpu.CompilerParams(vmem_limit_bytes=60 << 20),
        name="emit",
    )(mlp, attn, small, tokens, output)


def swap(value):
    return lax.ppermute(value, "head", [(0, 1), (1, 0)])


def ordered(own, other, axis):
    size = own.shape[axis]
    joined = jnp.concatenate([own, other, own], axis=axis)
    return lax.dynamic_slice_in_dim(joined, lax.axis_index("head") * size, 2 * size, axis)


def half_of(value, which, axis):
    size = value.shape[axis] // 2
    return lax.dynamic_slice_in_dim(value, which * size, size, axis)


def sum_rows(partial, here):
    other = swap(half_of(partial, 1 - here, 0).astype(BF16))
    return half_of(partial, here, 0) + other.astype(F32)


def norm_backward(grad_in, gain, normed_in, scale_in):
    scaled = grad_in * gain
    return scale_in * (scaled - normed_in * jnp.mean(scaled * normed_in, axis=-1, keepdims=True))


def per_device(
    tokens, lengths, initial_memory, norm_attn_gain, w_query, w_key, w_value, w_gate_out, w_low_in, w_low_out,
    decay_bias, out_gain, w_out, norm_mlp_gain, w_mlp, cotangent,
):
    here = lax.axis_index("head")
    own_rows = tokens.shape[1]
    keys = w_query.shape[1]
    values = w_value.shape[1]
    hidden = w_mlp.shape[1] // 3
    half = hidden // 2
    shard_rows = w_mlp.shape[0]
    square = lax.axis_size("dp") == 16

    tokens_own = tokens[0]
    if square:
        (
            h_low, query, key, value, gate, logits, low_rank, attended, mixed, states,
            grad_zero, grad_mlp, output, resid_total, attn_low, gain_two_grad,
        ) = layer(
            tokens_own, cotangent[0], lengths, norm_attn_gain, norm_mlp_gain, out_gain, decay_bias,
            initial_memory[0], w_query, w_key, w_value, w_gate_out, w_low_in.T, w_low_out, w_out, w_mlp,
        )
        grad_mlp, attn_grads, packed, tokens_grad = backward(
            grad_zero, grad_mlp, attn_low, h_low, query, key, value, gate, logits, low_rank, attended, mixed, states,
            w_query, w_key, w_value, w_gate_out, w_low_in.T, w_low_out, w_out, tokens_own, resid_total,
            norm_attn_gain, out_gain, gain_two_grad,
        )
        results = emit(grad_mlp, attn_grads, packed, tokens_grad, output, keys, values, w_low_out.shape[0])
        (
            output, tokens_grad, gain_one_grad, query_grad, key_grad, value_grad, gate_grad, low_in_grad, low_out_grad,
            bias_grad, out_gain_grad, out_grad, gain_two_grad, grad_mlp,
        ) = results
        return (
            output[None], tokens_grad[None], gain_one_grad[0], query_grad, key_grad, value_grad, gate_grad,
            low_in_grad.T, low_out_grad, bias_grad[0], out_gain_grad[0], out_grad.T, gain_two_grad[0], grad_mlp,
        )
    pieces = w_mlp.reshape(shard_rows, 3, 2, half)
    own_piece = lax.dynamic_index_in_dim(pieces, here, 2, keepdims=False)
    other_piece = lax.dynamic_index_in_dim(pieces, 1 - here, 2, keepdims=False)
    positions = here * own_rows + lax.iota(jnp.int32, own_rows)
    row_mask = (positions < lengths[0]).astype(F32)[:, None]
    resid_grad = row_mask * cotangent[0].astype(F32)
    low_own = resid_grad.astype(BF16)
    pair = swap(other_piece.reshape(shard_rows, 3 * half))
    weights = lax.all_gather(
        ordered(own_piece.reshape(shard_rows, 3 * half), pair, 0), "dp", axis=0, tiled=True
    )
    tokens_wide = ordered(tokens_own, swap(tokens_own), 0).astype(F32)
    length = tokens_wide.shape[0]
    scale_one = lax.rsqrt(jnp.mean(tokens_wide * tokens_wide, axis=1, keepdims=True) + EPSILON)
    h_low = (tokens_wide * scale_one * norm_attn_gain).astype(BF16)
    query = dot(h_low, w_query).astype(BF16)
    key = dot(h_low, w_key).astype(BF16)
    value = dot(h_low, w_value).astype(BF16)
    gate = dot(h_low, w_gate_out)
    low_rank = dot(h_low, w_low_in)
    low_high, low_rest = split_low(low_rank)
    logits = dot(low_high, w_low_out) + dot(low_rest, w_low_out) + decay_bias
    attended, mixed, states = attention_forward(query, key, value, logits, gate, out_gain, initial_memory[0])
    resid = tokens_own.astype(F32) + sum_rows(dot(mixed, w_out), here)
    scale_two = lax.rsqrt(jnp.mean(resid * resid, axis=1, keepdims=True) + EPSILON)
    normal_two = resid * scale_two
    h_two_own = (normal_two * norm_mlp_gain).astype(BF16)
    h_two = ordered(h_two_own, swap(h_two_own), 0)
    resid_low = ordered(low_own, swap(low_own), 0)
    pre_gate = dot(h_two, weights[:, :half])
    up_part = dot(h_two, weights[:, half : 2 * half])
    pre_sigmoid = sigmoid(pre_gate)
    inner = (pre_gate * pre_sigmoid * up_part).astype(BF16)
    inner_grad = dot(resid_low, weights[:, 2 * half :])
    pre_grad = (
        inner_grad * up_part * pre_sigmoid * (1.0 + pre_gate * (1.0 - pre_sigmoid))
    ).astype(BF16)
    up_grad = (inner_grad * pre_gate * pre_sigmoid).astype(BF16)
    mlp_out = sum_rows(dot(inner, weights[:, 2 * half :], 1, 1), here)
    output = (row_mask * (resid + mlp_out)).astype(BF16)[None]
    h_two_grad = sum_rows(
        dot(pre_grad, weights[:, :half], 1, 1) + dot(up_grad, weights[:, half : 2 * half], 1, 1), here
    )
    grad_mlp = jnp.concatenate(
        [
            dot(h_two, pre_grad, 0, 0).astype(BF16),
            dot(h_two, up_grad, 0, 0).astype(BF16),
            dot(resid_low, inner, 0, 0).astype(BF16),
        ],
        axis=1,
    )
    resid_total = resid_grad + norm_backward(h_two_grad, norm_mlp_gain, normal_two, scale_two)
    gain_two_grad = jnp.sum(h_two_grad * normal_two, axis=0)
    attn_own = resid_total.astype(BF16)
    attn_low = ordered(attn_own, swap(attn_own), 0)

    mixed_grad = dot(attn_low, w_out, 1, 1)
    out_grad = dot(attn_low, mixed, 0, 0)
    query_grad, key_grad, value_grad, gate_grad, logits_grad, out_gain_grad = attention_backward(
        mixed_grad, query, key, value, logits, gate, attended, states, out_gain
    )
    bias_grad = jnp.sum(logits_grad, axis=0)
    grad_high, grad_rest = split_low(logits_grad)
    low_out_grad = (
        dot(low_high, grad_high, 0, 0) + dot(low_rest, grad_high, 0, 0) + dot(low_high, grad_rest, 0, 0)
    )
    low_rank_low = (dot(grad_high, w_low_out, 1, 1) + dot(grad_rest, w_low_out, 1, 1)).astype(BF16)
    low_in_grad = dot(h_low, low_rank_low, 0, 0)
    attn_grads = jnp.concatenate(
        [
            dot(h_low, query_grad, 0, 0).astype(BF16),
            dot(h_low, key_grad, 0, 0).astype(BF16),
            dot(h_low, value_grad, 0, 0).astype(BF16),
            dot(h_low, gate_grad, 0, 0).astype(BF16),
            out_grad.astype(BF16),
        ],
        axis=1,
    )
    h_grad = sum_rows(
        dot(query_grad, w_query, 1, 1)
        + dot(key_grad, w_key, 1, 1)
        + dot(value_grad, w_value, 1, 1)
        + dot(gate_grad, w_gate_out, 1, 1)
        + dot(low_rank_low, w_low_in, 1, 1),
        here,
    )
    own_wide = tokens_own.astype(F32)
    own_scale = lax.rsqrt(jnp.mean(own_wide * own_wide, axis=1, keepdims=True) + EPSILON)
    normal_own = own_wide * own_scale
    tokens_grad = resid_total + norm_backward(h_grad, norm_attn_gain, normal_own, own_scale)
    gain_one_grad = jnp.sum(h_grad * normal_own, axis=0)
    low_rank_width = w_low_out.shape[0]
    decay_part = jnp.concatenate([low_out_grad, bias_grad[None]], axis=0)
    slots = jnp.zeros((2,) + decay_part.shape, F32)
    slots = lax.dynamic_update_slice(slots, decay_part[None], (here, 0, 0))
    packed = jnp.concatenate(
        [
            gain_one_grad, gain_two_grad, out_gain_grad.reshape(-1), low_in_grad.reshape(-1), slots.reshape(-1),
        ]
    )
    packed = lax.psum(packed, ("dp", "head"))
    attn_grads = lax.psum_scatter(attn_grads, "dp", scatter_dimension=0, tiled=True).astype(F32)
    grad_mlp = lax.psum_scatter(grad_mlp, "dp", scatter_dimension=0, tiled=True)
    own_half = half_of(grad_mlp, here, 0)
    other_half = swap(half_of(grad_mlp, 1 - here, 0))
    grad_mlp = ordered(
        own_half.reshape(shard_rows, 3, 1, half), other_half.reshape(shard_rows, 3, 1, half), 2
    ).reshape(shard_rows, 3 * hidden).astype(F32)
    width = gain_one_grad.shape[0]
    edges = [width, 2 * width, 2 * width + VALUE_HEAD]
    edges.append(edges[-1] + width * low_rank_width)
    low_in_grad = packed[edges[2] : edges[3]].reshape(width, low_rank_width)
    decay_part = lax.dynamic_index_in_dim(packed[edges[3] :].reshape(slots.shape), here, 0, keepdims=False)
    low_out_grad, bias_grad = decay_part[:low_rank_width], decay_part[low_rank_width]
    gain_one_grad, gain_two_grad = packed[: edges[0]], packed[edges[0] : edges[1]]
    out_gain_grad = packed[edges[1] : edges[2]]
    return (
        output,
        tokens_grad[None],
        gain_one_grad,
        attn_grads[:, :keys],
        attn_grads[:, keys : 2 * keys],
        attn_grads[:, 2 * keys : 2 * keys + values],
        attn_grads[:, 2 * keys + values : 2 * keys + 2 * values],
        low_in_grad,
        low_out_grad,
        bias_grad,
        out_gain_grad,
        attn_grads[:, 2 * keys + 2 * values :].T,
        gain_two_grad,
        grad_mlp,
    )


def solution(mesh):
    return jax.shard_map(
        per_device,
        mesh=mesh,
        in_specs=(
            P("dp", "head", None),
            P("dp"),
            P("dp", "head", None, None),
            P(),
            P(None, "head"),
            P(None, "head"),
            P(None, "head"),
            P(None, "head"),
            P(),
            P(None, "head"),
            P("head"),
            P(),
            P("head", None),
            P(),
            P(("dp", "head"), None),
            P("dp", "head", None),
        ),
        out_specs=(
            P("dp", "head", None),
            P("dp", "head", None),
            P(),
            P("dp", "head"),
            P("dp", "head"),
            P("dp", "head"),
            P("dp", "head"),
            P(),
            P(None, "head"),
            P("head"),
            P(),
            P("head", "dp"),
            P(),
            P(("dp", "head"), None),
        ),
        check_vma=False,
    )
```

```python
import functools

import jax
import jax.numpy as jnp
from jax import lax
from jax.experimental import pallas as pl
from jax.experimental.pallas import tpu as pltpu
from jax.sharding import PartitionSpec as P

HEADS = 4
KEY = 512
VALUE = 1024
BLOCK = 128
KEY_HEAD = KEY // HEADS
VALUE_HEAD = VALUE // HEADS

EPSILON = 1e-05
F32 = jnp.float32
BF16 = jnp.bfloat16
SCALE = KEY_HEAD ** (-0.5)


def dot(left, right, left_dim=1, right_dim=0):
    return lax.dot_general(
        left, right, (((left_dim,), (right_dim,)), ((), ())), preferred_element_type=F32
    )


def split_low(value):
    high = value.astype(BF16)
    return high, (value - high.astype(F32)).astype(BF16)


def sigmoid(value):
    return 1.0 / (1.0 + jnp.exp(-value))


def log_sigmoid(value):
    return jnp.minimum(value, 0.0) - jnp.log1p(jnp.exp(-jnp.abs(value)))


def triangle(lower):
    rows = lax.broadcasted_iota(jnp.int32, (BLOCK, BLOCK), 0)
    columns = lax.broadcasted_iota(jnp.int32, (BLOCK, BLOCK), 1)
    return rows >= columns if lower else rows <= columns


def decay_terms(logits):
    log_decay = log_sigmoid(logits) * (1.0 / 16.0)
    ones = jnp.where(triangle(True), 1.0, 0.0).astype(BF16)
    high, low = split_low(log_decay)
    total = dot(ones, high) + dot(ones, low)
    middle = total[BLOCK // 2 - 1 : BLOCK // 2, :]
    end = total[BLOCK - 1 :, :]
    rise = jnp.exp(total - middle)
    fall = jnp.exp(middle - total)
    early = rise * (jnp.exp(middle) * SCALE)
    late = fall * jnp.exp(end - middle)
    return rise * SCALE, fall, early, late, jnp.exp(end)


def as_column(row, width):
    column = jnp.transpose(jnp.broadcast_to(row, (KEY_HEAD, KEY_HEAD)))
    return jnp.concatenate([column] * (width // KEY_HEAD), axis=1)


def forward_block(query, key, value, logits, gate, gain, memory, states):
    rise, fall, early, late, decay = decay_terms(logits)
    lower = triangle(True)
    attended_parts = []
    mixed_parts = []
    for head in range(memory.shape[0]):
        keys_at = slice(head * KEY_HEAD, (head + 1) * KEY_HEAD)
        values_at = slice(head * VALUE_HEAD, (head + 1) * VALUE_HEAD)
        query_wide = query[:, keys_at].astype(F32)
        key_wide = key[:, keys_at].astype(F32)
        value_head = value[:, values_at]
        state = memory[head]
        state_low = state.astype(BF16)
        states[head] = state_low
        scores = dot(
            (query_wide * rise[:, keys_at]).astype(BF16), (key_wide * fall[:, keys_at]).astype(BF16), 1, 1
        )
        scores = jnp.where(lower, scores, 0.0).astype(BF16)
        left = jnp.concatenate([scores, (query_wide * early[:, keys_at]).astype(BF16)], axis=1)
        attended = dot(left, jnp.concatenate([value_head, state_low], axis=0))
        memory[head] = as_column(decay[:, keys_at], VALUE_HEAD) * state + dot(
            (key_wide * late[:, keys_at]).astype(BF16), value_head, 0, 0
        )
        scale = lax.rsqrt(jnp.mean(attended * attended, axis=1, keepdims=True) + EPSILON)
        gate_head = gate[:, values_at]
        attended_parts.append(attended)
        mixed_parts.append((attended * scale * gain * gate_head * sigmoid(gate_head)).astype(BF16))
    return jnp.concatenate(attended_parts, axis=1), jnp.concatenate(mixed_parts, axis=1)


def forward_kernel(
    query_ref, key_ref, value_ref, logits_ref, gate_ref, gain_ref, start_ref,
    attended_ref, mixed_ref, states_ref, memory
):
    @pl.when(pl.program_id(0) == 0)
    def _():
        memory[...] = start_ref[...]

    attended_ref[...], mixed_ref[...] = forward_block(
        query_ref[...], key_ref[...], value_ref[...], logits_ref[...], gate_ref[...], gain_ref[...],
        memory, states_ref.at[0],
    )


def attention_forward(query, key, value, logits, gate, gain, start):
    length, keys = query.shape
    values = value.shape[1]
    heads = start.shape[0]
    steps = length // BLOCK

    def rows(width):
        return pl.BlockSpec((BLOCK, width), lambda i: (i, 0))

    return pl.pallas_call(
        forward_kernel,
        grid=(steps,),
        in_specs=[
            rows(keys), rows(keys), rows(values), rows(keys), rows(values),
            pl.BlockSpec((1, VALUE_HEAD), lambda i: (0, 0)),
            pl.BlockSpec((heads, KEY_HEAD, VALUE_HEAD), lambda i: (0, 0, 0)),
        ],
        out_specs=[
            rows(values), rows(values),
            pl.BlockSpec((1, heads, KEY_HEAD, VALUE_HEAD), lambda i: (i, 0, 0, 0)),
        ],
        out_shape=[
            jax.ShapeDtypeStruct((length, values), F32),
            jax.ShapeDtypeStruct((length, values), BF16),
            jax.ShapeDtypeStruct((steps, heads, KEY_HEAD, VALUE_HEAD), BF16),
        ],
        scratch_shapes=[pltpu.VMEM((heads, KEY_HEAD, VALUE_HEAD), F32)],
        compiler_params=pltpu.CompilerParams(vmem_limit_bytes=48 << 20),
        name="attention_forward",
    )(query, key, value, logits, gate, gain.reshape(1, -1), start)


def backward_block(mixed_grad, query, key, value, logits, gate, attended, states, gain, memory_grad):
    rise, fall, early, late, decay = decay_terms(logits)
    lower = triangle(True)
    upper = triangle(False)
    last = lax.broadcasted_iota(jnp.int32, (BLOCK, KEY_HEAD), 0) == BLOCK - 1
    query_grads, key_grads, value_grads, gate_grads, total_grads = [], [], [], [], []
    gain_grad = jnp.zeros((1, VALUE_HEAD), F32)
    for head in range(memory_grad.shape[0]):
        keys_at = slice(head * KEY_HEAD, (head + 1) * KEY_HEAD)
        values_at = slice(head * VALUE_HEAD, (head + 1) * VALUE_HEAD)
        attended_head = attended[:, values_at]
        scale = lax.rsqrt(jnp.mean(attended_head * attended_head, axis=1, keepdims=True) + EPSILON)
        normal = attended_head * scale
        gate_head = gate[:, values_at]
        gate_sigmoid = sigmoid(gate_head)
        mixed_head = mixed_grad[:, values_at]
        gate_grads.append(
            (mixed_head * normal * gain * gate_sigmoid * (1.0 + gate_head * (1.0 - gate_sigmoid))).astype(BF16)
        )
        normed_grad = mixed_head * gate_head * gate_sigmoid
        gain_grad += jnp.sum(normed_grad * normal, axis=0, keepdims=True)
        scaled = normed_grad * gain
        attended_grad = (
            scale * (scaled - normal * jnp.mean(scaled * normal, axis=1, keepdims=True))
        ).astype(BF16)

        query_wide = query[:, keys_at].astype(F32)
        key_wide = key[:, keys_at].astype(F32)
        value_head = value[:, values_at]
        query_middle = query_wide * rise[:, keys_at]
        key_middle = key_wide * fall[:, keys_at]
        query_early = query_wide * early[:, keys_at]
        key_late = key_wide * late[:, keys_at]
        query_middle_low = query_middle.astype(BF16)
        key_middle_low = key_middle.astype(BF16)
        state = states[head]
        after = memory_grad[head]

        scores_turned = jnp.where(upper, dot(key_middle_low, query_middle_low, 1, 1), 0.0).astype(BF16)
        from_values = dot(attended_grad, jnp.concatenate([value_head, state], axis=0), 1, 1)
        to_values = jnp.concatenate([attended_grad, after.astype(BF16)], axis=0)
        from_grads = dot(value_head, to_values, 1, 1)
        scores_grad = jnp.where(lower, from_values[:, :BLOCK], 0.0).astype(BF16)
        scores_grad_turned = jnp.where(upper, from_grads[:, :BLOCK], 0.0).astype(BF16)
        query_early_grad = from_values[:, BLOCK:]
        key_late_grad = from_grads[:, BLOCK:]
        query_middle_grad = dot(scores_grad, key_middle_low)
        key_middle_grad = dot(scores_grad_turned, query_middle_low)
        value_grads.append(
            dot(jnp.concatenate([scores_turned, key_late.astype(BF16)], axis=1), to_values).astype(BF16)
        )
        carried = as_column(decay[:, keys_at], VALUE_HEAD) * after
        memory_grad[head] = carried + dot(query_early.astype(BF16), attended_grad, 0, 0)
        query_grads.append(
            (query_early_grad * early[:, keys_at] + query_middle_grad * rise[:, keys_at]).astype(BF16)
        )
        key_grads.append((key_middle_grad * fall[:, keys_at] + key_late_grad * late[:, keys_at]).astype(BF16))
        late_part = key_late_grad * key_late
        end_high, end_low = split_low(carried * state.astype(F32))
        ones = jnp.ones((8, VALUE_HEAD), BF16)
        end_grad = (dot(ones, end_high, 1, 1) + dot(ones, end_low, 1, 1))[:1] + jnp.sum(
            late_part, axis=0, keepdims=True
        )
        total_grads.append(
            query_early_grad * query_early
            + query_middle_grad * query_middle
            - key_middle_grad * key_middle
            - late_part
            + jnp.where(last, end_grad, 0.0)
        )
    ones = jnp.where(upper, 1.0, 0.0).astype(BF16)
    high, rest = split_low(jnp.concatenate(total_grads, axis=1))
    logits_grad = (dot(ones, high) + dot(ones, rest)) * sigmoid(-logits) * (1.0 / 16.0)
    grads = query_grads + key_grads + value_grads + gate_grads
    return jnp.concatenate(grads, axis=1), logits_grad, gain_grad


def backward_kernel_plain(
    mixed_grad_ref, query_ref, key_ref, value_ref, logits_ref, gate_ref, attended_ref, states_ref, gain_ref,
    query_grad_ref, key_grad_ref, value_grad_ref, gate_grad_ref, logits_grad_ref, gain_grad_ref, memory_grad
):
    @pl.when(pl.program_id(0) == 0)
    def _():
        memory_grad[...] = jnp.zeros_like(memory_grad)
        gain_grad_ref[...] = jnp.zeros_like(gain_grad_ref)

    grads, logits_grad, gain_grad = backward_block(
        mixed_grad_ref[...], query_ref[...], key_ref[...], value_ref[...], logits_ref[...], gate_ref[...],
        attended_ref[...], states_ref[0], gain_ref[...], memory_grad,
    )
    start = 0
    for ref in (query_grad_ref, key_grad_ref, value_grad_ref, gate_grad_ref):
        ref[...] = grads[:, start : start + ref.shape[1]]
        start += ref.shape[1]
    logits_grad_ref[...] = logits_grad
    gain_grad_ref[...] += gain_grad


def attention_backward(mixed_grad, query, key, value, logits, gate, attended, states, gain):
    length, keys = query.shape
    values = value.shape[1]
    heads = states.shape[1]
    steps = length // BLOCK

    def rows(width):
        return pl.BlockSpec((BLOCK, width), lambda i: (steps - 1 - i, 0))

    return pl.pallas_call(
        backward_kernel_plain,
        grid=(steps,),
        in_specs=[
            rows(values), rows(keys), rows(keys), rows(values), rows(keys), rows(values), rows(values),
            pl.BlockSpec((1, heads, KEY_HEAD, VALUE_HEAD), lambda i: (steps - 1 - i, 0, 0, 0)),
            pl.BlockSpec((1, VALUE_HEAD), lambda i: (0, 0)),
        ],
        out_specs=[
            rows(keys), rows(keys), rows(values), rows(values), rows(keys),
            pl.BlockSpec((1, VALUE_HEAD), lambda i: (0, 0)),
        ],
        out_shape=[
            jax.ShapeDtypeStruct((length, keys), BF16),
            jax.ShapeDtypeStruct((length, keys), BF16),
            jax.ShapeDtypeStruct((length, values), BF16),
            jax.ShapeDtypeStruct((length, values), BF16),
            jax.ShapeDtypeStruct((length, keys), F32),
            jax.ShapeDtypeStruct((1, VALUE_HEAD), F32),
        ],
        scratch_shapes=[pltpu.VMEM((heads, KEY_HEAD, VALUE_HEAD), F32)],
        compiler_params=pltpu.CompilerParams(vmem_limit_bytes=48 << 20),
        name="attention_backward",
    )(mixed_grad, query, key, value, logits, gate, attended, states, gain.reshape(1, -1))


MESH = pl.DeviceIdType.MESH
ANY = pl.BlockSpec(memory_space=pl.ANY)


class Place:
    def __init__(self):
        self.dp = lax.axis_index("dp")
        self.head = lax.axis_index("head")
        self.z = self.dp // 4
        self.flat = self.dp % 4
        self.flat_x = self.flat + 1 - 2 * (self.flat % 2)
        self.flat_y = self.flat + 2 - 4 * (self.flat // 2)
        self.flat_xy = 3 - self.flat
        self.sibling = (self.dp, 1 - self.head)
        self.beside_x = (self.z * 4 + self.flat_x, self.head)
        self.beside_y = (self.z * 4 + self.flat_y, self.head)
        self.along_z = [(((self.z + i) % 4) * 4 + self.flat, self.head) for i in range(1, 4)]

    def meet(self):
        barrier = pltpu.get_barrier_semaphore()
        others = [self.sibling, self.beside_x, self.beside_y] + self.along_z
        for other in others:
            pl.semaphore_signal(barrier, 1, device_id=other, device_id_type=MESH)
        pl.semaphore_wait(barrier, len(others))


def send(source, target, out_sem, in_sem, device):
    copy = pltpu.make_async_remote_copy(
        src_ref=source, dst_ref=target, send_sem=out_sem, recv_sem=in_sem, device_id=device, device_id_type=MESH
    )
    copy.start()
    return copy


def arrived(target, out_sem, in_sem, device):
    pltpu.make_async_remote_copy(
        src_ref=target, dst_ref=target, send_sem=out_sem, recv_sem=in_sem, device_id=device, device_id_type=MESH
    ).wait_recv()


def chunk_columns(width, sizes):
    starts = [sum(sizes[:i]) * 128 for i in range(len(sizes))]
    assert sum(sizes) * 128 == width
    return [slice(start, start + size * 128) for start, size in zip(starts, sizes)]


ROWS = 256
SMALL_TICKS = (0, 2, 5, 8)


class Gather:
    LAGS = (0, 1, 3)

    def __init__(self, place, source, targets, blocks, local_sems, swap_out, swap_in, out_sems, in_sems):
        self.place, self.source, self.targets, self.blocks = place, source, targets, blocks
        self.local_sems, self.swap_out, self.swap_in = local_sems, swap_out, swap_in
        self.out_sems, self.in_sems = out_sems, in_sems
        self.ticks = len(blocks) + self.LAGS[-1]

    def put(self, source, target, chunk, slot, device):
        send(source, target, self.out_sems.at[chunk, slot], self.in_sems.at[chunk, slot], device)

    def wait(self, target, chunk, slot):
        arrived(target, self.out_sems.at[chunk, slot], self.in_sems.at[chunk, slot], self.place.sibling)

    def start(self):
        at, source = self.place, self.source
        rows, half = source.shape[0], source.shape[1] // 6
        mine = pl.ds(at.head * rows, rows)
        offset = 0
        for i, block in enumerate(self.targets):
            size = block.shape[3] // 3
            for part in range(3):
                target = block.at[at.z, at.flat, mine, part * size : (part + 1) * size]
                base = 2 * part * half + offset
                here = pl.ds(pl.multiple_of(base + at.head * half, 128), size)
                there = pl.ds(pl.multiple_of(base + (1 - at.head) * half, 128), size)
                pltpu.make_async_copy(source.at[:, here], target, self.local_sems.at[i]).start()
                send(source.at[:, there], target, self.swap_out.at[i], self.swap_in.at[i], at.sibling)
            offset += size
    def pair_ready(self, i):
        at, block = self.place, self.targets[i]
        rows = self.source.shape[0]
        target = block.at[at.z, at.flat, pl.ds(at.head * rows, rows)]
        pltpu.make_async_copy(target, target, self.local_sems.at[i]).wait()
        theirs = pl.ds((1 - at.head) * rows, rows)
        arrived(block.at[at.z, at.flat, theirs], self.swap_out.at[i], self.swap_in.at[i], at.sibling)

    def stage(self, number, chunk):
        at, out = self.place, self.blocks[chunk]
        everything = slice(None)
        if number == 0:
            if chunk % 2 == 0:
                self.pair_ready(chunk // 2)
            block = out.at[at.z, at.flat]
            for i in range(3):
                self.put(block, block, chunk, i, at.along_z[i])
        if number == 1:
            for i in range(3):
                self.wait(out.at[(at.z + 3 - i) % 4, at.flat], chunk, i)
            block = out.at[everything, at.flat]
            self.put(block, block, chunk, 3, at.beside_x)
            self.put(block, block, chunk, 4, at.beside_y)
        if number == 2:
            self.wait(out.at[everything, at.flat_x], chunk, 3)
            block = out.at[pl.ds(0, 2), at.flat_x]
            self.put(block, block, chunk, 5, at.beside_y)
            self.wait(out.at[everything, at.flat_y], chunk, 4)
            block = out.at[pl.ds(2, 2), at.flat_y]
            self.put(block, block, chunk, 6, at.beside_x)

    def complete(self, chunk):
        at, out = self.place, self.blocks[chunk]
        self.wait(out.at[pl.ds(0, 2), at.flat_xy], chunk, 5)
        self.wait(out.at[pl.ds(2, 2), at.flat_xy], chunk, 6)

    def tick(self, number):
        for stage in (2, 1, 0):
            chunk = number - self.LAGS[stage]
            if 0 <= chunk < len(self.blocks):
                self.stage(stage, chunk)

    def finish(self):
        everything = slice(None)
        for chunk, block in enumerate(self.blocks):
            shapes = [block.at[0, 0]] * 3 + [block.at[everything, 0]] * 2 + [block.at[pl.ds(0, 2), 0]] * 2
            for slot, ref in enumerate(shapes):
                sent(ref, self.out_sems.at[chunk, slot], self.in_sems.at[chunk, slot], self.place.sibling)
        rows = self.source.shape[0]
        for i, block in enumerate(self.targets):
            sent(block.at[0, 0, pl.ds(0, rows)], self.swap_out.at[i], self.swap_in.at[i], self.place.sibling)


def sent(source, out_sem, in_sem, device):
    pltpu.make_async_remote_copy(
        src_ref=source, dst_ref=source, send_sem=out_sem, recv_sem=in_sem, device_id=device, device_id_type=MESH
    ).wait_send()


def layer_kernel(
    count,
    tokens_ref, cotangent_ref, length_ref, gain_one_ref, gain_two_ref, gain_out_ref, bias_ref, start_ref,
    w_query_ref, w_key_ref, w_value_ref, w_gate_ref, w_low_in, w_low_out, w_out_ref, w_mlp,
    h_ref, query_ref, key_ref, value_ref, gate_ref, logits_ref, low_rank_ref, attended_ref, mixed_ref, states_ref,
    grad_zero_ref, grad_ref, output_ref, total_ref, attn_ref, gain_grad_ref,
    tokens, low, low_turned, h_two, h_two_turned, weights_zero, weights, resid, part_out, part_in,
    mlp_sum, grad_sum, inner_all, pair_all, sums_out, sums_in, memory,
    w_query, w_key, w_value, w_gate, w_out, load_sems, local_sems, gather_local, swap_out, swap_in, gather_out, gather_in, pair_out, pair_in,
):
    step = pl.program_id(0)
    at = Place()
    own = tokens_ref.shape[0]
    length = 2 * own
    tiles = length // ROWS
    own_tiles = own // ROWS
    own_at = at.head * own
    gather = Gather(
        at,
        w_mlp,
        [weights.at[i] for i in range(count - 1)] + [weights_zero],
        [weights.at[i, :, :, :, j * 384 : (j + 1) * 384] for i in range(count - 1) for j in range(2)]
        + [weights_zero],
        gather_local, swap_out, swap_in, gather_out, gather_in,
    )
    plan = {(0, 0): (0, 1), (1, 0): (2,), (2, 0): (3,), (3, 0): (4,), (4, 0): (5,), (4, 1): (6,)}
    places = [(5, 0), (5, 1), (6, 1), (7, 0), (7, 1), (8, 1), (9, 1)]
    for i, key in enumerate(places):
        plan[key] = (7 + i,) if i < len(places) - 1 else tuple(range(7 + i, gather.ticks))
    attention_steps = tiles
    first_step = attention_steps + 1
    last_step = first_step + count - 1

    def own_rows(i, size=ROWS):
        return pl.ds(pl.multiple_of(own_at + i * ROWS, ROWS), size)

    def other_rows(i, size=ROWS):
        return pl.ds(pl.multiple_of(own - own_at + i * ROWS, ROWS), size)

    def row_mask(i):
        positions = own_at + i * ROWS + lax.broadcasted_iota(jnp.int32, (ROWS, 1), 0)
        return jnp.where(positions < length_ref[0], 1.0, 0.0)

    def put(source, target, slot):
        send(source, target, pair_out.at[slot], pair_in.at[slot], at.sibling)

    def wait(target, slot):
        arrived(target, pair_out.at[slot], pair_in.at[slot], at.sibling)

    @pl.when(step == 0)
    def _():
        here = [
            pltpu.make_async_copy(cotangent_ref, low.at[own_rows(0, own)], local_sems.at[1]),
            pltpu.make_async_copy(tokens_ref, tokens.at[own_rows(0, own)], local_sems.at[0]),
        ]
        loads = [
            pltpu.make_async_copy(source, target, load_sems.at[i])
            for i, (source, target) in enumerate(
                (
                    (w_query_ref, w_query), (w_key_ref, w_key), (w_value_ref, w_value), (w_gate_ref, w_gate),
                    (w_out_ref, w_out),
                )
            )
        ]
        for copy in here + loads:
            copy.start()
        at.meet()
        put(tokens_ref, tokens.at[own_rows(0, own)], 0)
        memory[...] = start_ref[...]
        gain_grad_ref[...] = jnp.zeros_like(gain_grad_ref)
        gather.start()
        for number in plan[0, 0]:
            gather.tick(number)
        for copy in here:
            copy.wait()
        for i in range(own_tiles):
            low[own_rows(i), :] = (low[own_rows(i), :].astype(F32) * row_mask(i)).astype(BF16)
        put(low.at[own_rows(0, own)], low.at[own_rows(0, own)], 1)
        for copy in loads:
            copy.wait()
        wait(tokens.at[other_rows(0, own)], 0)

    def gather_at(inside, among):
        for (when, which), numbers in plan.items():
            if which == inside and when in among:

                @pl.when(step == when)
                def _():
                    for number in numbers:
                        gather.tick(number)

    gather_at(0, range(1, attention_steps + 1))
    @pl.when(step < attention_steps)
    def _():
        rows = pl.ds(pl.multiple_of(step * ROWS, ROWS), ROWS)
        wide = tokens[rows, :].astype(F32)
        scale = lax.rsqrt(jnp.mean(wide * wide, axis=1, keepdims=True) + EPSILON)
        h_low = (wide * scale * gain_one_ref[...]).astype(BF16)
        h_ref[...] = h_low
        query = dot(h_low, w_query[...]).astype(BF16)
        key = dot(h_low, w_key[...]).astype(BF16)
        value = dot(h_low, w_value[...]).astype(BF16)
        gate = dot(h_low, w_gate[...])
        low_rank = dot(h_low, w_low_in[...], 1, 1)
        high, rest = split_low(low_rank)
        logits = dot(high, w_low_out[...]) + dot(rest, w_low_out[...]) + bias_ref[...]
        query_ref[...] = query
        key_ref[...] = key
        value_ref[...] = value
        gate_ref[...] = gate
        low_rank_ref[...] = low_rank
        logits_ref[...] = logits
        for i in range(ROWS // BLOCK):
            block = slice(i * BLOCK, (i + 1) * BLOCK)
            attended, mixed = forward_block(
                query[block], key[block], value[block], logits[block], gate[block], gain_out_ref[...],
                memory, states_ref.at[i],
            )
            attended_ref[block, :] = attended
            mixed_ref[block, :] = mixed
        part = dot(mixed_ref[...], w_out[...])
        tile = step % own_tiles
        tile_rows = pl.ds(pl.multiple_of(tile * ROWS, ROWS), ROWS)
        mine = step // own_tiles == at.head

        @pl.when(mine)
        def _():
            resid[tile_rows, :] = part

        @pl.when(jnp.logical_not(mine))
        def _():
            part_out[tile_rows, :] = part.astype(BF16)
            put(part_out.at[tile_rows], part_in.at[tile_rows], 2 + tile)

    @pl.when(step == attention_steps)
    def _():
        wait(low.at[other_rows(0, own)], 1)
        for i in range(own_tiles):
            rows = pl.ds(i * ROWS, ROWS)
            wait(part_in.at[rows], 2 + i)
            full = tokens[own_rows(i), :].astype(F32) + resid[rows, :] + part_in[rows, :].astype(F32)
            resid[rows, :] = full
            scale = lax.rsqrt(jnp.mean(full * full, axis=1, keepdims=True) + EPSILON)
            h_two[own_rows(i), :] = (full * scale * gain_two_ref[...]).astype(BF16)
            put(h_two.at[own_rows(i)], h_two.at[own_rows(i)], 4 + i)
        gather_at(1, [attention_steps])

        def turn(i, carry):
            rows = pl.ds(pl.multiple_of(i * ROWS, ROWS), ROWS)
            low_turned[:, rows] = jnp.transpose(low[rows, :])
            return carry

        lax.fori_loop(0, tiles, turn, 0)
        for i in range(own_tiles):
            wait(h_two.at[other_rows(i)], 4 + i)

        def turn_two(i, carry):
            rows = pl.ds(pl.multiple_of(i * ROWS, ROWS), ROWS)
            h_two_turned[:, rows] = jnp.transpose(h_two[rows, :])
            return carry

        lax.fori_loop(0, tiles, turn_two, 0)

    def hidden_rows(block, first, last=False):
        width = block.shape[3] // 3

        def body(i, carry):
            tile = (i + own_tiles * (1 - at.head)) % tiles if last else i
            rows = pl.ds(pl.multiple_of(tile * ROWS, ROWS), ROWS)
            w_pair = block[:, :, :, : 2 * width].reshape(-1, 2 * width)
            w_down = block[:, :, :, 2 * width :].reshape(-1, width)
            pair = dot(h_two[rows, :], w_pair)
            inner_grad = dot(low[rows, :], w_down)
            pre_gate = pair[:, :width]
            up_part = pair[:, width:]
            pre_sigmoid = sigmoid(pre_gate)
            swish = pre_gate * pre_sigmoid
            inner = (swish * up_part).astype(BF16)
            pre_grad = inner_grad * up_part * pre_sigmoid * (1.0 + pre_gate * (1.0 - pre_sigmoid))
            both = jnp.concatenate([pre_grad.astype(BF16), (inner_grad * swish).astype(BF16)], axis=1)
            inner_all[rows, :width] = inner
            pair_all[rows, : 2 * width] = both
            out_part = dot(inner, w_down, 1, 1)
            grad_part = dot(both, w_pair, 1, 1)
            if first:
                mlp_sum[rows, :] = out_part
                grad_sum[rows, :] = grad_part
            else:
                mlp_sum[rows, :] += out_part
                grad_sum[rows, :] += grad_part
            if last:

                @pl.when(i < own_tiles)
                def _():
                    there = pl.ds(pl.multiple_of(i * ROWS, ROWS), ROWS)
                    for k, source in ((1, grad_sum), (0, mlp_sum)):
                        sums_out[k, there, :] = source[rows, :].astype(BF16)
                        put(sums_out.at[k, there], sums_in.at[k, there], 6 + 2 * i + k)

            return carry

        lax.fori_loop(0, tiles, body, 0)

    def weight_rows(block, target):
        width = block.shape[3] // 3

        def body(i, carry):
            rows = pl.ds(pl.multiple_of(i * ROWS, ROWS), ROWS)
            shape = (target.shape[1], target.shape[2], -1)
            target[i, :, :, : 2 * width] = (
                dot(h_two_turned[rows, :], pair_all[:, : 2 * width]).astype(BF16).reshape(shape)
            )
            target[i, :, :, 2 * width :] = (
                dot(low_turned[rows, :], inner_all[:, :width]).astype(BF16).reshape(shape)
            )
            return carry

        lax.fori_loop(0, tiles, body, 0)

    for group in range(count):

        @pl.when(step == first_step + group)
        def _():
            gather_at(0, [first_step + group])
            gather.complete(2 * group)
            if group < count - 1:
                gather.complete(2 * group + 1)

    @pl.when(step == first_step)
    def _():
        hidden_rows(weights.at[0], True)
        gather_at(1, [first_step])
        weight_rows(weights.at[0], grad_ref.at[0])

    @pl.when(jnp.logical_and(step > first_step, step < last_step))
    def _():
        block = weights.at[step - first_step]
        hidden_rows(block, False)
        gather_at(1, range(first_step + 1, last_step))
        weight_rows(block, grad_ref.at[0])

    @pl.when(step == last_step)
    def _():
        hidden_rows(weights_zero, False, True)

    @pl.when(step == last_step)
    def _():
        for i in range(own_tiles):
            sent(h_two.at[pl.ds(0, ROWS)], pair_out.at[4 + i], pair_in.at[4 + i], at.sibling)
        for i in range(own_tiles):
            rows = pl.ds(i * ROWS, ROWS)
            wait(sums_in.at[1, rows], 7 + 2 * i)
            full = resid[rows, :]
            scale = lax.rsqrt(jnp.mean(full * full, axis=1, keepdims=True) + EPSILON)
            normal = full * scale
            grad = grad_sum[own_rows(i), :] + sums_in[1, rows, :].astype(F32)
            total = low[own_rows(i), :].astype(F32) + norm_backward(grad, gain_two_ref[...], normal, scale)
            total_ref[rows, :] = total
            gain_grad_ref[...] += jnp.sum(grad * normal, axis=0, keepdims=True)
            h_two[own_rows(i), :] = total.astype(BF16)
            put(h_two.at[own_rows(i)], h_two.at[own_rows(i)], 10 + i)
            pltpu.make_async_copy(h_two.at[own_rows(i)], attn_ref.at[own_rows(i)], local_sems.at[i]).start()
        for i in range(own_tiles):
            rows = pl.ds(i * ROWS, ROWS)
            wait(sums_in.at[0, rows], 6 + 2 * i)
            mlp_out = mlp_sum[own_rows(i), :] + sums_in[0, rows, :].astype(F32)
            output_ref[rows, :] = (row_mask(i) * (resid[rows, :] + mlp_out)).astype(BF16)
        weight_rows(weights_zero, grad_zero_ref)
        gather.finish()
        for i in range(own_tiles):
            wait(h_two.at[other_rows(i)], 10 + i)
            pltpu.make_async_copy(
                h_two.at[other_rows(i)], attn_ref.at[other_rows(i)], local_sems.at[own_tiles + i]
            ).start()
        for slot, ref in enumerate(
            [tokens_ref, low.at[pl.ds(0, own)]] + [part_out.at[pl.ds(0, ROWS)]] * 8 + [h_two.at[pl.ds(0, ROWS)]] * 2
        ):
            if slot not in (4, 5):
                sent(ref, pair_out.at[slot], pair_in.at[slot], at.sibling)
        for i in range(tiles):
            rows = own_rows(i) if i < own_tiles else other_rows(i - own_tiles)
            pltpu.make_async_copy(h_two.at[rows], attn_ref.at[rows], local_sems.at[i]).wait()


def whole(shape):
    return pl.BlockSpec(shape, lambda i: (0,) * len(shape), pipeline_mode=pl.Buffered(1))


def layer(
    tokens, cotangent, lengths, gain_one, gain_two, gain_out, bias, start,
    w_query, w_key, w_value, w_gate, w_low_in, w_low_out, w_out, w_mlp,
):
    own, width = tokens.shape
    length = 2 * own
    keys, values, heads = w_query.shape[1], w_value.shape[1], start.shape[0]
    rank = w_low_in.shape[0]
    count = (w_mlp.shape[1] // 6 - 128) // 256 + 1
    group = 2 * w_mlp.shape[0]
    tiles = length // ROWS
    first_step = tiles + 1
    steps = first_step + count

    def rows_spec(columns):
        return pl.BlockSpec((ROWS, columns), lambda i: (jnp.minimum(i, tiles - 1), 0))

    vmem = pl.BlockSpec(memory_space=pltpu.VMEM)
    row_shapes = [
        (width, BF16), (keys, BF16), (keys, BF16), (values, BF16), (values, F32), (keys, F32), (rank, F32),
        (values, F32), (values, BF16),
    ]
    blocks = ROWS // BLOCK
    return pl.pallas_call(
        functools.partial(layer_kernel, count),
        grid=(steps,),
        in_specs=[
            ANY, ANY, pl.BlockSpec(memory_space=pltpu.SMEM), whole((1, width)), whole((1, width)), whole((1, VALUE_HEAD)),
            whole((1, keys)), whole(start.shape), ANY, ANY, ANY, ANY, whole(w_low_in.shape), whole(w_low_out.shape),
            ANY, ANY,
        ],
        out_specs=[rows_spec(columns) for columns, _ in row_shapes]
        + [
            pl.BlockSpec((blocks, heads, KEY_HEAD, VALUE_HEAD), lambda i: (jnp.minimum(i, tiles - 1), 0, 0, 0)),
            whole((4, 4, group, 384)),
            pl.BlockSpec(
                (1, 4, 4, group, 768), lambda i: (jnp.clip(i - first_step, 0, count - 2), 0, 0, 0, 0)
            ),
            vmem, vmem, ANY, vmem,
        ],
        out_shape=[jax.ShapeDtypeStruct((length, columns), kind) for columns, kind in row_shapes]
        + [
            jax.ShapeDtypeStruct((length // BLOCK, heads, KEY_HEAD, VALUE_HEAD), BF16),
            jax.ShapeDtypeStruct((4, 4, group, 384), BF16),
            jax.ShapeDtypeStruct((count - 1, 4, 4, group, 768), BF16),
            jax.ShapeDtypeStruct((own, width), BF16),
            jax.ShapeDtypeStruct((own, width), F32),
            jax.ShapeDtypeStruct((length, width), BF16),
            jax.ShapeDtypeStruct((1, width), F32),
        ],
        scratch_shapes=[
            pltpu.VMEM((length, width), BF16),
            pltpu.VMEM((length, width), BF16),
            pltpu.VMEM((width, length), BF16),
            pltpu.VMEM((length, width), BF16),
            pltpu.VMEM((width, length), BF16),
            pltpu.VMEM((4, 4, group, 384), BF16),
            pltpu.VMEM((count - 1, 4, 4, group, 768), BF16),
            pltpu.VMEM((own, width), F32),
            pltpu.VMEM((own, width), BF16),
            pltpu.VMEM((own, width), BF16),
            pltpu.VMEM((length, width), F32),
            pltpu.VMEM((length, width), F32),
            pltpu.VMEM((length, 256), BF16),
            pltpu.VMEM((length, 512), BF16),
            pltpu.VMEM((2, own, width), BF16),
            pltpu.VMEM((2, own, width), BF16),
            pltpu.VMEM((heads, KEY_HEAD, VALUE_HEAD), F32),
            *[pltpu.VMEM(w.shape, w.dtype) for w in (w_query, w_key, w_value, w_gate, w_out)],
            pltpu.SemaphoreType.DMA((5,)),
            pltpu.SemaphoreType.DMA((tiles,)),
            pltpu.SemaphoreType.DMA((count,)),
            pltpu.SemaphoreType.DMA((count,)),
            pltpu.SemaphoreType.DMA((count,)),
            pltpu.SemaphoreType.DMA((2 * count - 1, 7)),
            pltpu.SemaphoreType.DMA((2 * count - 1, 7)),
            pltpu.SemaphoreType.DMA((12,)),
            pltpu.SemaphoreType.DMA((12,)),
        ],
        compiler_params=pltpu.CompilerParams(
            collective_id=0, has_side_effects=True, vmem_limit_bytes=63 << 20
        ),
        name="layer",
    )(
        tokens, cotangent, lengths, gain_one.reshape(1, -1), gain_two.reshape(1, -1), gain_out.reshape(1, -1),
        bias.reshape(1, -1), start, w_query, w_key, w_value, w_gate, w_low_in, w_low_out, w_out,
        w_mlp,
    )


class Reduce:
    def __init__(self, place, partial, via_x, via_y, from_x, from_y, from_z, chunks, out_sems, in_sems):
        self.place, self.partial, self.chunks = place, partial, chunks
        self.via_x, self.via_y, self.from_x, self.from_y, self.from_z = via_x, via_y, from_x, from_y, from_z
        self.out_sems, self.in_sems = out_sems, in_sems

    def put(self, source, target, chunk, slot, device):
        send(source, target, self.out_sems.at[chunk, slot], self.in_sems.at[chunk, slot], device)

    def wait(self, target, chunk, slot):
        arrived(target, self.out_sems.at[chunk, slot], self.in_sems.at[chunk, slot], self.place.sibling)

    def stage(self, number, chunk):
        at, partial, columns = self.place, self.partial, self.chunks[chunk]
        everything = slice(None)
        low, high = pl.ds(0, 2), pl.ds(2, 2)
        view = (everything, everything, columns)
        if number == 0:
            self.put(partial.at[low, at.flat_xy, everything, columns], self.via_x.at[view], chunk, 0, at.beside_x)
            self.put(partial.at[high, at.flat_xy, everything, columns], self.via_y.at[view], chunk, 1, at.beside_y)
        if number == 1:
            self.wait(self.via_x.at[view], chunk, 0)
            block = (low, at.flat_y, everything, columns)
            partial[block] = (partial[block].astype(F32) + self.via_x[view].astype(F32)).astype(BF16)
            self.put(
                partial.at[everything, at.flat_y, everything, columns], self.from_y.at[view], chunk, 2, at.beside_y
            )
            self.wait(self.via_y.at[view], chunk, 1)
            block = (high, at.flat_x, everything, columns)
            partial[block] = (partial[block].astype(F32) + self.via_y[view].astype(F32)).astype(BF16)
            self.put(
                partial.at[everything, at.flat_x, everything, columns], self.from_x.at[view], chunk, 3, at.beside_x
            )
        if number == 2:
            self.wait(self.from_y.at[view], chunk, 2)
            self.wait(self.from_x.at[view], chunk, 3)
            block = (everything, at.flat, everything, columns)
            partial[block] = (
                partial[block].astype(F32) + self.from_x[view].astype(F32) + self.from_y[view].astype(F32)
            ).astype(BF16)
            for i in range(3):
                self.put(
                    partial.at[(at.z + 1 + i) % 4, at.flat, everything, columns],
                    self.from_z.at[i, everything, columns],
                    chunk,
                    4 + i,
                    at.along_z[i],
                )

    def result(self, chunk):
        at, columns = self.place, self.chunks[chunk]
        total = self.partial[at.z, at.flat, :, columns].astype(F32)
        for i in range(3):
            self.wait(self.from_z.at[i, :, columns], chunk, 4 + i)
            total += self.from_z[i, :, columns].astype(F32)
        return total

    def finish(self):
        for chunk, columns in enumerate(self.chunks):
            pair, four, one = [self.partial.at[pl.ds(0, n), 0, :, columns] for n in (2, 4, 1)]
            for slot, ref in enumerate([pair] * 2 + [four] * 2 + [one] * 3):
                sent(ref, self.out_sems.at[chunk, slot], self.in_sems.at[chunk, slot], self.place.sibling)


GAIN_ONE, GAIN_TWO, GAIN_OUT, LOW_IN = 0, 8, 16, 24


def small_rows(width, rank, keys):
    decay = LOW_IN + rank * width // 128
    slot = -(-(rank + 1) * keys // 128 // 8) * 8
    return decay, slot, -(-(decay + 2 * slot) // 16) * 16


def backward_kernel(
    half, mlp_chunks, attn_chunks,
    zero_ref, groups_ref, attn_ref, h_ref, query_ref, key_ref, value_ref, gate_ref, logits_ref, low_rank_ref,
    attended_ref, mixed_ref, states_ref, w_query_ref, w_key_ref, w_value_ref, w_gate_ref, w_low_in, w_low_out,
    w_out_ref, tokens_any, total_any, gain_one_ref, gain_out_ref, gain_two_grad_ref,
    mlp_out, attn_out, small_out, tokens_out,
    mlp, attn, mlp_via_x, mlp_via_y, mlp_from_x, mlp_from_y, mlp_from_z,
    attn_via_x, attn_via_y, attn_from_x, attn_from_y, attn_from_z, summed, swapped,
    small_own, small_in, small_z, h_turned, attn_turned, right, mixed_all, h_grad, h_grad_out, h_grad_in,
    memory_grad, gain_out_sum, low_in_sum, low_out_sum, bias_sum,
    w_query, w_key, w_value, w_gate, w_out, tokens_ref, total_ref, weight_sems, load_sems, mlp_sems_out, mlp_sems_in, attn_sems_out, attn_sems_in, pair_out, pair_in, small_sems_out, small_sems_in,
):
    step = pl.program_id(0)
    at = Place()
    own = tokens_ref.shape[0]
    own_tiles = own // ROWS
    tiles = 2 * own_tiles
    keys, values = w_query.shape[1], w_value.shape[1]
    rank, width = w_low_out.shape[0], tokens_ref.shape[1]
    decay_at, decay_slot, _ = small_rows(width, rank, keys)
    last_step = 2 * tiles
    sides = [
        Reduce(at, mlp, mlp_via_x, mlp_via_y, mlp_from_x, mlp_from_y, mlp_from_z, mlp_chunks, mlp_sems_out, mlp_sems_in),
        Reduce(
            at, attn, attn_via_x, attn_via_y, attn_from_x, attn_from_y, attn_from_z, attn_chunks,
            attn_sems_out, attn_sems_in,
        ),
    ]
    order = [(0, i) for i in range(len(mlp_chunks))] + [(1, i) for i in range(len(attn_chunks))]
    count = len(order)
    rows = mlp.shape[2] // 2

    loads = list(range(0, len(mlp_chunks), 2))
    ticks = count + 6
    slots = [(i, j) for i in range(tiles) for j in range(2)] + [(tiles + i, 0) for i in range(tiles)]
    early = min(len(slots), len(mlp_chunks))
    plan = {slot: (i,) for i, slot in enumerate(slots[:early])}

    def load(chunk):
        if chunk == len(mlp_chunks) - 1:
            return pltpu.make_async_copy(zero_ref, mlp.at[:, :, :, mlp_chunks[chunk]], load_sems.at[chunk])
        columns = slice(mlp_chunks[chunk].start, mlp_chunks[chunk + 1].stop)
        return pltpu.make_async_copy(groups_ref.at[chunk // 2], mlp.at[:, :, :, columns], load_sems.at[chunk])

    def put(source, target, slot):
        send(source, target, pair_out.at[slot], pair_in.at[slot], at.sibling)

    def wait(target, slot):
        arrived(target, pair_out.at[slot], pair_in.at[slot], at.sibling)

    def small(number):
        def put_small(source, target, slot, device):
            send(source, target, small_sems_out.at[slot], small_sems_in.at[slot], device)

        def wait_small(target, slot):
            arrived(target, small_sems_out.at[slot], small_sems_in.at[slot], at.sibling)

        count = small_own.shape[0] // 2
        half = pl.ds(pl.multiple_of(at.head * count, 8), count)
        other = pl.ds(pl.multiple_of((1 - at.head) * count, 8), count)
        if number == 0:
            put_small(small_own, small_in.at[0], 0, at.sibling)
        elif number == 1:
            wait_small(small_in.at[0], 0)
            small_z[0, half] = small_own[half, :] + small_in[0, half]
            put_small(small_z.at[0, half], small_in.at[1, half], 1, at.beside_x)
        elif number == 2:
            wait_small(small_in.at[1, half], 1)
            small_z[1, half] = small_z[0, half] + small_in[1, half]
            put_small(small_z.at[1, half], small_in.at[2, half], 2, at.beside_y)
        elif number == 3:
            wait_small(small_in.at[2, half], 2)
            small_z[2 + at.z, half] = small_z[1, half] + small_in[2, half]
            for i in range(3):
                put_small(small_z.at[2 + at.z, half], small_z.at[2 + at.z, half], 3 + i, at.along_z[i])
        elif number == 4:
            for i in range(3):
                wait_small(small_z.at[2 + (at.z + 3 - i) % 4, half], 3 + i)
            small_z[6, half] = small_z[2, half] + small_z[3, half] + small_z[4, half] + small_z[5, half]
            put_small(small_z.at[6, half], small_z.at[6, half], 6, at.sibling)
        elif number == 5:
            wait_small(small_z.at[6, other], 6)
            small_out[...] = small_z[6]
            for slot in range(7):
                source = small_own if slot == 0 else small_z.at[0, half]
                sent(source, small_sems_out.at[slot], small_sems_in.at[slot], at.sibling)

    def result(side, chunk):
        total = sides[side].result(chunk)
        if side == 0:
            columns = mlp_chunks[chunk]
            summed[:, columns] = total
            put(
                summed.at[pl.ds(pl.multiple_of((1 - at.head) * rows, 8), rows), columns], swapped.at[:, columns],
                2 + chunk,
            )
        else:
            attn_out[:, attn_chunks[chunk]] = total

    def tick(number):
        for stage, lag in ((3, 6), (2, 4), (1, 2), (0, 0)):
            if 0 <= number - lag < count:
                side, chunk = order[number - lag]
                if stage == 3:
                    result(side, chunk)
                    continue
                if stage == 0 and side == 0 and chunk in loads:
                    load(chunk).wait()
                sides[side].stage(stage, chunk)

    def ticks_at(where, inside):
        for number in plan.get((where, inside), ()):
            tick(number)

    def own_rows(i):
        return pl.ds(pl.multiple_of(i * ROWS, ROWS), ROWS)

    held = [
        pltpu.make_async_copy(source, target, weight_sems.at[i])
        for i, (source, target) in enumerate(
            (
                (w_out_ref, w_out), (w_query_ref, w_query), (w_key_ref, w_key), (w_value_ref, w_value),
                (w_gate_ref, w_gate), (tokens_any, tokens_ref), (total_any, total_ref),
            )
        )
    ]

    @pl.when(step == 0)
    def _():
        for chunk in loads:
            load(chunk).start()
        for copy in held:
            copy.start()
        memory_grad[...] = jnp.zeros_like(memory_grad)
        gain_out_sum[...] = jnp.zeros_like(gain_out_sum)
        low_in_sum[...] = jnp.zeros_like(low_in_sum)
        low_out_sum[...] = jnp.zeros_like(low_out_sum)
        bias_sum[...] = jnp.zeros_like(bias_sum)
        at.meet()

    for where in range(2 * tiles):

        @pl.when(step == where)
        def _():
            ticks_at(where, 0)

    @pl.when(step == 0)
    def _():
        for copy in held[:5]:
            copy.wait()

    @pl.when(step < tiles)
    def _():
        tile = tiles - 1 - step
        here = pl.ds(pl.multiple_of(tile * ROWS, ROWS), ROWS)
        attn_tile = attn_ref[...]
        h_tile = h_ref[...]
        attn_turned[:, here] = jnp.transpose(attn_tile)
        h_turned[:, here] = jnp.transpose(h_tile)
        mixed_all[here, :] = mixed_ref[...]
        mixed_grad = dot(attn_tile, w_out[...], 1, 1)
        logits_parts = []
        for i in range(ROWS // BLOCK - 1, -1, -1):
            block = slice(i * BLOCK, (i + 1) * BLOCK)
            grads, logits_grad, gain_grad = backward_block(
                mixed_grad[block], query_ref[block, :], key_ref[block, :], value_ref[block, :], logits_ref[block, :],
                gate_ref[block, :], attended_ref[block, :], states_ref[i], gain_out_ref[...], memory_grad,
            )
            right[pl.ds(pl.multiple_of(tile * ROWS + i * BLOCK, BLOCK), BLOCK), :] = grads
            gain_out_sum[...] += gain_grad
            logits_parts.append(logits_grad)
            if i == ROWS // BLOCK - 1:
                for where in range(tiles):

                    @pl.when(step == where)
                    def _():
                        ticks_at(where, 1)

        logits_grad = jnp.concatenate(logits_parts[::-1], axis=0)
        high, rest = split_low(logits_grad)
        rank_high, rank_rest = split_low(low_rank_ref[...])
        bias_sum[...] += jnp.sum(logits_grad, axis=0, keepdims=True)
        low_out_sum[...] += dot(rank_high, high, 0, 0) + dot(rank_rest, high, 0, 0) + dot(rank_high, rest, 0, 0)
        low_rank_low = (dot(high, w_low_out[...], 1, 1) + dot(rest, w_low_out[...], 1, 1)).astype(BF16)
        low_in_sum[...] += dot(low_rank_low, h_tile, 0, 0)
        grads = right[here, :]
        part = (
            dot(grads[:, :keys], w_query[...], 1, 1)
            + dot(grads[:, keys : 2 * keys], w_key[...], 1, 1)
            + dot(grads[:, 2 * keys : 2 * keys + values], w_value[...], 1, 1)
            + dot(grads[:, 2 * keys + values :], w_gate[...], 1, 1)
            + dot(low_rank_low, w_low_in[...])
        )
        place = tile % own_tiles
        mine = tile // own_tiles == at.head

        @pl.when(mine)
        def _():
            h_grad[own_rows(place), :] = part

        @pl.when(jnp.logical_not(mine))
        def _():
            h_grad_out[own_rows(place), :] = part.astype(BF16)
            put(h_grad_out.at[own_rows(place)], h_grad_in.at[own_rows(place)], place)

    @pl.when(step == tiles)
    def _():
        for copy in held[5:]:
            copy.wait()
        gain_one = jnp.zeros((1, width), F32)
        for i in range(own_tiles):
            here = own_rows(i)
            wait(h_grad_in.at[here], i)
            wide = tokens_ref[here, :].astype(F32)
            scale = lax.rsqrt(jnp.mean(wide * wide, axis=1, keepdims=True) + EPSILON)
            normal = wide * scale
            grad = h_grad[here, :] + h_grad_in[here, :].astype(F32)
            tokens_out[here, :] = total_ref[here, :] + norm_backward(grad, gain_one_ref[...], normal, scale)
            gain_one += jnp.sum(grad * normal, axis=0, keepdims=True)
        small_own[...] = jnp.zeros_like(small_own)
        for i in range(width // 128):
            columns = slice(i * 128, (i + 1) * 128)
            small_own[GAIN_ONE + i : GAIN_ONE + i + 1, :] = gain_one[:, columns]
            small_own[GAIN_TWO + i : GAIN_TWO + i + 1, :] = gain_two_grad_ref[:, columns]
            small_own[LOW_IN + i * rank : LOW_IN + (i + 1) * rank, :] = low_in_sum[:, columns]
        for i in range(VALUE_HEAD // 128):
            small_own[GAIN_OUT + i : GAIN_OUT + i + 1, :] = gain_out_sum[:, i * 128 : (i + 1) * 128]
        for head in range(2):

            @pl.when(at.head == head)
            def _():
                base = decay_at + head * decay_slot
                for i in range(keys // 128):
                    columns = slice(i * 128, (i + 1) * 128)
                    small_own[base + i * rank : base + (i + 1) * rank, :] = low_out_sum[:, columns]
                    bias_at = base + keys // 128 * rank + i
                    small_own[bias_at : bias_at + 1, :] = bias_sum[:, columns]

        small(0)

    @pl.when(jnp.logical_and(step >= tiles, step < 2 * tiles))
    def _():
        part = step - tiles
        here = pl.ds(pl.multiple_of(part * ROWS, ROWS), ROWS)
        shape = (attn.shape[1], attn.shape[2], -1)
        edge = right.shape[1]
        attn[part, :, :, :edge] = dot(h_turned[here, :], right[...]).astype(BF16).reshape(shape)
        attn[part, :, :, edge:] = dot(attn_turned[here, :], mixed_all[...]).astype(BF16).reshape(shape)

    def spread(source, head):
        offset, start = 0, 0
        for size in [2 * mlp_chunks[0].stop // 3] * (len(mlp_chunks) // 2) + [mlp_chunks[0].stop // 3]:
            for part in range(3):
                target = pl.ds(pl.multiple_of(part * 2 * half + head * half + offset, 128), size)
                mlp_out[:, target] = source[:, start : start + size]
                start += size
            offset += size

    @pl.when(step == last_step - 1)
    def _():
        small(1)

    @pl.when(step == last_step)
    def _():
        for number in range(early, ticks):
            tick(number)
            if number - early in SMALL_TICKS:
                small(2 + SMALL_TICKS.index(number - early))
            if number == len(mlp_chunks) + 7:
                spread(summed.at[pl.ds(pl.multiple_of(at.head * rows, 8), rows)], at.head)
                for chunk, columns in enumerate(mlp_chunks):
                    wait(swapped.at[:, columns], 2 + chunk)
                spread(swapped, 1 - at.head)
        for i in range(own_tiles):
            sent(h_grad_out.at[own_rows(i)], pair_out.at[i], pair_in.at[i], at.sibling)
        for chunk, columns in enumerate(mlp_chunks):
            sent(swapped.at[:, columns], pair_out.at[2 + chunk], pair_in.at[2 + chunk], at.sibling)
        for side in sides:
            side.finish()


def backward(
    zero, groups, attn_low, h_low, query, key, value, gate, logits, low_rank, attended, mixed, states,
    w_query, w_key, w_value, w_gate, w_low_in, w_low_out, w_out, tokens, total, gain_one, gain_out, gain_two_grad,
):
    length, width = h_low.shape
    keys, values, heads = query.shape[1], value.shape[1], states.shape[1]
    rank = w_low_out.shape[0]
    own = tokens.shape[0]
    tiles = length // ROWS
    rows = width // 16
    mlp_count = 2 * groups.shape[0] + 1
    mlp_width = zero.shape[-1] * mlp_count
    mlp_chunks = chunk_columns(mlp_width, [zero.shape[-1] // 128] * mlp_count)
    attn_width = 2 * keys + 3 * values
    attn_tiles = attn_width // 128
    sizes = [3] * ((attn_tiles - 4) // 3) + [(attn_tiles - 4) % 3 + 1, 2, 1]
    attn_chunks = chunk_columns(attn_width, sizes)
    attn_count = len(attn_chunks)
    small_shape = (small_rows(width, rank, keys)[2], 128)
    vmem = pl.BlockSpec(memory_space=pltpu.VMEM)

    def rows_spec(columns):
        return pl.BlockSpec((ROWS, columns), lambda i: (jnp.maximum(tiles - 1 - i, 0), 0))

    buffers = []
    for columns in (mlp_width, attn_width):
        buffers += [pltpu.VMEM((n, rows, columns), BF16) for n in (2, 2, 4, 4, 3)]
    streamed = [attn_low, h_low, query, key, value, gate, logits, low_rank, attended, mixed]
    constant = [
        w_query, w_key, w_value, w_gate, w_low_in, w_low_out, w_out, tokens, total,
        gain_one.reshape(1, -1), gain_out.reshape(1, -1), gain_two_grad.reshape(1, -1),
    ]
    return pl.pallas_call(
        functools.partial(backward_kernel, mlp_width // 3, mlp_chunks, attn_chunks),
        grid=(2 * tiles + 1,),
        in_specs=[ANY, ANY]
        + [rows_spec(a.shape[1]) for a in streamed]
        + [
            pl.BlockSpec(
                (ROWS // BLOCK, heads, KEY_HEAD, VALUE_HEAD), lambda i: (jnp.maximum(tiles - 1 - i, 0), 0, 0, 0)
            )
        ]
        + [whole(a.shape) if i in (4, 5) or i > 8 else ANY for i, a in enumerate(constant)],
        out_specs=[vmem, vmem, vmem, vmem],
        out_shape=[
            jax.ShapeDtypeStruct((rows // 2, 2 * mlp_width), F32),
            jax.ShapeDtypeStruct((rows, attn_width), F32),
            jax.ShapeDtypeStruct(small_shape, F32),
            jax.ShapeDtypeStruct((own, width), F32),
        ],
        scratch_shapes=[
            pltpu.VMEM((4, 4, rows, mlp_width), BF16),
            pltpu.VMEM((4, 4, rows, attn_width), BF16),
            *buffers,
            pltpu.VMEM((rows, mlp_width), F32),
            pltpu.VMEM((rows // 2, mlp_width), F32),
            pltpu.VMEM(small_shape, F32),
            pltpu.VMEM((3,) + small_shape, F32),
            pltpu.VMEM((7,) + small_shape, F32),
            pltpu.VMEM((width, length), BF16),
            pltpu.VMEM((width, length), BF16),
            pltpu.VMEM((length, 2 * keys + 2 * values), BF16),
            pltpu.VMEM((length, values), BF16),
            pltpu.VMEM((own, width), F32),
            pltpu.VMEM((own, width), BF16),
            pltpu.VMEM((own, width), BF16),
            pltpu.VMEM((heads, KEY_HEAD, VALUE_HEAD), F32),
            pltpu.VMEM((1, VALUE_HEAD), F32),
            pltpu.VMEM((rank, width), F32),
            pltpu.VMEM((rank, keys), F32),
            pltpu.VMEM((1, keys), F32),
            *[pltpu.VMEM(a.shape, a.dtype) for a in (w_query, w_key, w_value, w_gate, w_out, tokens, total)],
            pltpu.SemaphoreType.DMA((7,)),
            pltpu.SemaphoreType.DMA((mlp_count,)),
            pltpu.SemaphoreType.DMA((mlp_count, 7)),
            pltpu.SemaphoreType.DMA((mlp_count, 7)),
            pltpu.SemaphoreType.DMA((attn_count, 7)),
            pltpu.SemaphoreType.DMA((attn_count, 7)),
            pltpu.SemaphoreType.DMA((2 + mlp_count,)),
            pltpu.SemaphoreType.DMA((2 + mlp_count,)),
            pltpu.SemaphoreType.DMA((7,)),
            pltpu.SemaphoreType.DMA((7,)),
        ],
        compiler_params=pltpu.CompilerParams(
            collective_id=1, has_side_effects=True, vmem_limit_bytes=63 << 20
        ),
        name="backward",
    )(zero, groups, *streamed, states, *constant)


def emit_kernel(
    half, edges, mlp_ref, attn_ref, small_ref, tokens_ref, output_ref,
    output_out, tokens_out, gain_one_out, query_out, key_out, value_out, gate_out, low_in_out, low_out_out, bias_out,
    gain_out_out, out_out, gain_two_out, mlp_out, tokens, output, mlp, attn, load_sems, sems,
):
    staged = [(attn_ref, attn)]
    moves = []
    for i, target in enumerate((query_out, key_out, value_out, gate_out, out_out)):
        moves.append((attn.at[:, edges[i] : edges[i + 1]], target))
    for source, stage, target in (
        (tokens_ref, tokens, tokens_out), (mlp_ref, mlp, mlp_out), (output_ref, output, output_out)
    ):
        size = source.shape[0] // 2
        for rows in (pl.ds(0, size), pl.ds(size, size)):
            staged.append((source.at[rows], stage.at[rows]))
            moves.append((stage.at[rows], target.at[rows]))
    loads = [pltpu.make_async_copy(source, target, load_sems.at[i]) for i, (source, target) in enumerate(staged)]
    for load in loads:
        load.start()
    copies = [pltpu.make_async_copy(source, target, sems.at[i]) for i, (source, target) in enumerate(moves)]
    for i, load in enumerate(loads):
        load.wait()
        for copy in copies[:5] if i == 0 else copies[4 + i : 5 + i]:
            copy.start()
    rank, width = low_in_out.shape
    keys = low_out_out.shape[1]
    decay_at, decay_slot, _ = small_rows(width, rank, keys)
    for i in range(width // 128):
        columns = slice(i * 128, (i + 1) * 128)
        gain_one_out[:, columns] = small_ref[GAIN_ONE + i : GAIN_ONE + i + 1, :]
        gain_two_out[:, columns] = small_ref[GAIN_TWO + i : GAIN_TWO + i + 1, :]
        low_in_out[:, columns] = small_ref[LOW_IN + i * rank : LOW_IN + (i + 1) * rank, :]
    for i in range(VALUE_HEAD // 128):
        gain_out_out[:, i * 128 : (i + 1) * 128] = small_ref[GAIN_OUT + i : GAIN_OUT + i + 1, :]
    for head in range(2):

        @pl.when(lax.axis_index("head") == head)
        def _():
            base = decay_at + head * decay_slot
            for i in range(keys // 128):
                columns = slice(i * 128, (i + 1) * 128)
                low_out_out[:, columns] = small_ref[base + i * rank : base + (i + 1) * rank, :]
                bias_at = base + keys // 128 * rank + i
                bias_out[:, columns] = small_ref[bias_at : bias_at + 1, :]

    for copy in copies:
        copy.wait()


def emit(mlp, attn, small, tokens, output, keys, values, rank):
    rows, width = attn.shape[0], tokens.shape[1]
    edges = [0, keys, 2 * keys, 2 * keys + values, 2 * keys + 2 * values, 2 * keys + 3 * values]
    vmem = pl.BlockSpec(memory_space=pltpu.VMEM)
    shapes = [
        (output.shape, BF16, ANY), (tokens.shape, F32, ANY), ((1, width), F32, vmem), ((rows, keys), F32, ANY),
        ((rows, keys), F32, ANY), ((rows, values), F32, ANY), ((rows, values), F32, ANY), ((rank, width), F32, vmem),
        ((rank, keys), F32, vmem), ((1, keys), F32, vmem), ((1, VALUE_HEAD), F32, vmem), ((rows, values), F32, ANY),
        ((1, width), F32, vmem), (mlp.shape, F32, ANY),
    ]
    return pl.pallas_call(
        functools.partial(emit_kernel, mlp.shape[1] // 6, edges),
        in_specs=[ANY, ANY, vmem, ANY, ANY],
        out_specs=[space for _, _, space in shapes],
        out_shape=[jax.ShapeDtypeStruct(shape, kind) for shape, kind, _ in shapes],
        scratch_shapes=[
            pltpu.VMEM(tokens.shape, F32),
            pltpu.VMEM(output.shape, BF16),
            pltpu.VMEM(mlp.shape, F32),
            pltpu.VMEM(attn.shape, F32),
            pltpu.SemaphoreType.DMA((7,)),
            pltpu.SemaphoreType.DMA((11,)),
        ],
        compiler_params=pltpu.CompilerParams(vmem_limit_bytes=60 << 20),
        name="emit",
    )(mlp, attn, small, tokens, output)


def swap(value):
    return lax.ppermute(value, "head", [(0, 1), (1, 0)])


def ordered(own, other, axis):
    size = own.shape[axis]
    joined = jnp.concatenate([own, other, own], axis=axis)
    return lax.dynamic_slice_in_dim(joined, lax.axis_index("head") * size, 2 * size, axis)


def half_of(value, which, axis):
    size = value.shape[axis] // 2
    return lax.dynamic_slice_in_dim(value, which * size, size, axis)


def sum_rows(partial, here):
    other = swap(half_of(partial, 1 - here, 0).astype(BF16))
    return half_of(partial, here, 0) + other.astype(F32)


def norm_backward(grad_in, gain, normed_in, scale_in):
    scaled = grad_in * gain
    return scale_in * (scaled - normed_in * jnp.mean(scaled * normed_in, axis=-1, keepdims=True))


def per_device(
    tokens, lengths, initial_memory, norm_attn_gain, w_query, w_key, w_value, w_gate_out, w_low_in, w_low_out,
    decay_bias, out_gain, w_out, norm_mlp_gain, w_mlp, cotangent,
):
    here = lax.axis_index("head")
    own_rows = tokens.shape[1]
    keys = w_query.shape[1]
    values = w_value.shape[1]
    hidden = w_mlp.shape[1] // 3
    half = hidden // 2
    shard_rows = w_mlp.shape[0]
    square = lax.axis_size("dp") == 16

    tokens_own = tokens[0]
    if square:
        (
            h_low, query, key, value, gate, logits, low_rank, attended, mixed, states,
            grad_zero, grad_mlp, output, resid_total, attn_low, gain_two_grad,
        ) = layer(
            tokens_own, cotangent[0], lengths, norm_attn_gain, norm_mlp_gain, out_gain, decay_bias,
            initial_memory[0], w_query, w_key, w_value, w_gate_out, w_low_in.T, w_low_out, w_out, w_mlp,
        )
        grad_mlp, attn_grads, packed, tokens_grad = backward(
            grad_zero, grad_mlp, attn_low, h_low, query, key, value, gate, logits, low_rank, attended, mixed, states,
            w_query, w_key, w_value, w_gate_out, w_low_in.T, w_low_out, w_out, tokens_own, resid_total,
            norm_attn_gain, out_gain, gain_two_grad,
        )
        results = emit(grad_mlp, attn_grads, packed, tokens_grad, output, keys, values, w_low_out.shape[0])
        (
            output, tokens_grad, gain_one_grad, query_grad, key_grad, value_grad, gate_grad, low_in_grad, low_out_grad,
            bias_grad, out_gain_grad, out_grad, gain_two_grad, grad_mlp,
        ) = results
        return (
            output[None], tokens_grad[None], gain_one_grad[0], query_grad, key_grad, value_grad, gate_grad,
            low_in_grad.T, low_out_grad, bias_grad[0], out_gain_grad[0], out_grad.T, gain_two_grad[0], grad_mlp,
        )
    pieces = w_mlp.reshape(shard_rows, 3, 2, half)
    own_piece = lax.dynamic_index_in_dim(pieces, here, 2, keepdims=False)
    other_piece = lax.dynamic_index_in_dim(pieces, 1 - here, 2, keepdims=False)
    positions = here * own_rows + lax.iota(jnp.int32, own_rows)
    row_mask = (positions < lengths[0]).astype(F32)[:, None]
    resid_grad = row_mask * cotangent[0].astype(F32)
    low_own = resid_grad.astype(BF16)
    pair = swap(other_piece.reshape(shard_rows, 3 * half))
    weights = lax.all_gather(
        ordered(own_piece.reshape(shard_rows, 3 * half), pair, 0), "dp", axis=0, tiled=True
    )
    tokens_wide = ordered(tokens_own, swap(tokens_own), 0).astype(F32)
    length = tokens_wide.shape[0]
    scale_one = lax.rsqrt(jnp.mean(tokens_wide * tokens_wide, axis=1, keepdims=True) + EPSILON)
    h_low = (tokens_wide * scale_one * norm_attn_gain).astype(BF16)
    query = dot(h_low, w_query).astype(BF16)
    key = dot(h_low, w_key).astype(BF16)
    value = dot(h_low, w_value).astype(BF16)
    gate = dot(h_low, w_gate_out)
    low_rank = dot(h_low, w_low_in)
    low_high, low_rest = split_low(low_rank)
    logits = dot(low_high, w_low_out) + dot(low_rest, w_low_out) + decay_bias
    attended, mixed, states = attention_forward(query, key, value, logits, gate, out_gain, initial_memory[0])
    resid = tokens_own.astype(F32) + sum_rows(dot(mixed, w_out), here)
    scale_two = lax.rsqrt(jnp.mean(resid * resid, axis=1, keepdims=True) + EPSILON)
    normal_two = resid * scale_two
    h_two_own = (normal_two * norm_mlp_gain).astype(BF16)
    h_two = ordered(h_two_own, swap(h_two_own), 0)
    resid_low = ordered(low_own, swap(low_own), 0)
    pre_gate = dot(h_two, weights[:, :half])
    up_part = dot(h_two, weights[:, half : 2 * half])
    pre_sigmoid = sigmoid(pre_gate)
    inner = (pre_gate * pre_sigmoid * up_part).astype(BF16)
    inner_grad = dot(resid_low, weights[:, 2 * half :])
    pre_grad = (
        inner_grad * up_part * pre_sigmoid * (1.0 + pre_gate * (1.0 - pre_sigmoid))
    ).astype(BF16)
    up_grad = (inner_grad * pre_gate * pre_sigmoid).astype(BF16)
    mlp_out = sum_rows(dot(inner, weights[:, 2 * half :], 1, 1), here)
    output = (row_mask * (resid + mlp_out)).astype(BF16)[None]
    h_two_grad = sum_rows(
        dot(pre_grad, weights[:, :half], 1, 1) + dot(up_grad, weights[:, half : 2 * half], 1, 1), here
    )
    grad_mlp = jnp.concatenate(
        [
            dot(h_two, pre_grad, 0, 0).astype(BF16),
            dot(h_two, up_grad, 0, 0).astype(BF16),
            dot(resid_low, inner, 0, 0).astype(BF16),
        ],
        axis=1,
    )
    resid_total = resid_grad + norm_backward(h_two_grad, norm_mlp_gain, normal_two, scale_two)
    gain_two_grad = jnp.sum(h_two_grad * normal_two, axis=0)
    attn_own = resid_total.astype(BF16)
    attn_low = ordered(attn_own, swap(attn_own), 0)

    mixed_grad = dot(attn_low, w_out, 1, 1)
    out_grad = dot(attn_low, mixed, 0, 0)
    query_grad, key_grad, value_grad, gate_grad, logits_grad, out_gain_grad = attention_backward(
        mixed_grad, query, key, value, logits, gate, attended, states, out_gain
    )
    bias_grad = jnp.sum(logits_grad, axis=0)
    grad_high, grad_rest = split_low(logits_grad)
    low_out_grad = (
        dot(low_high, grad_high, 0, 0) + dot(low_rest, grad_high, 0, 0) + dot(low_high, grad_rest, 0, 0)
    )
    low_rank_low = (dot(grad_high, w_low_out, 1, 1) + dot(grad_rest, w_low_out, 1, 1)).astype(BF16)
    low_in_grad = dot(h_low, low_rank_low, 0, 0)
    attn_grads = jnp.concatenate(
        [
            dot(h_low, query_grad, 0, 0).astype(BF16),
            dot(h_low, key_grad, 0, 0).astype(BF16),
            dot(h_low, value_grad, 0, 0).astype(BF16),
            dot(h_low, gate_grad, 0, 0).astype(BF16),
            out_grad.astype(BF16),
        ],
        axis=1,
    )
    h_grad = sum_rows(
        dot(query_grad, w_query, 1, 1)
        + dot(key_grad, w_key, 1, 1)
        + dot(value_grad, w_value, 1, 1)
        + dot(gate_grad, w_gate_out, 1, 1)
        + dot(low_rank_low, w_low_in, 1, 1),
        here,
    )
    own_wide = tokens_own.astype(F32)
    own_scale = lax.rsqrt(jnp.mean(own_wide * own_wide, axis=1, keepdims=True) + EPSILON)
    normal_own = own_wide * own_scale
    tokens_grad = resid_total + norm_backward(h_grad, norm_attn_gain, normal_own, own_scale)
    gain_one_grad = jnp.sum(h_grad * normal_own, axis=0)
    low_rank_width = w_low_out.shape[0]
    decay_part = jnp.concatenate([low_out_grad, bias_grad[None]], axis=0)
    slots = jnp.zeros((2,) + decay_part.shape, F32)
    slots = lax.dynamic_update_slice(slots, decay_part[None], (here, 0, 0))
    packed = jnp.concatenate(
        [
            gain_one_grad, gain_two_grad, out_gain_grad.reshape(-1), low_in_grad.reshape(-1), slots.reshape(-1),
        ]
    )
    packed = lax.psum(packed, ("dp", "head"))
    attn_grads = lax.psum_scatter(attn_grads, "dp", scatter_dimension=0, tiled=True).astype(F32)
    grad_mlp = lax.psum_scatter(grad_mlp, "dp", scatter_dimension=0, tiled=True)
    own_half = half_of(grad_mlp, here, 0)
    other_half = swap(half_of(grad_mlp, 1 - here, 0))
    grad_mlp = ordered(
        own_half.reshape(shard_rows, 3, 1, half), other_half.reshape(shard_rows, 3, 1, half), 2
    ).reshape(shard_rows, 3 * hidden).astype(F32)
    width = gain_one_grad.shape[0]
    edges = [width, 2 * width, 2 * width + VALUE_HEAD]
    edges.append(edges[-1] + width * low_rank_width)
    low_in_grad = packed[edges[2] : edges[3]].reshape(width, low_rank_width)
    decay_part = lax.dynamic_index_in_dim(packed[edges[3] :].reshape(slots.shape), here, 0, keepdims=False)
    low_out_grad, bias_grad = decay_part[:low_rank_width], decay_part[low_rank_width]
    gain_one_grad, gain_two_grad = packed[: edges[0]], packed[edges[0] : edges[1]]
    out_gain_grad = packed[edges[1] : edges[2]]
    return (
        output,
        tokens_grad[None],
        gain_one_grad,
        attn_grads[:, :keys],
        attn_grads[:, keys : 2 * keys],
        attn_grads[:, 2 * keys : 2 * keys + values],
        attn_grads[:, 2 * keys + values : 2 * keys + 2 * values],
        low_in_grad,
        low_out_grad,
        bias_grad,
        out_gain_grad,
        attn_grads[:, 2 * keys + 2 * values :].T,
        gain_two_grad,
        grad_mlp,
    )


def solution(mesh):
    return jax.shard_map(
        per_device,
        mesh=mesh,
        in_specs=(
            P("dp", "head", None),
            P("dp"),
            P("dp", "head", None, None),
            P(),
            P(None, "head"),
            P(None, "head"),
            P(None, "head"),
            P(None, "head"),
            P(),
            P(None, "head"),
            P("head"),
            P(),
            P("head", None),
            P(),
            P(("dp", "head"), None),
            P("dp", "head", None),
        ),
        out_specs=(
            P("dp", "head", None),
            P("dp", "head", None),
            P(),
            P("dp", "head"),
            P("dp", "head"),
            P("dp", "head"),
            P("dp", "head"),
            P(),
            P(None, "head"),
            P("head"),
            P(),
            P("head", "dp"),
            P(),
            P(("dp", "head"), None),
        ),
        check_vma=False,
    )
```

```python
import functools

import jax
import jax.numpy as jnp
from jax import lax
from jax.experimental import pallas as pl
from jax.experimental.pallas import tpu as pltpu
from jax.sharding import PartitionSpec as P

HEADS = 4
KEY = 512
VALUE = 1024
BLOCK = 128
KEY_HEAD = KEY // HEADS
VALUE_HEAD = VALUE // HEADS

EPSILON = 1e-05
F32 = jnp.float32
BF16 = jnp.bfloat16
SCALE = KEY_HEAD ** (-0.5)


def dot(left, right, left_dim=1, right_dim=0):
    return lax.dot_general(
        left, right, (((left_dim,), (right_dim,)), ((), ())), preferred_element_type=F32
    )


def split_low(value):
    high = value.astype(BF16)
    return high, (value - high.astype(F32)).astype(BF16)


def sigmoid(value):
    return 1.0 / (1.0 + jnp.exp(-value))


def log_sigmoid(value):
    return jnp.minimum(value, 0.0) - jnp.log1p(jnp.exp(-jnp.abs(value)))


def triangle(lower):
    rows = lax.broadcasted_iota(jnp.int32, (BLOCK, BLOCK), 0)
    columns = lax.broadcasted_iota(jnp.int32, (BLOCK, BLOCK), 1)
    return rows >= columns if lower else rows <= columns


def decay_terms(logits):
    log_decay = log_sigmoid(logits) * (1.0 / 16.0)
    ones = jnp.where(triangle(True), 1.0, 0.0).astype(BF16)
    high, low = split_low(log_decay)
    total = dot(ones, high) + dot(ones, low)
    middle = total[BLOCK // 2 - 1 : BLOCK // 2, :]
    end = total[BLOCK - 1 :, :]
    rise = jnp.exp(total - middle)
    fall = jnp.exp(middle - total)
    early = jnp.exp(total) * SCALE
    late = jnp.exp(end - total)
    return rise * SCALE, fall, early, late, jnp.exp(end)


def as_column(row, width):
    column = jnp.transpose(jnp.broadcast_to(row, (KEY_HEAD, KEY_HEAD)))
    return jnp.concatenate([column] * (width // KEY_HEAD), axis=1)


def forward_block(query, key, value, logits, gate, gain, memory, states):
    rise, fall, early, late, decay = decay_terms(logits)
    lower = triangle(True)
    attended_parts = []
    mixed_parts = []
    for head in range(memory.shape[0]):
        keys_at = slice(head * KEY_HEAD, (head + 1) * KEY_HEAD)
        values_at = slice(head * VALUE_HEAD, (head + 1) * VALUE_HEAD)
        query_wide = query[:, keys_at].astype(F32)
        key_wide = key[:, keys_at].astype(F32)
        value_head = value[:, values_at]
        state = memory[head]
        state_low = state.astype(BF16)
        states[head] = state_low
        scores = dot(
            (query_wide * rise[:, keys_at]).astype(BF16), (key_wide * fall[:, keys_at]).astype(BF16), 1, 1
        )
        scores = jnp.where(lower, scores, 0.0).astype(BF16)
        left = jnp.concatenate([scores, (query_wide * early[:, keys_at]).astype(BF16)], axis=1)
        attended = dot(left, jnp.concatenate([value_head, state_low], axis=0))
        memory[head] = as_column(decay[:, keys_at], VALUE_HEAD) * state + dot(
            (key_wide * late[:, keys_at]).astype(BF16), value_head, 0, 0
        )
        scale = lax.rsqrt(jnp.mean(attended * attended, axis=1, keepdims=True) + EPSILON)
        gate_head = gate[:, values_at]
        attended_parts.append(attended)
        mixed_parts.append((attended * scale * gain * gate_head * sigmoid(gate_head)).astype(BF16))
    return jnp.concatenate(attended_parts, axis=1), jnp.concatenate(mixed_parts, axis=1)


def forward_kernel(
    query_ref, key_ref, value_ref, logits_ref, gate_ref, gain_ref, start_ref,
    attended_ref, mixed_ref, states_ref, memory
):
    @pl.when(pl.program_id(0) == 0)
    def _():
        memory[...] = start_ref[...]

    attended_ref[...], mixed_ref[...] = forward_block(
        query_ref[...], key_ref[...], value_ref[...], logits_ref[...], gate_ref[...], gain_ref[...],
        memory, states_ref.at[0],
    )


def attention_forward(query, key, value, logits, gate, gain, start):
    length, keys = query.shape
    values = value.shape[1]
    heads = start.shape[0]
    steps = length // BLOCK

    def rows(width):
        return pl.BlockSpec((BLOCK, width), lambda i: (i, 0))

    return pl.pallas_call(
        forward_kernel,
        grid=(steps,),
        in_specs=[
            rows(keys), rows(keys), rows(values), rows(keys), rows(values),
            pl.BlockSpec((1, VALUE_HEAD), lambda i: (0, 0)),
            pl.BlockSpec((heads, KEY_HEAD, VALUE_HEAD), lambda i: (0, 0, 0)),
        ],
        out_specs=[
            rows(values), rows(values),
            pl.BlockSpec((1, heads, KEY_HEAD, VALUE_HEAD), lambda i: (i, 0, 0, 0)),
        ],
        out_shape=[
            jax.ShapeDtypeStruct((length, values), F32),
            jax.ShapeDtypeStruct((length, values), BF16),
            jax.ShapeDtypeStruct((steps, heads, KEY_HEAD, VALUE_HEAD), BF16),
        ],
        scratch_shapes=[pltpu.VMEM((heads, KEY_HEAD, VALUE_HEAD), F32)],
        compiler_params=pltpu.CompilerParams(vmem_limit_bytes=48 << 20),
        name="attention_forward",
    )(query, key, value, logits, gate, gain.reshape(1, -1), start)


def backward_block(mixed_grad, query, key, value, logits, gate, attended, states, gain, memory_grad):
    rise, fall, early, late, decay = decay_terms(logits)
    lower = triangle(True)
    upper = triangle(False)
    last = lax.broadcasted_iota(jnp.int32, (BLOCK, KEY_HEAD), 0) == BLOCK - 1
    query_grads, key_grads, value_grads, gate_grads, total_grads = [], [], [], [], []
    gain_grad = jnp.zeros((1, VALUE_HEAD), F32)
    for head in range(memory_grad.shape[0]):
        keys_at = slice(head * KEY_HEAD, (head + 1) * KEY_HEAD)
        values_at = slice(head * VALUE_HEAD, (head + 1) * VALUE_HEAD)
        attended_head = attended[:, values_at]
        scale = lax.rsqrt(jnp.mean(attended_head * attended_head, axis=1, keepdims=True) + EPSILON)
        normal = attended_head * scale
        gate_head = gate[:, values_at]
        gate_sigmoid = sigmoid(gate_head)
        mixed_head = mixed_grad[:, values_at]
        gate_grads.append(
            (mixed_head * normal * gain * gate_sigmoid * (1.0 + gate_head * (1.0 - gate_sigmoid))).astype(BF16)
        )
        normed_grad = mixed_head * gate_head * gate_sigmoid
        gain_grad += jnp.sum(normed_grad * normal, axis=0, keepdims=True)
        scaled = normed_grad * gain
        attended_grad = (
            scale * (scaled - normal * jnp.mean(scaled * normal, axis=1, keepdims=True))
        ).astype(BF16)

        query_wide = query[:, keys_at].astype(F32)
        key_wide = key[:, keys_at].astype(F32)
        value_head = value[:, values_at]
        query_middle = query_wide * rise[:, keys_at]
        key_middle = key_wide * fall[:, keys_at]
        query_early = query_wide * early[:, keys_at]
        key_late = key_wide * late[:, keys_at]
        query_middle_low = query_middle.astype(BF16)
        key_middle_low = key_middle.astype(BF16)
        state = states[head]
        after = memory_grad[head]

        scores_turned = jnp.where(upper, dot(key_middle_low, query_middle_low, 1, 1), 0.0).astype(BF16)
        from_values = dot(attended_grad, jnp.concatenate([value_head, state], axis=0), 1, 1)
        to_values = jnp.concatenate([attended_grad, after.astype(BF16)], axis=0)
        from_grads = dot(value_head, to_values, 1, 1)
        scores_grad = jnp.where(lower, from_values[:, :BLOCK], 0.0).astype(BF16)
        scores_grad_turned = jnp.where(upper, from_grads[:, :BLOCK], 0.0).astype(BF16)
        query_early_grad = from_values[:, BLOCK:]
        key_late_grad = from_grads[:, BLOCK:]
        query_middle_grad = dot(scores_grad, key_middle_low)
        key_middle_grad = dot(scores_grad_turned, query_middle_low)
        value_grads.append(
            dot(jnp.concatenate([scores_turned, key_late.astype(BF16)], axis=1), to_values).astype(BF16)
        )
        carried = as_column(decay[:, keys_at], VALUE_HEAD) * after
        memory_grad[head] = carried + dot(query_early.astype(BF16), attended_grad, 0, 0)
        query_grads.append(
            (query_early_grad * early[:, keys_at] + query_middle_grad * rise[:, keys_at]).astype(BF16)
        )
        key_grads.append((key_middle_grad * fall[:, keys_at] + key_late_grad * late[:, keys_at]).astype(BF16))
        late_part = key_late_grad * key_late
        end_high, end_low = split_low(carried * state.astype(F32))
        ones = jnp.ones((8, VALUE_HEAD), BF16)
        end_grad = (dot(ones, end_high, 1, 1) + dot(ones, end_low, 1, 1))[:1] + jnp.sum(
            late_part, axis=0, keepdims=True
        )
        total_grads.append(
            query_early_grad * query_early
            + query_middle_grad * query_middle
            - key_middle_grad * key_middle
            - late_part
            + jnp.where(last, end_grad, 0.0)
        )
    ones = jnp.where(upper, 1.0, 0.0).astype(BF16)
    high, rest = split_low(jnp.concatenate(total_grads, axis=1))
    logits_grad = (dot(ones, high) + dot(ones, rest)) * sigmoid(-logits) * (1.0 / 16.0)
    grads = query_grads + key_grads + value_grads + gate_grads
    return jnp.concatenate(grads, axis=1), logits_grad, gain_grad


def backward_kernel_plain(
    mixed_grad_ref, query_ref, key_ref, value_ref, logits_ref, gate_ref, attended_ref, states_ref, gain_ref,
    query_grad_ref, key_grad_ref, value_grad_ref, gate_grad_ref, logits_grad_ref, gain_grad_ref, memory_grad
):
    @pl.when(pl.program_id(0) == 0)
    def _():
        memory_grad[...] = jnp.zeros_like(memory_grad)
        gain_grad_ref[...] = jnp.zeros_like(gain_grad_ref)

    grads, logits_grad, gain_grad = backward_block(
        mixed_grad_ref[...], query_ref[...], key_ref[...], value_ref[...], logits_ref[...], gate_ref[...],
        attended_ref[...], states_ref[0], gain_ref[...], memory_grad,
    )
    start = 0
    for ref in (query_grad_ref, key_grad_ref, value_grad_ref, gate_grad_ref):
        ref[...] = grads[:, start : start + ref.shape[1]]
        start += ref.shape[1]
    logits_grad_ref[...] = logits_grad
    gain_grad_ref[...] += gain_grad


def attention_backward(mixed_grad, query, key, value, logits, gate, attended, states, gain):
    length, keys = query.shape
    values = value.shape[1]
    heads = states.shape[1]
    steps = length // BLOCK

    def rows(width):
        return pl.BlockSpec((BLOCK, width), lambda i: (steps - 1 - i, 0))

    return pl.pallas_call(
        backward_kernel_plain,
        grid=(steps,),
        in_specs=[
            rows(values), rows(keys), rows(keys), rows(values), rows(keys), rows(values), rows(values),
            pl.BlockSpec((1, heads, KEY_HEAD, VALUE_HEAD), lambda i: (steps - 1 - i, 0, 0, 0)),
            pl.BlockSpec((1, VALUE_HEAD), lambda i: (0, 0)),
        ],
        out_specs=[
            rows(keys), rows(keys), rows(values), rows(values), rows(keys),
            pl.BlockSpec((1, VALUE_HEAD), lambda i: (0, 0)),
        ],
        out_shape=[
            jax.ShapeDtypeStruct((length, keys), BF16),
            jax.ShapeDtypeStruct((length, keys), BF16),
            jax.ShapeDtypeStruct((length, values), BF16),
            jax.ShapeDtypeStruct((length, values), BF16),
            jax.ShapeDtypeStruct((length, keys), F32),
            jax.ShapeDtypeStruct((1, VALUE_HEAD), F32),
        ],
        scratch_shapes=[pltpu.VMEM((heads, KEY_HEAD, VALUE_HEAD), F32)],
        compiler_params=pltpu.CompilerParams(vmem_limit_bytes=48 << 20),
        name="attention_backward",
    )(mixed_grad, query, key, value, logits, gate, attended, states, gain.reshape(1, -1))


MESH = pl.DeviceIdType.MESH
ANY = pl.BlockSpec(memory_space=pl.ANY)


class Place:
    def __init__(self):
        self.dp = lax.axis_index("dp")
        self.head = lax.axis_index("head")
        self.z = self.dp // 4
        self.flat = self.dp % 4
        self.flat_x = self.flat + 1 - 2 * (self.flat % 2)
        self.flat_y = self.flat + 2 - 4 * (self.flat // 2)
        self.flat_xy = 3 - self.flat
        self.sibling = (self.dp, 1 - self.head)
        self.beside_x = (self.z * 4 + self.flat_x, self.head)
        self.beside_y = (self.z * 4 + self.flat_y, self.head)
        self.along_z = [(((self.z + i) % 4) * 4 + self.flat, self.head) for i in range(1, 4)]

    def meet(self):
        barrier = pltpu.get_barrier_semaphore()
        others = [self.sibling, self.beside_x, self.beside_y] + self.along_z
        for other in others:
            pl.semaphore_signal(barrier, 1, device_id=other, device_id_type=MESH)
        pl.semaphore_wait(barrier, len(others))


def send(source, target, out_sem, in_sem, device):
    copy = pltpu.make_async_remote_copy(
        src_ref=source, dst_ref=target, send_sem=out_sem, recv_sem=in_sem, device_id=device, device_id_type=MESH
    )
    copy.start()
    return copy


def arrived(target, out_sem, in_sem, device):
    pltpu.make_async_remote_copy(
        src_ref=target, dst_ref=target, send_sem=out_sem, recv_sem=in_sem, device_id=device, device_id_type=MESH
    ).wait_recv()


def chunk_columns(width, sizes):
    starts = [sum(sizes[:i]) * 128 for i in range(len(sizes))]
    assert sum(sizes) * 128 == width
    return [slice(start, start + size * 128) for start, size in zip(starts, sizes)]


ROWS = 256
SMALL_TICKS = (0, 2, 5, 8)


class Gather:
    LAGS = (0, 1, 3)

    def __init__(self, place, source, targets, blocks, local_sems, swap_out, swap_in, out_sems, in_sems):
        self.place, self.source, self.targets, self.blocks = place, source, targets, blocks
        self.local_sems, self.swap_out, self.swap_in = local_sems, swap_out, swap_in
        self.out_sems, self.in_sems = out_sems, in_sems
        self.ticks = len(blocks) + self.LAGS[-1]

    def put(self, source, target, chunk, slot, device):
        send(source, target, self.out_sems.at[chunk, slot], self.in_sems.at[chunk, slot], device)

    def wait(self, target, chunk, slot):
        arrived(target, self.out_sems.at[chunk, slot], self.in_sems.at[chunk, slot], self.place.sibling)

    def start(self):
        at, source = self.place, self.source
        rows, half = source.shape[0], source.shape[1] // 6
        mine = pl.ds(at.head * rows, rows)
        offset = 0
        for i, block in enumerate(self.targets):
            size = block.shape[3] // 3
            for part in range(3):
                target = block.at[at.z, at.flat, mine, part * size : (part + 1) * size]
                base = 2 * part * half + offset
                here = pl.ds(pl.multiple_of(base + at.head * half, 128), size)
                there = pl.ds(pl.multiple_of(base + (1 - at.head) * half, 128), size)
                pltpu.make_async_copy(source.at[:, here], target, self.local_sems.at[i]).start()
                send(source.at[:, there], target, self.swap_out.at[i], self.swap_in.at[i], at.sibling)
            offset += size
    def pair_ready(self, i):
        at, block = self.place, self.targets[i]
        rows = self.source.shape[0]
        target = block.at[at.z, at.flat, pl.ds(at.head * rows, rows)]
        pltpu.make_async_copy(target, target, self.local_sems.at[i]).wait()
        theirs = pl.ds((1 - at.head) * rows, rows)
        arrived(block.at[at.z, at.flat, theirs], self.swap_out.at[i], self.swap_in.at[i], at.sibling)

    def stage(self, number, chunk):
        at, out = self.place, self.blocks[chunk]
        everything = slice(None)
        if number == 0:
            if chunk % 2 == 0:
                self.pair_ready(chunk // 2)
            block = out.at[at.z, at.flat]
            for i in range(3):
                self.put(block, block, chunk, i, at.along_z[i])
        if number == 1:
            for i in range(3):
                self.wait(out.at[(at.z + 3 - i) % 4, at.flat], chunk, i)
            block = out.at[everything, at.flat]
            self.put(block, block, chunk, 3, at.beside_x)
            self.put(block, block, chunk, 4, at.beside_y)
        if number == 2:
            self.wait(out.at[everything, at.flat_x], chunk, 3)
            block = out.at[pl.ds(0, 2), at.flat_x]
            self.put(block, block, chunk, 5, at.beside_y)
            self.wait(out.at[everything, at.flat_y], chunk, 4)
            block = out.at[pl.ds(2, 2), at.flat_y]
            self.put(block, block, chunk, 6, at.beside_x)

    def complete(self, chunk):
        at, out = self.place, self.blocks[chunk]
        self.wait(out.at[pl.ds(0, 2), at.flat_xy], chunk, 5)
        self.wait(out.at[pl.ds(2, 2), at.flat_xy], chunk, 6)

    def tick(self, number):
        for stage in (2, 1, 0):
            chunk = number - self.LAGS[stage]
            if 0 <= chunk < len(self.blocks):
                self.stage(stage, chunk)

    def finish(self):
        everything = slice(None)
        for chunk, block in enumerate(self.blocks):
            shapes = [block.at[0, 0]] * 3 + [block.at[everything, 0]] * 2 + [block.at[pl.ds(0, 2), 0]] * 2
            for slot, ref in enumerate(shapes):
                sent(ref, self.out_sems.at[chunk, slot], self.in_sems.at[chunk, slot], self.place.sibling)
        rows = self.source.shape[0]
        for i, block in enumerate(self.targets):
            sent(block.at[0, 0, pl.ds(0, rows)], self.swap_out.at[i], self.swap_in.at[i], self.place.sibling)


def sent(source, out_sem, in_sem, device):
    pltpu.make_async_remote_copy(
        src_ref=source, dst_ref=source, send_sem=out_sem, recv_sem=in_sem, device_id=device, device_id_type=MESH
    ).wait_send()


def layer_kernel(
    count,
    tokens_ref, cotangent_ref, length_ref, gain_one_ref, gain_two_ref, gain_out_ref, bias_ref, start_ref,
    w_query_ref, w_key_ref, w_value_ref, w_gate_ref, w_low_in, w_low_out, w_out_ref, w_mlp,
    h_ref, query_ref, key_ref, value_ref, gate_ref, logits_ref, low_rank_ref, attended_ref, mixed_ref, states_ref,
    grad_zero_ref, grad_ref, output_ref, total_ref, attn_ref, gain_grad_ref,
    tokens, low, low_turned, h_two, h_two_turned, weights_zero, weights, resid, part_out, part_in,
    mlp_sum, grad_sum, inner_all, pair_all, sums_out, sums_in, memory,
    w_query, w_key, w_value, w_gate, w_out, load_sems, local_sems, gather_local, swap_out, swap_in, gather_out, gather_in, pair_out, pair_in,
):
    step = pl.program_id(0)
    at = Place()
    own = tokens_ref.shape[0]
    length = 2 * own
    tiles = length // ROWS
    own_tiles = own // ROWS
    own_at = at.head * own
    gather = Gather(
        at,
        w_mlp,
        [weights.at[i] for i in range(count - 1)] + [weights_zero],
        [weights.at[i, :, :, :, j * 384 : (j + 1) * 384] for i in range(count - 1) for j in range(2)]
        + [weights_zero],
        gather_local, swap_out, swap_in, gather_out, gather_in,
    )
    plan = {(0, 0): (0, 1), (1, 0): (2,), (2, 0): (3,), (3, 0): (4,), (4, 0): (5,), (4, 1): (6,)}
    places = [(5, 0), (5, 1), (6, 1), (7, 0), (7, 1), (8, 1), (9, 1)]
    for i, key in enumerate(places):
        plan[key] = (7 + i,) if i < len(places) - 1 else tuple(range(7 + i, gather.ticks))
    attention_steps = tiles
    first_step = attention_steps + 1
    last_step = first_step + count - 1

    def own_rows(i, size=ROWS):
        return pl.ds(pl.multiple_of(own_at + i * ROWS, ROWS), size)

    def other_rows(i, size=ROWS):
        return pl.ds(pl.multiple_of(own - own_at + i * ROWS, ROWS), size)

    def row_mask(i):
        positions = own_at + i * ROWS + lax.broadcasted_iota(jnp.int32, (ROWS, 1), 0)
        return jnp.where(positions < length_ref[0], 1.0, 0.0)

    def put(source, target, slot):
        send(source, target, pair_out.at[slot], pair_in.at[slot], at.sibling)

    def wait(target, slot):
        arrived(target, pair_out.at[slot], pair_in.at[slot], at.sibling)

    @pl.when(step == 0)
    def _():
        here = [
            pltpu.make_async_copy(cotangent_ref, low.at[own_rows(0, own)], local_sems.at[1]),
            pltpu.make_async_copy(tokens_ref, tokens.at[own_rows(0, own)], local_sems.at[0]),
        ]
        loads = [
            pltpu.make_async_copy(source, target, load_sems.at[i])
            for i, (source, target) in enumerate(
                (
                    (w_query_ref, w_query), (w_key_ref, w_key), (w_value_ref, w_value), (w_gate_ref, w_gate),
                    (w_out_ref, w_out),
                )
            )
        ]
        for copy in here + loads:
            copy.start()
        at.meet()
        put(tokens_ref, tokens.at[own_rows(0, own)], 0)
        memory[...] = start_ref[...]
        gain_grad_ref[...] = jnp.zeros_like(gain_grad_ref)
        gather.start()
        for number in plan[0, 0]:
            gather.tick(number)
        for copy in here:
            copy.wait()
        for i in range(own_tiles):
            low[own_rows(i), :] = (low[own_rows(i), :].astype(F32) * row_mask(i)).astype(BF16)
        put(low.at[own_rows(0, own)], low.at[own_rows(0, own)], 1)
        for copy in loads:
            copy.wait()
        wait(tokens.at[other_rows(0, own)], 0)

    def gather_at(inside, among):
        for (when, which), numbers in plan.items():
            if which == inside and when in among:

                @pl.when(step == when)
                def _():
                    for number in numbers:
                        gather.tick(number)

    gather_at(0, range(1, attention_steps + 1))
    @pl.when(step < attention_steps)
    def _():
        rows = pl.ds(pl.multiple_of(step * ROWS, ROWS), ROWS)
        wide = tokens[rows, :].astype(F32)
        scale = lax.rsqrt(jnp.mean(wide * wide, axis=1, keepdims=True) + EPSILON)
        h_low = (wide * scale * gain_one_ref[...]).astype(BF16)
        h_ref[...] = h_low
        query = dot(h_low, w_query[...]).astype(BF16)
        key = dot(h_low, w_key[...]).astype(BF16)
        value = dot(h_low, w_value[...]).astype(BF16)
        gate = dot(h_low, w_gate[...])
        low_rank = dot(h_low, w_low_in[...], 1, 1)
        high, rest = split_low(low_rank)
        logits = dot(high, w_low_out[...]) + dot(rest, w_low_out[...]) + bias_ref[...]
        query_ref[...] = query
        key_ref[...] = key
        value_ref[...] = value
        gate_ref[...] = gate
        low_rank_ref[...] = low_rank
        logits_ref[...] = logits
        for i in range(ROWS // BLOCK):
            block = slice(i * BLOCK, (i + 1) * BLOCK)
            attended, mixed = forward_block(
                query[block], key[block], value[block], logits[block], gate[block], gain_out_ref[...],
                memory, states_ref.at[i],
            )
            attended_ref[block, :] = attended
            mixed_ref[block, :] = mixed
        part = dot(mixed_ref[...], w_out[...])
        tile = step % own_tiles
        tile_rows = pl.ds(pl.multiple_of(tile * ROWS, ROWS), ROWS)
        mine = step // own_tiles == at.head

        @pl.when(mine)
        def _():
            resid[tile_rows, :] = part

        @pl.when(jnp.logical_not(mine))
        def _():
            part_out[tile_rows, :] = part.astype(BF16)
            put(part_out.at[tile_rows], part_in.at[tile_rows], 2 + tile)

    @pl.when(step == attention_steps)
    def _():
        wait(low.at[other_rows(0, own)], 1)
        for i in range(own_tiles):
            rows = pl.ds(i * ROWS, ROWS)
            wait(part_in.at[rows], 2 + i)
            full = tokens[own_rows(i), :].astype(F32) + resid[rows, :] + part_in[rows, :].astype(F32)
            resid[rows, :] = full
            scale = lax.rsqrt(jnp.mean(full * full, axis=1, keepdims=True) + EPSILON)
            h_two[own_rows(i), :] = (full * scale * gain_two_ref[...]).astype(BF16)
            put(h_two.at[own_rows(i)], h_two.at[own_rows(i)], 4 + i)
        gather_at(1, [attention_steps])

        def turn(i, carry):
            rows = pl.ds(pl.multiple_of(i * ROWS, ROWS), ROWS)
            low_turned[:, rows] = jnp.transpose(low[rows, :])
            return carry

        lax.fori_loop(0, tiles, turn, 0)
        for i in range(own_tiles):
            wait(h_two.at[other_rows(i)], 4 + i)

        def turn_two(i, carry):
            rows = pl.ds(pl.multiple_of(i * ROWS, ROWS), ROWS)
            h_two_turned[:, rows] = jnp.transpose(h_two[rows, :])
            return carry

        lax.fori_loop(0, tiles, turn_two, 0)

    def hidden_rows(block, first, last=False):
        width = block.shape[3] // 3

        def body(i, carry):
            tile = (i + own_tiles * (1 - at.head)) % tiles if last else i
            rows = pl.ds(pl.multiple_of(tile * ROWS, ROWS), ROWS)
            w_pair = block[:, :, :, : 2 * width].reshape(-1, 2 * width)
            w_down = block[:, :, :, 2 * width :].reshape(-1, width)
            pair = dot(h_two[rows, :], w_pair)
            inner_grad = dot(low[rows, :], w_down)
            pre_gate = pair[:, :width]
            up_part = pair[:, width:]
            pre_sigmoid = sigmoid(pre_gate)
            swish = pre_gate * pre_sigmoid
            inner = (swish * up_part).astype(BF16)
            pre_grad = inner_grad * up_part * pre_sigmoid * (1.0 + pre_gate * (1.0 - pre_sigmoid))
            both = jnp.concatenate([pre_grad.astype(BF16), (inner_grad * swish).astype(BF16)], axis=1)
            inner_all[rows, :width] = inner
            pair_all[rows, : 2 * width] = both
            out_part = dot(inner, w_down, 1, 1)
            grad_part = dot(both, w_pair, 1, 1)
            if first:
                mlp_sum[rows, :] = out_part
                grad_sum[rows, :] = grad_part
            else:
                mlp_sum[rows, :] += out_part
                grad_sum[rows, :] += grad_part
            if last:

                @pl.when(i < own_tiles)
                def _():
                    there = pl.ds(pl.multiple_of(i * ROWS, ROWS), ROWS)
                    for k, source in ((1, grad_sum), (0, mlp_sum)):
                        sums_out[k, there, :] = source[rows, :].astype(BF16)
                        put(sums_out.at[k, there], sums_in.at[k, there], 6 + 2 * i + k)

            return carry

        lax.fori_loop(0, tiles, body, 0)

    def weight_rows(block, target):
        width = block.shape[3] // 3

        def body(i, carry):
            rows = pl.ds(pl.multiple_of(i * ROWS, ROWS), ROWS)
            shape = (target.shape[1], target.shape[2], -1)
            target[i, :, :, : 2 * width] = (
                dot(h_two_turned[rows, :], pair_all[:, : 2 * width]).astype(BF16).reshape(shape)
            )
            target[i, :, :, 2 * width :] = (
                dot(low_turned[rows, :], inner_all[:, :width]).astype(BF16).reshape(shape)
            )
            return carry

        lax.fori_loop(0, tiles, body, 0)

    for group in range(count):

        @pl.when(step == first_step + group)
        def _():
            gather_at(0, [first_step + group])
            gather.complete(2 * group)
            if group < count - 1:
                gather.complete(2 * group + 1)

    @pl.when(step == first_step)
    def _():
        hidden_rows(weights.at[0], True)
        gather_at(1, [first_step])
        weight_rows(weights.at[0], grad_ref.at[0])

    @pl.when(jnp.logical_and(step > first_step, step < last_step))
    def _():
        block = weights.at[step - first_step]
        hidden_rows(block, False)
        gather_at(1, range(first_step + 1, last_step))
        weight_rows(block, grad_ref.at[0])

    @pl.when(step == last_step)
    def _():
        hidden_rows(weights_zero, False, True)

    @pl.when(step == last_step)
    def _():
        for i in range(own_tiles):
            sent(h_two.at[pl.ds(0, ROWS)], pair_out.at[4 + i], pair_in.at[4 + i], at.sibling)
        for i in range(own_tiles):
            rows = pl.ds(i * ROWS, ROWS)
            wait(sums_in.at[1, rows], 7 + 2 * i)
            full = resid[rows, :]
            scale = lax.rsqrt(jnp.mean(full * full, axis=1, keepdims=True) + EPSILON)
            normal = full * scale
            grad = grad_sum[own_rows(i), :] + sums_in[1, rows, :].astype(F32)
            total = low[own_rows(i), :].astype(F32) + norm_backward(grad, gain_two_ref[...], normal, scale)
            total_ref[rows, :] = total
            gain_grad_ref[...] += jnp.sum(grad * normal, axis=0, keepdims=True)
            h_two[own_rows(i), :] = total.astype(BF16)
            put(h_two.at[own_rows(i)], h_two.at[own_rows(i)], 10 + i)
            pltpu.make_async_copy(h_two.at[own_rows(i)], attn_ref.at[own_rows(i)], local_sems.at[i]).start()
        for i in range(own_tiles):
            rows = pl.ds(i * ROWS, ROWS)
            wait(sums_in.at[0, rows], 6 + 2 * i)
            mlp_out = mlp_sum[own_rows(i), :] + sums_in[0, rows, :].astype(F32)
            output_ref[rows, :] = (row_mask(i) * (resid[rows, :] + mlp_out)).astype(BF16)
        weight_rows(weights_zero, grad_zero_ref)
        gather.finish()
        for i in range(own_tiles):
            wait(h_two.at[other_rows(i)], 10 + i)
            pltpu.make_async_copy(
                h_two.at[other_rows(i)], attn_ref.at[other_rows(i)], local_sems.at[own_tiles + i]
            ).start()
        for slot, ref in enumerate(
            [tokens_ref, low.at[pl.ds(0, own)]] + [part_out.at[pl.ds(0, ROWS)]] * 8 + [h_two.at[pl.ds(0, ROWS)]] * 2
        ):
            if slot not in (4, 5):
                sent(ref, pair_out.at[slot], pair_in.at[slot], at.sibling)
        for i in range(tiles):
            rows = own_rows(i) if i < own_tiles else other_rows(i - own_tiles)
            pltpu.make_async_copy(h_two.at[rows], attn_ref.at[rows], local_sems.at[i]).wait()


def whole(shape):
    return pl.BlockSpec(shape, lambda i: (0,) * len(shape), pipeline_mode=pl.Buffered(1))


def layer(
    tokens, cotangent, lengths, gain_one, gain_two, gain_out, bias, start,
    w_query, w_key, w_value, w_gate, w_low_in, w_low_out, w_out, w_mlp,
):
    own, width = tokens.shape
    length = 2 * own
    keys, values, heads = w_query.shape[1], w_value.shape[1], start.shape[0]
    rank = w_low_in.shape[0]
    count = (w_mlp.shape[1] // 6 - 128) // 256 + 1
    group = 2 * w_mlp.shape[0]
    tiles = length // ROWS
    first_step = tiles + 1
    steps = first_step + count

    def rows_spec(columns):
        return pl.BlockSpec((ROWS, columns), lambda i: (jnp.minimum(i, tiles - 1), 0))

    vmem = pl.BlockSpec(memory_space=pltpu.VMEM)
    row_shapes = [
        (width, BF16), (keys, BF16), (keys, BF16), (values, BF16), (values, F32), (keys, F32), (rank, F32),
        (values, F32), (values, BF16),
    ]
    blocks = ROWS // BLOCK
    return pl.pallas_call(
        functools.partial(layer_kernel, count),
        grid=(steps,),
        in_specs=[
            ANY, ANY, pl.BlockSpec(memory_space=pltpu.SMEM), whole((1, width)), whole((1, width)), whole((1, VALUE_HEAD)),
            whole((1, keys)), whole(start.shape), ANY, ANY, ANY, ANY, whole(w_low_in.shape), whole(w_low_out.shape),
            ANY, ANY,
        ],
        out_specs=[rows_spec(columns) for columns, _ in row_shapes]
        + [
            pl.BlockSpec((blocks, heads, KEY_HEAD, VALUE_HEAD), lambda i: (jnp.minimum(i, tiles - 1), 0, 0, 0)),
            whole((4, 4, group, 384)),
            pl.BlockSpec(
                (1, 4, 4, group, 768), lambda i: (jnp.clip(i - first_step, 0, count - 2), 0, 0, 0, 0)
            ),
            vmem, vmem, ANY, vmem,
        ],
        out_shape=[jax.ShapeDtypeStruct((length, columns), kind) for columns, kind in row_shapes]
        + [
            jax.ShapeDtypeStruct((length // BLOCK, heads, KEY_HEAD, VALUE_HEAD), BF16),
            jax.ShapeDtypeStruct((4, 4, group, 384), BF16),
            jax.ShapeDtypeStruct((count - 1, 4, 4, group, 768), BF16),
            jax.ShapeDtypeStruct((own, width), BF16),
            jax.ShapeDtypeStruct((own, width), F32),
            jax.ShapeDtypeStruct((length, width), BF16),
            jax.ShapeDtypeStruct((1, width), F32),
        ],
        scratch_shapes=[
            pltpu.VMEM((length, width), BF16),
            pltpu.VMEM((length, width), BF16),
            pltpu.VMEM((width, length), BF16),
            pltpu.VMEM((length, width), BF16),
            pltpu.VMEM((width, length), BF16),
            pltpu.VMEM((4, 4, group, 384), BF16),
            pltpu.VMEM((count - 1, 4, 4, group, 768), BF16),
            pltpu.VMEM((own, width), F32),
            pltpu.VMEM((own, width), BF16),
            pltpu.VMEM((own, width), BF16),
            pltpu.VMEM((length, width), F32),
            pltpu.VMEM((length, width), F32),
            pltpu.VMEM((length, 256), BF16),
            pltpu.VMEM((length, 512), BF16),
            pltpu.VMEM((2, own, width), BF16),
            pltpu.VMEM((2, own, width), BF16),
            pltpu.VMEM((heads, KEY_HEAD, VALUE_HEAD), F32),
            *[pltpu.VMEM(w.shape, w.dtype) for w in (w_query, w_key, w_value, w_gate, w_out)],
            pltpu.SemaphoreType.DMA((5,)),
            pltpu.SemaphoreType.DMA((tiles,)),
            pltpu.SemaphoreType.DMA((count,)),
            pltpu.SemaphoreType.DMA((count,)),
            pltpu.SemaphoreType.DMA((count,)),
            pltpu.SemaphoreType.DMA((2 * count - 1, 7)),
            pltpu.SemaphoreType.DMA((2 * count - 1, 7)),
            pltpu.SemaphoreType.DMA((12,)),
            pltpu.SemaphoreType.DMA((12,)),
        ],
        compiler_params=pltpu.CompilerParams(
            collective_id=0, has_side_effects=True, vmem_limit_bytes=63 << 20
        ),
        name="layer",
    )(
        tokens, cotangent, lengths, gain_one.reshape(1, -1), gain_two.reshape(1, -1), gain_out.reshape(1, -1),
        bias.reshape(1, -1), start, w_query, w_key, w_value, w_gate, w_low_in, w_low_out, w_out,
        w_mlp,
    )


class Reduce:
    def __init__(self, place, partial, via_x, via_y, from_x, from_y, from_z, chunks, out_sems, in_sems):
        self.place, self.partial, self.chunks = place, partial, chunks
        self.via_x, self.via_y, self.from_x, self.from_y, self.from_z = via_x, via_y, from_x, from_y, from_z
        self.out_sems, self.in_sems = out_sems, in_sems

    def put(self, source, target, chunk, slot, device):
        send(source, target, self.out_sems.at[chunk, slot], self.in_sems.at[chunk, slot], device)

    def wait(self, target, chunk, slot):
        arrived(target, self.out_sems.at[chunk, slot], self.in_sems.at[chunk, slot], self.place.sibling)

    def stage(self, number, chunk):
        at, partial, columns = self.place, self.partial, self.chunks[chunk]
        everything = slice(None)
        low, high = pl.ds(0, 2), pl.ds(2, 2)
        view = (everything, everything, columns)
        if number == 0:
            self.put(partial.at[low, at.flat_xy, everything, columns], self.via_x.at[view], chunk, 0, at.beside_x)
            self.put(partial.at[high, at.flat_xy, everything, columns], self.via_y.at[view], chunk, 1, at.beside_y)
        if number == 1:
            self.wait(self.via_x.at[view], chunk, 0)
            block = (low, at.flat_y, everything, columns)
            partial[block] = (partial[block].astype(F32) + self.via_x[view].astype(F32)).astype(BF16)
            self.put(
                partial.at[everything, at.flat_y, everything, columns], self.from_y.at[view], chunk, 2, at.beside_y
            )
            self.wait(self.via_y.at[view], chunk, 1)
            block = (high, at.flat_x, everything, columns)
            partial[block] = (partial[block].astype(F32) + self.via_y[view].astype(F32)).astype(BF16)
            self.put(
                partial.at[everything, at.flat_x, everything, columns], self.from_x.at[view], chunk, 3, at.beside_x
            )
        if number == 2:
            self.wait(self.from_y.at[view], chunk, 2)
            self.wait(self.from_x.at[view], chunk, 3)
            block = (everything, at.flat, everything, columns)
            partial[block] = (
                partial[block].astype(F32) + self.from_x[view].astype(F32) + self.from_y[view].astype(F32)
            ).astype(BF16)
            for i in range(3):
                self.put(
                    partial.at[(at.z + 1 + i) % 4, at.flat, everything, columns],
                    self.from_z.at[i, everything, columns],
                    chunk,
                    4 + i,
                    at.along_z[i],
                )

    def result(self, chunk):
        at, columns = self.place, self.chunks[chunk]
        total = self.partial[at.z, at.flat, :, columns].astype(F32)
        for i in range(3):
            self.wait(self.from_z.at[i, :, columns], chunk, 4 + i)
            total += self.from_z[i, :, columns].astype(F32)
        return total

    def finish(self):
        for chunk, columns in enumerate(self.chunks):
            pair, four, one = [self.partial.at[pl.ds(0, n), 0, :, columns] for n in (2, 4, 1)]
            for slot, ref in enumerate([pair] * 2 + [four] * 2 + [one] * 3):
                sent(ref, self.out_sems.at[chunk, slot], self.in_sems.at[chunk, slot], self.place.sibling)


GAIN_ONE, GAIN_TWO, GAIN_OUT, LOW_IN = 0, 8, 16, 24


def small_rows(width, rank, keys):
    decay = LOW_IN + rank * width // 128
    slot = -(-(rank + 1) * keys // 128 // 8) * 8
    return decay, slot, -(-(decay + 2 * slot) // 16) * 16


def backward_kernel(
    half, mlp_chunks, attn_chunks,
    zero_ref, groups_ref, attn_ref, h_ref, query_ref, key_ref, value_ref, gate_ref, logits_ref, low_rank_ref,
    attended_ref, mixed_ref, states_ref, w_query_ref, w_key_ref, w_value_ref, w_gate_ref, w_low_in, w_low_out,
    w_out_ref, tokens_any, total_any, gain_one_ref, gain_out_ref, gain_two_grad_ref,
    mlp_out, attn_out, small_out, tokens_out,
    mlp, attn, mlp_via_x, mlp_via_y, mlp_from_x, mlp_from_y, mlp_from_z,
    attn_via_x, attn_via_y, attn_from_x, attn_from_y, attn_from_z, summed, swapped,
    small_own, small_in, small_z, h_turned, attn_turned, right, mixed_all, h_grad, h_grad_out, h_grad_in,
    memory_grad, gain_out_sum, low_in_sum, low_out_sum, bias_sum,
    w_query, w_key, w_value, w_gate, w_out, tokens_ref, total_ref, weight_sems, load_sems, mlp_sems_out, mlp_sems_in, attn_sems_out, attn_sems_in, pair_out, pair_in, small_sems_out, small_sems_in,
):
    step = pl.program_id(0)
    at = Place()
    own = tokens_ref.shape[0]
    own_tiles = own // ROWS
    tiles = 2 * own_tiles
    keys, values = w_query.shape[1], w_value.shape[1]
    rank, width = w_low_out.shape[0], tokens_ref.shape[1]
    decay_at, decay_slot, _ = small_rows(width, rank, keys)
    last_step = 2 * tiles
    sides = [
        Reduce(at, mlp, mlp_via_x, mlp_via_y, mlp_from_x, mlp_from_y, mlp_from_z, mlp_chunks, mlp_sems_out, mlp_sems_in),
        Reduce(
            at, attn, attn_via_x, attn_via_y, attn_from_x, attn_from_y, attn_from_z, attn_chunks,
            attn_sems_out, attn_sems_in,
        ),
    ]
    order = [(0, i) for i in range(len(mlp_chunks))] + [(1, i) for i in range(len(attn_chunks))]
    count = len(order)
    rows = mlp.shape[2] // 2

    loads = list(range(0, len(mlp_chunks), 2))
    ticks = count + 6
    slots = [(i, j) for i in range(tiles) for j in range(2)] + [(tiles + i, 0) for i in range(tiles)]
    early = min(len(slots), len(mlp_chunks))
    plan = {slot: (i,) for i, slot in enumerate(slots[:early])}

    def load(chunk):
        if chunk == len(mlp_chunks) - 1:
            return pltpu.make_async_copy(zero_ref, mlp.at[:, :, :, mlp_chunks[chunk]], load_sems.at[chunk])
        columns = slice(mlp_chunks[chunk].start, mlp_chunks[chunk + 1].stop)
        return pltpu.make_async_copy(groups_ref.at[chunk // 2], mlp.at[:, :, :, columns], load_sems.at[chunk])

    def put(source, target, slot):
        send(source, target, pair_out.at[slot], pair_in.at[slot], at.sibling)

    def wait(target, slot):
        arrived(target, pair_out.at[slot], pair_in.at[slot], at.sibling)

    def small(number):
        def put_small(source, target, slot, device):
            send(source, target, small_sems_out.at[slot], small_sems_in.at[slot], device)

        def wait_small(target, slot):
            arrived(target, small_sems_out.at[slot], small_sems_in.at[slot], at.sibling)

        count = small_own.shape[0] // 2
        half = pl.ds(pl.multiple_of(at.head * count, 8), count)
        other = pl.ds(pl.multiple_of((1 - at.head) * count, 8), count)
        if number == 0:
            put_small(small_own, small_in.at[0], 0, at.sibling)
        elif number == 1:
            wait_small(small_in.at[0], 0)
            small_z[0, half] = small_own[half, :] + small_in[0, half]
            put_small(small_z.at[0, half], small_in.at[1, half], 1, at.beside_x)
        elif number == 2:
            wait_small(small_in.at[1, half], 1)
            small_z[1, half] = small_z[0, half] + small_in[1, half]
            put_small(small_z.at[1, half], small_in.at[2, half], 2, at.beside_y)
        elif number == 3:
            wait_small(small_in.at[2, half], 2)
            small_z[2 + at.z, half] = small_z[1, half] + small_in[2, half]
            for i in range(3):
                put_small(small_z.at[2 + at.z, half], small_z.at[2 + at.z, half], 3 + i, at.along_z[i])
        elif number == 4:
            for i in range(3):
                wait_small(small_z.at[2 + (at.z + 3 - i) % 4, half], 3 + i)
            small_z[6, half] = small_z[2, half] + small_z[3, half] + small_z[4, half] + small_z[5, half]
            put_small(small_z.at[6, half], small_z.at[6, half], 6, at.sibling)
        elif number == 5:
            wait_small(small_z.at[6, other], 6)
            small_out[...] = small_z[6]
            for slot in range(7):
                source = small_own if slot == 0 else small_z.at[0, half]
                sent(source, small_sems_out.at[slot], small_sems_in.at[slot], at.sibling)

    def result(side, chunk):
        total = sides[side].result(chunk)
        if side == 0:
            columns = mlp_chunks[chunk]
            summed[:, columns] = total
            put(
                summed.at[pl.ds(pl.multiple_of((1 - at.head) * rows, 8), rows), columns], swapped.at[:, columns],
                2 + chunk,
            )
        else:
            attn_out[:, attn_chunks[chunk]] = total

    def tick(number):
        for stage, lag in ((3, 6), (2, 4), (1, 2), (0, 0)):
            if 0 <= number - lag < count:
                side, chunk = order[number - lag]
                if stage == 3:
                    result(side, chunk)
                    continue
                if stage == 0 and side == 0 and chunk in loads:
                    load(chunk).wait()
                sides[side].stage(stage, chunk)

    def ticks_at(where, inside):
        for number in plan.get((where, inside), ()):
            tick(number)

    def own_rows(i):
        return pl.ds(pl.multiple_of(i * ROWS, ROWS), ROWS)

    held = [
        pltpu.make_async_copy(source, target, weight_sems.at[i])
        for i, (source, target) in enumerate(
            (
                (w_out_ref, w_out), (w_query_ref, w_query), (w_key_ref, w_key), (w_value_ref, w_value),
                (w_gate_ref, w_gate), (tokens_any, tokens_ref), (total_any, total_ref),
            )
        )
    ]

    @pl.when(step == 0)
    def _():
        for chunk in loads:
            load(chunk).start()
        for copy in held:
            copy.start()
        memory_grad[...] = jnp.zeros_like(memory_grad)
        gain_out_sum[...] = jnp.zeros_like(gain_out_sum)
        low_in_sum[...] = jnp.zeros_like(low_in_sum)
        low_out_sum[...] = jnp.zeros_like(low_out_sum)
        bias_sum[...] = jnp.zeros_like(bias_sum)
        at.meet()

    for where in range(2 * tiles):

        @pl.when(step == where)
        def _():
            ticks_at(where, 0)

    @pl.when(step == 0)
    def _():
        for copy in held[:5]:
            copy.wait()

    @pl.when(step < tiles)
    def _():
        tile = tiles - 1 - step
        here = pl.ds(pl.multiple_of(tile * ROWS, ROWS), ROWS)
        attn_tile = attn_ref[...]
        h_tile = h_ref[...]
        attn_turned[:, here] = jnp.transpose(attn_tile)
        h_turned[:, here] = jnp.transpose(h_tile)
        mixed_all[here, :] = mixed_ref[...]
        mixed_grad = dot(attn_tile, w_out[...], 1, 1)
        logits_parts = []
        for i in range(ROWS // BLOCK - 1, -1, -1):
            block = slice(i * BLOCK, (i + 1) * BLOCK)
            grads, logits_grad, gain_grad = backward_block(
                mixed_grad[block], query_ref[block, :], key_ref[block, :], value_ref[block, :], logits_ref[block, :],
                gate_ref[block, :], attended_ref[block, :], states_ref[i], gain_out_ref[...], memory_grad,
            )
            right[pl.ds(pl.multiple_of(tile * ROWS + i * BLOCK, BLOCK), BLOCK), :] = grads
            gain_out_sum[...] += gain_grad
            logits_parts.append(logits_grad)
            if i == ROWS // BLOCK - 1:
                for where in range(tiles):

                    @pl.when(step == where)
                    def _():
                        ticks_at(where, 1)

        logits_grad = jnp.concatenate(logits_parts[::-1], axis=0)
        high, rest = split_low(logits_grad)
        rank_high, rank_rest = split_low(low_rank_ref[...])
        bias_sum[...] += jnp.sum(logits_grad, axis=0, keepdims=True)
        low_out_sum[...] += dot(rank_high, high, 0, 0) + dot(rank_rest, high, 0, 0) + dot(rank_high, rest, 0, 0)
        low_rank_low = (dot(high, w_low_out[...], 1, 1) + dot(rest, w_low_out[...], 1, 1)).astype(BF16)
        low_in_sum[...] += dot(low_rank_low, h_tile, 0, 0)
        grads = right[here, :]
        part = (
            dot(grads[:, :keys], w_query[...], 1, 1)
            + dot(grads[:, keys : 2 * keys], w_key[...], 1, 1)
            + dot(grads[:, 2 * keys : 2 * keys + values], w_value[...], 1, 1)
            + dot(grads[:, 2 * keys + values :], w_gate[...], 1, 1)
            + dot(low_rank_low, w_low_in[...])
        )
        place = tile % own_tiles
        mine = tile // own_tiles == at.head

        @pl.when(mine)
        def _():
            h_grad[own_rows(place), :] = part

        @pl.when(jnp.logical_not(mine))
        def _():
            h_grad_out[own_rows(place), :] = part.astype(BF16)
            put(h_grad_out.at[own_rows(place)], h_grad_in.at[own_rows(place)], place)

    @pl.when(step == tiles)
    def _():
        for copy in held[5:]:
            copy.wait()
        gain_one = jnp.zeros((1, width), F32)
        for i in range(own_tiles):
            here = own_rows(i)
            wait(h_grad_in.at[here], i)
            wide = tokens_ref[here, :].astype(F32)
            scale = lax.rsqrt(jnp.mean(wide * wide, axis=1, keepdims=True) + EPSILON)
            normal = wide * scale
            grad = h_grad[here, :] + h_grad_in[here, :].astype(F32)
            tokens_out[here, :] = total_ref[here, :] + norm_backward(grad, gain_one_ref[...], normal, scale)
            gain_one += jnp.sum(grad * normal, axis=0, keepdims=True)
        small_own[...] = jnp.zeros_like(small_own)
        for i in range(width // 128):
            columns = slice(i * 128, (i + 1) * 128)
            small_own[GAIN_ONE + i : GAIN_ONE + i + 1, :] = gain_one[:, columns]
            small_own[GAIN_TWO + i : GAIN_TWO + i + 1, :] = gain_two_grad_ref[:, columns]
            small_own[LOW_IN + i * rank : LOW_IN + (i + 1) * rank, :] = low_in_sum[:, columns]
        for i in range(VALUE_HEAD // 128):
            small_own[GAIN_OUT + i : GAIN_OUT + i + 1, :] = gain_out_sum[:, i * 128 : (i + 1) * 128]
        for head in range(2):

            @pl.when(at.head == head)
            def _():
                base = decay_at + head * decay_slot
                for i in range(keys // 128):
                    columns = slice(i * 128, (i + 1) * 128)
                    small_own[base + i * rank : base + (i + 1) * rank, :] = low_out_sum[:, columns]
                    bias_at = base + keys // 128 * rank + i
                    small_own[bias_at : bias_at + 1, :] = bias_sum[:, columns]

        small(0)

    @pl.when(jnp.logical_and(step >= tiles, step < 2 * tiles))
    def _():
        part = step - tiles
        here = pl.ds(pl.multiple_of(part * ROWS, ROWS), ROWS)
        shape = (attn.shape[1], attn.shape[2], -1)
        edge = right.shape[1]
        attn[part, :, :, :edge] = dot(h_turned[here, :], right[...]).astype(BF16).reshape(shape)
        attn[part, :, :, edge:] = dot(attn_turned[here, :], mixed_all[...]).astype(BF16).reshape(shape)

    def spread(source, head):
        offset, start = 0, 0
        for size in [2 * mlp_chunks[0].stop // 3] * (len(mlp_chunks) // 2) + [mlp_chunks[0].stop // 3]:
            for part in range(3):
                target = pl.ds(pl.multiple_of(part * 2 * half + head * half + offset, 128), size)
                mlp_out[:, target] = source[:, start : start + size]
                start += size
            offset += size

    @pl.when(step == last_step - 1)
    def _():
        small(1)

    @pl.when(step == last_step)
    def _():
        for number in range(early, ticks):
            tick(number)
            if number - early in SMALL_TICKS:
                small(2 + SMALL_TICKS.index(number - early))
            if number == len(mlp_chunks) + 7:
                spread(summed.at[pl.ds(pl.multiple_of(at.head * rows, 8), rows)], at.head)
                for chunk, columns in enumerate(mlp_chunks):
                    wait(swapped.at[:, columns], 2 + chunk)
                spread(swapped, 1 - at.head)
        for i in range(own_tiles):
            sent(h_grad_out.at[own_rows(i)], pair_out.at[i], pair_in.at[i], at.sibling)
        for chunk, columns in enumerate(mlp_chunks):
            sent(swapped.at[:, columns], pair_out.at[2 + chunk], pair_in.at[2 + chunk], at.sibling)
        for side in sides:
            side.finish()


def backward(
    zero, groups, attn_low, h_low, query, key, value, gate, logits, low_rank, attended, mixed, states,
    w_query, w_key, w_value, w_gate, w_low_in, w_low_out, w_out, tokens, total, gain_one, gain_out, gain_two_grad,
):
    length, width = h_low.shape
    keys, values, heads = query.shape[1], value.shape[1], states.shape[1]
    rank = w_low_out.shape[0]
    own = tokens.shape[0]
    tiles = length // ROWS
    rows = width // 16
    mlp_count = 2 * groups.shape[0] + 1
    mlp_width = zero.shape[-1] * mlp_count
    mlp_chunks = chunk_columns(mlp_width, [zero.shape[-1] // 128] * mlp_count)
    attn_width = 2 * keys + 3 * values
    attn_tiles = attn_width // 128
    sizes = [3] * ((attn_tiles - 4) // 3) + [(attn_tiles - 4) % 3 + 1, 2, 1]
    attn_chunks = chunk_columns(attn_width, sizes)
    attn_count = len(attn_chunks)
    small_shape = (small_rows(width, rank, keys)[2], 128)
    vmem = pl.BlockSpec(memory_space=pltpu.VMEM)

    def rows_spec(columns):
        return pl.BlockSpec((ROWS, columns), lambda i: (jnp.maximum(tiles - 1 - i, 0), 0))

    buffers = []
    for columns in (mlp_width, attn_width):
        buffers += [pltpu.VMEM((n, rows, columns), BF16) for n in (2, 2, 4, 4, 3)]
    streamed = [attn_low, h_low, query, key, value, gate, logits, low_rank, attended, mixed]
    constant = [
        w_query, w_key, w_value, w_gate, w_low_in, w_low_out, w_out, tokens, total,
        gain_one.reshape(1, -1), gain_out.reshape(1, -1), gain_two_grad.reshape(1, -1),
    ]
    return pl.pallas_call(
        functools.partial(backward_kernel, mlp_width // 3, mlp_chunks, attn_chunks),
        grid=(2 * tiles + 1,),
        in_specs=[ANY, ANY]
        + [rows_spec(a.shape[1]) for a in streamed]
        + [
            pl.BlockSpec(
                (ROWS // BLOCK, heads, KEY_HEAD, VALUE_HEAD), lambda i: (jnp.maximum(tiles - 1 - i, 0), 0, 0, 0)
            )
        ]
        + [whole(a.shape) if i in (4, 5) or i > 8 else ANY for i, a in enumerate(constant)],
        out_specs=[vmem, vmem, vmem, vmem],
        out_shape=[
            jax.ShapeDtypeStruct((rows // 2, 2 * mlp_width), F32),
            jax.ShapeDtypeStruct((rows, attn_width), F32),
            jax.ShapeDtypeStruct(small_shape, F32),
            jax.ShapeDtypeStruct((own, width), F32),
        ],
        scratch_shapes=[
            pltpu.VMEM((4, 4, rows, mlp_width), BF16),
            pltpu.VMEM((4, 4, rows, attn_width), BF16),
            *buffers,
            pltpu.VMEM((rows, mlp_width), F32),
            pltpu.VMEM((rows // 2, mlp_width), F32),
            pltpu.VMEM(small_shape, F32),
            pltpu.VMEM((3,) + small_shape, F32),
            pltpu.VMEM((7,) + small_shape, F32),
            pltpu.VMEM((width, length), BF16),
            pltpu.VMEM((width, length), BF16),
            pltpu.VMEM((length, 2 * keys + 2 * values), BF16),
            pltpu.VMEM((length, values), BF16),
            pltpu.VMEM((own, width), F32),
            pltpu.VMEM((own, width), BF16),
            pltpu.VMEM((own, width), BF16),
            pltpu.VMEM((heads, KEY_HEAD, VALUE_HEAD), F32),
            pltpu.VMEM((1, VALUE_HEAD), F32),
            pltpu.VMEM((rank, width), F32),
            pltpu.VMEM((rank, keys), F32),
            pltpu.VMEM((1, keys), F32),
            *[pltpu.VMEM(a.shape, a.dtype) for a in (w_query, w_key, w_value, w_gate, w_out, tokens, total)],
            pltpu.SemaphoreType.DMA((7,)),
            pltpu.SemaphoreType.DMA((mlp_count,)),
            pltpu.SemaphoreType.DMA((mlp_count, 7)),
            pltpu.SemaphoreType.DMA((mlp_count, 7)),
            pltpu.SemaphoreType.DMA((attn_count, 7)),
            pltpu.SemaphoreType.DMA((attn_count, 7)),
            pltpu.SemaphoreType.DMA((2 + mlp_count,)),
            pltpu.SemaphoreType.DMA((2 + mlp_count,)),
            pltpu.SemaphoreType.DMA((7,)),
            pltpu.SemaphoreType.DMA((7,)),
        ],
        compiler_params=pltpu.CompilerParams(
            collective_id=1, has_side_effects=True, vmem_limit_bytes=63 << 20
        ),
        name="backward",
    )(zero, groups, *streamed, states, *constant)


def emit_kernel(
    half, edges, mlp_ref, attn_ref, small_ref, tokens_ref, output_ref,
    output_out, tokens_out, gain_one_out, query_out, key_out, value_out, gate_out, low_in_out, low_out_out, bias_out,
    gain_out_out, out_out, gain_two_out, mlp_out, tokens, output, mlp, attn, load_sems, sems,
):
    staged = [(attn_ref, attn)]
    moves = []
    for i, target in enumerate((query_out, key_out, value_out, gate_out, out_out)):
        moves.append((attn.at[:, edges[i] : edges[i + 1]], target))
    for source, stage, target in (
        (tokens_ref, tokens, tokens_out), (mlp_ref, mlp, mlp_out), (output_ref, output, output_out)
    ):
        size = source.shape[0] // 2
        for rows in (pl.ds(0, size), pl.ds(size, size)):
            staged.append((source.at[rows], stage.at[rows]))
            moves.append((stage.at[rows], target.at[rows]))
    loads = [pltpu.make_async_copy(source, target, load_sems.at[i]) for i, (source, target) in enumerate(staged)]
    for load in loads:
        load.start()
    copies = [pltpu.make_async_copy(source, target, sems.at[i]) for i, (source, target) in enumerate(moves)]
    for i, load in enumerate(loads):
        load.wait()
        for copy in copies[:5] if i == 0 else copies[4 + i : 5 + i]:
            copy.start()
    rank, width = low_in_out.shape
    keys = low_out_out.shape[1]
    decay_at, decay_slot, _ = small_rows(width, rank, keys)
    for i in range(width // 128):
        columns = slice(i * 128, (i + 1) * 128)
        gain_one_out[:, columns] = small_ref[GAIN_ONE + i : GAIN_ONE + i + 1, :]
        gain_two_out[:, columns] = small_ref[GAIN_TWO + i : GAIN_TWO + i + 1, :]
        low_in_out[:, columns] = small_ref[LOW_IN + i * rank : LOW_IN + (i + 1) * rank, :]
    for i in range(VALUE_HEAD // 128):
        gain_out_out[:, i * 128 : (i + 1) * 128] = small_ref[GAIN_OUT + i : GAIN_OUT + i + 1, :]
    for head in range(2):

        @pl.when(lax.axis_index("head") == head)
        def _():
            base = decay_at + head * decay_slot
            for i in range(keys // 128):
                columns = slice(i * 128, (i + 1) * 128)
                low_out_out[:, columns] = small_ref[base + i * rank : base + (i + 1) * rank, :]
                bias_at = base + keys // 128 * rank + i
                bias_out[:, columns] = small_ref[bias_at : bias_at + 1, :]

    for copy in copies:
        copy.wait()


def emit(mlp, attn, small, tokens, output, keys, values, rank):
    rows, width = attn.shape[0], tokens.shape[1]
    edges = [0, keys, 2 * keys, 2 * keys + values, 2 * keys + 2 * values, 2 * keys + 3 * values]
    vmem = pl.BlockSpec(memory_space=pltpu.VMEM)
    shapes = [
        (output.shape, BF16, ANY), (tokens.shape, F32, ANY), ((1, width), F32, vmem), ((rows, keys), F32, ANY),
        ((rows, keys), F32, ANY), ((rows, values), F32, ANY), ((rows, values), F32, ANY), ((rank, width), F32, vmem),
        ((rank, keys), F32, vmem), ((1, keys), F32, vmem), ((1, VALUE_HEAD), F32, vmem), ((rows, values), F32, ANY),
        ((1, width), F32, vmem), (mlp.shape, F32, ANY),
    ]
    return pl.pallas_call(
        functools.partial(emit_kernel, mlp.shape[1] // 6, edges),
        in_specs=[ANY, ANY, vmem, ANY, ANY],
        out_specs=[space for _, _, space in shapes],
        out_shape=[jax.ShapeDtypeStruct(shape, kind) for shape, kind, _ in shapes],
        scratch_shapes=[
            pltpu.VMEM(tokens.shape, F32),
            pltpu.VMEM(output.shape, BF16),
            pltpu.VMEM(mlp.shape, F32),
            pltpu.VMEM(attn.shape, F32),
            pltpu.SemaphoreType.DMA((7,)),
            pltpu.SemaphoreType.DMA((11,)),
        ],
        compiler_params=pltpu.CompilerParams(vmem_limit_bytes=60 << 20),
        name="emit",
    )(mlp, attn, small, tokens, output)


def swap(value):
    return lax.ppermute(value, "head", [(0, 1), (1, 0)])


def ordered(own, other, axis):
    size = own.shape[axis]
    joined = jnp.concatenate([own, other, own], axis=axis)
    return lax.dynamic_slice_in_dim(joined, lax.axis_index("head") * size, 2 * size, axis)


def half_of(value, which, axis):
    size = value.shape[axis] // 2
    return lax.dynamic_slice_in_dim(value, which * size, size, axis)


def sum_rows(partial, here):
    other = swap(half_of(partial, 1 - here, 0).astype(BF16))
    return half_of(partial, here, 0) + other.astype(F32)


def norm_backward(grad_in, gain, normed_in, scale_in):
    scaled = grad_in * gain
    return scale_in * (scaled - normed_in * jnp.mean(scaled * normed_in, axis=-1, keepdims=True))


def per_device(
    tokens, lengths, initial_memory, norm_attn_gain, w_query, w_key, w_value, w_gate_out, w_low_in, w_low_out,
    decay_bias, out_gain, w_out, norm_mlp_gain, w_mlp, cotangent,
):
    here = lax.axis_index("head")
    own_rows = tokens.shape[1]
    keys = w_query.shape[1]
    values = w_value.shape[1]
    hidden = w_mlp.shape[1] // 3
    half = hidden // 2
    shard_rows = w_mlp.shape[0]
    square = lax.axis_size("dp") == 16

    tokens_own = tokens[0]
    if square:
        (
            h_low, query, key, value, gate, logits, low_rank, attended, mixed, states,
            grad_zero, grad_mlp, output, resid_total, attn_low, gain_two_grad,
        ) = layer(
            tokens_own, cotangent[0], lengths, norm_attn_gain, norm_mlp_gain, out_gain, decay_bias,
            initial_memory[0], w_query, w_key, w_value, w_gate_out, w_low_in.T, w_low_out, w_out, w_mlp,
        )
        grad_mlp, attn_grads, packed, tokens_grad = backward(
            grad_zero, grad_mlp, attn_low, h_low, query, key, value, gate, logits, low_rank, attended, mixed, states,
            w_query, w_key, w_value, w_gate_out, w_low_in.T, w_low_out, w_out, tokens_own, resid_total,
            norm_attn_gain, out_gain, gain_two_grad,
        )
        results = emit(grad_mlp, attn_grads, packed, tokens_grad, output, keys, values, w_low_out.shape[0])
        (
            output, tokens_grad, gain_one_grad, query_grad, key_grad, value_grad, gate_grad, low_in_grad, low_out_grad,
            bias_grad, out_gain_grad, out_grad, gain_two_grad, grad_mlp,
        ) = results
        return (
            output[None], tokens_grad[None], gain_one_grad[0], query_grad, key_grad, value_grad, gate_grad,
            low_in_grad.T, low_out_grad, bias_grad[0], out_gain_grad[0], out_grad.T, gain_two_grad[0], grad_mlp,
        )
    pieces = w_mlp.reshape(shard_rows, 3, 2, half)
    own_piece = lax.dynamic_index_in_dim(pieces, here, 2, keepdims=False)
    other_piece = lax.dynamic_index_in_dim(pieces, 1 - here, 2, keepdims=False)
    positions = here * own_rows + lax.iota(jnp.int32, own_rows)
    row_mask = (positions < lengths[0]).astype(F32)[:, None]
    resid_grad = row_mask * cotangent[0].astype(F32)
    low_own = resid_grad.astype(BF16)
    pair = swap(other_piece.reshape(shard_rows, 3 * half))
    weights = lax.all_gather(
        ordered(own_piece.reshape(shard_rows, 3 * half), pair, 0), "dp", axis=0, tiled=True
    )
    tokens_wide = ordered(tokens_own, swap(tokens_own), 0).astype(F32)
    length = tokens_wide.shape[0]
    scale_one = lax.rsqrt(jnp.mean(tokens_wide * tokens_wide, axis=1, keepdims=True) + EPSILON)
    h_low = (tokens_wide * scale_one * norm_attn_gain).astype(BF16)
    query = dot(h_low, w_query).astype(BF16)
    key = dot(h_low, w_key).astype(BF16)
    value = dot(h_low, w_value).astype(BF16)
    gate = dot(h_low, w_gate_out)
    low_rank = dot(h_low, w_low_in)
    low_high, low_rest = split_low(low_rank)
    logits = dot(low_high, w_low_out) + dot(low_rest, w_low_out) + decay_bias
    attended, mixed, states = attention_forward(query, key, value, logits, gate, out_gain, initial_memory[0])
    resid = tokens_own.astype(F32) + sum_rows(dot(mixed, w_out), here)
    scale_two = lax.rsqrt(jnp.mean(resid * resid, axis=1, keepdims=True) + EPSILON)
    normal_two = resid * scale_two
    h_two_own = (normal_two * norm_mlp_gain).astype(BF16)
    h_two = ordered(h_two_own, swap(h_two_own), 0)
    resid_low = ordered(low_own, swap(low_own), 0)
    pre_gate = dot(h_two, weights[:, :half])
    up_part = dot(h_two, weights[:, half : 2 * half])
    pre_sigmoid = sigmoid(pre_gate)
    inner = (pre_gate * pre_sigmoid * up_part).astype(BF16)
    inner_grad = dot(resid_low, weights[:, 2 * half :])
    pre_grad = (
        inner_grad * up_part * pre_sigmoid * (1.0 + pre_gate * (1.0 - pre_sigmoid))
    ).astype(BF16)
    up_grad = (inner_grad * pre_gate * pre_sigmoid).astype(BF16)
    mlp_out = sum_rows(dot(inner, weights[:, 2 * half :], 1, 1), here)
    output = (row_mask * (resid + mlp_out)).astype(BF16)[None]
    h_two_grad = sum_rows(
        dot(pre_grad, weights[:, :half], 1, 1) + dot(up_grad, weights[:, half : 2 * half], 1, 1), here
    )
    grad_mlp = jnp.concatenate(
        [
            dot(h_two, pre_grad, 0, 0).astype(BF16),
            dot(h_two, up_grad, 0, 0).astype(BF16),
            dot(resid_low, inner, 0, 0).astype(BF16),
        ],
        axis=1,
    )
    resid_total = resid_grad + norm_backward(h_two_grad, norm_mlp_gain, normal_two, scale_two)
    gain_two_grad = jnp.sum(h_two_grad * normal_two, axis=0)
    attn_own = resid_total.astype(BF16)
    attn_low = ordered(attn_own, swap(attn_own), 0)

    mixed_grad = dot(attn_low, w_out, 1, 1)
    out_grad = dot(attn_low, mixed, 0, 0)
    query_grad, key_grad, value_grad, gate_grad, logits_grad, out_gain_grad = attention_backward(
        mixed_grad, query, key, value, logits, gate, attended, states, out_gain
    )
    bias_grad = jnp.sum(logits_grad, axis=0)
    grad_high, grad_rest = split_low(logits_grad)
    low_out_grad = (
        dot(low_high, grad_high, 0, 0) + dot(low_rest, grad_high, 0, 0) + dot(low_high, grad_rest, 0, 0)
    )
    low_rank_low = (dot(grad_high, w_low_out, 1, 1) + dot(grad_rest, w_low_out, 1, 1)).astype(BF16)
    low_in_grad = dot(h_low, low_rank_low, 0, 0)
    attn_grads = jnp.concatenate(
        [
            dot(h_low, query_grad, 0, 0).astype(BF16),
            dot(h_low, key_grad, 0, 0).astype(BF16),
            dot(h_low, value_grad, 0, 0).astype(BF16),
            dot(h_low, gate_grad, 0, 0).astype(BF16),
            out_grad.astype(BF16),
        ],
        axis=1,
    )
    h_grad = sum_rows(
        dot(query_grad, w_query, 1, 1)
        + dot(key_grad, w_key, 1, 1)
        + dot(value_grad, w_value, 1, 1)
        + dot(gate_grad, w_gate_out, 1, 1)
        + dot(low_rank_low, w_low_in, 1, 1),
        here,
    )
    own_wide = tokens_own.astype(F32)
    own_scale = lax.rsqrt(jnp.mean(own_wide * own_wide, axis=1, keepdims=True) + EPSILON)
    normal_own = own_wide * own_scale
    tokens_grad = resid_total + norm_backward(h_grad, norm_attn_gain, normal_own, own_scale)
    gain_one_grad = jnp.sum(h_grad * normal_own, axis=0)
    low_rank_width = w_low_out.shape[0]
    decay_part = jnp.concatenate([low_out_grad, bias_grad[None]], axis=0)
    slots = jnp.zeros((2,) + decay_part.shape, F32)
    slots = lax.dynamic_update_slice(slots, decay_part[None], (here, 0, 0))
    packed = jnp.concatenate(
        [
            gain_one_grad, gain_two_grad, out_gain_grad.reshape(-1), low_in_grad.reshape(-1), slots.reshape(-1),
        ]
    )
    packed = lax.psum(packed, ("dp", "head"))
    attn_grads = lax.psum_scatter(attn_grads, "dp", scatter_dimension=0, tiled=True).astype(F32)
    grad_mlp = lax.psum_scatter(grad_mlp, "dp", scatter_dimension=0, tiled=True)
    own_half = half_of(grad_mlp, here, 0)
    other_half = swap(half_of(grad_mlp, 1 - here, 0))
    grad_mlp = ordered(
        own_half.reshape(shard_rows, 3, 1, half), other_half.reshape(shard_rows, 3, 1, half), 2
    ).reshape(shard_rows, 3 * hidden).astype(F32)
    width = gain_one_grad.shape[0]
    edges = [width, 2 * width, 2 * width + VALUE_HEAD]
    edges.append(edges[-1] + width * low_rank_width)
    low_in_grad = packed[edges[2] : edges[3]].reshape(width, low_rank_width)
    decay_part = lax.dynamic_index_in_dim(packed[edges[3] :].reshape(slots.shape), here, 0, keepdims=False)
    low_out_grad, bias_grad = decay_part[:low_rank_width], decay_part[low_rank_width]
    gain_one_grad, gain_two_grad = packed[: edges[0]], packed[edges[0] : edges[1]]
    out_gain_grad = packed[edges[1] : edges[2]]
    return (
        output,
        tokens_grad[None],
        gain_one_grad,
        attn_grads[:, :keys],
        attn_grads[:, keys : 2 * keys],
        attn_grads[:, 2 * keys : 2 * keys + values],
        attn_grads[:, 2 * keys + values : 2 * keys + 2 * values],
        low_in_grad,
        low_out_grad,
        bias_grad,
        out_gain_grad,
        attn_grads[:, 2 * keys + 2 * values :].T,
        gain_two_grad,
        grad_mlp,
    )


def solution(mesh):
    return jax.shard_map(
        per_device,
        mesh=mesh,
        in_specs=(
            P("dp", "head", None),
            P("dp"),
            P("dp", "head", None, None),
            P(),
            P(None, "head"),
            P(None, "head"),
            P(None, "head"),
            P(None, "head"),
            P(),
            P(None, "head"),
            P("head"),
            P(),
            P("head", None),
            P(),
            P(("dp", "head"), None),
            P("dp", "head", None),
        ),
        out_specs=(
            P("dp", "head", None),
            P("dp", "head", None),
            P(),
            P("dp", "head"),
            P("dp", "head"),
            P("dp", "head"),
            P("dp", "head"),
            P(),
            P(None, "head"),
            P("head"),
            P(),
            P("head", "dp"),
            P(),
            P(("dp", "head"), None),
        ),
        check_vma=False,
    )
```
